32 devices in a mesh: dp: 16 (over z, y, x), tensor: 2 (over core).
Axes of the slice: x: 2, y: 2, z: 4, core: 2. Of those that a mesh axis runs over, the one named last changes fastest.
Arguments:
- frames: bfloat16 [2, 32, 512, 512], P(None, ('dp', 'tensor')), may hold values from -6 to 6
- lengths: int32 [2, 32], P(None, 'dp'), may hold values from 128 to 512, as said below
- ffn1_in: bfloat16 [512, 2048], P('dp', 'tensor'), may hold values from -0.25 to 0.25
- ffn1_out: bfloat16 [2048, 512], P('tensor', 'dp'), may hold values from -0.125 to 0.125
- ffn1_bias: bfloat16 [16, 128], P('tensor', 'dp'), may hold values from -3 to 3
- qkv_weight: bfloat16 [512, 3, 512], P('dp', None, 'tensor'), may hold values from -0.25 to 0.25
- pos_weight: bfloat16 [512, 512], P('dp', 'tensor'), may hold values from -0.25 to 0.25
- out_weight: bfloat16 [512, 512], P('tensor', 'dp'), may hold values from -1 to 1
- attn_bias: bfloat16 [4, 4, 128], P(None, 'tensor', 'dp'), may hold values from -3 to 3
- conv_in: bfloat16 [512, 2, 512], P('dp', None, 'tensor'), may hold values from -0.25 to 0.25
- conv_out: bfloat16 [512, 512], P('tensor', 'dp'), may hold values from -0.25 to 0.25
- conv_channel: bfloat16 [13, 4, 128], P(None, 'tensor', 'dp'), may hold values from -2 to 2
- ffn2_in: bfloat16 [512, 2048], P('dp', 'tensor'), may hold values from -0.25 to 0.25
- ffn2_out: bfloat16 [2048, 512], P('tensor', 'dp'), may hold values from -0.125 to 0.125
- ffn2_bias: bfloat16 [16, 128], P('tensor', 'dp'), may hold values from -3 to 3
- norm_params: bfloat16 [14, 512], P(None, ('dp', 'tensor')), may hold values from -1.2 to 1.4
- cotangent: bfloat16 [2, 32, 512, 512], P(None, ('dp', 'tensor')), may hold values from -6 to 6
Outputs:
- activations: bfloat16 [2, 32, 512, 512], P(None, ('dp', 'tensor'))
- frame_grad: bfloat16 [2, 32, 512, 512], P(None, ('dp', 'tensor'))
- ffn1_in_grad: float32 [512, 2048], P('dp', 'tensor')
- ffn1_out_grad: float32 [2048, 512], P('tensor', 'dp')
- ffn1_bias_grad: float32 [16, 128], P('tensor', 'dp')
- qkv_grad: float32 [512, 3, 512], P('dp', None, 'tensor')
- pos_grad: float32 [512, 512], P('dp', 'tensor')
- out_grad: float32 [512, 512], P('tensor', 'dp')
- attn_bias_grad: float32 [4, 4, 128], P(None, 'tensor', 'dp')
- conv_in_grad: float32 [512, 2, 512], P('dp', None, 'tensor')
- conv_out_grad: float32 [512, 512], P('tensor', 'dp')
- conv_channel_grad: float32 [13, 4, 128], P(None, 'tensor', 'dp')
- ffn2_in_grad: float32 [512, 2048], P('dp', 'tensor')
- ffn2_out_grad: float32 [2048, 512], P('tensor', 'dp')
- ffn2_bias_grad: float32 [16, 128], P('tensor', 'dp')
- norm_grad: float32 [14, 512], P(None, ('dp', 'tensor'))
The draws below stay inside these ranges and needn't reach their ends.
Inputs may be any that keep to these rules, and one draw needn't show every extreme that they name: `lengths`: the last utterance of every micro-batch has 512 frames.
All inputs are finite; a program needn't handle non-finite values.
Results may differ from the reference program's by a relative error of at most 0.04.
Values may be sent and summed in bfloat16 or wider, within the bound.
A program may use at most 256 MiB of HBM per device.

```python
import math
import jax
import jax.numpy as jnp
from jax import lax

D = 512
HEADS = 8
DK = 64
FF = 2048
KERNEL = 9
MAXLEN = 512
MB = 2
SEQS = 2
UTTS = 32


def draw_lengths(key, part):
    device_count = UTTS // SEQS
    device = jnp.arange(UTTS, dtype=jnp.int32) // SEQS
    low_len = MAXLEN // 4 + (MAXLEN - MAXLEN // 4) * device // device_count
    offsets = jax.random.randint(key, (MB, UTTS), 0, MAXLEN // 6 + 1)
    lengths_all = jnp.minimum(low_len[None, :] + offsets, MAXLEN)
    lengths_all = lengths_all.at[:, UTTS - 1].set(MAXLEN)
    return lengths_all.astype(jnp.int32)


def draw_conv_channel(key, part):
    full_shape = (4 + KERNEL, D // 128, 128)
    base_draw = jnp.clip(jax.random.normal(key, full_shape, jnp.float32), -4.0, 4.0)
    lifted = jax.random.uniform(jax.random.fold_in(key, 1), full_shape, jnp.float32, 0.6, 1.4)
    row_ids = jnp.arange(4 + KERNEL, dtype=jnp.int32)[:, None, None]
    row_scale = jnp.where(row_ids < 2, 0.5, jnp.where(row_ids == 3, 0.3, 1.0 / 3.0))
    return jnp.where(row_ids == 2, lifted, row_scale * base_draw).astype(jnp.bfloat16)


def draw_norm_params(key, part):
    base_draw = jnp.clip(jax.random.normal(key, (14, D), jnp.float32), -4.0, 4.0)
    lifted = jax.random.uniform(jax.random.fold_in(key, 1), (14, D), jnp.float32, 0.6, 1.4)
    row_ids = jnp.arange(14, dtype=jnp.int32)[:, None]
    return jnp.where(row_ids % 3 == 0, lifted, 0.3 * base_draw).astype(jnp.bfloat16)


def raised(entries, stream_key, source, target, parts, factor):
    owner, partner = [(jnp.arange(entries.shape[axis_at]) // (entries.shape[axis_at] // parts)).reshape([-1 if axis == axis_at else 1 for axis in range(entries.ndim)]) for axis_at in (source, target)]
    chosen = jax.random.permutation(stream_key, parts)[partner]
    strong = (owner == chosen) | (owner == (partner + parts // 2) % parts)
    return jnp.where(strong, factor * entries, entries)


def block_scale(key, dims, shards, least, top_value):
    def one(axis_at, parts):
        steps = jax.random.uniform(jax.random.fold_in(jax.random.fold_in(key, 6), axis_at), (parts,), jnp.float32, least / len(shards), top_value / len(shards))
        return jnp.repeat(jnp.exp(steps), dims[axis_at] // parts).reshape((-1,) + (1,) * (len(dims) - axis_at - 1))

    level = one(*shards[0])
    for cut in shards[1:]:
        level = level * one(*cut)
    return level


def centred(rng, dims, scale, bound, split=(), held_as=jnp.bfloat16):
    drawn = jax.random.normal(rng, dims, jnp.float32) * scale
    if len(split) > 0:
        drawn = block_scale(rng, dims, split, -0.22, 0.18) * drawn
    return jnp.clip(drawn, min=-bound, max=bound).astype(held_as)


def bell_draw_with(key, shape, scale, most, split, heavy, held_as=jnp.bfloat16):
    array = scale * jax.random.normal(key, shape, jnp.float32)
    if split:
        array = array * block_scale(key, shape, split, -0.22, 0.18)
    return jnp.clip(raised(array, jax.random.fold_in(key, 3), *heavy), -most, most).astype(held_as)


def setup_inputs(seed: int = 0) -> dict:
    streams_of = jax.random.split(jax.random.key(seed), 18)
    frames = centred(streams_of[0], (MB, UTTS, MAXLEN, D), 1.0, 6.0, ((1, 32),))
    lengths = draw_lengths(jax.random.fold_in(streams_of[17], 71), 0)
    ffn1_in = centred(streams_of[2], (D, FF), D ** -0.5, 0.25, ((0, 16), (1, 2)))
    ffn1_out = centred(streams_of[3], (FF, D), FF ** -0.5, 0.125, ((0, 2), (1, 16)))
    ffn1_bias = centred(streams_of[4], (FF // 128, 128), 0.5, 3.0, ((0, 2), (1, 16)))
    qkv_weight = centred(streams_of[5], (D, 3, D), D ** -0.5, 0.25, ((0, 16), (2, 2)))
    pos_weight = centred(streams_of[6], (D, D), D ** -0.5, 0.25, ((0, 16), (1, 2)))
    out_weight = centred(streams_of[7], (D, D), (D // 16) ** -0.5, 1.0, ((0, 2), (1, 16)))
    attn_bias = centred(streams_of[8], (4, D // 128, 128), 0.5, 3.0, ((1, 2), (2, 16)))
    conv_in = centred(streams_of[9], (D, 2, D), D ** -0.5, 0.25, ((0, 16), (2, 2)))
    conv_out = centred(streams_of[10], (D, D), D ** -0.5, 0.25, ((0, 2), (1, 16)))
    conv_channel = draw_conv_channel(jax.random.fold_in(streams_of[17], 71), 0)
    ffn2_in = centred(streams_of[12], (D, FF), D ** -0.5, 0.25, ((0, 16), (1, 2)))
    ffn2_out = centred(streams_of[13], (FF, D), FF ** -0.5, 0.125, ((0, 2), (1, 16)))
    ffn2_bias = centred(streams_of[14], (FF // 128, 128), 0.5, 3.0, ((0, 2), (1, 16)))
    norm_params = draw_norm_params(jax.random.fold_in(streams_of[17], 71), 0)
    cotangent = bell_draw_with(streams_of[16], (MB, UTTS, MAXLEN, D), 1.0, 6.0, ((1, 32),), (1, 3, 32, 2.75))
    return {"frames": frames, "lengths": lengths, "ffn1_in": ffn1_in, "ffn1_out": ffn1_out, "ffn1_bias": ffn1_bias, "qkv_weight": qkv_weight, "pos_weight": pos_weight, "out_weight": out_weight, "attn_bias": attn_bias, "conv_in": conv_in, "conv_out": conv_out, "conv_channel": conv_channel, "ffn2_in": ffn2_in, "ffn2_out": ffn2_out, "ffn2_bias": ffn2_bias, "norm_params": norm_params, "cotangent": cotangent}


norm_eps = 1e-05
mask_fill = -1000000000.0
top_precision = lax.Precision.HIGHEST

@jax.custom_vjp
def low(v):
    return lax.optimization_barrier(v.astype(jnp.bfloat16)).astype(jnp.float32)

@jax.custom_vjp
def low_back(v):
    return v

def low_keep(v):
    return (low(v), None)

def low_pass(kept, grad):
    return (grad,)

def back_keep(v):
    return (v, None)

def back_low(kept, grad):
    return (low(grad),)
low.defvjp(low_keep, low_pass)
low_back.defvjp(back_keep, back_low)

def position_table(length, width):
    offsets = (length - 1 - jnp.arange(2 * length - 1, dtype=jnp.int32)).astype(jnp.float32)
    freq_rates = jnp.exp(jnp.arange(0, width, 2, dtype=jnp.int32).astype(jnp.float32) * (-math.log(10000.0) / width))
    angles = offsets[:, None] * freq_rates[None, :]
    return jnp.stack([jnp.sin(angles), jnp.cos(angles)], axis=-1).reshape(2 * length - 1, width)

def rel_shift(scores):
    leading = scores.shape[:-2]
    row_count = scores.shape[-2]
    col_count = scores.shape[-1]
    padded = jnp.pad(scores, [(0, 0)] * len(leading) + [(0, 0), (1, 0)])
    padded = padded.reshape(leading + (col_count + 1, row_count))
    return padded[..., 1:, :].reshape(leading + (row_count, col_count))[..., :row_count]

def layer_norm(values, gain, shift):
    average = lax.optimization_barrier(jnp.mean(values, axis=-1, keepdims=True))
    centered = values - average
    spread_sq = lax.optimization_barrier(jnp.mean(centered * centered, axis=-1, keepdims=True))
    return centered * lax.rsqrt(spread_sq + norm_eps) * gain + shift

def swish_act(values):
    return values * jax.nn.sigmoid(values)

def depthwise(signal, taps_all):
    reach = (taps_all.shape[0] - 1) // 2
    length_now = signal.shape[1]
    padded = jnp.pad(signal, ((0, 0), (reach, reach), (0, 0)))
    summed = jnp.zeros_like(signal)
    for tap_idx in range(taps_all.shape[0]):
        summed = summed + taps_all[tap_idx] * padded[:, tap_idx:tap_idx + length_now]
    return summed

def feed_forward(residual, gain, shift, input_weight, input_bias, output_weight, out_bias):
    normed = low(layer_norm(residual, gain, shift))
    hidden_rows = low_back(jnp.matmul(normed, input_weight, precision=top_precision) + input_bias)
    activated_rows = low(swish_act(hidden_rows))
    return low_back(jnp.matmul(activated_rows, output_weight, precision=top_precision) + out_bias)

def attention(residual, valid, gain, shift, query_key_value_weight, pos_w, out_w, vectors, out_bias, table):
    normed = low(layer_norm(residual, gain, shift))

    def one_utterance(paired):
        rows_in, valid_one = paired
        projected_rows = jnp.einsum('ld,dkc->lkc', rows_in, query_key_value_weight, precision=top_precision)
        query = low_back(projected_rows[:, 0] + vectors[0])
        key_rows = low(low_back(projected_rows[:, 1])).reshape(MAXLEN, HEADS, DK)
        value_rows = low(low_back(projected_rows[:, 2] + vectors[1])).reshape(MAXLEN, HEADS, DK)
        query_u = low(query + vectors[2]).reshape(MAXLEN, HEADS, DK)
        query_v = low(query + vectors[3]).reshape(MAXLEN, HEADS, DK)
        pos_rows = low(low_back(jnp.matmul(table, pos_w, precision=top_precision))).reshape(2 * MAXLEN - 1, HEADS, DK)
        content = jnp.einsum('qhd,khd->hqk', query_u, key_rows, precision=top_precision)
        relative = rel_shift(jnp.einsum('qhd,phd->hqp', query_v, pos_rows, precision=top_precision))
        scores = low_back((content + relative) * (1.0 / math.sqrt(DK)))
        scores = jnp.where(valid_one[None, None, :] > 0.5, scores, mask_fill)
        attn_probs = jax.nn.softmax(scores, axis=-1)
        mixed = jnp.einsum('hqk,khd->qhd', low(attn_probs), value_rows, precision=top_precision)
        return low(low_back(mixed)).reshape(MAXLEN, D)
    mixed_all = lax.map(jax.checkpoint(one_utterance), (normed, valid))
    return low_back(jnp.matmul(mixed_all, out_w, precision=top_precision) + out_bias)

def convolve(residual, valid, gain, shift, input_weight, output_weight, vectors, out_bias):
    normed = low(layer_norm(residual, gain, shift))
    halves = low_back(jnp.einsum('uld,dkc->ulkc', normed, input_weight, precision=top_precision) + vectors[0:2])
    gated = halves[:, :, 0] * jax.nn.sigmoid(halves[:, :, 1]) * valid[:, :, None]
    mixed = depthwise(gated, vectors[4:])
    mask_three = valid[:, :, None]
    counted = jnp.sum(valid)
    average = lax.optimization_barrier(jnp.sum(mixed * mask_three, axis=(0, 1))) / counted
    variance = lax.optimization_barrier(jnp.sum(mixed * mixed * mask_three, axis=(0, 1))) / counted - average * average
    normal = (mixed - average) * lax.rsqrt(variance + norm_eps)
    activated_rows = low(swish_act(normal * vectors[2] + vectors[3]))
    return low_back(jnp.matmul(activated_rows, output_weight, precision=top_precision) + out_bias)

def layer_block(residual, valid, weights_all, table):
    f1_in, f1_out, f1_bias, query_key_value_weight, pos_w, out_w, attn_vec, cv_in, cv_out, cv_vec, f2_in, f2_out, f2_bias, norm_rows = weights_all
    residual = residual + 0.5 * feed_forward(residual, norm_rows[0], norm_rows[1], f1_in, f1_bias.reshape(FF), f1_out, norm_rows[2])
    residual = residual + attention(residual, valid, norm_rows[3], norm_rows[4], query_key_value_weight, pos_w, out_w, attn_vec.reshape(4, D), norm_rows[5], table)
    residual = residual + convolve(residual, valid, norm_rows[6], norm_rows[7], cv_in, cv_out, cv_vec.reshape(4 + KERNEL, D), norm_rows[8])
    residual = residual + 0.5 * feed_forward(residual, norm_rows[9], norm_rows[10], f2_in, f2_bias.reshape(FF), f2_out, norm_rows[11])
    return layer_norm(residual, norm_rows[12], norm_rows[13])

def reference(frames, lengths, ffn1_in, ffn1_out, ffn1_bias, qkv_weight, pos_weight, out_weight, attn_bias, conv_in, conv_out, conv_channel, ffn2_in, ffn2_out, ffn2_bias, norm_params, cotangent):
    weights_all = tuple((item.astype(jnp.float32) for item in (ffn1_in, ffn1_out, ffn1_bias, qkv_weight, pos_weight, out_weight, attn_bias, conv_in, conv_out, conv_channel, ffn2_in, ffn2_out, ffn2_bias, norm_params)))
    table = low(position_table(MAXLEN, D))
    positions = jnp.arange(MAXLEN, dtype=jnp.int32)
    outputs_all = []
    inputs_all = []
    totals = None
    for batch_idx in range(MB):
        valid = (positions[None, :] < lengths[batch_idx][:, None]).astype(jnp.float32)
        frames_now = frames[batch_idx].astype(jnp.float32)

        def forward(frames_in, *weight_list):
            return layer_block(frames_in, valid, weight_list, table)
        result, pull_back = jax.vjp(forward, frames_now, *weights_all)
        gradients = pull_back(cotangent[batch_idx].astype(jnp.float32) * valid[:, :, None])
        outputs_all.append(result.astype(jnp.bfloat16))
        inputs_all.append(gradients[0].astype(jnp.bfloat16))
        if totals is None:
            totals = gradients[1:]
        else:
            totals = tuple((first_one + second_one for first_one, second_one in zip(totals, gradients[1:])))
    return (jnp.stack(outputs_all), jnp.stack(inputs_all), totals[0], totals[1], totals[2], totals[3], totals[4], totals[5], totals[6], totals[7], totals[8], totals[9], totals[10], totals[11], totals[12], totals[13])
```

```python
import math

import jax
import jax.numpy as jnp
from jax import lax
from jax.experimental import pallas as pl
from jax.experimental.pallas import tpu as pltpu
from jax.sharding import PartitionSpec as P

DK = 64
norm_eps = 1e-05
mask_fill = -1000000000.0
BF = jnp.bfloat16
F32 = jnp.float32
BLK = 128


def nn(a, b):
    return lax.dot_general(a, b, (((1,), (0,)), ((), ())), preferred_element_type=F32)


def nt(a, b):
    return lax.dot_general(a, b, (((1,), (1,)), ((), ())), preferred_element_type=F32)


def tn(a, b):
    return lax.dot_general(a, b, (((0,), (0,)), ((), ())), preferred_element_type=F32)


def position_table(length, width):
    cols = jnp.arange(width, dtype=jnp.int32)
    rate = jnp.exp((cols // 2 * 2).astype(F32) * (-math.log(10000.0) / width))[None, :]
    phase = (cols % 2).astype(F32)[None, :] * (0.5 * math.pi)
    step = 32
    coarse = (length - 1 - step * jnp.arange(2 * length // step, dtype=jnp.int32)).astype(F32)
    fine = jnp.arange(step, dtype=jnp.int32).astype(F32)
    big = coarse[:, None] * rate
    small = fine[:, None] * rate
    even = (cols % 2 == 0)[None, :]
    sin_big, cos_big = jnp.sin(big), jnp.cos(big)
    first = jnp.where(even, sin_big, cos_big)
    second = jnp.where(even, cos_big, -sin_big)
    rows = first[:, None] * jnp.cos(small)[None] - second[:, None] * jnp.sin(small)[None]
    return rows.reshape(2 * length, width)


def swish_act(values):
    return values * jax.nn.sigmoid(values)


def swish_slope(values):
    sigma = jax.nn.sigmoid(values)
    return sigma + values * sigma * (1.0 - sigma)


def norm_forward(values, gain, shift):
    average = jnp.mean(values, axis=-1, keepdims=True)
    centered = values - average
    inv_std = lax.rsqrt(jnp.mean(centered * centered, axis=-1, keepdims=True) + norm_eps)
    scaled = centered * inv_std
    return (scaled * gain + shift, scaled, inv_std)


def norm_backward(upstream, scaled, inv_std, gain):
    grad_gain = jnp.sum(upstream * scaled, axis=(0, 1))
    grad_shift = jnp.sum(upstream, axis=(0, 1))
    grad_scaled = upstream * gain
    inner = (
        grad_scaled
        - jnp.mean(grad_scaled, axis=-1, keepdims=True)
        - scaled * jnp.mean(grad_scaled * scaled, axis=-1, keepdims=True)
    )
    return (inv_std * inner, grad_gain, grad_shift)


def depthwise(signal, taps_all):
    reach = (taps_all.shape[0] - 1) // 2
    length_now = signal.shape[1]
    padded = jnp.pad(signal, ((0, 0), (reach, reach), (0, 0)))
    summed = jnp.zeros_like(signal)
    for tap_idx in range(taps_all.shape[0]):
        summed = summed + taps_all[tap_idx] * padded[:, tap_idx : tap_idx + length_now]
    return summed


def depthwise_back(upstream, signal, taps_all):
    reach = (taps_all.shape[0] - 1) // 2
    length_now = upstream.shape[1]
    padded_grad = jnp.pad(upstream, ((0, 0), (reach, reach), (0, 0)))
    padded_sig = jnp.pad(signal, ((0, 0), (reach, reach), (0, 0)))
    grad_signal = jnp.zeros_like(signal)
    tap_grads = []
    for tap_idx in range(taps_all.shape[0]):
        begin = 2 * reach - tap_idx
        grad_signal = grad_signal + taps_all[tap_idx] * padded_grad[:, begin : begin + length_now]
        tap_grads.append(
            jnp.sum(upstream * padded_sig[:, tap_idx : tap_idx + length_now], axis=(0, 1))
        )
    return (grad_signal, jnp.stack(tap_grads))


def attn_fwd_kernel(len_ref, qu, qv, k, v, pos, o_ref, lse_ref):
    count = len_ref[pl.program_id(0)]
    full = k.shape[1]
    lane = lax.broadcasted_iota(jnp.int32, (BLK, 2 * DK), 1)
    col = lax.broadcasted_iota(jnp.int32, (BLK, full), 1)
    keep = col < count
    zero = jnp.zeros((), BF)
    for blk in range(full // BLK):
        i0 = blk * BLK
        base = full - BLK - i0
        outs, logs = [], []
        for h in range(2):
            mine = (lane < DK) if h == 0 else (lane >= DK)
            q_u = jnp.where(mine, qu[0, i0 : i0 + BLK, :], zero)
            q_v = jnp.where(mine, qv[0, i0 : i0 + BLK, :], zero)
            rel = nt(q_v, pos[base : base + full + BLK, :])
            rel = pltpu.roll(rel, full + 1, 1, stride=1, stride_axis=0)[:, :full]
            s = (nt(q_u, k[0]) + rel) * (1.0 / math.sqrt(DK))
            s = jnp.where(keep, s, mask_fill)
            top = jnp.max(s, axis=1, keepdims=True)
            e = jnp.exp(s - top)
            total = jnp.sum(e, axis=1, keepdims=True)
            outs.append(nn(e.astype(BF), v[0]) / total)
            logs.append(top + jnp.log(total))
        left = lane < DK
        o_ref[0, i0 : i0 + BLK, :] = jnp.where(left, outs[0], outs[1]).astype(BF)
        lse_ref[0, i0 : i0 + BLK, :] = jnp.where(left, logs[0], logs[1])


def attn_bwd_kernel(
    len_ref, qu, qv, k, v, pos, o, lse, do, dq_ref, dk_ref, dv_ref, dpos_ref, sum_ref, dkt, dvt, dpt
):
    count = len_ref[pl.program_id(0)]
    full = k.shape[1]
    scale = 1.0 / math.sqrt(DK)
    lane = lax.broadcasted_iota(jnp.int32, (BLK, 2 * DK), 1)
    left = lane < DK
    keep = lax.broadcasted_iota(jnp.int32, (BLK, full), 1) < count
    zero = jnp.zeros((), BF)
    flip = (lane + lax.broadcasted_iota(jnp.int32, (BLK, 2 * DK), 0) == BLK - 1).astype(F32).astype(BF)
    dkt[...] = jnp.zeros_like(dkt)
    dvt[...] = jnp.zeros_like(dvt)
    dpt[...] = jnp.zeros_like(dpt)
    sum_q = jnp.zeros((1, 2 * DK), F32)
    sum_u = jnp.zeros((1, 2 * DK), F32)
    sum_v = jnp.zeros((1, 2 * DK), F32)
    for blk in range(full // BLK):
        i0 = blk * BLK
        base = full - BLK - i0
        rows = slice(i0, i0 + BLK)
        win = slice(base, base + full + BLK)
        qu_t = qu[0, rows, :].astype(F32).T.astype(BF)
        do_t = do[0, rows, :].astype(F32).T.astype(BF)
        qv_t = tn(qv[0, rows, :], flip).astype(BF)
        dot_o = do[0, rows, :].astype(F32) * o[0, rows, :].astype(F32)
        parts_u, parts_v = [], []
        for h in range(2):
            mine = left if h == 0 else lane >= DK
            hs = slice(h * DK, h * DK + DK)
            q_u = jnp.where(mine, qu[0, rows, :], zero)
            q_v = jnp.where(mine, qv[0, rows, :], zero)
            d_o = jnp.where(mine, do[0, rows, :], zero)
            rel = nt(q_v, pos[win, :])
            rel = pltpu.roll(rel, full + 1, 1, stride=1, stride_axis=0)[:, :full]
            s = (nt(q_u, k[0]) + rel) * scale - lse[0, rows, h * DK : h * DK + 1]
            p = jnp.where(keep, jnp.exp(jnp.minimum(s, 0.0)), 0.0)
            delta = jnp.sum(jnp.where(mine, dot_o, 0.0), axis=1, keepdims=True)
            ds = (p * (nt(d_o, v[0]) - delta)).astype(BF)
            dvt[hs, :] += nn(do_t[hs, :], p.astype(BF))
            dkt[hs, :] += nn(qu_t[hs, :], ds)
            parts_u.append(nn(ds, k[0]))
            wide = jnp.concatenate([nn(flip, ds), jnp.zeros((BLK, BLK), F32)], axis=1)
            wide = pltpu.roll(wide, 0, 1, stride=1, stride_axis=0).astype(BF)
            parts_v.append(nn(wide, pos[win, :]))
            dpt[hs, win] += nn(qv_t[hs, :], wide)
        d_u = jnp.where(left, parts_u[0], parts_u[1]) * scale
        d_v = jnp.where(left, parts_v[0], parts_v[1]) * scale
        high = d_v.astype(BF)
        low = (d_v - high.astype(F32)).astype(BF)
        d_q = (d_u + nn(flip, high) + nn(flip, low)).astype(BF)
        dq_ref[0, rows, :] = d_q
        sum_q += jnp.sum(d_q.astype(F32), axis=0, keepdims=True)
        sum_u += jnp.sum(d_u, axis=0, keepdims=True)
        sum_v += jnp.sum(d_v, axis=0, keepdims=True)
    dk_ref[0] = (dkt[...].T * scale).astype(BF)
    d_val = dvt[...].T.astype(BF)
    dv_ref[0] = d_val
    dpos_ref[0] = (dpt[...].T * scale).astype(BF)
    sum_ref[0, 0:1, :] = sum_q
    sum_ref[0, 1:2, :] = jnp.sum(d_val.astype(F32), axis=0, keepdims=True)
    sum_ref[0, 2:3, :] = sum_u
    sum_ref[0, 3:4, :] = sum_v
    sum_ref[0, 4:8, :] = jnp.zeros((4, 2 * DK), F32)


def attn_specs(rows, full, width):
    pairs = width // (2 * DK)
    main = pl.BlockSpec((1, full, 2 * DK), lambda u, p, n: (u, 0, p))
    pos = pl.BlockSpec((2 * full, 2 * DK), lambda u, p, n: (0, p))
    return (rows, pairs), main, pos


def attn_fwd_call(lens, qu, qv, k, v, pos):
    rows, full, width = qu.shape
    grid, main, pspec = attn_specs(rows, full, width)
    return pl.pallas_call(
        attn_fwd_kernel,
        grid_spec=pltpu.PrefetchScalarGridSpec(
            num_scalar_prefetch=1,
            grid=grid,
            in_specs=[main] * 4 + [pspec],
            out_specs=[main, main],
        ),
        out_shape=[
            jax.ShapeDtypeStruct((rows, full, width), BF),
            jax.ShapeDtypeStruct((rows, full, width), F32),
        ],
        name="attn_fwd",
    )(lens, qu, qv, k, v, pos)


def attn_bwd_call(lens, qu, qv, k, v, pos, o, lse, do):
    rows, full, width = qu.shape
    grid, main, pspec = attn_specs(rows, full, width)
    return pl.pallas_call(
        attn_bwd_kernel,
        grid_spec=pltpu.PrefetchScalarGridSpec(
            num_scalar_prefetch=1,
            grid=grid,
            in_specs=[main] * 4 + [pspec] + [main] * 3,
            out_specs=[
                main,
                main,
                main,
                pl.BlockSpec((1, 2 * full, 2 * DK), lambda u, p, n: (u, 0, p)),
                pl.BlockSpec((1, 8, 2 * DK), lambda u, p, n: (u, 0, p)),
            ],
            scratch_shapes=[
                pltpu.VMEM((2 * DK, full), F32),
                pltpu.VMEM((2 * DK, full), F32),
                pltpu.VMEM((2 * DK, 2 * full), F32),
            ],
        ),
        out_shape=[jax.ShapeDtypeStruct((rows, full, width), BF)] * 3
        + [
            jax.ShapeDtypeStruct((rows, 2 * full, width), BF),
            jax.ShapeDtypeStruct((rows, 8, width), F32),
        ],
        name="attn_bwd",
    )(lens, qu, qv, k, v, pos, o, lse, do)


def ffn_forward(residual, gain, shift, out_bias, weights):
    w_in, w_out_t, b_in = weights
    normed, scaled, inv_std = norm_forward(residual, gain, shift)
    hn = normed.astype(BF)
    zf = jnp.einsum("uth,hf->utf", hn, w_in, preferred_element_type=F32) + b_in
    af = swish_act(zf).astype(BF)
    out = jnp.einsum("utf,hf->uth", af, w_out_t, preferred_element_type=F32) + out_bias
    return out, (scaled, inv_std, hn, zf, af)


def ffn_backward(upstream, kept, gain, weights):
    scaled, inv_std, hn, zf, af = kept
    w_in, w_out_t, b_in = weights
    g = upstream.astype(BF)
    g_bias = jnp.sum(g.astype(F32), axis=(0, 1))
    g_out = jnp.einsum("uth,utf->hf", g, af, preferred_element_type=F32)
    d_af = jnp.einsum("uth,hf->utf", g, w_out_t, preferred_element_type=F32)
    dz = (d_af * swish_slope(zf)).astype(BF)
    g_b = jnp.sum(dz.astype(F32), axis=(0, 1))
    g_in = jnp.einsum("uth,utf->hf", hn, dz, preferred_element_type=F32)
    d_hn = jnp.einsum("utf,hf->uth", dz, w_in, preferred_element_type=F32)
    d_x, g_gain, g_shift = norm_backward(d_hn, scaled, inv_std, gain)
    return d_x, (g_in, g_out, g_b), (g_gain, g_shift, g_bias)


SEGS = ("f1i", "f1o", "qkv", "pos", "out", "ci", "co", "f2i", "f2o")


def local(
    frames,
    lengths,
    ffn1_in,
    ffn1_out,
    ffn1_bias,
    qkv_weight,
    pos_weight,
    out_weight,
    attn_bias,
    conv_in,
    conv_out,
    conv_channel,
    ffn2_in,
    ffn2_out,
    ffn2_bias,
    norm_params,
    cotangent,
):
    micro, seqs, full, width = frames.shape
    both = ("dp", "tensor")
    n_dp = lax.axis_size("dp")
    rows = ffn1_in.shape[0]
    batch = micro * seqs
    shards = (
        ffn1_in,
        ffn1_out.T,
        qkv_weight.reshape(rows, -1),
        pos_weight,
        out_weight.T,
        conv_in.reshape(rows, -1),
        conv_out.T,
        ffn2_in,
        ffn2_out.T,
    )
    sizes = [item.shape[1] for item in shards]
    starts = [sum(sizes[:i]) for i in range(len(sizes))]
    packed = jnp.concatenate(shards, axis=1)
    every = lax.all_gather(packed, both, axis=0, tiled=True)
    every = every.reshape(n_dp, 2, rows, -1).transpose(1, 0, 2, 3).reshape(2, n_dp * rows, -1)
    full_w = {}
    for name, start, size in zip(SEGS, starts, sizes):
        full_w[name] = (every[0, :, start : start + size], every[1, :, start : start + size])
    small = jnp.concatenate(
        [item.reshape(-1) for item in (ffn1_bias, attn_bias, conv_channel, ffn2_bias, norm_params)]
    )
    smalls = lax.all_gather(small, both, axis=0, tiled=False).reshape(n_dp, 2, -1).astype(F32)

    def take(item, offset):
        return smalls[:, :, offset : offset + item.size].reshape((n_dp, 2) + item.shape)

    off = 0
    pieces = []
    for item in (ffn1_bias, attn_bias, conv_channel, ffn2_bias, norm_params):
        pieces.append(take(item, off))
        off += item.size
    b1 = pieces[0].transpose(1, 2, 0, 3).reshape(-1)
    vec = pieces[1].transpose(2, 1, 3, 0, 4).reshape(attn_bias.shape[0], -1)
    cvec = pieces[2].transpose(2, 1, 3, 0, 4).reshape(conv_channel.shape[0], -1)
    b2 = pieces[3].transpose(1, 2, 0, 3).reshape(-1)
    norms = pieces[4].transpose(2, 0, 1, 3).reshape(norm_params.shape[0], -1)

    def cat(name):
        return jnp.concatenate(full_w[name], axis=1)

    def cat3(name, parts):
        pair = [item.reshape(item.shape[0], parts, -1) for item in full_w[name]]
        return jnp.concatenate(pair, axis=2)

    ffn1_w = (cat("f1i"), cat("f1o"), b1)
    ffn2_w = (cat("f2i"), cat("f2o"), b2)
    w_qkv, w_pos, w_out_t = cat3("qkv", 3), cat("pos"), cat("out")
    w_ci, w_co_t = cat3("ci", 2), cat("co")
    mine = lax.axis_index("tensor")
    lens = lax.dynamic_slice_in_dim(lengths, mine * seqs, seqs, 1).reshape(-1)
    positions = jnp.arange(full, dtype=jnp.int32)
    valid = (positions[None, :] < lens[:, None]).astype(F32)
    mask3 = valid[:, :, None]
    table = position_table(full, width).astype(BF)
    x0 = frames.reshape(batch, full, width).astype(F32)
    y1, kept1 = ffn_forward(x0, norms[0], norms[1], norms[2], ffn1_w)
    x1 = x0 + 0.5 * y1
    normed, scaled2, inv2 = norm_forward(x1, norms[3], norms[4])
    hn2 = normed.astype(BF)
    proj = jnp.einsum("uth,hkc->utkc", hn2, w_qkv, preferred_element_type=F32)
    query = proj[:, :, 0] + vec[0]
    keys = proj[:, :, 1].astype(BF)
    values = (proj[:, :, 2] + vec[1]).astype(BF)
    q_u = (query + vec[2]).astype(BF)
    q_v = (query + vec[3]).astype(BF)
    pos = jnp.dot(table, w_pos, preferred_element_type=F32).astype(BF)
    mixed, lse = attn_fwd_call(lens, q_u, q_v, keys, values, pos)
    y2 = jnp.einsum("utc,hc->uth", mixed, w_out_t, preferred_element_type=F32) + norms[5]
    x2 = x1 + y2
    normed, scaled3, inv3 = norm_forward(x2, norms[6], norms[7])
    hn3 = normed.astype(BF)
    halves = jnp.einsum("uth,hkc->utkc", hn3, w_ci, preferred_element_type=F32) + cvec[0:2]
    gate = jax.nn.sigmoid(halves[:, :, 1])
    gated = halves[:, :, 0] * gate * mask3
    conv = depthwise(gated, cvec[4:])

    def by_micro(item):
        return jnp.sum(item.reshape(micro, seqs, full, width), axis=(1, 2))

    stats = lax.psum(
        jnp.stack(
            [
                by_micro(conv * mask3),
                by_micro(conv * conv * mask3),
                by_micro(jnp.broadcast_to(mask3, conv.shape)),
            ]
        ),
        both,
    )
    avg = stats[0] / stats[2]
    var = stats[1] / stats[2] - avg * avg
    rstd = lax.rsqrt(var + norm_eps)

    def spread(item):
        return jnp.repeat(item, seqs, axis=0)[:, None, :]

    yhat = (conv - spread(avg)) * spread(rstd)
    bn = yhat * cvec[2] + cvec[3]
    act = swish_act(bn).astype(BF)
    y3 = jnp.einsum("utc,hc->uth", act, w_co_t, preferred_element_type=F32) + norms[8]
    x3 = x2 + y3
    y4, kept4 = ffn_forward(x3, norms[9], norms[10], norms[11], ffn2_w)
    x4 = x3 + 0.5 * y4
    result, scaled5, inv5 = norm_forward(x4, norms[12], norms[13])
    seed = cotangent.reshape(batch, full, width).astype(F32) * mask3
    d4, g12, g13 = norm_backward(seed, scaled5, inv5, norms[12])
    delta, grads_f2, norms_f2 = ffn_backward(0.5 * d4, kept4, norms[9], ffn2_w)
    d3 = d4 + delta
    g = d3.astype(BF)
    g8 = jnp.sum(g.astype(F32), axis=(0, 1))
    g_co = jnp.einsum("uth,utc->hc", g, act, preferred_element_type=F32)
    d_bn = jnp.einsum("uth,hc->utc", g, w_co_t, preferred_element_type=F32) * swish_slope(bn)
    g_scale = jnp.sum(d_bn * yhat, axis=(0, 1))
    g_offset = jnp.sum(d_bn, axis=(0, 1))
    d_yhat = d_bn * cvec[2]
    sums = lax.psum(jnp.stack([by_micro(d_yhat), by_micro(d_yhat * yhat)]), both)
    d_conv = spread(rstd) * (
        d_yhat - mask3 * (spread(sums[0]) + yhat * spread(sums[1])) / spread(stats[2])
    )
    d_gated, g_taps = depthwise_back(d_conv, gated, cvec[4:])
    d_glu = d_gated * mask3
    d_half = jnp.stack(
        [d_glu * gate, d_glu * halves[:, :, 0] * gate * (1.0 - gate)], axis=2
    ).astype(BF)
    g_cbias = jnp.sum(d_half.astype(F32), axis=(0, 1))
    g_ci = jnp.einsum("uth,utkc->hkc", hn3, d_half, preferred_element_type=F32)
    d_hn3 = jnp.einsum("utkc,hkc->uth", d_half, w_ci, preferred_element_type=F32)
    delta, g6, g7 = norm_backward(d_hn3, scaled3, inv3, norms[6])
    d2 = d3 + delta
    g = d2.astype(BF)
    g5 = jnp.sum(g.astype(F32), axis=(0, 1))
    g_out = jnp.einsum("uth,utc->hc", g, mixed, preferred_element_type=F32)
    d_mixed = jnp.einsum("uth,hc->utc", g, w_out_t, preferred_element_type=F32).astype(BF)
    dq, dk, dv, dpos, asums = attn_bwd_call(
        lens, q_u, q_v, keys, values, pos, mixed, lse, d_mixed
    )
    g_vec = jnp.sum(asums, axis=0)[0:4]
    g_pos = jnp.einsum("ph,upc->hc", table, dpos, preferred_element_type=F32)
    d_proj = jnp.stack([dq, dk, dv], axis=2)
    g_qkv = jnp.einsum("uth,utkc->hkc", hn2, d_proj, preferred_element_type=F32)
    d_hn2 = jnp.einsum("utkc,hkc->uth", d_proj, w_qkv, preferred_element_type=F32)
    delta, g3, g4 = norm_backward(d_hn2, scaled2, inv2, norms[3])
    d1 = d2 + delta
    delta, grads_f1, norms_f1 = ffn_backward(0.5 * d1, kept1, norms[0], ffn1_w)
    d0 = (d1 + delta).astype(BF)
    g_norm = jnp.stack(
        norms_f1 + (g3, g4, g5) + (g6, g7, g8) + norms_f2 + (g12, g13)
    )
    g_cvec = jnp.concatenate([g_cbias, g_scale[None], g_offset[None], g_taps], axis=0)

    def half(item, t):
        part = item.reshape(item.shape[0], -1, item.shape[-1])
        step = part.shape[-1] // 2
        return part[:, :, t * step : (t + 1) * step].reshape(n_dp, rows, -1)

    wide = (
        grads_f1[0], grads_f1[1], g_qkv, g_pos, g_out, g_ci, g_co, grads_f2[0], grads_f2[1],
    )
    grads = jnp.stack(
        [jnp.concatenate([half(item, t) for item in wide], axis=2).astype(BF) for t in (0, 1)],
        axis=1,
    ).reshape(n_dp * 2 * rows, -1)
    own = lax.psum_scatter(grads, both, scatter_dimension=0, tiled=True).astype(F32)
    outs = [own[:, start : start + size] for start, size in zip(starts, sizes)]
    tiny = lax.psum(
        jnp.concatenate(
            [item.reshape(-1) for item in (grads_f1[2], grads_f2[2], g_vec, g_cvec, g_norm)]
        ),
        both,
    )
    at = lax.axis_index("dp")

    def owned(offset, like, lead):
        groups = 2 * like.shape[-2]
        area = tiny[offset : offset + lead * groups * 128].reshape(lead, groups, 128)
        area = lax.dynamic_slice_in_dim(area, mine * like.shape[-2], like.shape[-2], 1)
        return lax.dynamic_slice_in_dim(area, at * like.shape[-1], like.shape[-1], 2).reshape(
            like.shape
        )

    o1 = 0
    o2 = grads_f1[2].size
    o3 = o2 + grads_f2[2].size
    o4 = o3 + g_vec.size
    o5 = o4 + g_cvec.size
    gn = tiny[o5 : o5 + g_norm.size].reshape(g_norm.shape)
    cols = norm_params.shape[1]
    gn = lax.dynamic_slice_in_dim(gn, (at * 2 + mine) * cols, cols, 1)
    return (
        result.astype(BF).reshape(frames.shape),
        d0.reshape(frames.shape),
        outs[0],
        outs[1].T,
        owned(o1, ffn1_bias, 1),
        outs[2].reshape(qkv_weight.shape),
        outs[3],
        outs[4].T,
        owned(o3, attn_bias, attn_bias.shape[0]),
        outs[5].reshape(conv_in.shape),
        outs[6].T,
        owned(o4, conv_channel, conv_channel.shape[0]),
        outs[7],
        outs[8].T,
        owned(o2, ffn2_bias, 1),
        gn,
    )


def solution(mesh):
    in_specs = (
        P(None, ("dp", "tensor"), None, None),
        P(None, "dp"),
        P("dp", "tensor"),
        P("tensor", "dp"),
        P("tensor", "dp"),
        P("dp", None, "tensor"),
        P("dp", "tensor"),
        P("tensor", "dp"),
        P(None, "tensor", "dp"),
        P("dp", None, "tensor"),
        P("tensor", "dp"),
        P(None, "tensor", "dp"),
        P("dp", "tensor"),
        P("tensor", "dp"),
        P("tensor", "dp"),
        P(None, ("dp", "tensor")),
        P(None, ("dp", "tensor"), None, None),
    )
    out_specs = (
        P(None, ("dp", "tensor"), None, None),
        P(None, ("dp", "tensor"), None, None),
        P("dp", "tensor"),
        P("tensor", "dp"),
        P("tensor", "dp"),
        P("dp", None, "tensor"),
        P("dp", "tensor"),
        P("tensor", "dp"),
        P(None, "tensor", "dp"),
        P("dp", None, "tensor"),
        P("tensor", "dp"),
        P(None, "tensor", "dp"),
        P("dp", "tensor"),
        P("tensor", "dp"),
        P("tensor", "dp"),
        P(None, ("dp", "tensor")),
    )
    return jax.shard_map(local, mesh=mesh, in_specs=in_specs, out_specs=out_specs, check_vma=False)
```

```python
import math

import jax
import jax.numpy as jnp
from jax import lax
from jax.experimental import pallas as pl
from jax.experimental.pallas import tpu as pltpu
from jax.sharding import PartitionSpec as P

DK = 64
norm_eps = 1e-05
mask_fill = -1000000000.0
BF = jnp.bfloat16
F32 = jnp.float32
BLK = 128


def nn(a, b):
    return lax.dot_general(a, b, (((1,), (0,)), ((), ())), preferred_element_type=F32)


def nt(a, b):
    return lax.dot_general(a, b, (((1,), (1,)), ((), ())), preferred_element_type=F32)


def tn(a, b):
    return lax.dot_general(a, b, (((0,), (0,)), ((), ())), preferred_element_type=F32)


def position_table(length, width):
    cols = jnp.arange(width, dtype=jnp.int32)
    rate = jnp.exp((cols // 2 * 2).astype(F32) * (-math.log(10000.0) / width))[None, :]
    phase = (cols % 2).astype(F32)[None, :] * (0.5 * math.pi)
    step = 32
    coarse = (length - 1 - step * jnp.arange(2 * length // step, dtype=jnp.int32)).astype(F32)
    fine = jnp.arange(step, dtype=jnp.int32).astype(F32)
    big = coarse[:, None] * rate
    small = fine[:, None] * rate
    even = (cols % 2 == 0)[None, :]
    sin_big, cos_big = jnp.sin(big), jnp.cos(big)
    first = jnp.where(even, sin_big, cos_big)
    second = jnp.where(even, cos_big, -sin_big)
    rows = first[:, None] * jnp.cos(small)[None] - second[:, None] * jnp.sin(small)[None]
    return rows.reshape(2 * length, width)


def swish_act(values):
    return values * jax.nn.sigmoid(values)


def swish_slope(values):
    sigma = jax.nn.sigmoid(values)
    return sigma + values * sigma * (1.0 - sigma)


def norm_forward(values, gain, shift):
    average = jnp.mean(values, axis=-1, keepdims=True)
    centered = values - average
    inv_std = lax.rsqrt(jnp.mean(centered * centered, axis=-1, keepdims=True) + norm_eps)
    scaled = centered * inv_std
    return (scaled * gain + shift, scaled, inv_std)


def norm_backward(upstream, scaled, inv_std, gain):
    grad_gain = jnp.sum(upstream * scaled, axis=(0, 1))
    grad_shift = jnp.sum(upstream, axis=(0, 1))
    grad_scaled = upstream * gain
    inner = (
        grad_scaled
        - jnp.mean(grad_scaled, axis=-1, keepdims=True)
        - scaled * jnp.mean(grad_scaled * scaled, axis=-1, keepdims=True)
    )
    return (inv_std * inner, grad_gain, grad_shift)


def depthwise(signal, taps_all):
    reach = (taps_all.shape[0] - 1) // 2
    length_now = signal.shape[1]
    padded = jnp.pad(signal, ((0, 0), (reach, reach), (0, 0)))
    summed = jnp.zeros_like(signal)
    for tap_idx in range(taps_all.shape[0]):
        summed = summed + taps_all[tap_idx] * padded[:, tap_idx : tap_idx + length_now]
    return summed


def depthwise_back(upstream, signal, taps_all):
    reach = (taps_all.shape[0] - 1) // 2
    length_now = upstream.shape[1]
    padded_grad = jnp.pad(upstream, ((0, 0), (reach, reach), (0, 0)))
    padded_sig = jnp.pad(signal, ((0, 0), (reach, reach), (0, 0)))
    grad_signal = jnp.zeros_like(signal)
    tap_grads = []
    for tap_idx in range(taps_all.shape[0]):
        begin = 2 * reach - tap_idx
        grad_signal = grad_signal + taps_all[tap_idx] * padded_grad[:, begin : begin + length_now]
        tap_grads.append(
            jnp.sum(upstream * padded_sig[:, tap_idx : tap_idx + length_now], axis=(0, 1))
        )
    return (grad_signal, jnp.stack(tap_grads))


def attn_fwd_kernel(len_ref, qu, qv, k, v, pos, o_ref, lse_ref):
    count = len_ref[pl.program_id(0)]
    full = k.shape[1]
    lane = lax.broadcasted_iota(jnp.int32, (BLK, 2 * DK), 1)
    col = lax.broadcasted_iota(jnp.int32, (BLK, full), 1)
    keep = col < count
    zero = jnp.zeros((), BF)
    for blk in range(full // BLK):
        i0 = blk * BLK
        base = full - BLK - i0
        outs, logs = [], []
        for h in range(2):
            mine = (lane < DK) if h == 0 else (lane >= DK)
            q_u = jnp.where(mine, qu[0, i0 : i0 + BLK, :], zero)
            q_v = jnp.where(mine, qv[0, i0 : i0 + BLK, :], zero)
            rel = nt(q_v, pos[base : base + full + BLK, :])
            rel = pltpu.roll(rel, full + 1, 1, stride=1, stride_axis=0)[:, :full]
            s = (nt(q_u, k[0]) + rel) * (1.0 / math.sqrt(DK))
            s = jnp.where(keep, s, mask_fill)
            top = jnp.max(s, axis=1, keepdims=True)
            e = jnp.exp(s - top)
            total = jnp.sum(e, axis=1, keepdims=True)
            outs.append(nn(e.astype(BF), v[0]) / total)
            logs.append(top + jnp.log(total))
        left = lane < DK
        o_ref[0, i0 : i0 + BLK, :] = jnp.where(left, outs[0], outs[1]).astype(BF)
        lse_ref[0, i0 : i0 + BLK, :] = jnp.where(left, logs[0], logs[1])


def attn_bwd_kernel(
    len_ref, qu, qv, k, v, pos, o, lse, do, dq_ref, dk_ref, dv_ref, dpos_ref, sum_ref, dkt, dvt, dpt
):
    count = len_ref[pl.program_id(0)]
    full = k.shape[1]
    scale = 1.0 / math.sqrt(DK)
    lane = lax.broadcasted_iota(jnp.int32, (BLK, 2 * DK), 1)
    left = lane < DK
    keep = lax.broadcasted_iota(jnp.int32, (BLK, full), 1) < count
    zero = jnp.zeros((), BF)
    flip = (lane + lax.broadcasted_iota(jnp.int32, (BLK, 2 * DK), 0) == BLK - 1).astype(F32).astype(BF)
    dkt[...] = jnp.zeros_like(dkt)
    dvt[...] = jnp.zeros_like(dvt)
    dpt[...] = jnp.zeros_like(dpt)
    sum_q = jnp.zeros((1, 2 * DK), F32)
    sum_u = jnp.zeros((1, 2 * DK), F32)
    sum_v = jnp.zeros((1, 2 * DK), F32)
    for blk in range(full // BLK):
        i0 = blk * BLK
        base = full - BLK - i0
        rows = slice(i0, i0 + BLK)
        win = slice(base, base + full + BLK)
        qu_t = qu[0, rows, :].astype(F32).T.astype(BF)
        do_t = do[0, rows, :].astype(F32).T.astype(BF)
        qv_t = tn(qv[0, rows, :], flip).astype(BF)
        dot_o = do[0, rows, :].astype(F32) * o[0, rows, :].astype(F32)
        parts_u, parts_v = [], []
        for h in range(2):
            mine = left if h == 0 else lane >= DK
            hs = slice(h * DK, h * DK + DK)
            q_u = jnp.where(mine, qu[0, rows, :], zero)
            q_v = jnp.where(mine, qv[0, rows, :], zero)
            d_o = jnp.where(mine, do[0, rows, :], zero)
            rel = nt(q_v, pos[win, :])
            rel = pltpu.roll(rel, full + 1, 1, stride=1, stride_axis=0)[:, :full]
            s = (nt(q_u, k[0]) + rel) * scale - lse[0, rows, h * DK : h * DK + 1]
            p = jnp.where(keep, jnp.exp(jnp.minimum(s, 0.0)), 0.0)
            delta = jnp.sum(jnp.where(mine, dot_o, 0.0), axis=1, keepdims=True)
            ds = (p * (nt(d_o, v[0]) - delta)).astype(BF)
            dvt[hs, :] += nn(do_t[hs, :], p.astype(BF))
            dkt[hs, :] += nn(qu_t[hs, :], ds)
            parts_u.append(nn(ds, k[0]))
            wide = jnp.concatenate([nn(flip, ds), jnp.zeros((BLK, BLK), F32)], axis=1)
            wide = pltpu.roll(wide, 0, 1, stride=1, stride_axis=0).astype(BF)
            parts_v.append(nn(wide, pos[win, :]))
            dpt[hs, win] += nn(qv_t[hs, :], wide)
        d_u = jnp.where(left, parts_u[0], parts_u[1]) * scale
        d_v = jnp.where(left, parts_v[0], parts_v[1]) * scale
        high = d_v.astype(BF)
        low = (d_v - high.astype(F32)).astype(BF)
        d_q = (d_u + nn(flip, high) + nn(flip, low)).astype(BF)
        dq_ref[0, rows, :] = d_q
        sum_q += jnp.sum(d_q.astype(F32), axis=0, keepdims=True)
        sum_u += jnp.sum(d_u, axis=0, keepdims=True)
        sum_v += jnp.sum(d_v, axis=0, keepdims=True)
    dk_ref[0] = (dkt[...].T * scale).astype(BF)
    d_val = dvt[...].T.astype(BF)
    dv_ref[0] = d_val
    dpos_ref[0] = (dpt[...].T * scale).astype(BF)
    sum_ref[0, 0:1, :] = sum_q
    sum_ref[0, 1:2, :] = jnp.sum(d_val.astype(F32), axis=0, keepdims=True)
    sum_ref[0, 2:3, :] = sum_u
    sum_ref[0, 3:4, :] = sum_v
    sum_ref[0, 4:8, :] = jnp.zeros((4, 2 * DK), F32)


def attn_specs(rows, full, width):
    pairs = width // (2 * DK)
    main = pl.BlockSpec((1, full, 2 * DK), lambda u, p, n: (u, 0, p))
    pos = pl.BlockSpec((2 * full, 2 * DK), lambda u, p, n: (0, p))
    return (rows, pairs), main, pos


def attn_fwd_call(lens, qu, qv, k, v, pos):
    rows, full, width = qu.shape
    grid, main, pspec = attn_specs(rows, full, width)
    return pl.pallas_call(
        attn_fwd_kernel,
        grid_spec=pltpu.PrefetchScalarGridSpec(
            num_scalar_prefetch=1,
            grid=grid,
            in_specs=[main] * 4 + [pspec],
            out_specs=[main, main],
        ),
        out_shape=[
            jax.ShapeDtypeStruct((rows, full, width), BF),
            jax.ShapeDtypeStruct((rows, full, width), F32),
        ],
        name="attn_fwd",
    )(lens, qu, qv, k, v, pos)


def attn_bwd_call(lens, qu, qv, k, v, pos, o, lse, do):
    rows, full, width = qu.shape
    grid, main, pspec = attn_specs(rows, full, width)
    return pl.pallas_call(
        attn_bwd_kernel,
        grid_spec=pltpu.PrefetchScalarGridSpec(
            num_scalar_prefetch=1,
            grid=grid,
            in_specs=[main] * 4 + [pspec] + [main] * 3,
            out_specs=[
                main,
                main,
                main,
                pl.BlockSpec((1, 2 * full, 2 * DK), lambda u, p, n: (u, 0, p)),
                pl.BlockSpec((1, 8, 2 * DK), lambda u, p, n: (u, 0, p)),
            ],
            scratch_shapes=[
                pltpu.VMEM((2 * DK, full), F32),
                pltpu.VMEM((2 * DK, full), F32),
                pltpu.VMEM((2 * DK, 2 * full), F32),
            ],
        ),
        out_shape=[jax.ShapeDtypeStruct((rows, full, width), BF)] * 3
        + [
            jax.ShapeDtypeStruct((rows, 2 * full, width), BF),
            jax.ShapeDtypeStruct((rows, 8, width), F32),
        ],
        name="attn_bwd",
    )(lens, qu, qv, k, v, pos, o, lse, do)


MESH = pl.DeviceIdType.MESH
NZ, NY, NX = 4, 2, 2
ANY = pl.BlockSpec(memory_space=pl.ANY)
VM = pl.BlockSpec(memory_space=pltpu.VMEM)


def own_mesh(sizes):
    return sizes == (NZ * NY * NX, 2)


def place():
    dp = lax.axis_index("dp")
    return dp // (NY * NX), dp // NX % NY, dp % NX, lax.axis_index("tensor")


def dev(z, y, x, t):
    return (z * (NY * NX) + y * NX + x, t)


def greet(peers):
    barrier = pltpu.get_barrier_semaphore()
    for peer in peers:
        pl.semaphore_signal(barrier, inc=1, device_id=peer, device_id_type=MESH)
    pl.semaphore_wait(barrier, len(peers))


def rcopy(src, dst, send, recv, peer):
    return pltpu.make_async_remote_copy(
        src_ref=src, dst_ref=dst, send_sem=send, recv_sem=recv, device_id=peer, device_id_type=MESH
    )


def link_peers(z, y, x, t):
    peers = [dev(lax.rem(z + d, NZ), y, x, t) for d in range(1, NZ)]
    return peers + [dev(z, 1 - y, x, t), dev(z, y, 1 - x, t), dev(z, y, x, 1 - t)]


def sum_kernel(x_ref, o_ref, mid, b1, b2, s1, r1, s2, r2):
    z, y, x, t = place()
    spot = (y * NX + x) * 2 + t
    zs = [dev(lax.rem(z + d, NZ), y, x, t) for d in range(1, NZ)]
    flat = [lax.rem(spot + d, 8) for d in range(1, 8)]
    plane = [dev(z, p // 4, p // 2 % 2, p % 2) for p in flat]
    greet(zs + plane)
    first = [rcopy(x_ref, b1.at[i], s1.at[i], r1.at[i], peer) for i, peer in enumerate(zs)]
    for copy in first:
        copy.start()
    for copy in first:
        copy.wait_recv()
    mid[...] = (x_ref[...] + b1[0]) + (b1[1] + b1[2])
    second = [rcopy(mid, b2.at[i], s2.at[i], r2.at[i], peer) for i, peer in enumerate(plane)]
    for copy in second:
        copy.start()
    for copy in second:
        copy.wait_recv()
    total = mid[...]
    for i in range(7):
        total = total + b2[i]
    o_ref[...] = total
    for copy in first + second:
        copy.wait_send()


def sum_all(item, cid):
    return pl.pallas_call(
        sum_kernel,
        out_shape=jax.ShapeDtypeStruct(item.shape, F32),
        in_specs=[VM],
        out_specs=VM,
        scratch_shapes=[
            pltpu.VMEM(item.shape, F32),
            pltpu.VMEM((3,) + item.shape, F32),
            pltpu.VMEM((7,) + item.shape, F32),
            pltpu.SemaphoreType.DMA((3,)),
            pltpu.SemaphoreType.DMA((3,)),
            pltpu.SemaphoreType.DMA((7,)),
            pltpu.SemaphoreType.DMA((7,)),
        ],
        compiler_params=pltpu.CompilerParams(collective_id=cid, has_side_effects=True),
        name="sum_all",
    )(item)


def gather_kernel(widths, x_ref, g_ref, zs, zr, as_, ar, bs, br, cs, cr, own_sem):
    z, y, x, t = place()
    greet(link_peers(z, y, x, t))
    count = len(widths)
    cols = []
    at = 0
    for w in widths:
        cols.append(pl.ds(at, w))
        at += w
    own = pltpu.make_async_copy(x_ref, g_ref.at[t, z, y, x], own_sem)
    own.start()
    zc, ac, bc, cc = [], [], [], []
    for p, c in enumerate(cols):
        for d in range(1, NZ):
            zc.append(
                rcopy(
                    x_ref.at[:, c],
                    g_ref.at[t, z, y, x, :, c],
                    zs.at[p, d - 1],
                    zr.at[p, d - 1],
                    dev(lax.rem(z + d, NZ), y, x, t),
                )
            )
            zc[-1].start()
        along_x, along_y = dev(z, y, 1 - x, t), dev(z, 1 - y, x, t)
        line = g_ref.at[t, :, y, x, :, c]
        ac.append(rcopy(line, line, as_.at[p], ar.at[p], along_x if p % 2 == 0 else along_y))
        half = g_ref.at[t, :, y, :, :, c] if p % 2 == 0 else g_ref.at[t, :, :, x, :, c]
        bc.append(rcopy(half, half, bs.at[p], br.at[p], along_y if p % 2 == 0 else along_x))
        full = g_ref.at[t, :, :, :, :, c]
        cc.append(rcopy(full, full, cs.at[p], cr.at[p], dev(z, y, x, 1 - t)))
    own.wait()
    pairs = count // 2
    for q in range(pairs + 2):
        for p in (2 * q, 2 * q + 1):
            if p < count:
                for d in range(NZ - 1):
                    zc[p * (NZ - 1) + d].wait_recv()
                ac[p].start()
        for p in (2 * q - 2, 2 * q - 1):
            if 0 <= p < count:
                ac[p].wait_recv()
                bc[p].start()
        for p in (2 * q - 4, 2 * q - 3):
            if 0 <= p < count:
                bc[p].wait_recv()
                cc[p].start()
    for copy in cc:
        copy.wait_recv()
    for copy in zc + ac + bc + cc:
        copy.wait_send()


def gather_all(packed, widths, cid):
    rows, total = packed.shape
    n = len(widths)
    dma = pltpu.SemaphoreType.DMA
    return pl.pallas_call(
        lambda *refs: gather_kernel(widths, *refs),
        out_shape=jax.ShapeDtypeStruct((2, NZ, NY, NX, rows, total), packed.dtype),
        in_specs=[VM],
        out_specs=ANY,
        scratch_shapes=[
            dma((n, NZ - 1)), dma((n, NZ - 1)), dma((n,)), dma((n,)), dma((n,)), dma((n,)),
            dma((n,)), dma((n,)), dma,
        ],
        compiler_params=pltpu.CompilerParams(collective_id=cid, has_side_effects=True),
        name="gather_all",
    )(packed)


def scatter_kernel(
    widths, g_ref, s_ref, o_ref, os_ref, own, rc, ra, rb, rz, sown, src, sra, srb, srz,
    lsem, cs, cr, as_, ar, bs, br, zs, zr,
):
    z, y, x, t = place()
    along_x, along_y = dev(z, y, 1 - x, t), dev(z, 1 - y, x, t)
    mate = dev(z, y, x, 1 - t)
    count = len(widths) + 1
    bufs = []
    at = 0
    for w in widths:
        c = pl.ds(at, w)
        cut = (slice(None),) * 4 + (c,)
        bufs.append(
            dict(
                g=lambda i, c=c: g_ref.at[i, :, :, :, :, c],
                own=own.at[:, :, :, :, c], rc=rc.at[:, :, :, :, c],
                ra=ra.at[:, :, :, c], rb=rb.at[:, :, c], rz=rz.at[:, :, c], out=o_ref.at[:, c],
            )
        )
        at += w
    bufs.append(
        dict(g=lambda i: s_ref.at[i], own=sown, rc=src, ra=sra, rb=srb, rz=srz, out=os_ref)
    )
    greet(link_peers(z, y, x, t))
    lc, cc, ac, bc, zc = [], [], [], [], []
    for p, b in enumerate(bufs):
        even = p % 2 == 0
        lc.append(pltpu.make_async_copy(b["g"](t), b["own"], lsem.at[p]))
        cc.append(rcopy(b["g"](1 - t), b["rc"], cs.at[p], cr.at[p], mate))
        away = b["own"].at[:, 1 - y] if even else b["own"].at[:, :, 1 - x]
        ac.append(rcopy(away, b["ra"], as_.at[p], ar.at[p], along_y if even else along_x))
        line = b["own"].at[:, y, 1 - x] if even else b["own"].at[:, 1 - y, x]
        bc.append(rcopy(line, b["rb"], bs.at[p], br.at[p], along_x if even else along_y))
        for d in range(1, NZ):
            far = lax.rem(z + d, NZ)
            zc.append(
                rcopy(
                    b["own"].at[far, y, x], b["rz"].at[d - 1], zs.at[p, d - 1], zr.at[p, d - 1],
                    dev(far, y, x, t),
                )
            )
        lc[p].start()
        cc[p].start()
    for q in range(count + 3):
        if q < count:
            lc[q].wait()
            cc[q].wait_recv()
            b = bufs[q]
            for i in range(NZ):
                b["own"][i] = b["own"][i] + b["rc"][i]
            ac[q].start()
        p = q - 1
        if 0 <= p < count:
            ac[p].wait_recv()
            b = bufs[p]
            for i in range(NZ):
                if p % 2 == 0:
                    b["own"][i, y] = b["own"][i, y] + b["ra"][i]
                else:
                    b["own"][i, :, x] = b["own"][i, :, x] + b["ra"][i]
            bc[p].start()
        p = q - 2
        if 0 <= p < count:
            bc[p].wait_recv()
            b = bufs[p]
            for i in range(NZ):
                b["own"][i, y, x] = b["own"][i, y, x] + b["rb"][i]
            for d in range(NZ - 1):
                zc[p * (NZ - 1) + d].start()
        p = q - 3
        if 0 <= p < count:
            for d in range(NZ - 1):
                zc[p * (NZ - 1) + d].wait_recv()
            b = bufs[p]
            total = b["own"][z, y, x].astype(F32)
            for d in range(NZ - 1):
                total = total + b["rz"][d].astype(F32)
            b["out"][...] = total
    for copy in cc + ac + bc + zc:
        copy.wait_send()


def scatter_all(grads, small, widths, cid):
    rows, total = grads.shape[-2:]
    n = len(widths) + 1
    dma = pltpu.SemaphoreType.DMA
    tail = small.shape[-2:]

    def set_of(shape, dtype):
        return [
            pltpu.VMEM((NZ, NY, NX) + shape, dtype),
            pltpu.VMEM((NZ, NY, NX) + shape, dtype),
            pltpu.VMEM((NZ, 2) + shape, dtype),
            pltpu.VMEM((NZ,) + shape, dtype),
            pltpu.VMEM((NZ - 1,) + shape, dtype),
        ]

    return pl.pallas_call(
        lambda *refs: scatter_kernel(widths, *refs),
        out_shape=[
            jax.ShapeDtypeStruct((rows, total), F32),
            jax.ShapeDtypeStruct(tail, F32),
        ],
        in_specs=[ANY, ANY],
        out_specs=[VM, VM],
        scratch_shapes=set_of((rows, total), BF)
        + set_of(tail, F32)
        + [
            dma((n,)), dma((n,)), dma((n,)), dma((n,)), dma((n,)), dma((n,)), dma((n,)),
            dma((n, NZ - 1)), dma((n, NZ - 1)),
        ],
        compiler_params=pltpu.CompilerParams(
            collective_id=cid, has_side_effects=True, vmem_limit_bytes=56 * 1024 * 1024
        ),
        name="scatter_all",
    )(grads, small)


def ffn_forward(residual, gain, shift, out_bias, weights):
    w_in, w_out_t, b_in = weights
    normed, scaled, inv_std = norm_forward(residual, gain, shift)
    hn = normed.astype(BF)
    zf = jnp.einsum("uth,hf->utf", hn, w_in, preferred_element_type=F32) + b_in
    af = swish_act(zf).astype(BF)
    out = jnp.einsum("utf,hf->uth", af, w_out_t, preferred_element_type=F32) + out_bias
    return out, (scaled, inv_std, hn, zf, af)


def ffn_backward(upstream, kept, gain, weights):
    scaled, inv_std, hn, zf, af = kept
    w_in, w_out_t, b_in = weights
    g = upstream.astype(BF)
    g_bias = jnp.sum(g.astype(F32), axis=(0, 1))
    g_out = jnp.einsum("uth,utf->hf", g, af, preferred_element_type=F32)
    d_af = jnp.einsum("uth,hf->utf", g, w_out_t, preferred_element_type=F32)
    dz = (d_af * swish_slope(zf)).astype(BF)
    g_b = jnp.sum(dz.astype(F32), axis=(0, 1))
    g_in = jnp.einsum("uth,utf->hf", hn, dz, preferred_element_type=F32)
    d_hn = jnp.einsum("utf,hf->uth", dz, w_in, preferred_element_type=F32)
    d_x, g_gain, g_shift = norm_backward(d_hn, scaled, inv_std, gain)
    return d_x, (g_in, g_out, g_b), (g_gain, g_shift, g_bias)


EXTRA = 256


def split_cols(total):
    tiles = total // 128
    count = 10
    base = tiles // count
    return [128 * (base + (1 if i < tiles - base * count else 0)) for i in range(count)]


SEGS = ("f1i", "f1o", "qkv", "pos", "out", "ci", "co", "f2i", "f2o")


def local(
    frames,
    lengths,
    ffn1_in,
    ffn1_out,
    ffn1_bias,
    qkv_weight,
    pos_weight,
    out_weight,
    attn_bias,
    conv_in,
    conv_out,
    conv_channel,
    ffn2_in,
    ffn2_out,
    ffn2_bias,
    norm_params,
    cotangent,
):
    micro, seqs, full, width = frames.shape
    both = ("dp", "tensor")
    n_dp = lax.axis_size("dp")
    rows = ffn1_in.shape[0]
    batch = micro * seqs
    shards = (
        ffn1_in,
        ffn1_out.T,
        qkv_weight.reshape(rows, -1),
        pos_weight,
        out_weight.T,
        conv_in.reshape(rows, -1),
        conv_out.T,
        ffn2_in,
        ffn2_out.T,
    )
    sizes = [item.shape[1] for item in shards]
    starts = [sum(sizes[:i]) for i in range(len(sizes))]
    small_ins = (ffn1_bias, attn_bias, conv_channel, ffn2_bias, norm_params)
    small = jnp.concatenate([item.reshape(-1) for item in small_ins])
    extra = jnp.pad(small, (0, rows * EXTRA - small.size)).reshape(rows, EXTRA)
    packed = jnp.concatenate(shards + (extra,), axis=1)
    mine_mesh = own_mesh((n_dp, lax.axis_size("tensor"))) and rows % 16 == 0
    if mine_mesh:
        every = gather_all(packed, split_cols(packed.shape[1]), 1)
        every = every.reshape(2, n_dp * rows, -1)
    else:
        every = lax.all_gather(packed, both, axis=0, tiled=True)
        every = every.reshape(n_dp, 2, rows, -1).transpose(1, 0, 2, 3).reshape(2, n_dp * rows, -1)
    full_w = {}
    for name, start, size in zip(SEGS, starts, sizes):
        full_w[name] = (every[0, :, start : start + size], every[1, :, start : start + size])
    smalls = every[:, :, -EXTRA:].reshape(2, n_dp, -1).transpose(1, 0, 2).astype(F32)

    def take(item, offset):
        return smalls[:, :, offset : offset + item.size].reshape((n_dp, 2) + item.shape)

    off = 0
    pieces = []
    for item in (ffn1_bias, attn_bias, conv_channel, ffn2_bias, norm_params):
        pieces.append(take(item, off))
        off += item.size
    b1 = pieces[0].transpose(1, 2, 0, 3).reshape(-1)
    vec = pieces[1].transpose(2, 1, 3, 0, 4).reshape(attn_bias.shape[0], -1)
    cvec = pieces[2].transpose(2, 1, 3, 0, 4).reshape(conv_channel.shape[0], -1)
    b2 = pieces[3].transpose(1, 2, 0, 3).reshape(-1)
    norms = pieces[4].transpose(2, 0, 1, 3).reshape(norm_params.shape[0], -1)

    def cat(name):
        return jnp.concatenate(full_w[name], axis=1)

    def cat3(name, parts):
        pair = [item.reshape(item.shape[0], parts, -1) for item in full_w[name]]
        return jnp.concatenate(pair, axis=2)

    ffn1_w = (cat("f1i"), cat("f1o"), b1)
    ffn2_w = (cat("f2i"), cat("f2o"), b2)
    w_qkv, w_pos, w_out_t = cat3("qkv", 3), cat("pos"), cat("out")
    w_ci, w_co_t = cat3("ci", 2), cat("co")
    mine = lax.axis_index("tensor")
    lens = lax.dynamic_slice_in_dim(lengths, mine * seqs, seqs, 1).reshape(-1)
    positions = jnp.arange(full, dtype=jnp.int32)
    valid = (positions[None, :] < lens[:, None]).astype(F32)
    mask3 = valid[:, :, None]
    table = position_table(full, width).astype(BF)
    x0 = frames.reshape(batch, full, width).astype(F32)
    y1, kept1 = ffn_forward(x0, norms[0], norms[1], norms[2], ffn1_w)
    x1 = x0 + 0.5 * y1
    normed, scaled2, inv2 = norm_forward(x1, norms[3], norms[4])
    hn2 = normed.astype(BF)
    proj = jnp.einsum("uth,hkc->utkc", hn2, w_qkv, preferred_element_type=F32)
    query = proj[:, :, 0] + vec[0]
    keys = proj[:, :, 1].astype(BF)
    values = (proj[:, :, 2] + vec[1]).astype(BF)
    q_u = (query + vec[2]).astype(BF)
    q_v = (query + vec[3]).astype(BF)
    pos = jnp.dot(table, w_pos, preferred_element_type=F32).astype(BF)
    mixed, lse = attn_fwd_call(lens, q_u, q_v, keys, values, pos)
    y2 = jnp.einsum("utc,hc->uth", mixed, w_out_t, preferred_element_type=F32) + norms[5]
    x2 = x1 + y2
    normed, scaled3, inv3 = norm_forward(x2, norms[6], norms[7])
    hn3 = normed.astype(BF)
    halves = jnp.einsum("uth,hkc->utkc", hn3, w_ci, preferred_element_type=F32) + cvec[0:2]
    gate = jax.nn.sigmoid(halves[:, :, 1])
    gated = halves[:, :, 0] * gate * mask3
    conv = depthwise(gated, cvec[4:])

    def by_micro(item):
        return jnp.sum(item.reshape(micro, seqs, full, width), axis=(1, 2))

    def reduce_sum(item, cid):
        if mine_mesh:
            return sum_all(item.reshape(-1, 128), cid).reshape(item.shape)
        return lax.psum(item, both)

    counts = jnp.sum(lens.reshape(micro, seqs), axis=1).astype(F32)
    stats = reduce_sum(
        jnp.stack(
            [
                by_micro(conv * mask3),
                by_micro(conv * conv * mask3),
                jnp.broadcast_to(counts[:, None], (micro, width)),
            ]
        ),
        2,
    )
    avg = stats[0] / stats[2]
    var = stats[1] / stats[2] - avg * avg
    rstd = lax.rsqrt(var + norm_eps)

    def spread(item):
        return jnp.repeat(item, seqs, axis=0)[:, None, :]

    yhat = (conv - spread(avg)) * spread(rstd)
    bn = yhat * cvec[2] + cvec[3]
    act = swish_act(bn).astype(BF)
    y3 = jnp.einsum("utc,hc->uth", act, w_co_t, preferred_element_type=F32) + norms[8]
    x3 = x2 + y3
    y4, kept4 = ffn_forward(x3, norms[9], norms[10], norms[11], ffn2_w)
    x4 = x3 + 0.5 * y4
    result, scaled5, inv5 = norm_forward(x4, norms[12], norms[13])
    seed = cotangent.reshape(batch, full, width).astype(F32) * mask3
    d4, g12, g13 = norm_backward(seed, scaled5, inv5, norms[12])
    delta, grads_f2, norms_f2 = ffn_backward(0.5 * d4, kept4, norms[9], ffn2_w)
    d3 = d4 + delta
    g = d3.astype(BF)
    g8 = jnp.sum(g.astype(F32), axis=(0, 1))
    g_co = jnp.einsum("uth,utc->hc", g, act, preferred_element_type=F32)
    d_bn = jnp.einsum("uth,hc->utc", g, w_co_t, preferred_element_type=F32) * swish_slope(bn)
    g_scale = jnp.sum(d_bn * yhat, axis=(0, 1))
    g_offset = jnp.sum(d_bn, axis=(0, 1))
    d_yhat = d_bn * cvec[2]
    sums = reduce_sum(jnp.stack([by_micro(d_yhat), by_micro(d_yhat * yhat)]), 3)
    d_conv = spread(rstd) * (
        d_yhat - mask3 * (spread(sums[0]) + yhat * spread(sums[1])) / spread(stats[2])
    )
    d_gated, g_taps = depthwise_back(d_conv, gated, cvec[4:])
    d_glu = d_gated * mask3
    d_half = jnp.stack(
        [d_glu * gate, d_glu * halves[:, :, 0] * gate * (1.0 - gate)], axis=2
    ).astype(BF)
    g_cbias = jnp.sum(d_half.astype(F32), axis=(0, 1))
    g_ci = jnp.einsum("uth,utkc->hkc", hn3, d_half, preferred_element_type=F32)
    d_hn3 = jnp.einsum("utkc,hkc->uth", d_half, w_ci, preferred_element_type=F32)
    delta, g6, g7 = norm_backward(d_hn3, scaled3, inv3, norms[6])
    d2 = d3 + delta
    g = d2.astype(BF)
    g5 = jnp.sum(g.astype(F32), axis=(0, 1))
    g_out = jnp.einsum("uth,utc->hc", g, mixed, preferred_element_type=F32)
    d_mixed = jnp.einsum("uth,hc->utc", g, w_out_t, preferred_element_type=F32).astype(BF)
    dq, dk, dv, dpos, asums = attn_bwd_call(
        lens, q_u, q_v, keys, values, pos, mixed, lse, d_mixed
    )
    g_vec = jnp.sum(asums, axis=0)[0:4]
    g_pos = jnp.einsum("ph,upc->hc", table, dpos, preferred_element_type=F32)
    d_proj = jnp.stack([dq, dk, dv], axis=2)
    g_qkv = jnp.einsum("uth,utkc->hkc", hn2, d_proj, preferred_element_type=F32)
    d_hn2 = jnp.einsum("utkc,hkc->uth", d_proj, w_qkv, preferred_element_type=F32)
    delta, g3, g4 = norm_backward(d_hn2, scaled2, inv2, norms[3])
    d1 = d2 + delta
    delta, grads_f1, norms_f1 = ffn_backward(0.5 * d1, kept1, norms[0], ffn1_w)
    d0 = (d1 + delta).astype(BF)
    g_norm = jnp.stack(
        norms_f1 + (g3, g4, g5) + (g6, g7, g8) + norms_f2 + (g12, g13)
    )
    g_cvec = jnp.concatenate([g_cbias, g_scale[None], g_offset[None], g_taps], axis=0)

    def half(item, t):
        part = item.reshape(item.shape[0], -1, item.shape[-1])
        step = part.shape[-1] // 2
        return part[:, :, t * step : (t + 1) * step].reshape(n_dp, rows, -1)

    wide = (
        grads_f1[0], grads_f1[1], g_qkv, g_pos, g_out, g_ci, g_co, grads_f2[0], grads_f2[1],
    )
    vecs = (
        grads_f1[2].reshape(1, -1), g_vec, g_cvec, grads_f2[2].reshape(1, -1),
    )

    def small_of(item, like):
        lead = item.shape[0]
        item = item.reshape(lead, 2, like.shape[-2], n_dp, like.shape[-1])
        return item.transpose(1, 3, 0, 2, 4).reshape(2, n_dp, -1)

    cols = norm_params.shape[1]
    small_g = jnp.concatenate(
        [small_of(item, like) for item, like in zip(vecs, small_ins)]
        + [
            g_norm.reshape(-1, n_dp, 2, cols).transpose(2, 1, 0, 3).reshape(2, n_dp, -1),
        ],
        axis=2,
    )
    grads = jnp.stack(
        [jnp.concatenate([half(item, t) for item in wide], axis=2).astype(BF) for t in (0, 1)]
    )
    if mine_mesh:
        small_g = jnp.pad(small_g, ((0, 0), (0, 0), (0, 1024 - small_g.shape[2])))
        own, own_small = scatter_all(
            grads.reshape(2, NZ, NY, NX, rows, -1),
            small_g.reshape(2, NZ, NY, NX, 8, 128),
            split_cols(grads.shape[-1]),
            4,
        )
        own_small = own_small.reshape(-1)
    else:
        grads = grads.swapaxes(0, 1).reshape(n_dp * 2 * rows, -1)
        own = lax.psum_scatter(grads, both, scatter_dimension=0, tiled=True).astype(F32)
        small_g = small_g.swapaxes(0, 1).reshape(n_dp * 2, -1)
        own_small = lax.psum_scatter(small_g, both, scatter_dimension=0, tiled=True).reshape(-1)
    outs = [own[:, start : start + size] for start, size in zip(starts, sizes)]
    small_outs = []
    off = 0
    for item in small_ins:
        small_outs.append(own_small[off : off + item.size].reshape(item.shape))
        off += item.size
    return (
        result.astype(BF).reshape(frames.shape),
        d0.reshape(frames.shape),
        outs[0],
        outs[1].T,
        small_outs[0],
        outs[2].reshape(qkv_weight.shape),
        outs[3],
        outs[4].T,
        small_outs[1],
        outs[5].reshape(conv_in.shape),
        outs[6].T,
        small_outs[2],
        outs[7],
        outs[8].T,
        small_outs[3],
        small_outs[4],
    )


def solution(mesh):
    in_specs = (
        P(None, ("dp", "tensor"), None, None),
        P(None, "dp"),
        P("dp", "tensor"),
        P("tensor", "dp"),
        P("tensor", "dp"),
        P("dp", None, "tensor"),
        P("dp", "tensor"),
        P("tensor", "dp"),
        P(None, "tensor", "dp"),
        P("dp", None, "tensor"),
        P("tensor", "dp"),
        P(None, "tensor", "dp"),
        P("dp", "tensor"),
        P("tensor", "dp"),
        P("tensor", "dp"),
        P(None, ("dp", "tensor")),
        P(None, ("dp", "tensor"), None, None),
    )
    out_specs = (
        P(None, ("dp", "tensor"), None, None),
        P(None, ("dp", "tensor"), None, None),
        P("dp", "tensor"),
        P("tensor", "dp"),
        P("tensor", "dp"),
        P("dp", None, "tensor"),
        P("dp", "tensor"),
        P("tensor", "dp"),
        P(None, "tensor", "dp"),
        P("dp", None, "tensor"),
        P("tensor", "dp"),
        P(None, "tensor", "dp"),
        P("dp", "tensor"),
        P("tensor", "dp"),
        P("tensor", "dp"),
        P(None, ("dp", "tensor")),
    )
    return jax.shard_map(local, mesh=mesh, in_specs=in_specs, out_specs=out_specs, check_vma=False)
```

```python
import math

import jax
import jax.numpy as jnp
from jax import lax
from jax.experimental import pallas as pl
from jax.experimental.pallas import tpu as pltpu
from jax.sharding import PartitionSpec as P

DK = 64
norm_eps = 1e-05
mask_fill = -1000000000.0
BF = jnp.bfloat16
F32 = jnp.float32
BLK = 128


def nn(a, b):
    return lax.dot_general(a, b, (((1,), (0,)), ((), ())), preferred_element_type=F32)


def nt(a, b):
    return lax.dot_general(a, b, (((1,), (1,)), ((), ())), preferred_element_type=F32)


def tn(a, b):
    return lax.dot_general(a, b, (((0,), (0,)), ((), ())), preferred_element_type=F32)


def attn_fwd_kernel(len_ref, qu, qv, k, v, pos, o_ref, lse_ref, hook=None):
    count = len_ref[pl.program_id(0)]
    full = k.shape[1]
    lane = lax.broadcasted_iota(jnp.int32, (BLK, 2 * DK), 1)
    col = lax.broadcasted_iota(jnp.int32, (BLK, full), 1)
    keep = col < count
    zero = jnp.zeros((), BF)
    for blk in range(full // BLK):
        i0 = blk * BLK
        base = full - BLK - i0
        if hook is not None:
            hook(blk)
        outs, logs = [], []
        for h in range(2):
            mine = (lane < DK) if h == 0 else (lane >= DK)
            q_u = jnp.where(mine, qu[0, i0 : i0 + BLK, :], zero)
            q_v = jnp.where(mine, qv[0, i0 : i0 + BLK, :], zero)
            rel = nt(q_v, pos[base : base + full + BLK, :])
            rel = pltpu.roll(rel, full + 1, 1, stride=1, stride_axis=0)[:, :full]
            s = (nt(q_u, k[0]) + rel) * (1.0 / math.sqrt(DK))
            s = jnp.where(keep, s, mask_fill)
            top = jnp.max(s, axis=1, keepdims=True)
            e = jnp.exp(s - top)
            total = jnp.sum(e, axis=1, keepdims=True)
            outs.append(nn(e.astype(BF), v[0]) / total)
            logs.append(top + jnp.log(total))
        left = lane < DK
        o_ref[0, i0 : i0 + BLK, :] = jnp.where(left, outs[0], outs[1]).astype(BF)
        lse_ref[0, i0 : i0 + BLK, :] = jnp.where(left, logs[0], logs[1])


def attn_bwd_kernel(
    len_ref, qu, qv, k, v, pos, o, lse, do, dq_ref, dk_ref, dv_ref, dpos_ref, sum_ref, dkt, dvt, dpt,
    hook=None,
):
    count = len_ref[pl.program_id(0)]
    full = k.shape[1]
    scale = 1.0 / math.sqrt(DK)
    lane = lax.broadcasted_iota(jnp.int32, (BLK, 2 * DK), 1)
    left = lane < DK
    keep = lax.broadcasted_iota(jnp.int32, (BLK, full), 1) < count
    zero = jnp.zeros((), BF)
    flip = (lane + lax.broadcasted_iota(jnp.int32, (BLK, 2 * DK), 0) == BLK - 1).astype(F32).astype(BF)
    dkt[...] = jnp.zeros_like(dkt)
    dvt[...] = jnp.zeros_like(dvt)
    dpt[...] = jnp.zeros_like(dpt)
    sum_q = jnp.zeros((1, 2 * DK), F32)
    sum_u = jnp.zeros((1, 2 * DK), F32)
    sum_v = jnp.zeros((1, 2 * DK), F32)
    for blk in range(full // BLK):
        i0 = blk * BLK
        base = full - BLK - i0
        rows = slice(i0, i0 + BLK)
        win = slice(base, base + full + BLK)
        if hook is not None:
            hook(blk)
        qu_t = qu[0, rows, :].astype(F32).T.astype(BF)
        do_t = do[0, rows, :].astype(F32).T.astype(BF)
        qv_t = tn(qv[0, rows, :], flip).astype(BF)
        dot_o = do[0, rows, :].astype(F32) * o[0, rows, :].astype(F32)
        parts_u, parts_v = [], []
        for h in range(2):
            mine = left if h == 0 else lane >= DK
            hs = slice(h * DK, h * DK + DK)
            q_u = jnp.where(mine, qu[0, rows, :], zero)
            q_v = jnp.where(mine, qv[0, rows, :], zero)
            d_o = jnp.where(mine, do[0, rows, :], zero)
            rel = nt(q_v, pos[win, :])
            rel = pltpu.roll(rel, full + 1, 1, stride=1, stride_axis=0)[:, :full]
            s = (nt(q_u, k[0]) + rel) * scale - lse[0, rows, h * DK : h * DK + 1]
            p = jnp.where(keep, jnp.exp(jnp.minimum(s, 0.0)), 0.0)
            delta = jnp.sum(jnp.where(mine, dot_o, 0.0), axis=1, keepdims=True)
            ds = (p * (nt(d_o, v[0]) - delta)).astype(BF)
            dvt[hs, :] += nn(do_t[hs, :], p.astype(BF))
            dkt[hs, :] += nn(qu_t[hs, :], ds)
            parts_u.append(nn(ds, k[0]))
            wide = jnp.concatenate([nn(flip, ds), jnp.zeros((BLK, BLK), F32)], axis=1)
            wide = pltpu.roll(wide, 0, 1, stride=1, stride_axis=0).astype(BF)
            parts_v.append(nn(wide, pos[win, :]))
            dpt[hs, win] += nn(qv_t[hs, :], wide)
        d_u = jnp.where(left, parts_u[0], parts_u[1]) * scale
        d_v = jnp.where(left, parts_v[0], parts_v[1]) * scale
        high = d_v.astype(BF)
        low = (d_v - high.astype(F32)).astype(BF)
        d_q = (d_u + nn(flip, high) + nn(flip, low)).astype(BF)
        dq_ref[0, rows, :] = d_q
        sum_q += jnp.sum(d_q.astype(F32), axis=0, keepdims=True)
        sum_u += jnp.sum(d_u, axis=0, keepdims=True)
        sum_v += jnp.sum(d_v, axis=0, keepdims=True)
    dk_ref[0] = (dkt[...].T * scale).astype(BF)
    d_val = dvt[...].T.astype(BF)
    dv_ref[0] = d_val
    dpos_ref[0] = (dpt[...].T * scale).astype(BF)
    sum_ref[0, 0:1, :] = sum_q
    sum_ref[0, 1:2, :] = jnp.sum(d_val.astype(F32), axis=0, keepdims=True)
    sum_ref[0, 2:3, :] = sum_u
    sum_ref[0, 3:4, :] = sum_v
    sum_ref[0, 4:8, :] = jnp.zeros((4, 2 * DK), F32)


def attn_specs(rows, full, width):
    pairs = width // (2 * DK)
    main = pl.BlockSpec((1, full, 2 * DK), lambda u, p, n: (u, 0, p))
    pos = pl.BlockSpec((2 * full, 2 * DK), lambda u, p, n: (0, p))
    return (rows, pairs), main, pos


def attn_fwd_call(lens, qu, qv, k, v, pos, packed=None, cid=None):
    rows, full, width = qu.shape
    grid, main, pspec = attn_specs(rows, full, width)
    out_shape = [
        jax.ShapeDtypeStruct((rows, full, width), BF),
        jax.ShapeDtypeStruct((rows, full, width), F32),
    ]
    args = [lens, qu, qv, k, v, pos]
    in_specs, out_specs, scratch = [main] * 4 + [pspec], [main, main], []
    body, params = attn_fwd_kernel, dense_params()
    if packed is not None:
        widths = even_cols(packed.shape[1], 6)
        in_specs.append(pl.BlockSpec(packed.shape, lambda u, p, n: (0, 0)))
        out_specs.append(ANY)
        out_shape.append(gathered_shape(packed))
        scratch = gather_scratch(len(widths))
        args.append(packed)
        params = comm_params(cid)

        def body(len_ref, qu, qv, k, v, pos, x_ref, o_ref, lse_ref, g_ref, *sems):
            at = pl.program_id(0) * grid[1] + pl.program_id(1)
            steps = gather_steps(widths, x_ref, g_ref, sems)
            last = grid[0] * grid[1] - 1
            attn_fwd_kernel(
                len_ref, qu, qv, k, v, pos, o_ref, lse_ref, hooks_of(steps[:-1], at, last, full // BLK)
            )

            @pl.when(at == last)
            def _():
                steps[-1]()

    return pl.pallas_call(
        body,
        grid_spec=pltpu.PrefetchScalarGridSpec(
            num_scalar_prefetch=1,
            grid=grid,
            in_specs=in_specs,
            out_specs=out_specs,
            scratch_shapes=scratch,
        ),
        out_shape=out_shape,
        compiler_params=params,
        name="attn_fwd",
    )(*args)


def attn_bwd_call(lens, qu, qv, k, v, pos, o, lse, do, early=None, kinds=None, cid=None):
    rows, full, width = qu.shape
    grid, main, pspec = attn_specs(rows, full, width)
    args = [lens, qu, qv, k, v, pos, o, lse, do]
    in_specs = [main] * 4 + [pspec] + [main] * 3
    out_specs = [
        main,
        main,
        main,
        pl.BlockSpec((1, 2 * full, 2 * DK), lambda u, p, n: (u, 0, p)),
        pl.BlockSpec((1, 8, 2 * DK), lambda u, p, n: (u, 0, p)),
    ]
    scratch = [
        pltpu.VMEM((2 * DK, full), F32),
        pltpu.VMEM((2 * DK, full), F32),
        pltpu.VMEM((2 * DK, 2 * full), F32),
    ]
    out_shape = [jax.ShapeDtypeStruct((rows, full, width), BF)] * 3 + [
        jax.ShapeDtypeStruct((rows, 2 * full, width), BF),
        jax.ShapeDtypeStruct((rows, 8, width), F32),
    ]
    body, params = attn_bwd_kernel, dense_params()
    if early is not None:
        items = [split_owners(item) for item in early]
        outs = [scattered_shape(item, kind) for item, kind in zip(items, kinds)]
        n_in, n_out = len(args) - 1, len(out_shape)
        args += items
        in_specs += [ANY] * len(items)
        out_specs += [
            pl.BlockSpec(o.shape, lambda u, p, n, rank=len(o.shape): (0,) * rank) for o in outs
        ]
        out_shape += outs
        scratch += scatter_scratch(items)
        params = comm_params(cid)

        def body(*refs):
            at = pl.program_id(0) * grid[1] + pl.program_id(1)
            last = grid[0] * grid[1] - 1
            m = len(items)
            ins, rest = refs[: 1 + n_in], refs[1 + n_in :]
            g_refs, rest = rest[:m], rest[m:]
            mains, rest = rest[:n_out], rest[n_out:]
            o_refs, rest = rest[:m], rest[m:]
            own, sems = rest[:3], rest[3:]
            steps = scatter_steps(g_refs, o_refs, kinds, sems, 2)
            attn_bwd_kernel(*ins, *mains, *own, hook=hooks_of(steps[:-1], at, last, full // BLK))

            @pl.when(at == last)
            def _():
                steps[-1]()

    return pl.pallas_call(
        body,
        grid_spec=pltpu.PrefetchScalarGridSpec(
            num_scalar_prefetch=1,
            grid=grid,
            in_specs=in_specs,
            out_specs=out_specs,
            scratch_shapes=scratch,
        ),
        out_shape=out_shape,
        compiler_params=params,
        name="attn_bwd",
    )(*args)


def hooks_of(steps, at, last, spots):
    def hook(blk):
        for i, step in enumerate(steps):
            where, spot = divmod(i * (last + 1) * spots // len(steps), spots)
            if spot == blk:

                @pl.when(at == where)
                def _(step=step):
                    step()

    return hook


MESH = pl.DeviceIdType.MESH
NZ, NY, NX = 4, 2, 2
ANY = pl.BlockSpec(memory_space=pl.ANY)
VM = pl.BlockSpec(memory_space=pltpu.VMEM)


def own_mesh(sizes):
    return sizes == (NZ * NY * NX, 2)


def place():
    dp = lax.axis_index("dp")
    return dp // (NY * NX), dp // NX % NY, dp % NX, lax.axis_index("tensor")


def dev(z, y, x, t):
    return (z * (NY * NX) + y * NX + x, t)


def greet(peers):
    barrier = pltpu.get_barrier_semaphore()
    for peer in peers:
        pl.semaphore_signal(barrier, inc=1, device_id=peer, device_id_type=MESH)
    pl.semaphore_wait(barrier, len(peers))


def rcopy(src, dst, send, recv, peer):
    return pltpu.make_async_remote_copy(
        src_ref=src, dst_ref=dst, send_sem=send, recv_sem=recv, device_id=peer, device_id_type=MESH
    )


def link_peers(z, y, x, t):
    peers = [dev(lax.rem(z + d, NZ), y, x, t) for d in range(1, NZ)]
    return peers + [dev(z, 1 - y, x, t), dev(z, y, 1 - x, t), dev(z, y, x, 1 - t)]


def sum_kernel(x_ref, o_ref, mid, b1, b2, s1, r1, s2, r2):
    z, y, x, t = place()
    spot = (y * NX + x) * 2 + t
    zs = [dev(lax.rem(z + d, NZ), y, x, t) for d in range(1, NZ)]
    flat = [lax.rem(spot + d, 8) for d in range(1, 8)]
    plane = [dev(z, p // 4, p // 2 % 2, p % 2) for p in flat]
    greet(zs + plane)
    first = [rcopy(x_ref, b1.at[i], s1.at[i], r1.at[i], peer) for i, peer in enumerate(zs)]
    for copy in first:
        copy.start()
    for copy in first:
        copy.wait_recv()
    mid[...] = (x_ref[...] + b1[0]) + (b1[1] + b1[2])
    second = [rcopy(mid, b2.at[i], s2.at[i], r2.at[i], peer) for i, peer in enumerate(plane)]
    for copy in second:
        copy.start()
    for copy in second:
        copy.wait_recv()
    total = mid[...]
    for i in range(7):
        total = total + b2[i]
    o_ref[...] = total
    for copy in first + second:
        copy.wait_send()


def sum_all(item, cid):
    return pl.pallas_call(
        sum_kernel,
        out_shape=jax.ShapeDtypeStruct(item.shape, F32),
        in_specs=[VM],
        out_specs=VM,
        scratch_shapes=[
            pltpu.VMEM(item.shape, F32),
            pltpu.VMEM((3,) + item.shape, F32),
            pltpu.VMEM((7,) + item.shape, F32),
            pltpu.SemaphoreType.DMA((3,)),
            pltpu.SemaphoreType.DMA((3,)),
            pltpu.SemaphoreType.DMA((7,)),
            pltpu.SemaphoreType.DMA((7,)),
        ],
        compiler_params=pltpu.CompilerParams(collective_id=cid, has_side_effects=True),
        name="sum_all",
    )(item)


def even_cols(total, count):
    tiles = total // 128
    base = tiles // count
    return [128 * (base + (1 if i < tiles - base * count else 0)) for i in range(count)]


def comm_params(cid):
    return pltpu.CompilerParams(
        collective_id=cid, has_side_effects=True, vmem_limit_bytes=60 * 1024 * 1024
    )


def gathered_shape(packed):
    return jax.ShapeDtypeStruct((2, NZ, NY, NX) + packed.shape, packed.dtype)


def gather_scratch(n):
    dma = pltpu.SemaphoreType.DMA
    return [dma((n, NZ - 1)), dma((n, NZ - 1))] + [dma((n,))] * 6 + [dma]


def gather_steps(widths, x_ref, g_ref, sems):
    zs, zr, as_, ar, bs, br, cs, cr, own_sem = sems
    z, y, x, t = place()
    along_x, along_y = dev(z, y, 1 - x, t), dev(z, 1 - y, x, t)
    count = len(widths)
    zc, ac, bc, cc = [], [], [], []
    at = 0
    for p, w in enumerate(widths):
        c = pl.ds(at, w)
        at += w
        zc.append(
            [
                rcopy(
                    x_ref.at[:, c],
                    g_ref.at[t, z, y, x, :, c],
                    zs.at[p, d - 1],
                    zr.at[p, d - 1],
                    dev(lax.rem(z + d, NZ), y, x, t),
                )
                for d in range(1, NZ)
            ]
        )
        line = g_ref.at[t, :, y, x, :, c]
        ac.append(rcopy(line, line, as_.at[p], ar.at[p], along_x if p % 2 == 0 else along_y))
        half = g_ref.at[t, :, y, :, :, c] if p % 2 == 0 else g_ref.at[t, :, :, x, :, c]
        bc.append(rcopy(half, half, bs.at[p], br.at[p], along_y if p % 2 == 0 else along_x))
        full = g_ref.at[t, :, :, :, :, c]
        cc.append(rcopy(full, full, cs.at[p], cr.at[p], dev(z, y, x, 1 - t)))

    def begin(greeted=False):
        if not greeted:
            greet(link_peers(z, y, x, t))
        own = pltpu.make_async_copy(x_ref, g_ref.at[t, z, y, x], own_sem)
        own.start()
        for copies in zc:
            for copy in copies:
                copy.start()
        own.wait()

    def advance(q):
        for p in (2 * q, 2 * q + 1):
            if p < count:
                for copy in zc[p]:
                    copy.wait_recv()
                ac[p].start()
        for p in (2 * q - 2, 2 * q - 1):
            if 0 <= p < count:
                ac[p].wait_recv()
                bc[p].start()
        for p in (2 * q - 4, 2 * q - 3):
            if 0 <= p < count:
                bc[p].wait_recv()
                cc[p].start()

    def finish():
        for copy in cc:
            copy.wait_recv()
        for copy in sum(zc, []) + ac + bc + cc:
            copy.wait_send()

    rounds = (count + 1) // 2 + 2
    return [begin] + [lambda q=q: advance(q) for q in range(rounds)] + [finish]


def small_steps(s_ref, v_ref, mid, b1, b2, s1, r1, s2, r2):
    z, y, x, t = place()
    spot = (y * NX + x) * 2 + t
    zs = [dev(lax.rem(z + d, NZ), y, x, t) for d in range(1, NZ)]
    flat = [lax.rem(spot + d, 8) for d in range(1, 8)]
    plane = [dev(z, p // 4, p // 2 % 2, p % 2) for p in flat]
    first = [rcopy(s_ref, b1.at[i], s1.at[i], r1.at[i], peer) for i, peer in enumerate(zs)]
    second = [rcopy(mid, b2.at[i], s2.at[i], r2.at[i], peer) for i, peer in enumerate(plane)]

    def begin():
        for copy in first:
            copy.start()

    def spread():
        for copy in first:
            copy.wait_recv()
        mid[...] = (s_ref[...] + b1[0]) + (b1[1] + b1[2])
        for copy in second:
            copy.start()

    def finish():
        for copy in second:
            copy.wait_recv()
        same, other = mid[...].astype(F32), b2[0].astype(F32)
        for i in range(1, 7):
            if i % 2 == 1:
                same = same + b2[i].astype(F32)
            else:
                other = other + b2[i].astype(F32)
        low = jnp.where(t == 0, same, other)
        high = jnp.where(t == 0, other, same)
        v_ref[...] = jnp.zeros_like(v_ref)
        for q in range(4):
            r = S_NORM + 14 * q
            v_ref[0:14, 128 * q : 128 * q + 128] = low[r : r + 14] + high[r : r + 14]
        for i, part in enumerate((low, high)):
            for q in range(2):
                c = slice((2 * i + q) * 128, (2 * i + q) * 128 + 128)
                v_ref[R_ATT:R_CV, c] = part[S_ATT + 4 * q : S_ATT + 4 * q + 4]
                v_ref[R_CV:R_B1, c] = part[S_CV + 13 * q : S_CV + 13 * q + 13]
            for q in range(8):
                r, c = 2 * i + q // 4, slice(q % 4 * 128, q % 4 * 128 + 128)
                v_ref[R_B1 + r : R_B1 + r + 1, c] = part[S_B1 + q : S_B1 + q + 1]
                v_ref[R_B2 + r : R_B2 + r + 1, c] = part[S_B2 + q : S_B2 + q + 1]
        for copy in first + second:
            copy.wait_send()

    return plane, begin, spread, finish


S_B1, S_ATT, S_CV, S_B2, S_NORM, S_ALL = 0, 8, 16, 42, 50, 112


def lanes_of(n, offset):
    at = lax.broadcasted_iota(jnp.int32, (n, 128), 0) + offset
    return (lax.broadcasted_iota(jnp.int32, (n, 128), 1) == at).astype(F32)


def prep_kernel(
    f1i, f1o, pos, qkv, f2i, f2o, ci, out, co, b1, att, cv, b2, norm,
    pa_ref, pb_ref, slab_ref, table_ref, slab,
):
    def put(ref, at, value):
        ref[:, at : at + value.shape[1]] = value

    def flip(ref):
        return ref[...].astype(F32).T.astype(BF)

    put(pa_ref, 0, f1i[...])
    put(pa_ref, 1024, flip(f1o))
    put(pa_ref, 2048, pos[...])
    put(pb_ref, 0, f2i[...])
    put(pb_ref, 1024, flip(f2o))
    put(pa_ref, 2304, qkv[...])
    put(pb_ref, 2048, ci[...])
    put(pb_ref, 2560, flip(out))
    put(pb_ref, 2816, flip(co))
    z, y, x, t = place()
    dp = z * (NY * NX) + y * NX + x
    sel = lanes_of(8, dp * 8).astype(BF)
    slab[...] = jnp.zeros_like(slab)
    slab[S_B1 : S_B1 + 8] = nn(b1[...], sel)
    slab[S_ATT : S_ATT + 8] = nn(att[...], sel)
    slab[S_CV : S_CV + 26] = nn(cv[...], sel)
    slab[S_B2 : S_B2 + 8] = nn(b2[...], sel)
    at = dp * 2 + t
    here = nn(norm[...], lanes_of(16, lax.rem(at, 8) * 16).astype(BF))
    for q in range(4):
        slab[S_NORM + 14 * q : S_NORM + 14 * q + 14] = here * (at // 8 == q).astype(F32)
    slab_ref[...] = slab[...].astype(BF)
    fill_table(table_ref)


def prep_call(items, smalls, full, width):
    rows = items[0].shape[0]
    return pl.pallas_call(
        prep_kernel,
        in_specs=[VM] * 14,
        out_specs=[VM] * 4,
        out_shape=[
            jax.ShapeDtypeStruct((rows, C_A), BF),
            jax.ShapeDtypeStruct((rows, C_B), BF),
            jax.ShapeDtypeStruct((S_ALL, 128), BF),
            jax.ShapeDtypeStruct((2 * full, width), BF),
        ],
        scratch_shapes=[pltpu.VMEM((S_ALL, 128), F32)],
        name="prepare",
    )(*items, *smalls)


def gather_call(packed, slab, width, cid):
    widths = even_cols(packed.shape[1], 8)
    dma = pltpu.SemaphoreType.DMA
    small = [
        pltpu.VMEM(slab.shape, BF), pltpu.VMEM((3,) + slab.shape, BF),
        pltpu.VMEM((7,) + slab.shape, BF), dma((3,)), dma((3,)), dma((7,)), dma((7,)),
    ]

    def body(x_ref, s_ref, g_ref, v_ref, *rest):
        steps = gather_steps(widths, x_ref, g_ref, rest[len(small) :])
        plane, begin, spread, finish = small_steps(s_ref, v_ref, *rest[: len(small)])
        barrier = pltpu.get_barrier_semaphore()
        z, y, x, t = place()
        peers = [dev(lax.rem(z + d, NZ), y, x, t) for d in range(1, NZ)] + plane
        for peer in peers:
            pl.semaphore_signal(barrier, inc=1, device_id=peer, device_id_type=MESH)
        pl.semaphore_wait(barrier, len(peers))
        steps[0](greeted=True)
        begin()
        for step in steps[1:3]:
            step()
        spread()
        for step in steps[3:5]:
            step()
        finish()
        for step in steps[5:]:
            step()

    return pl.pallas_call(
        body,
        out_shape=[gathered_shape(packed), jax.ShapeDtypeStruct((R_ALL, width), F32)],
        in_specs=[VM, VM],
        out_specs=[ANY, VM],
        scratch_shapes=small + gather_scratch(len(widths)),
        compiler_params=comm_params(cid),
        name="gather_first",
    )(packed, slab)


def split_owners(item):
    return item.reshape(2, NZ, NY, NX, item.shape[1] // (NZ * NY * NX), item.shape[2])


def scattered_shape(item, kind):
    rows, w = item.shape[-2:]
    shape = {"plain": (rows, w), "flip": (w, rows)}.get(kind[0])
    return jax.ShapeDtypeStruct(shape or (rows, kind[1], w // kind[1]), F32)


def piece_widths(items):
    pieces = []
    for i, item in enumerate(items):
        w = item.shape[-1]
        step = min(w, 256)
        pieces += [(i, at, step) for at in range(0, w, step)]
    return pieces


def scatter_scratch(items):
    pieces = piece_widths(items)
    n = len(pieces)
    rows = items[0].shape[-2]
    total = sum(w for _, _, w in pieces)
    dma = pltpu.SemaphoreType.DMA
    shape = (rows, total)
    return [
        pltpu.VMEM((NZ, NY, NX) + shape, BF),
        pltpu.VMEM((NZ, NY, NX) + shape, BF),
        pltpu.VMEM((NZ, 2) + shape, BF),
        pltpu.VMEM((NZ,) + shape, BF),
        pltpu.VMEM((NZ - 1,) + shape, BF),
    ] + [dma((n,))] * 7 + [dma((n, NZ - 1))] * 2


def scatter_steps(g_refs, o_refs, kinds, scratch, lag=1):
    own, rc, ra, rb, rz, lsem, cs, cr, as_, ar, bs, br, zs, zr = scratch
    z, y, x, t = place()
    along_x, along_y = dev(z, y, 1 - x, t), dev(z, 1 - y, x, t)
    mate = dev(z, y, x, 1 - t)
    pieces = piece_widths(g_refs)
    count = len(pieces)
    bufs, lc, cc, ac, bc, zc = [], [], [], [], [], []
    at = 0
    for p, (i, start, w) in enumerate(pieces):
        c = pl.ds(at, w)
        at += w
        g = pl.ds(start, w)
        b = dict(
            own=own.at[:, :, :, :, c], rc=rc.at[:, :, :, :, c], ra=ra.at[:, :, :, c],
            rb=rb.at[:, :, c], rz=rz.at[:, :, c],
        )
        bufs.append(b)
        even = p % 2 == 0
        lc.append(
            pltpu.make_async_copy(g_refs[i].at[t, :, :, :, :, g], b["own"], lsem.at[p])
        )
        cc.append(rcopy(g_refs[i].at[1 - t, :, :, :, :, g], b["rc"], cs.at[p], cr.at[p], mate))
        away = b["own"].at[:, 1 - y] if even else b["own"].at[:, :, 1 - x]
        ac.append(rcopy(away, b["ra"], as_.at[p], ar.at[p], along_y if even else along_x))
        line = b["own"].at[:, y, 1 - x] if even else b["own"].at[:, 1 - y, x]
        bc.append(rcopy(line, b["rb"], bs.at[p], br.at[p], along_x if even else along_y))
        zc.append([])
        for d in range(1, NZ):
            far = lax.rem(z + d, NZ)
            zc[p].append(
                rcopy(
                    b["own"].at[far, y, x], b["rz"].at[d - 1], zs.at[p, d - 1], zr.at[p, d - 1],
                    dev(far, y, x, t),
                )
            )

    def begin(greeted=False):
        if not greeted:
            greet(link_peers(z, y, x, t))
        for p in range(count):
            lc[p].start()
            cc[p].start()

    def advance(q):
        if q < count:
            lc[q].wait()
            cc[q].wait_recv()
            b = bufs[q]
            for i in range(NZ):
                b["own"][i] = b["own"][i] + b["rc"][i]
            ac[q].start()
        p = q - lag
        if 0 <= p < count:
            ac[p].wait_recv()
            b = bufs[p]
            for i in range(NZ):
                if p % 2 == 0:
                    b["own"][i, y] = b["own"][i, y] + b["ra"][i]
                else:
                    b["own"][i, :, x] = b["own"][i, :, x] + b["ra"][i]
            bc[p].start()
        p = q - 2 * lag
        if 0 <= p < count:
            bc[p].wait_recv()
            b = bufs[p]
            for i in range(NZ):
                b["own"][i, y, x] = b["own"][i, y, x] + b["rb"][i]
            for copy in zc[p]:
                copy.start()
        p = q - 3 * lag
        if 0 <= p < count:
            for copy in zc[p]:
                copy.wait_recv()
            b = bufs[p]
            total = b["own"][z, y, x].astype(F32)
            for d in range(NZ - 1):
                total = total + b["rz"][d].astype(F32)
            i, start, w = pieces[p]
            kind, o = kinds[i], o_refs[i]
            if kind[0] == "plain":
                o[:, start : start + w] = total
            elif kind[0] == "flip":
                o[start : start + w, :] = total.T
            else:
                part = o.shape[2]
                for at in range(0, w, 128):
                    k, c = (start + at) // part, (start + at) % part
                    o[:, k, c : c + 128] = total[:, at : at + 128]

    def finish():
        for copy in cc + ac + bc + sum(zc, []):
            copy.wait_send()

    return [begin] + [lambda q=q: advance(q) for q in range(count + 3 * lag)] + [finish]


def small_sum_steps(parts, o_refs, scratch):
    acc_s, ext, bc_, bz, bp, sc, rc, sz, rz, sp, rp, sm, rm = scratch
    z, y, x, t = place()
    dp = z * (NY * NX) + y * NX + x
    half = acc_s.shape[0] // 2
    mine = pl.ds(pl.multiple_of(t * half, 8), half)
    mate = dev(z, y, x, 1 - t)
    spot = y * NX + x
    zp = [dev(lax.rem(z + d, NZ), y, x, t) for d in range(1, NZ)]
    flat = [lax.rem(spot + d, 4) for d in range(1, 4)]
    pp = [dev(z, p // 2, p % 2, t) for p in flat]
    one = rcopy(acc_s, bc_, sc, rc, mate)
    two = [rcopy(acc_s.at[mine], bz.at[i], sz.at[i], rz.at[i], peer) for i, peer in enumerate(zp)]
    three = [rcopy(bz.at[3], bp.at[i], sp.at[i], rp.at[i], peer) for i, peer in enumerate(pp)]
    four = rcopy(bp.at[3], ext.at[mine], sm, rm, mate)

    def a():
        acc_s[...] = jnp.zeros_like(acc_s)
        acc_s[0:R_ALL] = parts[0][...] + parts[1][...] + parts[2][...]
        one.start()

    def b():
        one.wait()
        acc_s[...] = acc_s[...] + bc_[...]
        for copy in two:
            copy.start()

    def c():
        for copy in two:
            copy.wait()
        bz[3] = (acc_s[mine] + bz[0]) + (bz[1] + bz[2])
        for copy in three:
            copy.start()

    def d():
        for copy in three:
            copy.wait()
        bp[3] = (bz[3] + bp[0]) + (bp[1] + bp[2])
        four.start()
        ext[mine] = bp[3]

    def e():
        four.wait()
        b1, att, cv, b2, norm = o_refs
        sel = lanes_of(8, dp * 8)

        def own(v, pick):
            return lax.dot_general(
                v, pick, (((1,), (1,)), ((), ())), precision=lax.Precision.HIGHEST,
                preferred_element_type=F32,
            )

        for q in range(2):
            c = pl.ds(pl.multiple_of((2 * t + q) * 128, 128), 128)
            att[:, q, :] = own(ext[R_ATT:R_CV, c], sel)
            cv[:, q, :] = own(ext[R_CV:R_B1, c], sel)
        for o, at in ((b1, R_B1), (b2, R_B2)):
            for q in range(8):
                r, c = at + q // 4, slice(q % 4 * 128, q % 4 * 128 + 128)
                line = jnp.where(t == 0, ext[r : r + 1, c], ext[r + 2 : r + 3, c])
                o[q : q + 1, :] = own(line, sel)
        at = dp * 2 + t
        lane = pl.ds(pl.multiple_of(at // 8 * 128, 128), 128)
        norm[...] = own(ext[0:14, lane], lanes_of(16, lax.rem(at, 8) * 16))

    return pp, [a, b, c, d, e]


def scatter_call(grads, kinds, parts, like, cid):
    items = [split_owners(item) for item in grads]
    outs = [scattered_shape(item, kind) for item, kind in zip(items, kinds)]
    outs += [jax.ShapeDtypeStruct(item.shape, F32) for item in like]
    m = len(items)
    width = parts[0].shape[1]
    rows = 48
    dma = pltpu.SemaphoreType.DMA
    small = [
        pltpu.VMEM((rows, width), F32), pltpu.VMEM((rows, width), F32),
        pltpu.VMEM((rows, width), F32), pltpu.VMEM((4, rows // 2, width), F32),
        pltpu.VMEM((4, rows // 2, width), F32),
        dma, dma, dma((3,)), dma((3,)), dma((3,)), dma((3,)), dma, dma,
    ]

    def body(*refs):
        g_refs, rest = refs[:m], refs[m:]
        p_refs, rest = rest[:3], rest[3:]
        o_refs, rest = rest[: len(outs)], rest[len(outs) :]
        steps = scatter_steps(g_refs, o_refs[:m], kinds, rest[len(small) :], 2)
        pp, small_list = small_sum_steps(p_refs, o_refs[m:], rest[: len(small)])
        z, y, x, t = place()
        greet(link_peers(z, y, x, t)[: NZ - 1] + pp + [dev(z, y, x, 1 - t)])
        steps[0](greeted=True)
        small_list[0]()
        for i, step in enumerate(steps[1:]):
            step()
            if i + 1 < len(small_list):
                small_list[i + 1]()
        for extra in small_list[len(steps) :]:
            extra()

    return pl.pallas_call(
        body,
        out_shape=outs,
        in_specs=[ANY] * m + [VM] * 3,
        out_specs=[VM] * len(outs),
        scratch_shapes=small + scatter_scratch(items),
        compiler_params=comm_params(cid),
        name="scatter_last",
    )(*items, *parts)

SEG = {
    "f1i": (0, 1024), "f1o": (1024, 1024), "pos": (2048, 256), "qkv": (2304, 768),
    "f2i": (0, 1024), "f2o": (1024, 1024), "ci": (2048, 512), "out": (2560, 256),
    "co": (2816, 256),
}
C_A, C_B = 3072, 3072
R_ATT, R_CV, R_B1, R_B2, R_ALL = 14, 18, 31, 35, 40
TB = 256


def seg_spec(name, depth):
    start, width = SEG[name]
    return pl.BlockSpec(
        (2, depth, width), lambda i, *_: (0, 0, start // width), pipeline_mode=pl.Buffered(1)
    )


def whole(shape):
    zeros = (0,) * len(shape)
    return pl.BlockSpec(shape, lambda i, *_: zeros)


def tall(rows, width):
    return pl.BlockSpec((rows, width), lambda i, *_: (i, 0))


def sig(v):
    return 0.5 * jnp.tanh(0.5 * v) + 0.5


def row(ref, i):
    return ref[i : i + 1, :]


def col_sum(v):
    return jnp.sum(v, axis=0, keepdims=True)


def ln_stats(v):
    centered = v - jnp.mean(v, axis=1, keepdims=True)
    inv = lax.rsqrt(jnp.mean(centered * centered, axis=1, keepdims=True) + norm_eps)
    return centered * inv, inv


def ln_back(up, scaled, inv, gain):
    g = up * gain
    return inv * (
        g
        - jnp.mean(g, axis=1, keepdims=True)
        - scaled * jnp.mean(g * scaled, axis=1, keepdims=True)
    )


def bias_half(vecs, at, t):
    return jnp.concatenate([row(vecs, at + 2 * t), row(vecs, at + 2 * t + 1)], axis=1)


def row_mask(start, rows, count):
    at = start + lax.broadcasted_iota(jnp.int32, (rows, 1), 0)
    return (at < count).astype(F32)


def ffn1_kernel(
    x_ref, table, w_in, w_out, w_qkv, w_pos, vecs,
    first_ref, z_ref, qu_ref, qv_ref, k_ref, v_ref, pos_ref,
):
    x = x_ref[...].astype(F32)
    scaled, _ = ln_stats(x)
    hn = (scaled * row(vecs, 0) + row(vecs, 1)).astype(BF)
    half = w_in.shape[2]
    y = row(vecs, 2)
    for t in range(2):
        z = nn(hn, w_in[t]) + bias_half(vecs, R_B1, t)
        z_ref[:, t * half : (t + 1) * half] = z.astype(BF)
        y = y + nt((z * sig(z)).astype(BF), w_out[t])
    first = x + 0.5 * y
    first_ref[...] = first
    scaled, _ = ln_stats(first)
    hn = (scaled * row(vecs, 3) + row(vecs, 4)).astype(BF)
    part = w_qkv.shape[2] // 3
    for t in range(2):
        c = slice(t * part, (t + 1) * part)
        proj = nn(hn, w_qkv[t])
        q = proj[:, :part] + vecs[R_ATT : R_ATT + 1, c]
        qu_ref[:, c] = (q + vecs[R_ATT + 2 : R_ATT + 3, c]).astype(BF)
        qv_ref[:, c] = (q + vecs[R_ATT + 3 : R_ATT + 4, c]).astype(BF)
        k_ref[:, c] = proj[:, part : 2 * part].astype(BF)
        v_ref[:, c] = (proj[:, 2 * part :] + vecs[R_ATT + 1 : R_ATT + 2, c]).astype(BF)
        pos_ref[:, c] = nn(table[...], w_pos[t]).astype(BF)


def dense_params(mib=60):
    return pltpu.CompilerParams(vmem_limit_bytes=mib * 1024 * 1024)


def ffn1_call(x, table, g, vecs):
    tokens, width = x.shape
    steps = tokens // TB
    places = tall(table.shape[0] // steps, width)
    return pl.pallas_call(
        ffn1_kernel,
        grid=(steps,),
        in_specs=[
            tall(TB, width), places, seg_spec("f1i", width), seg_spec("f1o", width),
            seg_spec("qkv", width), seg_spec("pos", width), whole(vecs.shape),
        ],
        out_specs=[tall(TB, width), tall(TB, 4 * width)] + [tall(TB, width)] * 4 + [places],
        out_shape=[
            jax.ShapeDtypeStruct((tokens, width), F32),
            jax.ShapeDtypeStruct((tokens, 4 * width), BF),
        ]
        + [jax.ShapeDtypeStruct((tokens, width), BF)] * 4
        + [jax.ShapeDtypeStruct(table.shape, BF)],
        compiler_params=dense_params(),
        name="ffn1_forward",
    )(x, table, g, g, g, g, vecs)


def fill_table(table_ref):
    length, width = table_ref.shape[0] // 2, table_ref.shape[1]
    step = 32
    cols = lax.broadcasted_iota(jnp.int32, (step, width), 1)
    rows = lax.broadcasted_iota(jnp.int32, (step, width), 0)
    rate = jnp.exp((cols // 2 * 2).astype(F32) * (-math.log(10000.0) / width))
    even = cols % 2 == 0
    big = (length - 1 - step * rows).astype(F32) * rate
    small = rows.astype(F32) * rate
    sin_big, cos_big = jnp.sin(big), jnp.cos(big)
    first = jnp.where(even, sin_big, cos_big)
    second = jnp.where(even, cos_big, -sin_big)
    cos_small, sin_small = jnp.cos(small), jnp.sin(small)
    for a in range(2 * length // step):
        block = first[a : a + 1] * cos_small - second[a : a + 1] * sin_small
        table_ref[a * step : (a + 1) * step, :] = block.astype(BF)


def table_call(full, width):
    return pl.pallas_call(
        fill_table,
        out_specs=VM,
        out_shape=jax.ShapeDtypeStruct((2 * full, width), BF),
        name="position_table",
    )()


def conv1_kernel(
    lens, mixed, first, w_out, w_ci, vecs, second_ref, half_ref, conv_ref, stat_ref, pad
):
    u = pl.program_id(0)
    full = first.shape[0]
    count = lens[u]
    part = w_out.shape[2]
    y = row(vecs, 5)
    for t in range(2):
        y = y + nt(mixed[:, t * part : (t + 1) * part], w_out[t])
    second = first[...] + y
    second_ref[...] = second
    scaled, _ = ln_stats(second)
    hn = (scaled * row(vecs, 6) + row(vecs, 7)).astype(BF)
    mask = row_mask(0, full, count)
    pad[0:8, :] = jnp.zeros((8, part), F32)
    pad[full + 8 : full + 16, :] = jnp.zeros((8, part), F32)
    for t in range(2):
        c = slice(t * part, (t + 1) * part)
        proj = nn(hn, w_ci[t])
        za = proj[:, :part] + vecs[R_CV : R_CV + 1, c]
        zg = proj[:, part:] + vecs[R_CV + 1 : R_CV + 2, c]
        half_ref[:, 2 * t * part : (2 * t + 1) * part] = za.astype(BF)
        half_ref[:, (2 * t + 1) * part : (2 * t + 2) * part] = zg.astype(BF)
        pad[8 : full + 8, :] = za * sig(zg) * mask
        total = jnp.zeros((full, part), F32)
        for k in range(9):
            total = total + vecs[R_CV + 4 + k : R_CV + 5 + k, c] * pad[4 + k : 4 + k + full, :]
        conv_ref[:, c] = total
        kept = total * mask
        stat_ref[pl.ds(4 * u, 1), c] = col_sum(kept)
        stat_ref[pl.ds(4 * u + 1, 1), c] = col_sum(kept * total)
    for k in (2, 3):
        stat_ref[pl.ds(4 * u + k, 1), :] = jnp.full((1, 2 * part), 1.0, F32) * count.astype(F32)


def conv1_call(lens, mixed, first, g, vecs):
    tokens, width = first.shape
    batch = lens.shape[0]
    full = tokens // batch
    return pl.pallas_call(
        conv1_kernel,
        grid_spec=pltpu.PrefetchScalarGridSpec(
            num_scalar_prefetch=1,
            grid=(batch,),
            in_specs=[
                tall(full, width), tall(full, width), seg_spec("out", width),
                seg_spec("ci", width), whole(vecs.shape),
            ],
            out_specs=[
                tall(full, width), tall(full, 2 * width), tall(full, width),
                whole((4 * batch, width)),
            ],
            scratch_shapes=[pltpu.VMEM((full + 16, width // 2), F32)],
        ),
        out_shape=[
            jax.ShapeDtypeStruct((tokens, width), F32),
            jax.ShapeDtypeStruct((tokens, 2 * width), BF),
            jax.ShapeDtypeStruct((tokens, width), F32),
            jax.ShapeDtypeStruct((4 * batch, width), F32),
        ],
        compiler_params=dense_params(),
        name="conv_forward",
    )(lens, mixed, first, g, g, vecs)


def bn_of(stats, u):
    n = stats[pl.ds(4 * u + 2, 1), :]
    avg = stats[pl.ds(4 * u, 1), :] / n
    var = stats[pl.ds(4 * u + 1, 1), :] / n - avg * avg
    return avg, lax.rsqrt(var + norm_eps), n


def swish_parts(z):
    s = sig(z)
    a = z * s
    return a, s + a * (1.0 - s)


def middle_kernel(
    lens, second, conv, cot, stats, w_co, w_in, w_out, vecs,
    act_ref, d3_ref, dy_ref, sum_ref, small_ref, gi_ref, go_ref, gc_ref,
    a_s, slope_s, gi, go, gc,
):
    i = pl.program_id(0)
    steps = pl.num_programs(0)
    rows, width = second.shape
    batch = lens.shape[0]
    per = steps // batch
    u = i // per
    mask = row_mask(lax.rem(i, per) * rows, rows, lens[u])

    @pl.when(i == 0)
    def _():
        small_ref[...] = jnp.zeros_like(small_ref)
        sum_ref[...] = jnp.zeros_like(sum_ref)
        gi[...] = jnp.zeros_like(gi)
        go[...] = jnp.zeros_like(go)
        gc[...] = jnp.zeros_like(gc)

    avg, rstd, _ = bn_of(stats, u)
    part = w_co.shape[2]
    half = w_in.shape[2]
    yhat = (conv[...] - avg) * rstd
    bn, bn_slope = swish_parts(yhat * row(vecs, R_CV + 2) + row(vecs, R_CV + 3))
    act = bn.astype(BF)
    y = row(vecs, 8)
    for t in range(2):
        y = y + nt(act[:, t * part : (t + 1) * part], w_co[t])
    third = second[...] + y
    scaled9, inv9 = ln_stats(third)
    hn = (scaled9 * row(vecs, 9) + row(vecs, 10)).astype(BF)
    y = row(vecs, 11)
    for t in range(2):
        c = slice(t * half, (t + 1) * half)
        a, slope = swish_parts(nn(hn, w_in[t]) + bias_half(vecs, R_B2, t))
        a = a.astype(BF)
        a_s[:, c] = a
        slope_s[:, c] = slope
        y = y + nt(a, w_out[t])
    scaled, inv = ln_stats(third + 0.5 * y)
    act_ref[...] = (scaled * row(vecs, 12) + row(vecs, 13)).astype(BF)
    up = cot[...].astype(F32) * mask
    small_ref[12:13, :] += col_sum(up * scaled)
    small_ref[13:14, :] += col_sum(up)
    d4 = ln_back(up, scaled, inv, row(vecs, 12))
    g = (0.5 * d4).astype(BF)
    small_ref[11:12, :] += col_sum(g.astype(F32))
    d_hn = jnp.zeros((rows, width), F32)
    for t in range(2):
        c = slice(t * half, (t + 1) * half)
        go[t] += tn(g, a_s[:, c])
        dz = (nn(g, w_out[t]) * slope_s[:, c]).astype(BF)
        bias = col_sum(dz.astype(F32))
        small_ref[R_B2 + 2 * t : R_B2 + 2 * t + 1, :] += bias[:, :width]
        small_ref[R_B2 + 2 * t + 1 : R_B2 + 2 * t + 2, :] += bias[:, width:]
        gi[t] += tn(hn, dz)
        d_hn = d_hn + nt(dz, w_in[t])
    small_ref[9:10, :] += col_sum(d_hn * scaled9)
    small_ref[10:11, :] += col_sum(d_hn)
    d3 = d4 + ln_back(d_hn, scaled9, inv9, row(vecs, 9))
    d3_ref[...] = d3
    g = d3.astype(BF)
    small_ref[8:9, :] += col_sum(g.astype(F32))
    d_act = []
    for t in range(2):
        gc[t] += tn(g, act[:, t * part : (t + 1) * part])
        d_act.append(nn(g, w_co[t]))
    d_bn = jnp.concatenate(d_act, axis=1) * bn_slope
    small_ref[R_CV + 2 : R_CV + 3, :] += col_sum(d_bn * yhat)
    small_ref[R_CV + 3 : R_CV + 4, :] += col_sum(d_bn)
    d_yhat = d_bn * row(vecs, R_CV + 2)
    dy_ref[...] = d_yhat
    sum_ref[pl.ds(4 * u, 1), :] += col_sum(d_yhat)
    sum_ref[pl.ds(4 * u + 1, 1), :] += col_sum(d_yhat * yhat)

    @pl.when(i == steps - 1)
    def _():
        gi_ref[...] = gi[...].astype(BF)
        go_ref[...] = go[...].astype(BF)
        gc_ref[...] = gc[...].astype(BF)


def grad_shape(name, width):
    return jax.ShapeDtypeStruct((2, width, SEG[name][1]), BF)


def acc(name, width):
    return pltpu.VMEM((2, width, SEG[name][1]), F32)


def once(shape):
    zeros = (0,) * len(shape)
    return pl.BlockSpec(shape, lambda i, *_: zeros, pipeline_mode=pl.Buffered(1))


def middle_call(lens, second, conv, cot, stats, g, vecs):
    tokens, width = second.shape
    small = (R_ALL, width)
    names = ("f2i", "f2o", "co")
    return pl.pallas_call(
        middle_kernel,
        grid_spec=pltpu.PrefetchScalarGridSpec(
            num_scalar_prefetch=1,
            grid=(tokens // TB,),
            in_specs=[tall(TB, width)] * 3
            + [whole(stats.shape), seg_spec("co", width), seg_spec("f2i", width)]
            + [seg_spec("f2o", width), whole(vecs.shape)],
            out_specs=[tall(TB, width)] * 3
            + [whole(stats.shape), whole(small)]
            + [whole(grad_shape(name, width).shape) for name in names],
            scratch_shapes=[
                pltpu.VMEM((TB, 4 * width), BF),
                pltpu.VMEM((TB, 4 * width), F32),
            ]
            + [acc(name, width) for name in names],
        ),
        out_shape=[
            jax.ShapeDtypeStruct((tokens, width), BF),
            jax.ShapeDtypeStruct((tokens, width), F32),
            jax.ShapeDtypeStruct((tokens, width), F32),
            jax.ShapeDtypeStruct(stats.shape, F32),
            jax.ShapeDtypeStruct(small, F32),
        ]
        + [grad_shape(name, width) for name in names],
        compiler_params=dense_params(),
        name="conv_out_ffn2",
    )(lens, second, conv, cot, stats, g, g, g, vecs)


def conv2_kernel(
    lens, dy, conv, d3, halves, second, mixed, stats, sums, w_ci, w_out, vecs,
    d2_ref, dm_ref, small_ref, gi_ref, go_ref, pad, gi, go,
):
    u = pl.program_id(0)
    full, width = d3.shape
    part = w_out.shape[2]

    @pl.when(u == 0)
    def _():
        small_ref[...] = jnp.zeros_like(small_ref)
        gi[...] = jnp.zeros_like(gi)
        go[...] = jnp.zeros_like(go)

    avg, rstd, n = bn_of(stats, u)
    mask = row_mask(0, full, lens[u])
    scaled, inv = ln_stats(second[...])
    hn = (scaled * row(vecs, 6) + row(vecs, 7)).astype(BF)
    pad[0:8, :] = jnp.zeros((8, part), F32)
    pad[full + 8 : full + 16, :] = jnp.zeros((8, part), F32)
    b1 = sums[pl.ds(4 * u, 1), :]
    b2 = sums[pl.ds(4 * u + 1, 1), :]
    d_hn = jnp.zeros((full, width), F32)
    for t in range(2):
        c = slice(t * part, (t + 1) * part)
        yhat = (conv[:, c] - avg[:, c]) * rstd[:, c]
        pad[8 : full + 8, :] = rstd[:, c] * (
            dy[:, c] - mask * ((b1[:, c] + yhat * b2[:, c]) / n[:, c])
        )
        za = halves[:, 2 * t * part : (2 * t + 1) * part].astype(F32)
        gate = sig(halves[:, (2 * t + 1) * part : (2 * t + 2) * part].astype(F32))
        gated = za * gate * mask
        total = jnp.zeros((full, part), F32)
        for k in range(9):
            moved = pad[12 - k : 12 - k + full, :]
            total = total + vecs[R_CV + 4 + k : R_CV + 5 + k, c] * moved
            small_ref[R_CV + 4 + k : R_CV + 5 + k, c] += col_sum(gated * moved)
        d_glu = total * mask
        d_a = (d_glu * gate).astype(BF)
        d_g = (d_glu * gated * (1.0 - gate)).astype(BF)
        small_ref[R_CV : R_CV + 1, c] += col_sum(d_a.astype(F32))
        small_ref[R_CV + 1 : R_CV + 2, c] += col_sum(d_g.astype(F32))
        both = jnp.concatenate([d_a, d_g], axis=1)
        gi[t] += tn(hn, both)
        d_hn = d_hn + nt(both, w_ci[t])
    small_ref[6:7, :] += col_sum(d_hn * scaled)
    small_ref[7:8, :] += col_sum(d_hn)
    d2 = d3[...] + ln_back(d_hn, scaled, inv, row(vecs, 6))
    d2_ref[...] = d2
    g = d2.astype(BF)
    small_ref[5:6, :] += col_sum(g.astype(F32))
    for t in range(2):
        c = slice(t * part, (t + 1) * part)
        go[t] += tn(g, mixed[:, c])
        dm_ref[:, c] = nn(g, w_out[t]).astype(BF)

    @pl.when(u == pl.num_programs(0) - 1)
    def _():
        gi_ref[...] = gi[...].astype(BF)
        go_ref[...] = go[...].astype(BF)


def conv2_call(lens, dy, conv, d3, halves, second, mixed, stats, sums, g, vecs):
    tokens, width = second.shape
    batch = lens.shape[0]
    full = tokens // batch
    small = (R_ALL, width)
    names = ("ci", "out")
    return pl.pallas_call(
        conv2_kernel,
        grid_spec=pltpu.PrefetchScalarGridSpec(
            num_scalar_prefetch=1,
            grid=(batch,),
            in_specs=[tall(full, width)] * 3
            + [tall(full, 2 * width), tall(full, width), tall(full, width)]
            + [whole(stats.shape)] * 2
            + [seg_spec("ci", width), seg_spec("out", width), whole(vecs.shape)],
            out_specs=[tall(full, width)] * 2
            + [whole(small)]
            + [whole(grad_shape(name, width).shape) for name in names],
            scratch_shapes=[pltpu.VMEM((full + 16, width // 2), F32)]
            + [acc(name, width) for name in names],
        ),
        out_shape=[
            jax.ShapeDtypeStruct((tokens, width), F32),
            jax.ShapeDtypeStruct((tokens, width), BF),
            jax.ShapeDtypeStruct(small, F32),
        ]
        + [grad_shape(name, width) for name in names],
        compiler_params=dense_params(),
        name="conv_backward",
    )(lens, dy, conv, d3, halves, second, mixed, stats, sums, g, g, vecs)


def last_kernel(
    dq, dk, dv, first, x_ref, d2, z_ref, table, dpos, asums, w_qkv, w_in, w_out, vecs,
    d0_ref, small_ref, gq_ref, gi_ref, go_ref, gp_ref, gq, gi, go, gp,
):
    i = pl.program_id(0)
    rows, width = first.shape
    part = w_qkv.shape[2] // 3
    half = w_in.shape[2]

    @pl.when(i == 0)
    def _():
        small_ref[...] = jnp.zeros_like(small_ref)
        small_ref[R_ATT:R_CV, :] = jnp.sum(asums[...], axis=0)[0:4]
        gp[...] = jnp.zeros_like(gp)
        gq[...] = jnp.zeros_like(gq)
        gi[...] = jnp.zeros_like(gi)
        go[...] = jnp.zeros_like(go)

    scaled, inv = ln_stats(first[...])
    hn = (scaled * row(vecs, 3) + row(vecs, 4)).astype(BF)
    d_hn = jnp.zeros((rows, width), F32)
    for t in range(2):
        c = slice(t * part, (t + 1) * part)
        dp = jnp.concatenate([dq[:, c], dk[:, c], dv[:, c]], axis=1)
        gq[t] += tn(hn, dp)
        for u in range(dpos.shape[0]):
            gp[t] += tn(table[...], dpos[u, :, c])
        d_hn = d_hn + nt(dp, w_qkv[t])
    small_ref[3:4, :] += col_sum(d_hn * scaled)
    small_ref[4:5, :] += col_sum(d_hn)
    d1 = d2[...] + ln_back(d_hn, scaled, inv, row(vecs, 3))
    g = (0.5 * d1).astype(BF)
    small_ref[2:3, :] += col_sum(g.astype(F32))
    scaled, inv = ln_stats(x_ref[...].astype(F32))
    hn = (scaled * row(vecs, 0) + row(vecs, 1)).astype(BF)
    d_hn = jnp.zeros((rows, width), F32)
    for t in range(2):
        c = slice(t * half, (t + 1) * half)
        a, slope = swish_parts(z_ref[:, c].astype(F32))
        go[t] += tn(g, a.astype(BF))
        dz = (nn(g, w_out[t]) * slope).astype(BF)
        bias = col_sum(dz.astype(F32))
        small_ref[R_B1 + 2 * t : R_B1 + 2 * t + 1, :] += bias[:, :width]
        small_ref[R_B1 + 2 * t + 1 : R_B1 + 2 * t + 2, :] += bias[:, width:]
        gi[t] += tn(hn, dz)
        d_hn = d_hn + nt(dz, w_in[t])
    small_ref[0:1, :] += col_sum(d_hn * scaled)
    small_ref[1:2, :] += col_sum(d_hn)
    d0_ref[...] = (d1 + ln_back(d_hn, scaled, inv, row(vecs, 0))).astype(BF)

    @pl.when(i == pl.num_programs(0) - 1)
    def _():
        gq_ref[...] = gq[...].astype(BF)
        gp_ref[...] = gp[...].astype(BF)
        gi_ref[...] = gi[...].astype(BF)
        go_ref[...] = go[...].astype(BF)


def last_call(dq, dk, dv, first, x, d2, z, table, dpos, asums, g, vecs):
    tokens, width = first.shape
    steps = tokens // TB
    small = (R_ALL, width)
    names = ("qkv", "f1i", "f1o", "pos")
    places = table.shape[0] // steps
    return pl.pallas_call(
        last_kernel,
        grid=(steps,),
        in_specs=[tall(TB, width)] * 6
        + [tall(TB, 4 * width), tall(places, width)]
        + [pl.BlockSpec((dpos.shape[0], places, width), lambda i: (0, i, 0)), whole(asums.shape)]
        + [seg_spec(name, width) for name in names[:3]]
        + [whole(vecs.shape)],
        out_specs=[tall(TB, width), whole(small)]
        + [once(grad_shape(name, width).shape) for name in names],
        scratch_shapes=[acc(name, width) for name in names],
        out_shape=[
            jax.ShapeDtypeStruct((tokens, width), BF),
            jax.ShapeDtypeStruct(small, F32),
        ]
        + [grad_shape(name, width) for name in names],
        compiler_params=dense_params(),
        name="qkv_ffn1_backward",
    )(dq, dk, dv, first, x, d2, z, table, dpos, asums, g, g, g, vecs)


def gather_plain(big, kinds, names_a, names_b, small_ins, both, n_dp):
    def pack(names):
        return jnp.concatenate(
            [big[n].T if kinds[n][0] == "flip" else big[n] for n in names], axis=1
        )

    def every(item):
        g = lax.all_gather(item, both, axis=0, tiled=True)
        g = g.reshape(n_dp, 2, item.shape[0], -1).transpose(1, 0, 2, 3)
        return g.reshape(2, n_dp * item.shape[0], -1)

    small = jnp.concatenate([item.reshape(-1) for item in small_ins])
    smalls = lax.all_gather(small, both, axis=0, tiled=False).reshape(n_dp, 2, -1).astype(F32)
    off = 0
    pieces = []
    for item in small_ins:
        pieces.append(smalls[:, :, off : off + item.size].reshape((n_dp, 2) + item.shape))
        off += item.size
    width = small_ins[4].shape[1] * n_dp * 2
    vecs = jnp.concatenate(
        [
            pieces[4].transpose(2, 0, 1, 3).reshape(-1, width),
            pieces[1].transpose(2, 1, 3, 0, 4).reshape(-1, width),
            pieces[2].transpose(2, 1, 3, 0, 4).reshape(-1, width),
            pieces[0].transpose(1, 2, 0, 3).reshape(-1, width),
            pieces[3].transpose(1, 2, 0, 3).reshape(-1, width),
            jnp.zeros((1, width), F32),
        ],
        axis=0,
    )
    return every(pack(names_a)), every(pack(names_b)), vecs


def scatter_plain(grads, kinds, names, small_g, small_ins, both, n_dp):
    vec_g = (
        small_g[R_B1:R_B2].reshape(1, -1), small_g[R_ATT:R_CV], small_g[R_CV:R_B1],
        small_g[R_B2 : R_B2 + 4].reshape(1, -1),
    )

    def small_of(item, like):
        item = item.reshape(item.shape[0], 2, like.shape[-2], n_dp, like.shape[-1])
        return item.transpose(1, 3, 0, 2, 4).reshape(2, n_dp, -1)

    cols = small_ins[4].shape[1]
    norm_g = small_g[:R_ATT].reshape(-1, n_dp, 2, cols).transpose(2, 1, 0, 3).reshape(2, n_dp, -1)
    packed = jnp.concatenate(
        [small_of(item, like) for item, like in zip(vec_g, small_ins)] + [norm_g], axis=2
    )
    packed = packed.swapaxes(0, 1).reshape(n_dp * 2, -1)
    own_small = lax.psum_scatter(packed, both, scatter_dimension=0, tiled=True).reshape(-1)
    wide = jnp.concatenate([grads[name] for name in names], axis=2)
    rows = wide.shape[1] // n_dp
    wide = wide.reshape(2, n_dp, rows, -1).swapaxes(0, 1).reshape(n_dp * 2 * rows, -1)
    own = lax.psum_scatter(wide, both, scatter_dimension=0, tiled=True).astype(F32)
    outs, at = {}, 0
    for name in names:
        w = grads[name].shape[2]
        item = own[:, at : at + w]
        outs[name] = item.T if kinds[name][0] == "flip" else item
        at += w
    small_outs, at = [], 0
    for item in small_ins:
        small_outs.append(own_small[at : at + item.size].reshape(item.shape))
        at += item.size
    return outs, small_outs


def local(
    frames,
    lengths,
    ffn1_in,
    ffn1_out,
    ffn1_bias,
    qkv_weight,
    pos_weight,
    out_weight,
    attn_bias,
    conv_in,
    conv_out,
    conv_channel,
    ffn2_in,
    ffn2_out,
    ffn2_bias,
    norm_params,
    cotangent,
):
    micro, seqs, full, width = frames.shape
    both = ("dp", "tensor")
    n_dp = lax.axis_size("dp")
    rows = ffn1_in.shape[0]
    batch = micro * seqs
    tokens = batch * full
    small_ins = (ffn1_bias, attn_bias, conv_channel, ffn2_bias, norm_params)
    names_a, names_b = ("f1i", "f1o", "pos", "qkv"), ("f2i", "f2o", "ci", "out", "co")
    big = {
        "f1i": ffn1_in, "f1o": ffn1_out, "pos": pos_weight, "qkv": qkv_weight.reshape(rows, -1),
        "f2i": ffn2_in, "f2o": ffn2_out, "ci": conv_in.reshape(rows, -1), "out": out_weight,
        "co": conv_out,
    }
    kinds = {name: ("plain",) for name in big}
    kinds.update({name: ("flip",) for name in ("f1o", "f2o", "out", "co")})
    kinds.update({"qkv": ("parts", 3), "ci": ("parts", 2)})
    mine_mesh = own_mesh((n_dp, lax.axis_size("tensor"))) and rows % 16 == 0
    if mine_mesh:
        packed_a, packed_b, slab, table = prep_call(
            [big[name] for name in names_a + names_b],
            [
                ffn1_bias, attn_bias.swapaxes(0, 1).reshape(-1, attn_bias.shape[2]),
                conv_channel.swapaxes(0, 1).reshape(-1, conv_channel.shape[2]), ffn2_bias,
                norm_params,
            ],
            full, width,
        )
        g_a, vecs = gather_call(packed_a, slab, width, 1)
        g_a = g_a.reshape(2, width, -1)
    else:
        table = table_call(full, width)
        packed_b = None
        g_a, g_b, vecs = gather_plain(big, kinds, names_a, names_b, small_ins, both, n_dp)

    def reduce_sum(item, cid):
        if mine_mesh:
            return sum_all(item, cid)
        return lax.psum(item, both)

    mine = lax.axis_index("tensor")
    lens = lax.dynamic_slice_in_dim(lengths, mine * seqs, seqs, 1).reshape(-1)
    x = frames.reshape(tokens, width)
    cot = cotangent.reshape(tokens, width)

    def utt(item):
        return item.reshape(batch, full, -1)

    def flat(item):
        return item.reshape(tokens, -1)

    first, z1, q_u, q_v, keys, values, pos = ffn1_call(x, table, g_a, vecs)
    heads = (lens, utt(q_u), utt(q_v), utt(keys), utt(values), pos)
    if mine_mesh:
        mixed, lse, g_b = attn_fwd_call(*heads, packed_b, 2)
        g_b = g_b.reshape(2, width, -1)
    else:
        mixed, lse = attn_fwd_call(*heads)
    second, halves, conv, stats = conv1_call(lens, flat(mixed), first, g_b, vecs)
    stats = reduce_sum(stats, 3)
    grads = {}
    result, d3, d_yhat, sums, small_m, grads["f2i"], grads["f2o"], grads["co"] = middle_call(
        lens, second, conv, cot, stats, g_b, vecs
    )
    sums = reduce_sum(sums, 4)
    d2, d_mixed, small_c, grads["ci"], grads["out"] = conv2_call(
        lens, d_yhat, conv, d3, halves, second, flat(mixed), stats, sums, g_b, vecs
    )
    outs = {}
    if mine_mesh:
        dq, dk, dv, dpos, asums, *early = attn_bwd_call(
            *heads, mixed, lse, utt(d_mixed), [grads[name] for name in names_b],
            [kinds[name] for name in names_b], 5,
        )
        outs.update(zip(names_b, early))
    else:
        dq, dk, dv, dpos, asums = attn_bwd_call(*heads, mixed, lse, utt(d_mixed))
    d0, small_l, grads["qkv"], grads["f1i"], grads["f1o"], grads["pos"] = last_call(
        flat(dq), flat(dk), flat(dv), first, x, d2, z1, table, dpos, asums, g_a, vecs
    )
    if mine_mesh:
        late = scatter_call(
            [grads[name] for name in names_a], [kinds[name] for name in names_a],
            (small_m, small_c, small_l), small_ins, 6,
        )
        outs.update(zip(names_a, late))
        small_outs = late[len(names_a) :]
    else:
        outs, small_outs = scatter_plain(
            grads, kinds, names_a + names_b, small_m + small_c + small_l, small_ins, both, n_dp
        )
    return (
        result.reshape(frames.shape),
        d0.reshape(frames.shape),
        outs["f1i"],
        outs["f1o"],
        small_outs[0],
        outs["qkv"].reshape(qkv_weight.shape),
        outs["pos"],
        outs["out"],
        small_outs[1],
        outs["ci"].reshape(conv_in.shape),
        outs["co"],
        small_outs[2],
        outs["f2i"],
        outs["f2o"],
        small_outs[3],
        small_outs[4],
    )


def solution(mesh):
    in_specs = (
        P(None, ("dp", "tensor"), None, None),
        P(None, "dp"),
        P("dp", "tensor"),
        P("tensor", "dp"),
        P("tensor", "dp"),
        P("dp", None, "tensor"),
        P("dp", "tensor"),
        P("tensor", "dp"),
        P(None, "tensor", "dp"),
        P("dp", None, "tensor"),
        P("tensor", "dp"),
        P(None, "tensor", "dp"),
        P("dp", "tensor"),
        P("tensor", "dp"),
        P("tensor", "dp"),
        P(None, ("dp", "tensor")),
        P(None, ("dp", "tensor"), None, None),
    )
    out_specs = (
        P(None, ("dp", "tensor"), None, None),
        P(None, ("dp", "tensor"), None, None),
        P("dp", "tensor"),
        P("tensor", "dp"),
        P("tensor", "dp"),
        P("dp", None, "tensor"),
        P("dp", "tensor"),
        P("tensor", "dp"),
        P(None, "tensor", "dp"),
        P("dp", None, "tensor"),
        P("tensor", "dp"),
        P(None, "tensor", "dp"),
        P("dp", "tensor"),
        P("tensor", "dp"),
        P("tensor", "dp"),
        P(None, ("dp", "tensor")),
    )
    return jax.shard_map(local, mesh=mesh, in_specs=in_specs, out_specs=out_specs, check_vma=False)
```

```python
import math

import jax
import jax.numpy as jnp
from jax import lax
from jax.experimental import pallas as pl
from jax.experimental.pallas import tpu as pltpu
from jax.sharding import PartitionSpec as P

DK = 64
norm_eps = 1e-05
mask_fill = -1000000000.0
BF = jnp.bfloat16
F32 = jnp.float32
BLK = 128


def nn(a, b):
    return lax.dot_general(a, b, (((1,), (0,)), ((), ())), preferred_element_type=F32)


def nt(a, b):
    return lax.dot_general(a, b, (((1,), (1,)), ((), ())), preferred_element_type=F32)


def tn(a, b):
    return lax.dot_general(a, b, (((0,), (0,)), ((), ())), preferred_element_type=F32)


def attn_fwd_kernel(len_ref, qu, qv, k, v, pos, o_ref, lse_ref, u=None, hook=None):
    count = len_ref[pl.program_id(0) if u is None else u]
    full = k.shape[1]
    lane = lax.broadcasted_iota(jnp.int32, (BLK, 2 * DK), 1)
    col = lax.broadcasted_iota(jnp.int32, (BLK, full), 1)
    keep = col < count
    zero = jnp.zeros((), BF)
    for blk in range(full // BLK):
        i0 = blk * BLK
        base = full - BLK - i0
        if hook is not None:
            hook(blk)
        outs, logs = [], []
        for h in range(2):
            mine = (lane < DK) if h == 0 else (lane >= DK)
            q_u = jnp.where(mine, qu[0, i0 : i0 + BLK, :], zero)
            q_v = jnp.where(mine, qv[0, i0 : i0 + BLK, :], zero)
            rel = nt(q_v, pos[base : base + full + BLK, :])
            rel = pltpu.roll(rel, full + 1, 1, stride=1, stride_axis=0)[:, :full]
            s = (nt(q_u, k[0]) + rel) * (1.0 / math.sqrt(DK))
            s = jnp.where(keep, s, mask_fill)
            top = jnp.max(s, axis=1, keepdims=True)
            e = jnp.exp(s - top)
            total = jnp.sum(e, axis=1, keepdims=True)
            outs.append(nn(e.astype(BF), v[0]) / total)
            logs.append(top + jnp.log(total))
        left = lane < DK
        o_ref[0, i0 : i0 + BLK, :] = jnp.where(left, outs[0], outs[1]).astype(BF)
        lse_ref[0, i0 : i0 + BLK, :] = jnp.where(left, logs[0], logs[1])


def attn_bwd_kernel(
    len_ref, qu, qv, k, v, pos, o, lse, do, dq_ref, dk_ref, dv_ref, dpos_ref, sum_ref, dkt, dvt, dpt,
    hook=None,
):
    count = len_ref[pl.program_id(0)]
    full = k.shape[1]
    scale = 1.0 / math.sqrt(DK)
    lane = lax.broadcasted_iota(jnp.int32, (BLK, 2 * DK), 1)
    left = lane < DK
    keep = lax.broadcasted_iota(jnp.int32, (BLK, full), 1) < count
    zero = jnp.zeros((), BF)
    flip = (lane + lax.broadcasted_iota(jnp.int32, (BLK, 2 * DK), 0) == BLK - 1).astype(F32).astype(BF)
    dkt[...] = jnp.zeros_like(dkt)
    dvt[...] = jnp.zeros_like(dvt)
    dpt[...] = jnp.zeros_like(dpt)
    sum_q = jnp.zeros((1, 2 * DK), F32)
    sum_u = jnp.zeros((1, 2 * DK), F32)
    sum_v = jnp.zeros((1, 2 * DK), F32)
    for blk in range(full // BLK):
        i0 = blk * BLK
        base = full - BLK - i0
        rows = slice(i0, i0 + BLK)
        win = slice(base, base + full + BLK)
        if hook is not None:
            hook(blk)
        qu_t = qu[0, rows, :].astype(F32).T.astype(BF)
        do_t = do[0, rows, :].astype(F32).T.astype(BF)
        qv_t = tn(qv[0, rows, :], flip).astype(BF)
        dot_o = do[0, rows, :].astype(F32) * o[0, rows, :].astype(F32)
        parts_u, parts_v = [], []
        for h in range(2):
            mine = left if h == 0 else lane >= DK
            hs = slice(h * DK, h * DK + DK)
            q_u = jnp.where(mine, qu[0, rows, :], zero)
            q_v = jnp.where(mine, qv[0, rows, :], zero)
            d_o = jnp.where(mine, do[0, rows, :], zero)
            rel = nt(q_v, pos[win, :])
            rel = pltpu.roll(rel, full + 1, 1, stride=1, stride_axis=0)[:, :full]
            s = (nt(q_u, k[0]) + rel) * scale - lse[0, rows, h * DK : h * DK + 1]
            p = jnp.where(keep, jnp.exp(jnp.minimum(s, 0.0)), 0.0)
            delta = jnp.sum(jnp.where(mine, dot_o, 0.0), axis=1, keepdims=True)
            ds = (p * (nt(d_o, v[0]) - delta)).astype(BF)
            dvt[hs, :] += nn(do_t[hs, :], p.astype(BF))
            dkt[hs, :] += nn(qu_t[hs, :], ds)
            parts_u.append(nn(ds, k[0]))
            wide = jnp.concatenate([nn(flip, ds), jnp.zeros((BLK, BLK), F32)], axis=1)
            wide = pltpu.roll(wide, 0, 1, stride=1, stride_axis=0).astype(BF)
            parts_v.append(nn(wide, pos[win, :]))
            dpt[hs, win] += nn(qv_t[hs, :], wide)
        d_u = jnp.where(left, parts_u[0], parts_u[1]) * scale
        d_v = jnp.where(left, parts_v[0], parts_v[1]) * scale
        high = d_v.astype(BF)
        low = (d_v - high.astype(F32)).astype(BF)
        d_q = (d_u + nn(flip, high) + nn(flip, low)).astype(BF)
        dq_ref[0, rows, :] = d_q
        sum_q += jnp.sum(d_q.astype(F32), axis=0, keepdims=True)
        sum_u += jnp.sum(d_u, axis=0, keepdims=True)
        sum_v += jnp.sum(d_v, axis=0, keepdims=True)
    dk_ref[0] = (dkt[...].T * scale).astype(BF)
    d_val = dvt[...].T.astype(BF)
    dv_ref[0] = d_val
    dpos_ref[0] = (dpt[...].T * scale).astype(BF)
    sum_ref[0, 0:1, :] = sum_q
    sum_ref[0, 1:2, :] = jnp.sum(d_val.astype(F32), axis=0, keepdims=True)
    sum_ref[0, 2:3, :] = sum_u
    sum_ref[0, 3:4, :] = sum_v
    sum_ref[0, 4:8, :] = jnp.zeros((4, 2 * DK), F32)


def attn_specs(rows, full, width):
    pairs = width // (2 * DK)
    main = pl.BlockSpec((1, full, 2 * DK), lambda u, p, n: (u, 0, p))
    pos = pl.BlockSpec((2 * full, 2 * DK), lambda u, p, n: (0, p))
    return (rows, pairs), main, pos


def attn_fwd_call(lens, qu, qv, k, v, pos):
    rows, full, width = qu.shape
    grid, main, pspec = attn_specs(rows, full, width)
    return pl.pallas_call(
        attn_fwd_kernel,
        grid_spec=pltpu.PrefetchScalarGridSpec(
            num_scalar_prefetch=1,
            grid=grid,
            in_specs=[main] * 4 + [pspec],
            out_specs=[main, main],
        ),
        out_shape=[
            jax.ShapeDtypeStruct((rows, full, width), BF),
            jax.ShapeDtypeStruct((rows, full, width), F32),
        ],
        compiler_params=dense_params(),
        name="attn_fwd",
    )(lens, qu, qv, k, v, pos)


def attn_bwd_call(lens, qu, qv, k, v, pos, o, lse, do, early=None, cid=None):
    rows, full, width = qu.shape
    grid, main, pspec = attn_specs(rows, full, width)
    args = [lens, qu, qv, k, v, pos, o, lse, do]
    in_specs = [main] * 4 + [pspec] + [main] * 3
    out_specs = [
        main,
        main,
        main,
        pl.BlockSpec((1, 2 * full, 2 * DK), lambda u, p, n: (u, 0, p)),
        pl.BlockSpec((1, 8, 2 * DK), lambda u, p, n: (u, 0, p)),
    ]
    scratch = [
        pltpu.VMEM((2 * DK, full), F32),
        pltpu.VMEM((2 * DK, full), F32),
        pltpu.VMEM((2 * DK, 2 * full), F32),
    ]
    out_shape = [jax.ShapeDtypeStruct((rows, full, width), BF)] * 3 + [
        jax.ShapeDtypeStruct((rows, 2 * full, width), BF),
        jax.ShapeDtypeStruct((rows, 8, width), F32),
    ]
    body, params = attn_bwd_kernel, dense_params()
    if early is not None:
        items = [split_owners(item) for item in early]
        pieces = pieces_of([item.shape[-1] for item in items])
        owned = items[0].shape[-2]
        n_in, n_out, m = len(args) - 1, len(out_shape), len(items)
        args += items
        in_specs += [ANY] * m
        out_specs.append(pl.BlockSpec((owned, C_B), lambda u, p, n: (0, 0)))
        out_shape.append(jax.ShapeDtypeStruct((owned, C_B), F32))
        scratch += scatter_scratch(pieces, owned)
        params = comm_params(cid)

        def body(*refs):
            at = pl.program_id(0) * grid[1] + pl.program_id(1)
            last = grid[0] * grid[1] - 1
            ins, rest = refs[: 1 + n_in], refs[1 + n_in :]
            g_refs, rest = rest[:m], rest[m:]
            mains, o_ref, own, sems = rest[:n_out], rest[n_out], rest[n_out + 1 : n_out + 4], rest[n_out + 4 :]
            start, advance, finish, rounds = scatter_steps(pieces, g_refs, o_ref, sems, 2)

            def begin():
                greet(link_peers(*place()))
                for p in range(len(pieces)):
                    start(p)

            steps = [begin] + [lambda q=q: advance(q) for q in range(rounds)]
            attn_bwd_kernel(*ins, *mains, *own, hook=hooks_of(steps, at, last, full // BLK))

            @pl.when(at == last)
            def _():
                finish()

    return pl.pallas_call(
        body,
        grid_spec=pltpu.PrefetchScalarGridSpec(
            num_scalar_prefetch=1,
            grid=grid,
            in_specs=in_specs,
            out_specs=out_specs,
            scratch_shapes=scratch,
        ),
        out_shape=out_shape,
        compiler_params=params,
        name="attn_bwd",
    )(*args)


def hooks_of(steps, at, last, spots):
    def hook(blk):
        for i, step in enumerate(steps):
            where, spot = divmod(i * (last + 1) * spots // len(steps), spots)
            if spot == blk:

                @pl.when(at == where)
                def _(step=step):
                    step()

    return hook


MESH = pl.DeviceIdType.MESH
NZ, NY, NX = 4, 2, 2
ANY = pl.BlockSpec(memory_space=pl.ANY)
VM = pl.BlockSpec(memory_space=pltpu.VMEM)


def own_mesh(sizes):
    return sizes == (NZ * NY * NX, 2)


def place():
    dp = lax.axis_index("dp")
    return dp // (NY * NX), dp // NX % NY, dp % NX, lax.axis_index("tensor")


def dev(z, y, x, t):
    return (z * (NY * NX) + y * NX + x, t)


def greet(peers):
    barrier = pltpu.get_barrier_semaphore()
    for peer in peers:
        pl.semaphore_signal(barrier, inc=1, device_id=peer, device_id_type=MESH)
    pl.semaphore_wait(barrier, len(peers))


def rcopy(src, dst, send, recv, peer):
    return pltpu.make_async_remote_copy(
        src_ref=src, dst_ref=dst, send_sem=send, recv_sem=recv, device_id=peer, device_id_type=MESH
    )


def link_peers(z, y, x, t):
    peers = [dev(lax.rem(z + d, NZ), y, x, t) for d in range(1, NZ)]
    return peers + [dev(z, 1 - y, x, t), dev(z, y, 1 - x, t), dev(z, y, x, 1 - t)]


def sum_kernel(x_ref, o_ref, mid, b1, b2, s1, r1, s2, r2):
    z, y, x, t = place()
    spot = (y * NX + x) * 2 + t
    zs = [dev(lax.rem(z + d, NZ), y, x, t) for d in range(1, NZ)]
    flat = [lax.rem(spot + d, 8) for d in range(1, 8)]
    plane = [dev(z, p // 4, p // 2 % 2, p % 2) for p in flat]
    greet(zs + plane)
    first = [rcopy(x_ref, b1.at[i], s1.at[i], r1.at[i], peer) for i, peer in enumerate(zs)]
    for copy in first:
        copy.start()
    for copy in first:
        copy.wait_recv()
    mid[...] = (x_ref[...] + b1[0]) + (b1[1] + b1[2])
    second = [rcopy(mid, b2.at[i], s2.at[i], r2.at[i], peer) for i, peer in enumerate(plane)]
    for copy in second:
        copy.start()
    for copy in second:
        copy.wait_recv()
    total = mid[...]
    for i in range(7):
        total = total + b2[i]
    o_ref[...] = total
    for copy in first + second:
        copy.wait_send()


def sum_all(item, cid):
    return pl.pallas_call(
        sum_kernel,
        out_shape=jax.ShapeDtypeStruct(item.shape, F32),
        in_specs=[VM],
        out_specs=VM,
        scratch_shapes=[
            pltpu.VMEM(item.shape, F32),
            pltpu.VMEM((3,) + item.shape, F32),
            pltpu.VMEM((7,) + item.shape, F32),
            pltpu.SemaphoreType.DMA((3,)),
            pltpu.SemaphoreType.DMA((3,)),
            pltpu.SemaphoreType.DMA((7,)),
            pltpu.SemaphoreType.DMA((7,)),
        ],
        compiler_params=pltpu.CompilerParams(collective_id=cid, has_side_effects=True),
        name="sum_all",
    )(item)


def comm_params(cid):
    return pltpu.CompilerParams(
        collective_id=cid, has_side_effects=True, vmem_limit_bytes=60 * 1024 * 1024
    )


def gathered_shape(packed):
    return jax.ShapeDtypeStruct((2, NZ, NY, NX) + packed.shape, packed.dtype)


def gather_scratch(n):
    dma = pltpu.SemaphoreType.DMA
    return [dma((n, NZ - 1)), dma((n, NZ - 1))] + [dma((n,))] * 6 + [dma((2,))]


LEAD = 2


def gather_events(pieces, xs, gs, sems):
    zs, zr, as_, ar, bs, br, cs, cr, own_sem = sems
    z, y, x, t = place()
    along_x, along_y = dev(z, y, 1 - x, t), dev(z, 1 - y, x, t)
    zc, ac, bc, cc = [], [], [], []
    for p, (i, start, w) in enumerate(pieces):
        c = pl.ds(start, w)
        g = gs[i]
        zc.append(
            [
                rcopy(
                    xs[i].at[:, c],
                    g.at[t, z, y, x, :, c],
                    zs.at[p, d - 1],
                    zr.at[p, d - 1],
                    dev(lax.rem(z + d, NZ), y, x, t),
                )
                for d in range(1, NZ)
            ]
        )
        line = g.at[t, :, y, x, :, c]
        ac.append(rcopy(line, line, as_.at[p], ar.at[p], along_x if p % 2 == 0 else along_y))
        half = g.at[t, :, y, :, :, c] if p % 2 == 0 else g.at[t, :, :, x, :, c]
        bc.append(rcopy(half, half, bs.at[p], br.at[p], along_y if p % 2 == 0 else along_x))
        full = g.at[t, :, :, :, :, c]
        cc.append(rcopy(full, full, cs.at[p], cr.at[p], dev(z, y, x, 1 - t)))

    def begin():
        own = [
            pltpu.make_async_copy(item, g.at[t, z, y, x], own_sem.at[i])
            for i, (item, g) in enumerate(zip(xs, gs))
        ]
        for copy in own:
            copy.start()
        for copies in zc[: 2 * LEAD]:
            for copy in copies:
                copy.start()
        for copy in own:
            copy.wait()

    def event(kind, q):
        for p in (2 * q, 2 * q + 1):
            if kind == "z":
                for copy in zc[p]:
                    copy.wait_recv()
                ac[p].start()
                for copy in zc[p + 2 * LEAD] if p + 2 * LEAD < len(pieces) else []:
                    copy.start()
            elif kind == "a":
                ac[p].wait_recv()
                bc[p].start()
            elif kind == "b":
                bc[p].wait_recv()
                cc[p].start()
            else:
                cc[p].wait_recv()

    def finish():
        for copy in sum(zc, []) + ac + bc + cc:
            copy.wait_send()

    return begin, event, finish


def gather_order(pieces):
    unit = [0.42 * (pieces[2 * q][2] + pieces[2 * q + 1][2]) / 512 for q in range(len(pieces) // 2)]
    order, at = [], 3.0
    waiting = []
    for q, step in enumerate(unit):
        at += 8 * step
        waiting.append((at + 2.5, q, "z"))
    free = 0.0
    while waiting:
        waiting.sort()
        now, q, kind = waiting.pop(0)
        order.append((now, kind, q))
        if kind in "za":
            free = max(free, now) + (4 if kind == "z" else 8) * unit[q]
            waiting.append((free + 2.5, q, "a" if kind == "z" else "b"))
        elif kind == "b":
            waiting.append((now + 1.8, q, "c"))
    return order


def small_steps(s_ref, v_ref, mid, b1, b2, s1, r1, s2, r2):
    z, y, x, t = place()
    spot = (y * NX + x) * 2 + t
    zs = [dev(lax.rem(z + d, NZ), y, x, t) for d in range(1, NZ)]
    flat = [lax.rem(spot + d, 8) for d in range(1, 8)]
    plane = [dev(z, p // 4, p // 2 % 2, p % 2) for p in flat]
    first = [rcopy(s_ref, b1.at[i], s1.at[i], r1.at[i], peer) for i, peer in enumerate(zs)]
    second = [rcopy(mid, b2.at[i], s2.at[i], r2.at[i], peer) for i, peer in enumerate(plane)]

    def begin():
        for copy in first:
            copy.start()

    def spread():
        for copy in first:
            copy.wait_recv()
        mid[...] = (s_ref[...] + b1[0]) + (b1[1] + b1[2])
        for copy in second:
            copy.start()

    def finish():
        for copy in second:
            copy.wait_recv()
        same, other = mid[...].astype(F32), b2[0].astype(F32)
        for i in range(1, 7):
            if i % 2 == 1:
                same = same + b2[i].astype(F32)
            else:
                other = other + b2[i].astype(F32)
        low = jnp.where(t == 0, same, other)
        high = jnp.where(t == 0, other, same)
        v_ref[...] = jnp.zeros_like(v_ref)
        for q in range(4):
            r = S_NORM + 14 * q
            v_ref[0:14, 128 * q : 128 * q + 128] = low[r : r + 14] + high[r : r + 14]
        for i, part in enumerate((low, high)):
            for q in range(2):
                c = slice((2 * i + q) * 128, (2 * i + q) * 128 + 128)
                v_ref[R_ATT:R_CV, c] = part[S_ATT + 4 * q : S_ATT + 4 * q + 4]
                v_ref[R_CV:R_B1, c] = part[S_CV + 13 * q : S_CV + 13 * q + 13]
            for q in range(8):
                r, c = 2 * i + q // 4, slice(q % 4 * 128, q % 4 * 128 + 128)
                v_ref[R_B1 + r : R_B1 + r + 1, c] = part[S_B1 + q : S_B1 + q + 1]
                v_ref[R_B2 + r : R_B2 + r + 1, c] = part[S_B2 + q : S_B2 + q + 1]
        for copy in first + second:
            copy.wait_send()

    return plane, begin, spread, finish


S_B1, S_ATT, S_CV, S_B2, S_NORM, S_ALL = 0, 8, 16, 42, 50, 112


def lanes_of(n, offset):
    at = lax.broadcasted_iota(jnp.int32, (n, 128), 0) + offset
    return (lax.broadcasted_iota(jnp.int32, (n, 128), 1) == at).astype(F32)


def prep_kernel(
    f1i, f1o, pos, qkv, f2i, f2o, ci, out, co, b1, att, cv, b2, norm,
    pa_ref, pb_ref, slab_ref, table_ref, slab,
):
    def put(ref, name, value, shift=0):
        start = SEG[name][0] + shift
        ref[:, start : start + value.shape[1]] = value

    for ref, name, item in (
        (pa_ref, "f1i", f1i), (pa_ref, "f1o", f1o), (pa_ref, "pos", pos), (pb_ref, "f2i", f2i),
        (pb_ref, "f2o", f2o), (pb_ref, "out", out), (pb_ref, "co", co),
    ):
        put(ref, name, item[...])
    for k in range(3):
        put(pa_ref, "qkv", qkv[k], k * qkv.shape[2])
    for k in range(2):
        put(pb_ref, "ci", ci[:, k, :], k * ci.shape[2])
    z, y, x, t = place()
    dp = z * (NY * NX) + y * NX + x
    sel = lanes_of(8, dp * 8).astype(BF)
    slab[...] = jnp.zeros_like(slab)
    slab[S_B1 : S_B1 + 8] = nn(b1[...], sel)
    for q in range(2):
        slab[S_ATT + 4 * q : S_ATT + 4 * q + 4] = nn(att[:, q, :], sel)
        slab[S_CV + 13 * q : S_CV + 13 * q + 13] = tn(cv[q], sel)
    slab[S_B2 : S_B2 + 8] = nn(b2[...], sel)
    at = dp * 2 + t
    here = nn(norm[...], lanes_of(16, lax.rem(at, 8) * 16).astype(BF))
    for q in range(4):
        slab[S_NORM + 14 * q : S_NORM + 14 * q + 14] = here * (at // 8 == q).astype(F32)
    slab_ref[...] = slab[...].astype(BF)
    fill_table(table_ref)


def prep_call(items, smalls, full, width):
    rows = items[0].shape[0]
    return pl.pallas_call(
        prep_kernel,
        in_specs=[VM] * 14,
        out_specs=[VM] * 4,
        out_shape=[
            jax.ShapeDtypeStruct((rows, C_A), BF),
            jax.ShapeDtypeStruct((rows, C_B), BF),
            jax.ShapeDtypeStruct((S_ALL, 128), BF),
            jax.ShapeDtypeStruct((2 * full, width), BF),
        ],
        scratch_shapes=[pltpu.VMEM((S_ALL, 128), F32)],
        name="prepare",
    )(*items, *smalls)


def split_owners(item):
    return item.reshape(2, NZ, NY, NX, item.shape[1] // (NZ * NY * NX), item.shape[2])


def pieces_of(widths, step=256):
    pieces, at = [], 0
    for i, w in enumerate(widths):
        pieces += [(i, k, min(step, w), at + k) for k in range(0, w, step)]
        at += w
    return pieces


def scatter_scratch(pieces, rows):
    n = len(pieces)
    total = sum(piece[2] for piece in pieces)
    dma = pltpu.SemaphoreType.DMA
    shape = (rows, total)
    return [
        pltpu.VMEM((NZ, NY, NX) + shape, BF),
        pltpu.VMEM((NZ, NY, NX) + shape, BF),
        pltpu.VMEM((NZ, 2) + shape, BF),
        pltpu.VMEM((NZ,) + shape, BF),
        pltpu.VMEM((NZ - 1,) + shape, BF),
    ] + [dma((n,))] * 7 + [dma((n, NZ - 1))] * 2


def scatter_steps(pieces, g_refs, o_ref, scratch, lag):
    own, rc, ra, rb, rz, lsem, cs, cr, as_, ar, bs, br, zs, zr = scratch
    z, y, x, t = place()
    along_x, along_y = dev(z, y, 1 - x, t), dev(z, 1 - y, x, t)
    mate = dev(z, y, x, 1 - t)
    count = len(pieces)
    bufs, lc, cc, ac, bc, zc = [], [], [], [], [], []
    for p, (i, start, w, at) in enumerate(pieces):
        c = pl.ds(at, w)
        g = pl.ds(start, w)
        b = dict(
            own=own.at[:, :, :, :, c], rc=rc.at[:, :, :, :, c], ra=ra.at[:, :, :, c],
            rb=rb.at[:, :, c], rz=rz.at[:, :, c],
        )
        bufs.append(b)
        even = p % 2 == 0
        lc.append(
            pltpu.make_async_copy(g_refs[i].at[t, :, :, :, :, g], b["own"], lsem.at[p])
        )
        cc.append(rcopy(g_refs[i].at[1 - t, :, :, :, :, g], b["rc"], cs.at[p], cr.at[p], mate))
        away = b["own"].at[:, 1 - y] if even else b["own"].at[:, :, 1 - x]
        ac.append(rcopy(away, b["ra"], as_.at[p], ar.at[p], along_y if even else along_x))
        line = b["own"].at[:, y, 1 - x] if even else b["own"].at[:, 1 - y, x]
        bc.append(rcopy(line, b["rb"], bs.at[p], br.at[p], along_x if even else along_y))
        zc.append([])
        for d in range(1, NZ):
            far = lax.rem(z + d, NZ)
            zc[p].append(
                rcopy(
                    b["own"].at[far, y, x], b["rz"].at[d - 1], zs.at[p, d - 1], zr.at[p, d - 1],
                    dev(far, y, x, t),
                )
            )

    def start(p):
        lc[p].start()
        cc[p].start()

    def advance(q):
        if q < count:
            lc[q].wait()
            cc[q].wait_recv()
            b = bufs[q]
            for i in range(NZ):
                b["own"][i] = b["own"][i] + b["rc"][i]
            ac[q].start()
        p = q - lag
        if 0 <= p < count:
            ac[p].wait_recv()
            b = bufs[p]
            for i in range(NZ):
                if p % 2 == 0:
                    b["own"][i, y] = b["own"][i, y] + b["ra"][i]
                else:
                    b["own"][i, :, x] = b["own"][i, :, x] + b["ra"][i]
            bc[p].start()
        p = q - 2 * lag
        if 0 <= p < count:
            bc[p].wait_recv()
            b = bufs[p]
            for i in range(NZ):
                b["own"][i, y, x] = b["own"][i, y, x] + b["rb"][i]
            for copy in zc[p]:
                copy.start()
        p = q - 3 * lag
        if 0 <= p < count:
            for copy in zc[p]:
                copy.wait_recv()
            b = bufs[p]
            total = b["own"][z, y, x].astype(F32)
            for d in range(NZ - 1):
                total = total + b["rz"][d].astype(F32)
            o_ref[:, pieces[p][3] : pieces[p][3] + pieces[p][2]] = total

    def finish():
        for copy in cc + ac + bc + sum(zc, []):
            copy.wait_send()

    return start, advance, finish, count + 3 * lag


def small_sum_steps(parts, ext, scratch):
    acc_s, bc_, bz, bp, bm, sc, rc, sz, rz, sp, rp, sm, rm = scratch
    z, y, x, t = place()
    dp = z * (NY * NX) + y * NX + x
    half = acc_s.shape[0] // 2
    mine = pl.ds(pl.multiple_of(t * half, 8), half)
    mate = dev(z, y, x, 1 - t)
    spot = y * NX + x
    zp = [dev(lax.rem(z + d, NZ), y, x, t) for d in range(1, NZ)]
    flat = [lax.rem(spot + d, 4) for d in range(1, 4)]
    pp = [dev(z, p // 2, p % 2, t) for p in flat]
    one = rcopy(acc_s, bc_, sc, rc, mate)
    two = [rcopy(acc_s.at[mine], bz.at[i], sz.at[i], rz.at[i], peer) for i, peer in enumerate(zp)]
    three = [rcopy(bz.at[3], bp.at[i], sp.at[i], rp.at[i], peer) for i, peer in enumerate(pp)]
    four = rcopy(bp.at[3], bm, sm, rm, mate)

    def a():
        acc_s[...] = jnp.zeros_like(acc_s)
        total = parts[0][...]
        for part in parts[1:]:
            total = total + part[...]
        acc_s[0:R_ALL] = total
        one.start()

    def b():
        one.wait()
        acc_s[...] = acc_s[...] + bc_[...]
        for copy in two:
            copy.start()

    def c():
        for copy in two:
            copy.wait()
        bz[3] = (acc_s[mine] + bz[0]) + (bz[1] + bz[2])
        for copy in three:
            copy.start()

    def d():
        for copy in three:
            copy.wait()
        bp[3] = (bz[3] + bp[0]) + (bp[1] + bp[2])
        four.start()
        ext[mine] = bp[3]

    def e():
        four.wait()
        ext[pl.ds(pl.multiple_of((1 - t) * half, 8), half)] = bm[...]

    return pp, [a, b, c, d, e]


def small_sum_scratch(width):
    dma = pltpu.SemaphoreType.DMA
    return [
        pltpu.VMEM((R_SUM, width), F32), pltpu.VMEM((R_SUM, width), F32),
        pltpu.VMEM((4, R_SUM // 2, width), F32), pltpu.VMEM((4, R_SUM // 2, width), F32),
        pltpu.VMEM((R_SUM // 2, width), F32), dma, dma, dma((3,)), dma((3,)), dma((3,)), dma((3,)), dma, dma,
    ]


def finish_kernel(
    oa, ob, ext, f1i, f1o, b1, qkv, pos, out, att, ci, co, cv, f2i, f2o, b2, norm
):
    def take(ref, name):
        start, w = SEG[name]
        return ref[:, start : start + w]

    f1i[...] = take(oa, "f1i")
    f1o[...] = take(oa, "f1o")
    pos[...] = take(oa, "pos")
    f2i[...] = take(ob, "f2i")
    f2o[...] = take(ob, "f2o")
    out[...] = take(ob, "out")
    co[...] = take(ob, "co")
    for ref, src, name in ((qkv, oa, "qkv"), (ci, ob, "ci")):
        start, w = SEG[name]
        n = 3 if name == "qkv" else 2
        for k in range(n):
            part = src[:, start + k * w // n : start + (k + 1) * w // n]
            if name == "qkv":
                ref[k] = part
            else:
                ref[:, k, :] = part
    z, y, x, t = place()
    dp = z * (NY * NX) + y * NX + x
    sel = lanes_of(8, dp * 8)

    def own(v, pick):
        return lax.dot_general(
            v, pick, (((1,), (1,)), ((), ())), precision=lax.Precision.HIGHEST,
            preferred_element_type=F32,
        )

    for q in range(2):
        c = pl.ds(pl.multiple_of((2 * t + q) * 128, 128), 128)
        att[:, q, :] = own(ext[R_ATT:R_CV, c], sel)
        cv[q] = own(sel, ext[R_CV:R_B1, c])
    for o, at in ((b1, R_B1), (b2, R_B2)):
        for q in range(8):
            r, c = at + q // 4, slice(q % 4 * 128, q % 4 * 128 + 128)
            line = jnp.where(t == 0, ext[r : r + 1, c], ext[r + 2 : r + 3, c])
            o[q : q + 1, :] = own(line, sel)
    at = dp * 2 + t
    lane = pl.ds(pl.multiple_of(at // 8 * 128, 128), 128)
    norm[...] = own(ext[0:14, lane], lanes_of(16, lax.rem(at, 8) * 16))


def finish_call(oa, ob, ext, rows):
    shapes = [
        (rows, 1024), (rows, 1024), (8, 8), (3, rows, 256), (rows, 256), (rows, 256), (4, 2, 8),
        (rows, 2, 256), (rows, 256), (2, 8, 13), (rows, 1024), (rows, 1024), (8, 8), (14, 16),
    ]
    f1i, f1o, b1, qkv, pos, out, att, ci, co, cv, f2i, f2o, b2, norm = pl.pallas_call(
        finish_kernel,
        in_specs=[VM] * 3,
        out_specs=[VM] * 14,
        out_shape=[jax.ShapeDtypeStruct(shape, F32) for shape in shapes],
        name="own_gradients",
    )(oa, ob, ext)
    return (
        f1i, f1o.T, b1, qkv.transpose(1, 0, 2), pos, out.T, att, ci, co.T, cv.transpose(2, 0, 1),
        f2i, f2o.T, b2, norm,
    )

SEG = {
    "f1i": (0, 1024), "f1o": (1024, 1024), "pos": (2048, 256), "qkv": (2304, 768),
    "f2i": (0, 1024), "f2o": (1024, 1024), "ci": (2048, 512), "out": (2560, 256),
    "co": (2816, 256),
}
C_A, C_B = 3072, 3072
R_ATT, R_CV, R_B1, R_B2, R_ALL, R_SUM = 14, 18, 31, 35, 40, 48
TB = 256
HC = 256


def seg_spec(name, depth):
    start, width = SEG[name]
    return pl.BlockSpec(
        (2, depth, width), lambda i, *_: (0, 0, start // width), pipeline_mode=pl.Buffered(1)
    )


def whole(shape):
    zeros = (0,) * len(shape)
    return pl.BlockSpec(shape, lambda i, *_: zeros)


def tall(rows, width):
    return pl.BlockSpec((rows, width), lambda i, *_: (i, 0))


def sig(v):
    return 0.5 * jnp.tanh(0.5 * v) + 0.5


def row(ref, i):
    return ref[i : i + 1, :]


def col_sum(v):
    return jnp.sum(v, axis=0, keepdims=True)


def ln_stats(v):
    centered = v - jnp.mean(v, axis=1, keepdims=True)
    inv = lax.rsqrt(jnp.mean(centered * centered, axis=1, keepdims=True) + norm_eps)
    return centered * inv, inv


def ln_back(up, scaled, inv, gain):
    g = up * gain
    return inv * (
        g
        - jnp.mean(g, axis=1, keepdims=True)
        - scaled * jnp.mean(g * scaled, axis=1, keepdims=True)
    )


def bias_half(vecs, at, t):
    return jnp.concatenate([row(vecs, at + 2 * t), row(vecs, at + 2 * t + 1)], axis=1)


def row_mask(start, rows, count):
    at = start + lax.broadcasted_iota(jnp.int32, (rows, 1), 0)
    return (at < count).astype(F32)


def ffn1_kernel(
    x_ref, table, w_in, w_out, w_qkv, w_pos, vecs,
    first_ref, z_ref, qu_ref, qv_ref, k_ref, v_ref, pos_ref,
):
    x = x_ref[...].astype(F32)
    scaled, _ = ln_stats(x)
    hn = (scaled * row(vecs, 0) + row(vecs, 1)).astype(BF)
    half = w_in.shape[2]
    y = row(vecs, 2)
    for t in range(2):
        z = nn(hn, w_in[t]) + bias_half(vecs, R_B1, t)
        for j in range(half // HC):
            z_ref[:, (2 * j + t) * HC : (2 * j + t + 1) * HC] = z[:, j * HC : (j + 1) * HC].astype(BF)
        y = y + nt((z * sig(z)).astype(BF), w_out[t])
    first = x + 0.5 * y
    first_ref[...] = first
    scaled, _ = ln_stats(first)
    hn = (scaled * row(vecs, 3) + row(vecs, 4)).astype(BF)
    part = w_qkv.shape[2] // 3
    for t in range(2):
        c = slice(t * part, (t + 1) * part)
        proj = nn(hn, w_qkv[t])
        q = proj[:, :part] + vecs[R_ATT : R_ATT + 1, c]
        qu_ref[:, c] = (q + vecs[R_ATT + 2 : R_ATT + 3, c]).astype(BF)
        qv_ref[:, c] = (q + vecs[R_ATT + 3 : R_ATT + 4, c]).astype(BF)
        k_ref[:, c] = proj[:, part : 2 * part].astype(BF)
        v_ref[:, c] = (proj[:, 2 * part :] + vecs[R_ATT + 1 : R_ATT + 2, c]).astype(BF)
        pos_ref[:, c] = nn(table[...], w_pos[t]).astype(BF)


def dense_params(mib=60):
    return pltpu.CompilerParams(vmem_limit_bytes=mib * 1024 * 1024)


def ffn1_call(x, table, g, vecs):
    tokens, width = x.shape
    steps = tokens // TB
    places = tall(table.shape[0] // steps, width)
    return pl.pallas_call(
        ffn1_kernel,
        grid=(steps,),
        in_specs=[
            tall(TB, width), places, seg_spec("f1i", width), seg_spec("f1o", width),
            seg_spec("qkv", width), seg_spec("pos", width), whole(vecs.shape),
        ],
        out_specs=[tall(TB, width), tall(TB, 4 * width)] + [tall(TB, width)] * 4 + [places],
        out_shape=[
            jax.ShapeDtypeStruct((tokens, width), F32),
            jax.ShapeDtypeStruct((tokens, 4 * width), BF),
        ]
        + [jax.ShapeDtypeStruct((tokens, width), BF)] * 4
        + [jax.ShapeDtypeStruct(table.shape, BF)],
        compiler_params=dense_params(),
        name="ffn1_forward",
    )(x, table, g, g, g, g, vecs)


FRONT_PIECES = (
    [(0, at + 256 * j, 256) for j in range(4) for at in (0, 1024)]
    + [(0, 2048 + 256 * k, 256) for k in range(4)]
    + [(1, 256 * k, 256) for k in (10, 8, 9, 11, 0, 4, 1, 5, 2, 6, 3, 7)]
)


def front_call(lens, x, table, packed_a, packed_b, slab, batch, cid):
    tokens, width = x.shape
    full = tokens // batch
    pairs = width // (2 * DK)
    chunks = SEG["f1i"][1] // HC
    first_head = chunks + 1
    steps = first_head + batch * pairs
    order = gather_order(FRONT_PIECES)
    dma = pltpu.SemaphoreType.DMA
    small = [
        pltpu.VMEM(slab.shape, BF), pltpu.VMEM((3,) + slab.shape, BF),
        pltpu.VMEM((7,) + slab.shape, BF), dma((3,)), dma((3,)), dma((7,)), dma((7,)),
    ]
    heads_shape = (batch, full, width)
    scratch = [
        pltpu.VMEM((2, NZ, NY, NX) + packed_a.shape, BF),
        pltpu.VMEM((tokens, width), F32),
        pltpu.VMEM((tokens, width), BF),
    ]
    scratch += [pltpu.VMEM(heads_shape, BF)] * 5 + [pltpu.VMEM(heads_shape, F32)]
    scratch += [pltpu.VMEM(table.shape, BF), dma((10,))]
    n_own = len(scratch)

    def body(
        len_ref, x_ref, table_ref, xa_ref, xb_ref, s_ref,
        ga_ref, gb_ref, vecs, first_ref, z_ref, qu_ref, qv_ref, k_ref, v_ref, pos_ref, mix_ref,
        lse_ref, *rest,
    ):
        i = pl.program_id(0)
        ga, y_s, hn_s, qu, qv, k, v, mix, lse, pos, out_sem = rest[:n_own]
        smalls = rest[n_own : n_own + len(small)]
        begin, event, finish = gather_events(
            FRONT_PIECES, (xa_ref, xb_ref), (ga, gb_ref), rest[n_own + len(small) :]
        )
        plane, s_begin, s_spread, s_finish = small_steps(s_ref, vecs, *smalls)
        z, y, xx, t = place()
        sources = (ga, y_s, qu, qv, k, v, pos, mix, lse)
        targets = (ga_ref, first_ref, qu_ref, qv_ref, k_ref, v_ref, pos_ref, mix_ref, lse_ref)
        copies = [
            pltpu.make_async_copy(a, b, out_sem.at[n])
            for n, (a, b) in enumerate(zip(sources, targets))
        ]
        done = [0]

        def until(q):
            while True:
                _, kind, pair = order[done[0]]
                done[0] += 1
                event(kind, pair)
                if (kind, pair) == ("c", q):
                    break

        def weight(t, start, w):
            return ga[t, :, :, :, :, start : start + w].reshape(width, w)

        @pl.when(i == 0)
        def _():
            greet([dev(lax.rem(z + d, NZ), y, xx, t) for d in range(1, NZ)] + plane)
            begin()
            s_begin()
            for n in range(4):
                event(*order[n][1:])
            s_spread()
            for n in range(4, 7):
                event(*order[n][1:])
            done[0] = 7
            s_finish()
            for r in range(tokens // TB):
                here = slice(r * TB, (r + 1) * TB)
                scaled, _ = ln_stats(x_ref[here, :].astype(F32))
                hn_s[here, :] = (scaled * row(vecs, 0) + row(vecs, 1)).astype(BF)
                y_s[here, :] = jnp.zeros((TB, width), F32) + row(vecs, 2)

        for j in range(chunks):

            @pl.when(i == j)
            def _(j=j):
                until(j)
                for t in range(2):
                    w_in, w_out = weight(t, j * HC, HC), weight(t, 1024 + j * HC, HC)
                    r, c = divmod(t * chunks * HC + j * HC, width)
                    bias = vecs[R_B1 + r : R_B1 + r + 1, c : c + HC]
                    for k in range(tokens // TB):
                        here = slice(k * TB, (k + 1) * TB)
                        zf = nn(hn_s[here, :], w_in) + bias
                        z_ref[here, t * HC : (t + 1) * HC] = zf.astype(BF)
                        y_s[here, :] += nt((zf * sig(zf)).astype(BF), w_out)

        @pl.when(i == chunks)
        def _():
            for r in range(tokens // TB):
                here = slice(r * TB, (r + 1) * TB)
                first = x_ref[here, :].astype(F32) + 0.5 * y_s[here, :]
                y_s[here, :] = first
                scaled, _ = ln_stats(first)
                hn_s[here, :] = (scaled * row(vecs, 3) + row(vecs, 4)).astype(BF)
            copies[1].start()
            until(chunks)
            part = width // 2
            for t in range(2):
                c = slice(t * part, (t + 1) * part)
                pos[:, c] = nn(table_ref[...], weight(t, SEG["pos"][0], part)).astype(BF)
            copies[6].start()
            until(chunks + 1)
            copies[0].start()
            at = SEG["qkv"][0]
            for t in range(2):
                c = slice(t * part, (t + 1) * part)
                for u in range(batch):
                    hn = hn_s[u * full : (u + 1) * full, :]
                    q = nn(hn, weight(t, at, part)) + vecs[R_ATT : R_ATT + 1, c]
                    qu[u, :, c] = (q + vecs[R_ATT + 2 : R_ATT + 3, c]).astype(BF)
                    qv[u, :, c] = (q + vecs[R_ATT + 3 : R_ATT + 4, c]).astype(BF)
                    k[u, :, c] = nn(hn, weight(t, at + part, part)).astype(BF)
                    val = nn(hn, weight(t, at + 2 * part, part))
                    v[u, :, c] = (val + vecs[R_ATT + 1 : R_ATT + 2, c]).astype(BF)
            for n in (2, 3, 4, 5):
                copies[n].start()

        left = order[done[0] :]
        base = order[done[0] - 1][0] + 6.0
        blocks = full // BLK
        spots = batch * pairs * blocks
        slots = [min(max(int((now + 2.0 - base) / 0.9), 0), spots) for now, _, _ in left]

        def hook(blk):
            for slot, (_, kind, pair) in zip(slots, left):
                if slot % blocks == blk and slot < spots:

                    @pl.when(i == first_head + slot // blocks)
                    def _(kind=kind, pair=pair):
                        event(kind, pair)

        @pl.when(i >= first_head)
        def _():
            n = i - first_head
            u = n // pairs
            c = pl.ds(pl.multiple_of(lax.rem(n, pairs) * (2 * DK), 2 * DK), 2 * DK)

            def view(ref):
                return ref.at[pl.ds(u, 1), :, c]

            attn_fwd_kernel(
                len_ref, view(qu), view(qv), view(k), view(v), pos.at[:, c], view(mix), view(lse),
                u, hook,
            )

        @pl.when(i == steps - 1)
        def _():
            copies[7].start()
            copies[8].start()
            for slot, (_, kind, pair) in zip(slots, left):
                if slot >= spots:
                    event(kind, pair)
            finish()
            for copy in copies:
                copy.wait()

    def const(shape):
        return pl.BlockSpec(shape, lambda i, n: (0,) * len(shape), pipeline_mode=pl.Buffered(1))

    heads = jax.ShapeDtypeStruct(heads_shape, BF)
    return pl.pallas_call(
        body,
        grid_spec=pltpu.PrefetchScalarGridSpec(
            num_scalar_prefetch=1,
            grid=(steps,),
            in_specs=[
                const(x.shape), const(table.shape), const(packed_a.shape), const(packed_b.shape),
                const(slab.shape),
            ],
            out_specs=[
                ANY, ANY, pl.BlockSpec((R_ALL, width), lambda i, n: (0, 0)), ANY,
                pl.BlockSpec((tokens, 2 * HC), lambda i, n: (0, jnp.minimum(i, chunks - 1))),
            ]
            + [ANY] * 7,
            scratch_shapes=scratch + small + gather_scratch(len(FRONT_PIECES)),
        ),
        out_shape=[
            gathered_shape(packed_a),
            gathered_shape(packed_b),
            jax.ShapeDtypeStruct((R_ALL, width), F32),
            jax.ShapeDtypeStruct((tokens, width), F32),
            jax.ShapeDtypeStruct((tokens, 4 * width), BF),
            heads, heads, heads, heads,
            jax.ShapeDtypeStruct(table.shape, BF),
            heads,
            jax.ShapeDtypeStruct(heads_shape, F32),
        ],
        compiler_params=comm_params(cid),
        name="front",
    )(lens, x, table, packed_a, packed_b, slab)


def fill_table(table_ref):
    length, width = table_ref.shape[0] // 2, table_ref.shape[1]
    step = 32
    cols = lax.broadcasted_iota(jnp.int32, (step, width), 1)
    rows = lax.broadcasted_iota(jnp.int32, (step, width), 0)
    rate = jnp.exp((cols // 2 * 2).astype(F32) * (-math.log(10000.0) / width))
    even = cols % 2 == 0
    big = (length - 1 - step * rows).astype(F32) * rate
    small = rows.astype(F32) * rate
    sin_big, cos_big = jnp.sin(big), jnp.cos(big)
    first = jnp.where(even, sin_big, cos_big)
    second = jnp.where(even, cos_big, -sin_big)
    cos_small, sin_small = jnp.cos(small), jnp.sin(small)
    for a in range(2 * length // step):
        block = first[a : a + 1] * cos_small - second[a : a + 1] * sin_small
        table_ref[a * step : (a + 1) * step, :] = block.astype(BF)


def table_call(full, width):
    return pl.pallas_call(
        fill_table,
        out_specs=VM,
        out_shape=jax.ShapeDtypeStruct((2 * full, width), BF),
        name="position_table",
    )()


def conv1_kernel(
    lens, mixed, first, w_out, w_ci, vecs, second_ref, half_ref, conv_ref, stat_ref, pad
):
    u = pl.program_id(0)
    full = first.shape[0]
    count = lens[u]
    part = w_out.shape[2]
    y = row(vecs, 5)
    for t in range(2):
        y = y + nt(mixed[:, t * part : (t + 1) * part], w_out[t])
    second = first[...] + y
    second_ref[...] = second
    scaled, _ = ln_stats(second)
    hn = (scaled * row(vecs, 6) + row(vecs, 7)).astype(BF)
    mask = row_mask(0, full, count)
    pad[0:8, :] = jnp.zeros((8, part), F32)
    pad[full + 8 : full + 16, :] = jnp.zeros((8, part), F32)
    for t in range(2):
        c = slice(t * part, (t + 1) * part)
        proj = nn(hn, w_ci[t])
        za = proj[:, :part] + vecs[R_CV : R_CV + 1, c]
        zg = proj[:, part:] + vecs[R_CV + 1 : R_CV + 2, c]
        half_ref[:, 2 * t * part : (2 * t + 1) * part] = za.astype(BF)
        half_ref[:, (2 * t + 1) * part : (2 * t + 2) * part] = zg.astype(BF)
        pad[8 : full + 8, :] = za * sig(zg) * mask
        total = jnp.zeros((full, part), F32)
        for k in range(9):
            total = total + vecs[R_CV + 4 + k : R_CV + 5 + k, c] * pad[4 + k : 4 + k + full, :]
        conv_ref[:, c] = total
        kept = total * mask
        stat_ref[pl.ds(4 * u, 1), c] = col_sum(kept)
        stat_ref[pl.ds(4 * u + 1, 1), c] = col_sum(kept * total)
    for k in (2, 3):
        stat_ref[pl.ds(4 * u + k, 1), :] = jnp.full((1, 2 * part), 1.0, F32) * count.astype(F32)


def conv1_call(lens, mixed, first, g, vecs):
    tokens, width = first.shape
    batch = lens.shape[0]
    full = tokens // batch
    return pl.pallas_call(
        conv1_kernel,
        grid_spec=pltpu.PrefetchScalarGridSpec(
            num_scalar_prefetch=1,
            grid=(batch,),
            in_specs=[
                tall(full, width), tall(full, width), seg_spec("out", width),
                seg_spec("ci", width), whole(vecs.shape),
            ],
            out_specs=[
                tall(full, width), tall(full, 2 * width), tall(full, width),
                whole((4 * batch, width)),
            ],
            scratch_shapes=[pltpu.VMEM((full + 16, width // 2), F32)],
        ),
        out_shape=[
            jax.ShapeDtypeStruct((tokens, width), F32),
            jax.ShapeDtypeStruct((tokens, 2 * width), BF),
            jax.ShapeDtypeStruct((tokens, width), F32),
            jax.ShapeDtypeStruct((4 * batch, width), F32),
        ],
        compiler_params=dense_params(),
        name="conv_forward",
    )(lens, mixed, first, g, g, vecs)


def bn_of(stats, u):
    n = stats[pl.ds(4 * u + 2, 1), :]
    avg = stats[pl.ds(4 * u, 1), :] / n
    var = stats[pl.ds(4 * u + 1, 1), :] / n - avg * avg
    return avg, lax.rsqrt(var + norm_eps), n


def swish_parts(z):
    s = sig(z)
    a = z * s
    return a, s + a * (1.0 - s)


def middle_kernel(
    lens, second, conv, cot, stats, w_co, w_in, w_out, vecs,
    act_ref, d3_ref, dy_ref, sum_ref, small_ref, gi_ref, go_ref, gc_ref,
    a_s, slope_s, gi, go, gc,
):
    i = pl.program_id(0)
    steps = pl.num_programs(0)
    rows, width = second.shape
    batch = lens.shape[0]
    per = steps // batch
    u = i // per
    mask = row_mask(lax.rem(i, per) * rows, rows, lens[u])

    @pl.when(i == 0)
    def _():
        small_ref[...] = jnp.zeros_like(small_ref)
        sum_ref[...] = jnp.zeros_like(sum_ref)
        gi[...] = jnp.zeros_like(gi)
        go[...] = jnp.zeros_like(go)
        gc[...] = jnp.zeros_like(gc)

    avg, rstd, _ = bn_of(stats, u)
    part = w_co.shape[2]
    half = w_in.shape[2]
    yhat = (conv[...] - avg) * rstd
    bn, bn_slope = swish_parts(yhat * row(vecs, R_CV + 2) + row(vecs, R_CV + 3))
    act = bn.astype(BF)
    y = row(vecs, 8)
    for t in range(2):
        y = y + nt(act[:, t * part : (t + 1) * part], w_co[t])
    third = second[...] + y
    scaled9, inv9 = ln_stats(third)
    hn = (scaled9 * row(vecs, 9) + row(vecs, 10)).astype(BF)
    y = row(vecs, 11)
    for t in range(2):
        c = slice(t * half, (t + 1) * half)
        a, slope = swish_parts(nn(hn, w_in[t]) + bias_half(vecs, R_B2, t))
        a = a.astype(BF)
        a_s[:, c] = a
        slope_s[:, c] = slope
        y = y + nt(a, w_out[t])
    scaled, inv = ln_stats(third + 0.5 * y)
    act_ref[...] = (scaled * row(vecs, 12) + row(vecs, 13)).astype(BF)
    up = cot[...].astype(F32) * mask
    small_ref[12:13, :] += col_sum(up * scaled)
    small_ref[13:14, :] += col_sum(up)
    d4 = ln_back(up, scaled, inv, row(vecs, 12))
    g = (0.5 * d4).astype(BF)
    small_ref[11:12, :] += col_sum(g.astype(F32))
    d_hn = jnp.zeros((rows, width), F32)
    for t in range(2):
        c = slice(t * half, (t + 1) * half)
        go[t] += tn(g, a_s[:, c])
        dz = (nn(g, w_out[t]) * slope_s[:, c]).astype(BF)
        bias = col_sum(dz.astype(F32))
        small_ref[R_B2 + 2 * t : R_B2 + 2 * t + 1, :] += bias[:, :width]
        small_ref[R_B2 + 2 * t + 1 : R_B2 + 2 * t + 2, :] += bias[:, width:]
        gi[t] += tn(hn, dz)
        d_hn = d_hn + nt(dz, w_in[t])
    small_ref[9:10, :] += col_sum(d_hn * scaled9)
    small_ref[10:11, :] += col_sum(d_hn)
    d3 = d4 + ln_back(d_hn, scaled9, inv9, row(vecs, 9))
    d3_ref[...] = d3
    g = d3.astype(BF)
    small_ref[8:9, :] += col_sum(g.astype(F32))
    d_act = []
    for t in range(2):
        gc[t] += tn(g, act[:, t * part : (t + 1) * part])
        d_act.append(nn(g, w_co[t]))
    d_bn = jnp.concatenate(d_act, axis=1) * bn_slope
    small_ref[R_CV + 2 : R_CV + 3, :] += col_sum(d_bn * yhat)
    small_ref[R_CV + 3 : R_CV + 4, :] += col_sum(d_bn)
    d_yhat = d_bn * row(vecs, R_CV + 2)
    dy_ref[...] = d_yhat
    sum_ref[pl.ds(4 * u, 1), :] += col_sum(d_yhat)
    sum_ref[pl.ds(4 * u + 1, 1), :] += col_sum(d_yhat * yhat)

    @pl.when(i == steps - 1)
    def _():
        gi_ref[...] = gi[...].astype(BF)
        go_ref[...] = go[...].astype(BF)
        gc_ref[...] = gc[...].astype(BF)


def grad_shape(name, width):
    return jax.ShapeDtypeStruct((2, width, SEG[name][1]), BF)


def acc(name, width):
    return pltpu.VMEM((2, width, SEG[name][1]), F32)


def once(shape):
    zeros = (0,) * len(shape)
    return pl.BlockSpec(shape, lambda i, *_: zeros, pipeline_mode=pl.Buffered(1))


def middle_call(lens, second, conv, cot, stats, g, vecs):
    tokens, width = second.shape
    small = (R_ALL, width)
    names = ("f2i", "f2o", "co")
    return pl.pallas_call(
        middle_kernel,
        grid_spec=pltpu.PrefetchScalarGridSpec(
            num_scalar_prefetch=1,
            grid=(tokens // TB,),
            in_specs=[tall(TB, width)] * 3
            + [whole(stats.shape), seg_spec("co", width), seg_spec("f2i", width)]
            + [seg_spec("f2o", width), whole(vecs.shape)],
            out_specs=[tall(TB, width)] * 3
            + [whole(stats.shape), whole(small)]
            + [whole(grad_shape(name, width).shape) for name in names],
            scratch_shapes=[
                pltpu.VMEM((TB, 4 * width), BF),
                pltpu.VMEM((TB, 4 * width), F32),
            ]
            + [acc(name, width) for name in names],
        ),
        out_shape=[
            jax.ShapeDtypeStruct((tokens, width), BF),
            jax.ShapeDtypeStruct((tokens, width), F32),
            jax.ShapeDtypeStruct((tokens, width), F32),
            jax.ShapeDtypeStruct(stats.shape, F32),
            jax.ShapeDtypeStruct(small, F32),
        ]
        + [grad_shape(name, width) for name in names],
        compiler_params=dense_params(),
        name="conv_out_ffn2",
    )(lens, second, conv, cot, stats, g, g, g, vecs)


def conv2_kernel(
    lens, dy, conv, d3, halves, second, mixed, stats, sums, w_ci, w_out, vecs,
    d2_ref, dm_ref, small_ref, gi_ref, go_ref, pad, gi, go,
):
    u = pl.program_id(0)
    full, width = d3.shape
    part = w_out.shape[2]

    @pl.when(u == 0)
    def _():
        small_ref[...] = jnp.zeros_like(small_ref)
        gi[...] = jnp.zeros_like(gi)
        go[...] = jnp.zeros_like(go)

    avg, rstd, n = bn_of(stats, u)
    mask = row_mask(0, full, lens[u])
    scaled, inv = ln_stats(second[...])
    hn = (scaled * row(vecs, 6) + row(vecs, 7)).astype(BF)
    pad[0:8, :] = jnp.zeros((8, part), F32)
    pad[full + 8 : full + 16, :] = jnp.zeros((8, part), F32)
    b1 = sums[pl.ds(4 * u, 1), :]
    b2 = sums[pl.ds(4 * u + 1, 1), :]
    d_hn = jnp.zeros((full, width), F32)
    for t in range(2):
        c = slice(t * part, (t + 1) * part)
        yhat = (conv[:, c] - avg[:, c]) * rstd[:, c]
        pad[8 : full + 8, :] = rstd[:, c] * (
            dy[:, c] - mask * ((b1[:, c] + yhat * b2[:, c]) / n[:, c])
        )
        za = halves[:, 2 * t * part : (2 * t + 1) * part].astype(F32)
        gate = sig(halves[:, (2 * t + 1) * part : (2 * t + 2) * part].astype(F32))
        gated = za * gate * mask
        total = jnp.zeros((full, part), F32)
        for k in range(9):
            moved = pad[12 - k : 12 - k + full, :]
            total = total + vecs[R_CV + 4 + k : R_CV + 5 + k, c] * moved
            small_ref[R_CV + 4 + k : R_CV + 5 + k, c] += col_sum(gated * moved)
        d_glu = total * mask
        d_a = (d_glu * gate).astype(BF)
        d_g = (d_glu * gated * (1.0 - gate)).astype(BF)
        small_ref[R_CV : R_CV + 1, c] += col_sum(d_a.astype(F32))
        small_ref[R_CV + 1 : R_CV + 2, c] += col_sum(d_g.astype(F32))
        both = jnp.concatenate([d_a, d_g], axis=1)
        gi[t] += tn(hn, both)
        d_hn = d_hn + nt(both, w_ci[t])
    small_ref[6:7, :] += col_sum(d_hn * scaled)
    small_ref[7:8, :] += col_sum(d_hn)
    d2 = d3[...] + ln_back(d_hn, scaled, inv, row(vecs, 6))
    d2_ref[...] = d2
    g = d2.astype(BF)
    small_ref[5:6, :] += col_sum(g.astype(F32))
    for t in range(2):
        c = slice(t * part, (t + 1) * part)
        go[t] += tn(g, mixed[:, c])
        dm_ref[:, c] = nn(g, w_out[t]).astype(BF)

    @pl.when(u == pl.num_programs(0) - 1)
    def _():
        gi_ref[...] = gi[...].astype(BF)
        go_ref[...] = go[...].astype(BF)


def conv2_call(lens, dy, conv, d3, halves, second, mixed, stats, sums, g, vecs):
    tokens, width = second.shape
    batch = lens.shape[0]
    full = tokens // batch
    small = (R_ALL, width)
    names = ("ci", "out")
    return pl.pallas_call(
        conv2_kernel,
        grid_spec=pltpu.PrefetchScalarGridSpec(
            num_scalar_prefetch=1,
            grid=(batch,),
            in_specs=[tall(full, width)] * 3
            + [tall(full, 2 * width), tall(full, width), tall(full, width)]
            + [whole(stats.shape)] * 2
            + [seg_spec("ci", width), seg_spec("out", width), whole(vecs.shape)],
            out_specs=[tall(full, width)] * 2
            + [whole(small)]
            + [whole(grad_shape(name, width).shape) for name in names],
            scratch_shapes=[pltpu.VMEM((full + 16, width // 2), F32)]
            + [acc(name, width) for name in names],
        ),
        out_shape=[
            jax.ShapeDtypeStruct((tokens, width), F32),
            jax.ShapeDtypeStruct((tokens, width), BF),
            jax.ShapeDtypeStruct(small, F32),
        ]
        + [grad_shape(name, width) for name in names],
        compiler_params=dense_params(),
        name="conv_backward",
    )(lens, dy, conv, d3, halves, second, mixed, stats, sums, g, g, vecs)


def last_kernel(
    dq, dk, dv, first, x_ref, d2, z_ref, table, dpos, asums, w_qkv, w_in, w_out, vecs,
    d0_ref, small_ref, d1_s, g_s, hn_s, dh_s, gq, gp, put, ready, after,
):
    i = pl.program_id(0)
    blocks = x_ref.shape[0] // TB
    rows, width = first.shape
    part = w_qkv.shape[2] // 3

    @pl.when(i == 0)
    def _():
        small_ref[...] = jnp.zeros_like(small_ref)
        small_ref[R_ATT:R_CV, :] = jnp.sum(asums[...], axis=0)[0:4]
        gq[...] = jnp.zeros_like(gq)
        gp[...] = jnp.zeros_like(gp)
        dh_s[...] = jnp.zeros_like(dh_s)

    @pl.when(i < blocks)
    def _():
        here = pl.ds(pl.multiple_of(i * TB, TB), TB)
        scaled, inv = ln_stats(first[...])
        hn = (scaled * row(vecs, 3) + row(vecs, 4)).astype(BF)
        d_hn = jnp.zeros((rows, width), F32)
        for t in range(2):
            c = slice(t * part, (t + 1) * part)
            dp = jnp.concatenate([dq[:, c], dk[:, c], dv[:, c]], axis=1)
            gq[t] += tn(hn, dp)
            for u in range(dpos.shape[0]):
                gp[t] += tn(table[...], dpos[u, :, c])
            d_hn = d_hn + nt(dp, w_qkv[t])
        small_ref[3:4, :] += col_sum(d_hn * scaled)
        small_ref[4:5, :] += col_sum(d_hn)
        d1 = d2[...] + ln_back(d_hn, scaled, inv, row(vecs, 3))
        d1_s[here, :] = d1
        g = (0.5 * d1).astype(BF)
        g_s[here, :] = g
        small_ref[2:3, :] += col_sum(g.astype(F32))
        scaled, inv = ln_stats(x_ref[here, :].astype(F32))
        hn_s[here, :] = (scaled * row(vecs, 0) + row(vecs, 1)).astype(BF)

    @pl.when(i == blocks - 1)
    def _():
        for t in range(2):
            put("pos", t, 0, gp[t])
            put("qkv", t, 0, gq[t])
        ready(-1)

    chunks = w_in.shape[2] // HC
    for j in range(chunks):

        @pl.when(i == blocks + j)
        def _(j=j):
            for t in range(2):
                c = slice(j * HC, (j + 1) * HC)
                a, slope = swish_parts(z_ref[:, t * HC : (t + 1) * HC].astype(F32))
                put("f1o", t, j * HC, tn(g_s[...], a.astype(BF)))
                dz = (nn(g_s[...], w_out[t, :, c]) * slope).astype(BF)
                r, c0 = divmod(t * chunks * HC + j * HC, width)
                small_ref[R_B1 + r : R_B1 + r + 1, c0 : c0 + HC] += col_sum(dz.astype(F32))
                put("f1i", t, j * HC, tn(hn_s[...], dz))
                dh_s[...] += nt(dz, w_in[t, :, c])
                after(j, t)
            ready(j)

    @pl.when(i == blocks + chunks - 1)
    def _():
        for k in range(blocks):
            here = slice(k * TB, (k + 1) * TB)
            scaled, inv = ln_stats(x_ref[here, :].astype(F32))
            d_hn = dh_s[here, :]
            small_ref[0:1, :] += col_sum(d_hn * scaled)
            small_ref[1:2, :] += col_sum(d_hn)
            d0 = d1_s[here, :] + ln_back(d_hn, scaled, inv, row(vecs, 0))
            d0_ref[here, :] = d0.astype(BF)


def last_call(dq, dk, dv, first, x, d2, z, table, dpos, asums, g, vecs, others=None, cid=None):
    tokens, width = first.shape
    blocks, chunks = tokens // TB, SEG["f1i"][1] // HC
    small = (R_ALL, width)
    places = table.shape[0] // blocks

    def block(rows, cols):
        return pl.BlockSpec((rows, cols), lambda i: (jnp.minimum(i, blocks - 1), 0))

    in_specs = (
        [block(TB, width)] * 4
        + [whole(x.shape), block(TB, width)]
        + [pl.BlockSpec((tokens, 2 * HC), lambda i: (0, jnp.maximum(i - blocks, 0)))]
        + [block(places, width)]
        + [
            pl.BlockSpec(
                (dpos.shape[0], places, width), lambda i: (0, jnp.minimum(i, blocks - 1), 0)
            ),
            whole(asums.shape),
        ]
        + [seg_spec(name, width) for name in ("qkv", "f1i", "f1o")]
        + [whole(vecs.shape)]
    )
    args = [dq, dk, dv, first, x, d2, z, table, dpos, asums, g, g, g, vecs]
    scratch = [
        pltpu.VMEM((tokens, width), F32), pltpu.VMEM((tokens, width), BF),
        pltpu.VMEM((tokens, width), BF), pltpu.VMEM((tokens, width), F32),
        acc("qkv", width), acc("pos", width),
    ]
    out_specs = [whole((tokens, width)), whole(small)]
    out_shape = [jax.ShapeDtypeStruct((tokens, width), BF), jax.ShapeDtypeStruct(small, F32)]
    n_own = len(scratch)
    if others is None:
        names = ("qkv", "f1i", "f1o", "pos")
        out_specs += [once(grad_shape(name, width).shape) for name in names]
        out_shape += [grad_shape(name, width) for name in names]

        def body(*refs):
            ins, rest = refs[: len(args)], refs[len(args) :]
            outs = dict(zip(names, rest[2:6]))

            def put(name, t, at, value):
                outs[name][t, :, at : at + value.shape[1]] = value.astype(BF)

            last_kernel(*ins, *rest[:2], *rest[6:], put, lambda j: None, lambda j, t: None)

        params = dense_params()
    else:
        owned = width // (NZ * NY * NX)
        names = ("pos", "qkv", "f1i", "f1o")
        base = {name: SEG[name][0] for name in names}
        order = [("pos", 0), ("qkv", 0), ("qkv", 256), ("qkv", 512)]
        for j in range(chunks):
            order += [("f1i", j * HC), ("f1o", j * HC)]
        pieces = [(0, base[name] + at, 256, base[name] + at) for name, at in order]
        n_first = 4
        n_in = len(args)
        args += list(others)
        in_specs += [whole(item.shape) for item in others]
        out_specs = out_specs[:1] + [whole((owned, C_A)), whole((R_SUM, width))]
        out_shape = out_shape[:1] + [
            jax.ShapeDtypeStruct((owned, C_A), F32), jax.ShapeDtypeStruct((R_SUM, width), F32)
        ]
        small_scratch = small_sum_scratch(width)
        scratch += [pltpu.VMEM(small, F32), pltpu.VMEM((2, NZ, NY, NX, owned, C_A), BF)]
        scratch += small_scratch + scatter_scratch(pieces, owned)
        params = comm_params(cid)

        def body(*refs):
            i = pl.program_id(0)
            ins, rest = refs[:n_in], refs[n_in:]
            parts, rest = rest[: len(others)], rest[len(others) :]
            (d0_ref, o_ref, ext), rest = rest[:3], rest[3:]
            own, rest = rest[:n_own], rest[n_own:]
            (small_ref, buf), rest = rest[:2], rest[2:]
            sums, sems = rest[: len(small_scratch)], rest[len(small_scratch) :]
            start, advance, finish, rounds = scatter_steps(pieces, [buf], o_ref, sems, 2)
            pp, small_list = small_sum_steps(list(parts) + [small_ref], ext, sums)
            z, y, x, t = place()

            def put(name, t, at, value):
                w = value.shape[1]
                at = base[name] + at
                buf[t, :, :, :, :, at : at + w] = value.astype(BF).reshape(NZ, NY, NX, owned, w)

            def ready(j):
                for p in range(n_first) if j < 0 else (n_first + 2 * j, n_first + 2 * j + 1):
                    start(p)

            def after(j, t):
                if j == 0:
                    advance(2 * t)
                    advance(2 * t + 1)
                else:
                    advance(n_first + 2 * (j - 1) + t)

            @pl.when(i == 0)
            def _():
                greet(link_peers(z, y, x, t)[: NZ - 1] + pp + [dev(z, y, x, 1 - t)])

            last_kernel(*ins, d0_ref, small_ref, *own, put, ready, after)

            @pl.when(i == blocks + chunks - 1)
            def _():
                todo = [lambda q=q: advance(q) for q in range(n_first + 2 * (chunks - 1), rounds)]
                for k in range(max(len(todo), len(small_list))):
                    if k < len(small_list):
                        small_list[k]()
                    if k < len(todo):
                        todo[k]()
                finish()

    return pl.pallas_call(
        body,
        grid=(blocks + chunks,),
        in_specs=in_specs,
        out_specs=out_specs,
        scratch_shapes=scratch,
        out_shape=out_shape,
        compiler_params=params,
        name="qkv_ffn1_backward",
    )(*args)


def gather_plain(big, kinds, names_a, names_b, small_ins, both, n_dp):
    def pack(names):
        return jnp.concatenate(
            [big[n].T if kinds[n][0] == "flip" else big[n] for n in names], axis=1
        )

    def every(item):
        g = lax.all_gather(item, both, axis=0, tiled=True)
        g = g.reshape(n_dp, 2, item.shape[0], -1).transpose(1, 0, 2, 3)
        return g.reshape(2, n_dp * item.shape[0], -1)

    small = jnp.concatenate([item.reshape(-1) for item in small_ins])
    smalls = lax.all_gather(small, both, axis=0, tiled=False).reshape(n_dp, 2, -1).astype(F32)
    off = 0
    pieces = []
    for item in small_ins:
        pieces.append(smalls[:, :, off : off + item.size].reshape((n_dp, 2) + item.shape))
        off += item.size
    width = small_ins[4].shape[1] * n_dp * 2
    vecs = jnp.concatenate(
        [
            pieces[4].transpose(2, 0, 1, 3).reshape(-1, width),
            pieces[1].transpose(2, 1, 3, 0, 4).reshape(-1, width),
            pieces[2].transpose(2, 1, 3, 0, 4).reshape(-1, width),
            pieces[0].transpose(1, 2, 0, 3).reshape(-1, width),
            pieces[3].transpose(1, 2, 0, 3).reshape(-1, width),
            jnp.zeros((1, width), F32),
        ],
        axis=0,
    )
    return every(pack(names_a)), every(pack(names_b)), vecs


def scatter_plain(grads, kinds, names, small_g, small_ins, both, n_dp):
    vec_g = (
        small_g[R_B1:R_B2].reshape(1, -1), small_g[R_ATT:R_CV], small_g[R_CV:R_B1],
        small_g[R_B2 : R_B2 + 4].reshape(1, -1),
    )

    def small_of(item, like):
        item = item.reshape(item.shape[0], 2, like.shape[-2], n_dp, like.shape[-1])
        return item.transpose(1, 3, 0, 2, 4).reshape(2, n_dp, -1)

    cols = small_ins[4].shape[1]
    norm_g = small_g[:R_ATT].reshape(-1, n_dp, 2, cols).transpose(2, 1, 0, 3).reshape(2, n_dp, -1)
    packed = jnp.concatenate(
        [small_of(item, like) for item, like in zip(vec_g, small_ins)] + [norm_g], axis=2
    )
    packed = packed.swapaxes(0, 1).reshape(n_dp * 2, -1)
    own_small = lax.psum_scatter(packed, both, scatter_dimension=0, tiled=True).reshape(-1)
    wide = jnp.concatenate([grads[name] for name in names], axis=2)
    rows = wide.shape[1] // n_dp
    wide = wide.reshape(2, n_dp, rows, -1).swapaxes(0, 1).reshape(n_dp * 2 * rows, -1)
    own = lax.psum_scatter(wide, both, scatter_dimension=0, tiled=True).astype(F32)
    outs, at = {}, 0
    for name in names:
        w = grads[name].shape[2]
        item = own[:, at : at + w]
        outs[name] = item.T if kinds[name][0] == "flip" else item
        at += w
    small_outs, at = [], 0
    for item in small_ins:
        small_outs.append(own_small[at : at + item.size].reshape(item.shape))
        at += item.size
    return outs, small_outs


def local(
    frames,
    lengths,
    ffn1_in,
    ffn1_out,
    ffn1_bias,
    qkv_weight,
    pos_weight,
    out_weight,
    attn_bias,
    conv_in,
    conv_out,
    conv_channel,
    ffn2_in,
    ffn2_out,
    ffn2_bias,
    norm_params,
    cotangent,
):
    micro, seqs, full, width = frames.shape
    both = ("dp", "tensor")
    n_dp = lax.axis_size("dp")
    rows = ffn1_in.shape[0]
    batch = micro * seqs
    tokens = batch * full
    small_ins = (ffn1_bias, attn_bias, conv_channel, ffn2_bias, norm_params)
    names_a, names_b = ("f1i", "f1o", "pos", "qkv"), ("f2i", "f2o", "ci", "out", "co")
    big = {
        "f1i": ffn1_in, "f1o": ffn1_out, "pos": pos_weight, "qkv": qkv_weight.reshape(rows, -1),
        "f2i": ffn2_in, "f2o": ffn2_out, "ci": conv_in.reshape(rows, -1), "out": out_weight,
        "co": conv_out,
    }
    kinds = {name: ("plain",) for name in big}
    kinds.update({name: ("flip",) for name in ("f1o", "f2o", "out", "co")})
    mine_mesh = own_mesh((n_dp, lax.axis_size("tensor"))) and rows % 16 == 0
    if mine_mesh:
        packed_a, packed_b, slab, table = prep_call(
            [
                ffn1_in, ffn1_out.T, pos_weight, qkv_weight.transpose(1, 0, 2), ffn2_in,
                ffn2_out.T, conv_in, out_weight.T, conv_out.T,
            ],
            [ffn1_bias, attn_bias, conv_channel.transpose(1, 2, 0), ffn2_bias, norm_params],
            full, width,
        )
    else:
        table = table_call(full, width)
        g_a, g_b, vecs = gather_plain(big, kinds, names_a, names_b, small_ins, both, n_dp)

    def reduce_sum(item, cid):
        if mine_mesh:
            return sum_all(item, cid)
        return lax.psum(item, both)

    mine = lax.axis_index("tensor")
    lens = lax.dynamic_slice_in_dim(lengths, mine * seqs, seqs, 1).reshape(-1)
    x = frames.reshape(tokens, width)
    cot = cotangent.reshape(tokens, width)

    def utt(item):
        return item.reshape(batch, full, -1)

    def flat(item):
        return item.reshape(tokens, -1)

    if mine_mesh:
        g_a, g_b, vecs, first, z1, q_u, q_v, keys, values, pos, mixed, lse = front_call(
            lens, x, table, packed_a, packed_b, slab, batch, 1
        )
        g_a, g_b = g_a.reshape(2, width, -1), g_b.reshape(2, width, -1)
        heads = (lens, q_u, q_v, keys, values, pos)
    else:
        first, z1, q_u, q_v, keys, values, pos = ffn1_call(x, table, g_a, vecs)
        heads = (lens, utt(q_u), utt(q_v), utt(keys), utt(values), pos)
        mixed, lse = attn_fwd_call(*heads)
    second, halves, conv, stats = conv1_call(lens, flat(mixed), first, g_b, vecs)
    stats = reduce_sum(stats, 3)
    grads = {}
    result, d3, d_yhat, sums, small_m, grads["f2i"], grads["f2o"], grads["co"] = middle_call(
        lens, second, conv, cot, stats, g_b, vecs
    )
    sums = reduce_sum(sums, 4)
    d2, d_mixed, small_c, grads["ci"], grads["out"] = conv2_call(
        lens, d_yhat, conv, d3, halves, second, flat(mixed), stats, sums, g_b, vecs
    )
    if mine_mesh:
        dq, dk, dv, dpos, asums, own_b = attn_bwd_call(
            *heads, mixed, lse, utt(d_mixed), [grads[name] for name in names_b], 5
        )
        d0, own_a, ext = last_call(
            flat(dq), flat(dk), flat(dv), first, x, d2, z1, table, dpos, asums, g_a, vecs,
            (small_m, small_c), 6,
        )
        outs = finish_call(own_a, own_b, ext, rows)
    else:
        dq, dk, dv, dpos, asums = attn_bwd_call(*heads, mixed, lse, utt(d_mixed))
        d0, small_l, grads["qkv"], grads["f1i"], grads["f1o"], grads["pos"] = last_call(
            flat(dq), flat(dk), flat(dv), first, x, d2, z1, table, dpos, asums, g_a, vecs
        )
        o, small_outs = scatter_plain(
            grads, kinds, names_a + names_b, small_m + small_c + small_l, small_ins, both, n_dp
        )
        outs = (
            o["f1i"], o["f1o"], small_outs[0], o["qkv"].reshape(qkv_weight.shape), o["pos"],
            o["out"], small_outs[1], o["ci"].reshape(conv_in.shape), o["co"], small_outs[2],
            o["f2i"], o["f2o"], small_outs[3], small_outs[4],
        )
    return (result.reshape(frames.shape), d0.reshape(frames.shape)) + tuple(outs)


def solution(mesh):
    in_specs = (
        P(None, ("dp", "tensor"), None, None),
        P(None, "dp"),
        P("dp", "tensor"),
        P("tensor", "dp"),
        P("tensor", "dp"),
        P("dp", None, "tensor"),
        P("dp", "tensor"),
        P("tensor", "dp"),
        P(None, "tensor", "dp"),
        P("dp", None, "tensor"),
        P("tensor", "dp"),
        P(None, "tensor", "dp"),
        P("dp", "tensor"),
        P("tensor", "dp"),
        P("tensor", "dp"),
        P(None, ("dp", "tensor")),
        P(None, ("dp", "tensor"), None, None),
    )
    out_specs = (
        P(None, ("dp", "tensor"), None, None),
        P(None, ("dp", "tensor"), None, None),
        P("dp", "tensor"),
        P("tensor", "dp"),
        P("tensor", "dp"),
        P("dp", None, "tensor"),
        P("dp", "tensor"),
        P("tensor", "dp"),
        P(None, "tensor", "dp"),
        P("dp", None, "tensor"),
        P("tensor", "dp"),
        P(None, "tensor", "dp"),
        P("dp", "tensor"),
        P("tensor", "dp"),
        P("tensor", "dp"),
        P(None, ("dp", "tensor")),
    )
    return jax.shard_map(local, mesh=mesh, in_specs=in_specs, out_specs=out_specs, check_vma=False)
```

```python
import math

import jax
import jax.numpy as jnp
from jax import lax
from jax.experimental import pallas as pl
from jax.experimental.pallas import tpu as pltpu
from jax.sharding import PartitionSpec as P

DK = 64
norm_eps = 1e-05
mask_fill = -1000000000.0
BF = jnp.bfloat16
F32 = jnp.float32
BLK = 128


def nn(a, b):
    return lax.dot_general(a, b, (((1,), (0,)), ((), ())), preferred_element_type=F32)


def nt(a, b):
    return lax.dot_general(a, b, (((1,), (1,)), ((), ())), preferred_element_type=F32)


def tn(a, b):
    return lax.dot_general(a, b, (((0,), (0,)), ((), ())), preferred_element_type=F32)


def attn_fwd_kernel(len_ref, qu, qv, k, v, pos, o_ref, lse_ref, u=None, hook=None):
    count = len_ref[pl.program_id(0) if u is None else u]
    full = k.shape[1]
    lane = lax.broadcasted_iota(jnp.int32, (BLK, 2 * DK), 1)
    col = lax.broadcasted_iota(jnp.int32, (BLK, full), 1)
    keep = col < count
    zero = jnp.zeros((), BF)
    for blk in range(full // BLK):
        i0 = blk * BLK
        base = full - BLK - i0
        if hook is not None:
            hook(blk)
        outs, logs = [], []
        for h in range(2):
            mine = (lane < DK) if h == 0 else (lane >= DK)
            q_u = jnp.where(mine, qu[0, i0 : i0 + BLK, :], zero)
            q_v = jnp.where(mine, qv[0, i0 : i0 + BLK, :], zero)
            rel = nt(q_v, pos[base : base + full + BLK, :])
            rel = pltpu.roll(rel, full + 1, 1, stride=1, stride_axis=0)[:, :full]
            s = (nt(q_u, k[0]) + rel) * (1.0 / math.sqrt(DK))
            s = jnp.where(keep, s, mask_fill)
            top = jnp.max(s, axis=1, keepdims=True)
            e = jnp.exp(s - top)
            total = jnp.sum(e, axis=1, keepdims=True)
            outs.append(nn(e.astype(BF), v[0]) / total)
            logs.append(top + jnp.log(total))
        left = lane < DK
        o_ref[0, i0 : i0 + BLK, :] = jnp.where(left, outs[0], outs[1]).astype(BF)
        lse_ref[0, i0 : i0 + BLK, :] = jnp.where(left, logs[0], logs[1])


def attn_bwd_kernel(
    len_ref, qu, qv, k, v, pos, o, lse, do, dq_ref, dk_ref, dv_ref, dpos_ref, sum_ref, dkt, dvt, dpt,
    hook=None,
):
    count = len_ref[pl.program_id(0)]
    full = k.shape[1]
    scale = 1.0 / math.sqrt(DK)
    lane = lax.broadcasted_iota(jnp.int32, (BLK, 2 * DK), 1)
    left = lane < DK
    keep = lax.broadcasted_iota(jnp.int32, (BLK, full), 1) < count
    zero = jnp.zeros((), BF)
    flip = (lane + lax.broadcasted_iota(jnp.int32, (BLK, 2 * DK), 0) == BLK - 1).astype(F32).astype(BF)
    dkt[...] = jnp.zeros_like(dkt)
    dvt[...] = jnp.zeros_like(dvt)
    dpt[...] = jnp.zeros_like(dpt)
    sum_q = jnp.zeros((1, 2 * DK), F32)
    sum_u = jnp.zeros((1, 2 * DK), F32)
    sum_v = jnp.zeros((1, 2 * DK), F32)
    for blk in range(full // BLK):
        i0 = blk * BLK
        base = full - BLK - i0
        rows = slice(i0, i0 + BLK)
        win = slice(base, base + full + BLK)
        if hook is not None:
            hook(blk)
        qu_t = qu[0, rows, :].astype(F32).T.astype(BF)
        do_t = do[0, rows, :].astype(F32).T.astype(BF)
        qv_t = tn(qv[0, rows, :], flip).astype(BF)
        dot_o = do[0, rows, :].astype(F32) * o[0, rows, :].astype(F32)
        parts_u, parts_v = [], []
        for h in range(2):
            mine = left if h == 0 else lane >= DK
            hs = slice(h * DK, h * DK + DK)
            q_u = jnp.where(mine, qu[0, rows, :], zero)
            q_v = jnp.where(mine, qv[0, rows, :], zero)
            d_o = jnp.where(mine, do[0, rows, :], zero)
            rel = nt(q_v, pos[win, :])
            rel = pltpu.roll(rel, full + 1, 1, stride=1, stride_axis=0)[:, :full]
            s = (nt(q_u, k[0]) + rel) * scale - lse[0, rows, h * DK : h * DK + 1]
            p = jnp.where(keep, jnp.exp(jnp.minimum(s, 0.0)), 0.0)
            delta = jnp.sum(jnp.where(mine, dot_o, 0.0), axis=1, keepdims=True)
            ds = (p * (nt(d_o, v[0]) - delta)).astype(BF)
            dvt[hs, :] += nn(do_t[hs, :], p.astype(BF))
            dkt[hs, :] += nn(qu_t[hs, :], ds)
            parts_u.append(nn(ds, k[0]))
            wide = jnp.concatenate([nn(flip, ds), jnp.zeros((BLK, BLK), F32)], axis=1)
            wide = pltpu.roll(wide, 0, 1, stride=1, stride_axis=0).astype(BF)
            parts_v.append(nn(wide, pos[win, :]))
            dpt[hs, win] += nn(qv_t[hs, :], wide)
        d_u = jnp.where(left, parts_u[0], parts_u[1]) * scale
        d_v = jnp.where(left, parts_v[0], parts_v[1]) * scale
        high = d_v.astype(BF)
        low = (d_v - high.astype(F32)).astype(BF)
        d_q = (d_u + nn(flip, high) + nn(flip, low)).astype(BF)
        dq_ref[0, rows, :] = d_q
        sum_q += jnp.sum(d_q.astype(F32), axis=0, keepdims=True)
        sum_u += jnp.sum(d_u, axis=0, keepdims=True)
        sum_v += jnp.sum(d_v, axis=0, keepdims=True)
    dk_ref[0] = (dkt[...].T * scale).astype(BF)
    d_val = dvt[...].T.astype(BF)
    dv_ref[0] = d_val
    dpos_ref[0] = (dpt[...].T * scale).astype(BF)
    sum_ref[0, 0:1, :] = sum_q
    sum_ref[0, 1:2, :] = jnp.sum(d_val.astype(F32), axis=0, keepdims=True)
    sum_ref[0, 2:3, :] = sum_u
    sum_ref[0, 3:4, :] = sum_v
    sum_ref[0, 4:8, :] = jnp.zeros((4, 2 * DK), F32)


def attn_specs(rows, full, width):
    pairs = width // (2 * DK)
    main = pl.BlockSpec((1, full, 2 * DK), lambda u, p, n: (u, 0, p))
    pos = pl.BlockSpec((2 * full, 2 * DK), lambda u, p, n: (0, p))
    return (rows, pairs), main, pos


def attn_fwd_call(lens, qu, qv, k, v, pos):
    rows, full, width = qu.shape
    grid, main, pspec = attn_specs(rows, full, width)
    return pl.pallas_call(
        attn_fwd_kernel,
        grid_spec=pltpu.PrefetchScalarGridSpec(
            num_scalar_prefetch=1,
            grid=grid,
            in_specs=[main] * 4 + [pspec],
            out_specs=[main, main],
        ),
        out_shape=[
            jax.ShapeDtypeStruct((rows, full, width), BF),
            jax.ShapeDtypeStruct((rows, full, width), F32),
        ],
        compiler_params=dense_params(),
        name="attn_fwd",
    )(lens, qu, qv, k, v, pos)


def attn_bwd_call(lens, qu, qv, k, v, pos, o, lse, do, early=None, cid=None):
    rows, full, width = qu.shape
    grid, main, pspec = attn_specs(rows, full, width)
    args = [lens, qu, qv, k, v, pos, o, lse, do]
    in_specs = [main] * 4 + [pspec] + [main] * 3
    out_specs = [
        main,
        main,
        main,
        pl.BlockSpec((1, 2 * full, 2 * DK), lambda u, p, n: (u, 0, p)),
        pl.BlockSpec((1, 8, 2 * DK), lambda u, p, n: (u, 0, p)),
    ]
    scratch = [
        pltpu.VMEM((2 * DK, full), F32),
        pltpu.VMEM((2 * DK, full), F32),
        pltpu.VMEM((2 * DK, 2 * full), F32),
    ]
    out_shape = [jax.ShapeDtypeStruct((rows, full, width), BF)] * 3 + [
        jax.ShapeDtypeStruct((rows, 2 * full, width), BF),
        jax.ShapeDtypeStruct((rows, 8, width), F32),
    ]
    body, params = attn_bwd_kernel, dense_params()
    if early is not None:
        items = [split_owners(item) for item in early]
        pieces = pieces_of([item.shape[-1] for item in items])
        owned = items[0].shape[-2]
        n_in, n_out, m = len(args) - 1, len(out_shape), len(items)
        scratch += [pltpu.VMEM(item.shape, item.dtype) for item in args[1:]]
        scratch += [pltpu.SemaphoreType.DMA((grid[0] * grid[1], n_in))]
        args += items
        in_specs = [ANY] * (n_in + m)
        out_specs.append(pl.BlockSpec((owned, C_B), lambda u, p, n: (0, 0)))
        out_shape.append(jax.ShapeDtypeStruct((owned, C_B), F32))
        scratch += scatter_scratch(pieces, owned)
        params = comm_params(cid)

        def body(*refs):
            at = pl.program_id(0) * grid[1] + pl.program_id(1)
            last = grid[0] * grid[1] - 1
            ins, rest = refs[: 1 + n_in], refs[1 + n_in :]
            g_refs, rest = rest[:m], rest[m:]
            mains, o_ref, rest = rest[:n_out], rest[n_out], rest[n_out + 1 :]
            own, held, here_sem, sems = rest[:3], rest[3 : 3 + n_in], rest[3 + n_in], rest[4 + n_in :]
            start, advance, finish, rounds = scatter_steps(pieces, g_refs, o_ref, sems, 2)

            def cut(ref, u, p):
                c = pl.ds(p * 2 * DK if isinstance(p, int) else pl.multiple_of(p * 2 * DK, 2 * DK), 2 * DK)
                return ref.at[:, c] if len(ref.shape) == 2 else ref.at[pl.ds(u, 1), :, c]

            def fetch(k, u, p, n):
                return pltpu.make_async_copy(
                    cut(ins[1 + k], u, p), cut(held[k], u, p), here_sem.at[n, k]
                )

            @pl.when(at == 0)
            def _():
                for u in range(grid[0]):
                    for p in range(grid[1]):
                        for k in range(n_in):
                            if u == 0 or len(held[k].shape) == 3:
                                fetch(k, u, p, u * grid[1] + p).start()

            u, p = pl.program_id(0), pl.program_id(1)
            for k in range(n_in):
                if len(held[k].shape) == 3:
                    fetch(k, u, p, at).wait()
                else:

                    @pl.when(u == 0)
                    def _(k=k):
                        fetch(k, u, p, at).wait()

            ins = ins[:1] + tuple(cut(ref, u, p) for ref in held)

            def begin():
                greet(link_peers(*place()))
                for p in range(len(pieces)):
                    start(p)

            steps = [begin] + [lambda q=q: advance(q) for q in range(rounds)]
            attn_bwd_kernel(*ins, *mains, *own, hook=hooks_of(steps, at, last, full // BLK))

            @pl.when(at == last)
            def _():
                finish()

    return pl.pallas_call(
        body,
        grid_spec=pltpu.PrefetchScalarGridSpec(
            num_scalar_prefetch=1,
            grid=grid,
            in_specs=in_specs,
            out_specs=out_specs,
            scratch_shapes=scratch,
        ),
        out_shape=out_shape,
        compiler_params=params,
        name="attn_bwd",
    )(*args)


def hooks_of(steps, at, last, spots):
    def hook(blk):
        for i, step in enumerate(steps):
            where, spot = divmod(i * (last + 1) * spots // len(steps), spots)
            if spot == blk:

                @pl.when(at == where)
                def _(step=step):
                    step()

    return hook


MESH = pl.DeviceIdType.MESH
NZ, NY, NX = 4, 2, 2
ANY = pl.BlockSpec(memory_space=pl.ANY)
VM = pl.BlockSpec(memory_space=pltpu.VMEM)


def own_mesh(sizes):
    return sizes == (NZ * NY * NX, 2)


def place():
    dp = lax.axis_index("dp")
    return dp // (NY * NX), dp // NX % NY, dp % NX, lax.axis_index("tensor")


def dev(z, y, x, t):
    return (z * (NY * NX) + y * NX + x, t)


def greet(peers):
    barrier = pltpu.get_barrier_semaphore()
    for peer in peers:
        pl.semaphore_signal(barrier, inc=1, device_id=peer, device_id_type=MESH)
    pl.semaphore_wait(barrier, len(peers))


def rcopy(src, dst, send, recv, peer):
    return pltpu.make_async_remote_copy(
        src_ref=src, dst_ref=dst, send_sem=send, recv_sem=recv, device_id=peer, device_id_type=MESH
    )


def link_peers(z, y, x, t):
    peers = [dev(lax.rem(z + d, NZ), y, x, t) for d in range(1, NZ)]
    return peers + [dev(z, 1 - y, x, t), dev(z, y, 1 - x, t), dev(z, y, x, 1 - t)]


def sum_scratch(shape):
    dma = pltpu.SemaphoreType.DMA
    return [
        pltpu.VMEM(shape, F32), pltpu.VMEM(shape, F32), pltpu.VMEM((3,) + shape, F32),
        pltpu.VMEM((7,) + shape, F32), dma((3,)), dma((3,)), dma((7,)), dma((7,)),
    ]


def sum_steps(scratch):
    x_s, mid, b1, b2, s1, r1, s2, r2 = scratch
    z, y, x, t = place()
    spot = (y * NX + x) * 2 + t
    zs = [dev(lax.rem(z + d, NZ), y, x, t) for d in range(1, NZ)]
    flat = [lax.rem(spot + d, 8) for d in range(1, 8)]
    plane = [dev(z, p // 4, p // 2 % 2, p % 2) for p in flat]

    def call():
        barrier = pltpu.get_barrier_semaphore()
        for peer in zs + plane:
            pl.semaphore_signal(barrier, inc=1, device_id=peer, device_id_type=MESH)

    def meet(o_ref):
        pl.semaphore_wait(pltpu.get_barrier_semaphore(), len(zs + plane))
        first = [rcopy(x_s, b1.at[i], s1.at[i], r1.at[i], peer) for i, peer in enumerate(zs)]
        for copy in first:
            copy.start()
        for copy in first:
            copy.wait_recv()
        mid[...] = (x_s[...] + b1[0]) + (b1[1] + b1[2])
        second = [rcopy(mid, b2.at[i], s2.at[i], r2.at[i], peer) for i, peer in enumerate(plane)]
        for copy in second:
            copy.start()
        for copy in second:
            copy.wait_recv()
        total = mid[...]
        for i in range(7):
            total = total + b2[i]
        o_ref[...] = total
        for copy in first + second:
            copy.wait_send()

    return call, meet


def comm_params(cid):
    return pltpu.CompilerParams(
        collective_id=cid, has_side_effects=True, vmem_limit_bytes=60 * 1024 * 1024
    )


def gathered_shape(packed):
    return jax.ShapeDtypeStruct((2, NZ, NY, NX) + packed.shape, packed.dtype)


def gather_scratch(n):
    dma = pltpu.SemaphoreType.DMA
    return [dma((n, NZ - 1)), dma((n, NZ - 1))] + [dma((n,))] * 6 + [dma((2,))]


LEAD = 2


def gather_events(pieces, xs, gs, sems):
    zs, zr, as_, ar, bs, br, cs, cr, own_sem = sems
    z, y, x, t = place()
    along_x, along_y = dev(z, y, 1 - x, t), dev(z, 1 - y, x, t)
    zc, ac, bc, cc = [], [], [], []
    for p, (i, start, w) in enumerate(pieces):
        c = pl.ds(start, w)
        g = gs[i]
        zc.append(
            [
                rcopy(
                    xs[i].at[:, c],
                    g.at[t, z, y, x, :, c],
                    zs.at[p, d - 1],
                    zr.at[p, d - 1],
                    dev(lax.rem(z + d, NZ), y, x, t),
                )
                for d in range(1, NZ)
            ]
        )
        line = g.at[t, :, y, x, :, c]
        ac.append(rcopy(line, line, as_.at[p], ar.at[p], along_x if p % 2 == 0 else along_y))
        half = g.at[t, :, y, :, :, c] if p % 2 == 0 else g.at[t, :, :, x, :, c]
        bc.append(rcopy(half, half, bs.at[p], br.at[p], along_y if p % 2 == 0 else along_x))
        full = g.at[t, :, :, :, :, c]
        cc.append(rcopy(full, full, cs.at[p], cr.at[p], dev(z, y, x, 1 - t)))

    def begin():
        own = [
            pltpu.make_async_copy(item, g.at[t, z, y, x], own_sem.at[i])
            for i, (item, g) in enumerate(zip(xs, gs))
        ]
        for copy in own:
            copy.start()
        for copies in zc[: 2 * LEAD]:
            for copy in copies:
                copy.start()
        for copy in own:
            copy.wait()

    def event(kind, q):
        for p in (2 * q, 2 * q + 1):
            if kind == "z":
                for copy in zc[p]:
                    copy.wait_recv()
                ac[p].start()
                for copy in zc[p + 2 * LEAD] if p + 2 * LEAD < len(pieces) else []:
                    copy.start()
            elif kind == "a":
                ac[p].wait_recv()
                bc[p].start()
            elif kind == "b":
                bc[p].wait_recv()
                cc[p].start()
            else:
                cc[p].wait_recv()

    def finish():
        for copy in sum(zc, []) + ac + bc + cc:
            copy.wait_send()

    return begin, event, finish


def gather_order(pieces):
    unit = [0.42 * (pieces[2 * q][2] + pieces[2 * q + 1][2]) / 512 for q in range(len(pieces) // 2)]
    order, at = [], 3.0
    waiting = []
    for q, step in enumerate(unit):
        at += 8 * step
        waiting.append((at + 2.5, q, "z"))
    free = 0.0
    while waiting:
        waiting.sort()
        now, q, kind = waiting.pop(0)
        order.append((now, kind, q))
        if kind in "za":
            free = max(free, now) + (4 if kind == "z" else 8) * unit[q]
            waiting.append((free + 2.5, q, "a" if kind == "z" else "b"))
        elif kind == "b":
            waiting.append((now + 1.8, q, "c"))
    return order


def small_steps(s_ref, v_ref, mid, b1, b2, s1, r1, s2, r2):
    z, y, x, t = place()
    spot = (y * NX + x) * 2 + t
    zs = [dev(lax.rem(z + d, NZ), y, x, t) for d in range(1, NZ)]
    flat = [lax.rem(spot + d, 8) for d in range(1, 8)]
    plane = [dev(z, p // 4, p // 2 % 2, p % 2) for p in flat]
    first = [rcopy(s_ref, b1.at[i], s1.at[i], r1.at[i], peer) for i, peer in enumerate(zs)]
    second = [rcopy(mid, b2.at[i], s2.at[i], r2.at[i], peer) for i, peer in enumerate(plane)]

    def begin():
        for copy in first:
            copy.start()

    def spread():
        for copy in first:
            copy.wait_recv()
        mid[...] = (s_ref[...] + b1[0]) + (b1[1] + b1[2])
        for copy in second:
            copy.start()

    def finish():
        for copy in second:
            copy.wait_recv()
        same, other = mid[...].astype(F32), b2[0].astype(F32)
        for i in range(1, 7):
            if i % 2 == 1:
                same = same + b2[i].astype(F32)
            else:
                other = other + b2[i].astype(F32)
        low = jnp.where(t == 0, same, other)
        high = jnp.where(t == 0, other, same)
        v_ref[...] = jnp.zeros_like(v_ref)
        for q in range(4):
            r = S_NORM + 14 * q
            v_ref[0:14, 128 * q : 128 * q + 128] = low[r : r + 14] + high[r : r + 14]
        for i, part in enumerate((low, high)):
            for q in range(2):
                c = slice((2 * i + q) * 128, (2 * i + q) * 128 + 128)
                v_ref[R_ATT:R_CV, c] = part[S_ATT + 4 * q : S_ATT + 4 * q + 4]
                v_ref[R_CV:R_B1, c] = part[S_CV + 13 * q : S_CV + 13 * q + 13]
            for q in range(8):
                r, c = 2 * i + q // 4, slice(q % 4 * 128, q % 4 * 128 + 128)
                v_ref[R_B1 + r : R_B1 + r + 1, c] = part[S_B1 + q : S_B1 + q + 1]
                v_ref[R_B2 + r : R_B2 + r + 1, c] = part[S_B2 + q : S_B2 + q + 1]
        for copy in first + second:
            copy.wait_send()

    return plane, begin, spread, finish


S_B1, S_ATT, S_CV, S_B2, S_NORM, S_ALL = 0, 8, 16, 42, 50, 112


def lanes_of(n, offset):
    at = lax.broadcasted_iota(jnp.int32, (n, 128), 0) + offset
    return (lax.broadcasted_iota(jnp.int32, (n, 128), 1) == at).astype(F32)


def prep_kernel(
    f1i, f1o, pos, qkv, f2i, f2o, ci, out, co, b1, att, cv, b2, norm,
    pa_ref, pb_ref, slab_ref, table_ref, slab,
):
    def put(ref, name, value, shift=0):
        start = SEG[name][0] + shift
        ref[:, start : start + value.shape[1]] = value

    for ref, name, item in (
        (pa_ref, "f1i", f1i), (pa_ref, "f1o", f1o), (pa_ref, "pos", pos), (pb_ref, "f2i", f2i),
        (pb_ref, "f2o", f2o), (pb_ref, "out", out), (pb_ref, "co", co),
    ):
        put(ref, name, item[...])
    for k in range(3):
        put(pa_ref, "qkv", qkv[k], k * qkv.shape[2])
    for k in range(2):
        put(pb_ref, "ci", ci[:, k, :], k * ci.shape[2])
    z, y, x, t = place()
    dp = z * (NY * NX) + y * NX + x
    sel = lanes_of(8, dp * 8).astype(BF)
    slab[...] = jnp.zeros_like(slab)
    slab[S_B1 : S_B1 + 8] = nn(b1[...], sel)
    for q in range(2):
        slab[S_ATT + 4 * q : S_ATT + 4 * q + 4] = nn(att[:, q, :], sel)
        slab[S_CV + 13 * q : S_CV + 13 * q + 13] = tn(cv[q], sel)
    slab[S_B2 : S_B2 + 8] = nn(b2[...], sel)
    at = dp * 2 + t
    here = nn(norm[...], lanes_of(16, lax.rem(at, 8) * 16).astype(BF))
    for q in range(4):
        slab[S_NORM + 14 * q : S_NORM + 14 * q + 14] = here * (at // 8 == q).astype(F32)
    slab_ref[...] = slab[...].astype(BF)
    fill_table(table_ref)


def prep_call(items, smalls, full, width):
    rows = items[0].shape[0]
    return pl.pallas_call(
        prep_kernel,
        in_specs=[VM] * 14,
        out_specs=[VM] * 4,
        out_shape=[
            jax.ShapeDtypeStruct((rows, C_A), BF),
            jax.ShapeDtypeStruct((rows, C_B), BF),
            jax.ShapeDtypeStruct((S_ALL, 128), BF),
            jax.ShapeDtypeStruct((2 * full, width), BF),
        ],
        scratch_shapes=[pltpu.VMEM((S_ALL, 128), F32)],
        name="prepare",
    )(*items, *smalls)


def split_owners(item):
    return item.reshape(2, NZ, NY, NX, item.shape[1] // (NZ * NY * NX), item.shape[2])


def pieces_of(widths, step=256):
    pieces, at = [], 0
    for i, w in enumerate(widths):
        pieces += [(i, k, min(step, w), at + k) for k in range(0, w, step)]
        at += w
    return pieces


def scatter_scratch(pieces, rows):
    n = len(pieces)
    total = sum(piece[2] for piece in pieces)
    dma = pltpu.SemaphoreType.DMA
    shape = (rows, total)
    return [
        pltpu.VMEM((NZ, NY, NX) + shape, BF),
        pltpu.VMEM((NZ, NY, NX) + shape, BF),
        pltpu.VMEM((NZ, 2) + shape, BF),
        pltpu.VMEM((NZ,) + shape, BF),
        pltpu.VMEM((NZ - 1,) + shape, BF),
    ] + [dma((n,))] * 7 + [dma((n, NZ - 1))] * 2


def scatter_steps(pieces, g_refs, o_ref, scratch, lag):
    own, rc, ra, rb, rz, lsem, cs, cr, as_, ar, bs, br, zs, zr = scratch
    z, y, x, t = place()
    along_x, along_y = dev(z, y, 1 - x, t), dev(z, 1 - y, x, t)
    mate = dev(z, y, x, 1 - t)
    count = len(pieces)
    bufs, lc, cc, ac, bc, zc = [], [], [], [], [], []
    for p, (i, start, w, at) in enumerate(pieces):
        c = pl.ds(at, w)
        g = pl.ds(start, w)
        b = dict(
            own=own.at[:, :, :, :, c], rc=rc.at[:, :, :, :, c], ra=ra.at[:, :, :, c],
            rb=rb.at[:, :, c], rz=rz.at[:, :, c],
        )
        bufs.append(b)
        even = p % 2 == 0
        lc.append(
            pltpu.make_async_copy(g_refs[i].at[t, :, :, :, :, g], b["own"], lsem.at[p])
        )
        cc.append(rcopy(g_refs[i].at[1 - t, :, :, :, :, g], b["rc"], cs.at[p], cr.at[p], mate))
        away = b["own"].at[:, 1 - y] if even else b["own"].at[:, :, 1 - x]
        ac.append(rcopy(away, b["ra"], as_.at[p], ar.at[p], along_y if even else along_x))
        line = b["own"].at[:, y, 1 - x] if even else b["own"].at[:, 1 - y, x]
        bc.append(rcopy(line, b["rb"], bs.at[p], br.at[p], along_x if even else along_y))
        zc.append([])
        for d in range(1, NZ):
            far = lax.rem(z + d, NZ)
            zc[p].append(
                rcopy(
                    b["own"].at[far, y, x], b["rz"].at[d - 1], zs.at[p, d - 1], zr.at[p, d - 1],
                    dev(far, y, x, t),
                )
            )

    def start(p):
        lc[p].start()
        cc[p].start()

    def advance(q):
        if q < count:
            lc[q].wait()
            cc[q].wait_recv()
            b = bufs[q]
            for i in range(NZ):
                b["own"][i] = b["own"][i] + b["rc"][i]
            ac[q].start()
        p = q - lag
        if 0 <= p < count:
            ac[p].wait_recv()
            b = bufs[p]
            for i in range(NZ):
                if p % 2 == 0:
                    b["own"][i, y] = b["own"][i, y] + b["ra"][i]
                else:
                    b["own"][i, :, x] = b["own"][i, :, x] + b["ra"][i]
            bc[p].start()
        p = q - 2 * lag
        if 0 <= p < count:
            bc[p].wait_recv()
            b = bufs[p]
            for i in range(NZ):
                b["own"][i, y, x] = b["own"][i, y, x] + b["rb"][i]
            for copy in zc[p]:
                copy.start()
        p = q - 3 * lag
        if 0 <= p < count:
            for copy in zc[p]:
                copy.wait_recv()
            b = bufs[p]
            total = b["own"][z, y, x].astype(F32)
            for d in range(NZ - 1):
                total = total + b["rz"][d].astype(F32)
            o_ref[:, pieces[p][3] : pieces[p][3] + pieces[p][2]] = total

    def finish():
        for copy in cc + ac + bc + sum(zc, []):
            copy.wait_send()

    return start, advance, finish, count + 3 * lag


def small_sum_steps(parts, ext, scratch):
    acc_s, bc_, bz, bp, bm, sc, rc, sz, rz, sp, rp, sm, rm = scratch
    z, y, x, t = place()
    dp = z * (NY * NX) + y * NX + x
    half = acc_s.shape[0] // 2
    mine = pl.ds(pl.multiple_of(t * half, 8), half)
    mate = dev(z, y, x, 1 - t)
    spot = y * NX + x
    zp = [dev(lax.rem(z + d, NZ), y, x, t) for d in range(1, NZ)]
    flat = [lax.rem(spot + d, 4) for d in range(1, 4)]
    pp = [dev(z, p // 2, p % 2, t) for p in flat]
    one = rcopy(acc_s, bc_, sc, rc, mate)
    two = [rcopy(acc_s.at[mine], bz.at[i], sz.at[i], rz.at[i], peer) for i, peer in enumerate(zp)]
    three = [rcopy(bz.at[3], bp.at[i], sp.at[i], rp.at[i], peer) for i, peer in enumerate(pp)]
    four = rcopy(bp.at[3], bm, sm, rm, mate)

    def a():
        acc_s[...] = jnp.zeros_like(acc_s)
        total = parts[0][...]
        for part in parts[1:]:
            total = total + part[...]
        acc_s[0:R_ALL] = total
        one.start()

    def b():
        one.wait()
        acc_s[...] = acc_s[...] + bc_[...]
        for copy in two:
            copy.start()

    def c():
        for copy in two:
            copy.wait()
        bz[3] = (acc_s[mine] + bz[0]) + (bz[1] + bz[2])
        for copy in three:
            copy.start()

    def d():
        for copy in three:
            copy.wait()
        bp[3] = (bz[3] + bp[0]) + (bp[1] + bp[2])
        four.start()
        ext[mine] = bp[3]

    def e():
        four.wait()
        ext[pl.ds(pl.multiple_of((1 - t) * half, 8), half)] = bm[...]

    return pp, [a, b, c, d, e]


def small_sum_scratch(width):
    dma = pltpu.SemaphoreType.DMA
    return [
        pltpu.VMEM((R_SUM, width), F32), pltpu.VMEM((R_SUM, width), F32),
        pltpu.VMEM((4, R_SUM // 2, width), F32), pltpu.VMEM((4, R_SUM // 2, width), F32),
        pltpu.VMEM((R_SUM // 2, width), F32), dma, dma, dma((3,)), dma((3,)), dma((3,)), dma((3,)), dma, dma,
    ]


def finish_kernel(
    oa, ob, ext, f1i, f1o, b1, qkv, pos, out, att, ci, co, cv, f2i, f2o, b2, norm
):
    def take(ref, name):
        start, w = SEG[name]
        return ref[:, start : start + w]

    f1i[...] = take(oa, "f1i")
    f1o[...] = take(oa, "f1o")
    pos[...] = take(oa, "pos")
    f2i[...] = take(ob, "f2i")
    f2o[...] = take(ob, "f2o")
    out[...] = take(ob, "out")
    co[...] = take(ob, "co")
    for ref, src, name in ((qkv, oa, "qkv"), (ci, ob, "ci")):
        start, w = SEG[name]
        n = 3 if name == "qkv" else 2
        for k in range(n):
            part = src[:, start + k * w // n : start + (k + 1) * w // n]
            if name == "qkv":
                ref[k] = part
            else:
                ref[:, k, :] = part
    z, y, x, t = place()
    dp = z * (NY * NX) + y * NX + x
    sel = lanes_of(8, dp * 8)

    def own(v, pick):
        return lax.dot_general(
            v, pick, (((1,), (1,)), ((), ())), precision=lax.Precision.HIGHEST,
            preferred_element_type=F32,
        )

    for q in range(2):
        c = pl.ds(pl.multiple_of((2 * t + q) * 128, 128), 128)
        att[:, q, :] = own(ext[R_ATT:R_CV, c], sel)
        cv[q] = own(sel, ext[R_CV:R_B1, c])
    for o, at in ((b1, R_B1), (b2, R_B2)):
        for q in range(8):
            r, c = at + q // 4, slice(q % 4 * 128, q % 4 * 128 + 128)
            line = jnp.where(t == 0, ext[r : r + 1, c], ext[r + 2 : r + 3, c])
            o[q : q + 1, :] = own(line, sel)
    at = dp * 2 + t
    lane = pl.ds(pl.multiple_of(at // 8 * 128, 128), 128)
    norm[...] = own(ext[0:14, lane], lanes_of(16, lax.rem(at, 8) * 16))


def finish_call(oa, ob, ext, rows):
    shapes = [
        (rows, 1024), (rows, 1024), (8, 8), (3, rows, 256), (rows, 256), (rows, 256), (4, 2, 8),
        (rows, 2, 256), (rows, 256), (2, 8, 13), (rows, 1024), (rows, 1024), (8, 8), (14, 16),
    ]
    f1i, f1o, b1, qkv, pos, out, att, ci, co, cv, f2i, f2o, b2, norm = pl.pallas_call(
        finish_kernel,
        in_specs=[VM] * 3,
        out_specs=[VM] * 14,
        out_shape=[jax.ShapeDtypeStruct(shape, F32) for shape in shapes],
        name="own_gradients",
    )(oa, ob, ext)
    return (
        f1i, f1o.T, b1, qkv.transpose(1, 0, 2), pos, out.T, att, ci, co.T, cv.transpose(2, 0, 1),
        f2i, f2o.T, b2, norm,
    )

SEG = {
    "f1i": (0, 1024), "f1o": (1024, 1024), "pos": (2048, 256), "qkv": (2304, 768),
    "f2i": (0, 1024), "f2o": (1024, 1024), "ci": (2048, 512), "out": (2560, 256),
    "co": (2816, 256),
}
C_A, C_B = 3072, 3072
R_ATT, R_CV, R_B1, R_B2, R_ALL, R_SUM = 14, 18, 31, 35, 40, 48
TB = 256
HC = 256


def seg_spec(name, depth):
    start, width = SEG[name]
    return pl.BlockSpec(
        (2, depth, width), lambda i, *_: (0, 0, start // width), pipeline_mode=pl.Buffered(1)
    )


def whole(shape):
    zeros = (0,) * len(shape)
    return pl.BlockSpec(shape, lambda i, *_: zeros)


def tall(rows, width):
    return pl.BlockSpec((rows, width), lambda i, *_: (i, 0))


def sig(v):
    return 0.5 * jnp.tanh(0.5 * v) + 0.5


def row(ref, i):
    return ref[i : i + 1, :]


def col_sum(v):
    return jnp.sum(v, axis=0, keepdims=True)


def ln_stats(v):
    centered = v - jnp.mean(v, axis=1, keepdims=True)
    inv = lax.rsqrt(jnp.mean(centered * centered, axis=1, keepdims=True) + norm_eps)
    return centered * inv, inv


def ln_back(up, scaled, inv, gain):
    g = up * gain
    return inv * (
        g
        - jnp.mean(g, axis=1, keepdims=True)
        - scaled * jnp.mean(g * scaled, axis=1, keepdims=True)
    )


def bias_half(vecs, at, t):
    return jnp.concatenate([row(vecs, at + 2 * t), row(vecs, at + 2 * t + 1)], axis=1)


def row_mask(start, rows, count):
    at = start + lax.broadcasted_iota(jnp.int32, (rows, 1), 0)
    return (at < count).astype(F32)


def ffn1_kernel(
    x_ref, table, w_in, w_out, w_qkv, w_pos, vecs,
    first_ref, z_ref, qu_ref, qv_ref, k_ref, v_ref, pos_ref,
):
    x = x_ref[...].astype(F32)
    scaled, _ = ln_stats(x)
    hn = (scaled * row(vecs, 0) + row(vecs, 1)).astype(BF)
    half = w_in.shape[2]
    y = row(vecs, 2)
    for t in range(2):
        z = nn(hn, w_in[t]) + bias_half(vecs, R_B1, t)
        for j in range(half // HC):
            z_ref[:, (2 * j + t) * HC : (2 * j + t + 1) * HC] = z[:, j * HC : (j + 1) * HC].astype(BF)
        y = y + nt((z * sig(z)).astype(BF), w_out[t])
    first = x + 0.5 * y
    first_ref[...] = first
    scaled, _ = ln_stats(first)
    hn = (scaled * row(vecs, 3) + row(vecs, 4)).astype(BF)
    part = w_qkv.shape[2] // 3
    for t in range(2):
        c = slice(t * part, (t + 1) * part)
        proj = nn(hn, w_qkv[t])
        q = proj[:, :part] + vecs[R_ATT : R_ATT + 1, c]
        qu_ref[:, c] = (q + vecs[R_ATT + 2 : R_ATT + 3, c]).astype(BF)
        qv_ref[:, c] = (q + vecs[R_ATT + 3 : R_ATT + 4, c]).astype(BF)
        k_ref[:, c] = proj[:, part : 2 * part].astype(BF)
        v_ref[:, c] = (proj[:, 2 * part :] + vecs[R_ATT + 1 : R_ATT + 2, c]).astype(BF)
        pos_ref[:, c] = nn(table[...], w_pos[t]).astype(BF)


def dense_params(mib=60):
    return pltpu.CompilerParams(vmem_limit_bytes=mib * 1024 * 1024)


def ffn1_call(x, table, g, vecs):
    tokens, width = x.shape
    steps = tokens // TB
    places = tall(table.shape[0] // steps, width)
    return pl.pallas_call(
        ffn1_kernel,
        grid=(steps,),
        in_specs=[
            tall(TB, width), places, seg_spec("f1i", width), seg_spec("f1o", width),
            seg_spec("qkv", width), seg_spec("pos", width), whole(vecs.shape),
        ],
        out_specs=[tall(TB, width), tall(TB, 4 * width)] + [tall(TB, width)] * 4 + [places],
        out_shape=[
            jax.ShapeDtypeStruct((tokens, width), F32),
            jax.ShapeDtypeStruct((tokens, 4 * width), BF),
        ]
        + [jax.ShapeDtypeStruct((tokens, width), BF)] * 4
        + [jax.ShapeDtypeStruct(table.shape, BF)],
        compiler_params=dense_params(),
        name="ffn1_forward",
    )(x, table, g, g, g, g, vecs)


FRONT_PIECES = (
    [(0, at + 256 * j, 256) for j in range(4) for at in (0, 1024)]
    + [(0, 2048 + 256 * k, 256) for k in range(4)]
    + [(1, 256 * k, 256) for k in (10, 8, 9, 11, 0, 4, 1, 5, 2, 6, 3, 7)]
)


def front_call(lens, x, table, packed_a, packed_b, slab, batch, cid):
    tokens, width = x.shape
    full = tokens // batch
    pairs = width // (2 * DK)
    chunks = SEG["f1i"][1] // HC
    first_head = chunks + 1
    steps = first_head + batch * pairs
    order = gather_order(FRONT_PIECES)
    dma = pltpu.SemaphoreType.DMA
    small = [
        pltpu.VMEM(slab.shape, BF), pltpu.VMEM((3,) + slab.shape, BF),
        pltpu.VMEM((7,) + slab.shape, BF), dma((3,)), dma((3,)), dma((7,)), dma((7,)),
    ]
    heads_shape = (batch, full, width)
    scratch = [
        pltpu.VMEM((2, NZ, NY, NX) + packed_a.shape, BF),
        pltpu.VMEM((tokens, width), F32),
        pltpu.VMEM((tokens, width), BF),
    ]
    scratch += [pltpu.VMEM(heads_shape, BF)] * 5 + [pltpu.VMEM(heads_shape, F32)]
    scratch += [pltpu.VMEM(table.shape, BF), dma((10,))]
    n_own = len(scratch)

    def body(
        len_ref, x_ref, table_ref, xa_ref, xb_ref, s_ref,
        ga_ref, gb_ref, vecs, first_ref, z_ref, qu_ref, qv_ref, k_ref, v_ref, pos_ref, mix_ref,
        lse_ref, *rest,
    ):
        i = pl.program_id(0)
        ga, y_s, hn_s, qu, qv, k, v, mix, lse, pos, out_sem = rest[:n_own]
        smalls = rest[n_own : n_own + len(small)]
        begin, event, finish = gather_events(
            FRONT_PIECES, (xa_ref, xb_ref), (ga, gb_ref), rest[n_own + len(small) :]
        )
        plane, s_begin, s_spread, s_finish = small_steps(s_ref, vecs, *smalls)
        z, y, xx, t = place()
        sources = (ga, y_s, qu, qv, k, v, pos, mix, lse)
        targets = (ga_ref, first_ref, qu_ref, qv_ref, k_ref, v_ref, pos_ref, mix_ref, lse_ref)
        copies = [
            pltpu.make_async_copy(a, b, out_sem.at[n])
            for n, (a, b) in enumerate(zip(sources, targets))
        ]
        done = [0]

        def until(q):
            while True:
                _, kind, pair = order[done[0]]
                done[0] += 1
                event(kind, pair)
                if (kind, pair) == ("c", q):
                    break

        def weight(t, start, w):
            return ga[t, :, :, :, :, start : start + w].reshape(width, w)

        @pl.when(i == 0)
        def _():
            greet([dev(lax.rem(z + d, NZ), y, xx, t) for d in range(1, NZ)] + plane)
            begin()
            s_begin()
            for n in range(4):
                event(*order[n][1:])
            s_spread()
            for n in range(4, 7):
                event(*order[n][1:])
            done[0] = 7
            s_finish()

            @pl.loop(0, tokens // TB)
            def _(r):
                here = pl.ds(pl.multiple_of(r * TB, TB), TB)
                scaled, _ = ln_stats(x_ref[here, :].astype(F32))
                hn_s[here, :] = (scaled * row(vecs, 0) + row(vecs, 1)).astype(BF)
                y_s[here, :] = jnp.zeros((TB, width), F32) + row(vecs, 2)

        for j in range(chunks):

            @pl.when(i == j)
            def _(j=j):
                until(j)

        @pl.when(i < chunks)
        def _():
            at = pl.multiple_of(i * HC, HC)
            odd = lax.rem(i, 2) == 1
            for t in range(2):
                w_in = ga[t, :, :, :, :, pl.ds(at, HC)].reshape(width, HC)
                w_out = ga[t, :, :, :, :, pl.ds(1024 + at, HC)].reshape(width, HC)
                line = vecs[pl.ds(R_B1 + 2 * t + i // 2, 1), :]
                bias = jnp.where(odd, line[:, HC:], line[:, :HC])
                for k in range(tokens // TB):
                    here = slice(k * TB, (k + 1) * TB)
                    zf = nn(hn_s[here, :], w_in) + bias
                    z_ref[here, t * HC : (t + 1) * HC] = zf.astype(BF)
                    y_s[here, :] += nt((zf * sig(zf)).astype(BF), w_out)

        @pl.when(i == chunks)
        def _():

            @pl.loop(0, tokens // TB)
            def _(r):
                here = pl.ds(pl.multiple_of(r * TB, TB), TB)
                first = x_ref[here, :].astype(F32) + 0.5 * y_s[here, :]
                y_s[here, :] = first
                scaled, _ = ln_stats(first)
                hn_s[here, :] = (scaled * row(vecs, 3) + row(vecs, 4)).astype(BF)
            copies[1].start()
            until(chunks)
            part = width // 2
            for t in range(2):
                c = slice(t * part, (t + 1) * part)
                pos[:, c] = nn(table_ref[...], weight(t, SEG["pos"][0], part)).astype(BF)
            copies[6].start()
            until(chunks + 1)
            copies[0].start()
            at = SEG["qkv"][0]
            for t in range(2):
                c = slice(t * part, (t + 1) * part)

                @pl.loop(0, batch)
                def _(u):
                    hn = hn_s[pl.ds(pl.multiple_of(u * full, full), full), :]
                    q = nn(hn, weight(t, at, part)) + vecs[R_ATT : R_ATT + 1, c]
                    qu[u, :, c] = (q + vecs[R_ATT + 2 : R_ATT + 3, c]).astype(BF)
                    qv[u, :, c] = (q + vecs[R_ATT + 3 : R_ATT + 4, c]).astype(BF)
                    k[u, :, c] = nn(hn, weight(t, at + part, part)).astype(BF)
                    val = nn(hn, weight(t, at + 2 * part, part))
                    v[u, :, c] = (val + vecs[R_ATT + 1 : R_ATT + 2, c]).astype(BF)
            for n in (2, 3, 4, 5):
                copies[n].start()

        left = order[done[0] :]
        base = order[done[0] - 1][0] + 6.0
        blocks = full // BLK
        spots = batch * pairs * blocks
        slots = [min(max(int((now + 2.0 - base) / 0.9), 0), spots) for now, _, _ in left]

        def hook(blk):
            for slot, (_, kind, pair) in zip(slots, left):
                if slot % blocks == blk and slot < spots:

                    @pl.when(i == first_head + slot // blocks)
                    def _(kind=kind, pair=pair):
                        event(kind, pair)

        @pl.when(i >= first_head)
        def _():
            n = i - first_head
            u = n // pairs
            c = pl.ds(pl.multiple_of(lax.rem(n, pairs) * (2 * DK), 2 * DK), 2 * DK)

            def view(ref):
                return ref.at[pl.ds(u, 1), :, c]

            attn_fwd_kernel(
                len_ref, view(qu), view(qv), view(k), view(v), pos.at[:, c], view(mix), view(lse),
                u, hook,
            )

        @pl.when(i == steps - 1)
        def _():
            copies[7].start()
            copies[8].start()
            for slot, (_, kind, pair) in zip(slots, left):
                if slot >= spots:
                    event(kind, pair)
            finish()
            for copy in copies:
                copy.wait()

    def const(shape):
        return pl.BlockSpec(shape, lambda i, n: (0,) * len(shape), pipeline_mode=pl.Buffered(1))

    heads = jax.ShapeDtypeStruct(heads_shape, BF)
    return pl.pallas_call(
        body,
        grid_spec=pltpu.PrefetchScalarGridSpec(
            num_scalar_prefetch=1,
            grid=(steps,),
            in_specs=[
                const(x.shape), const(table.shape), const(packed_a.shape), const(packed_b.shape),
                const(slab.shape),
            ],
            out_specs=[
                ANY, ANY, pl.BlockSpec((R_ALL, width), lambda i, n: (0, 0)), ANY,
                pl.BlockSpec((tokens, 2 * HC), lambda i, n: (0, jnp.minimum(i, chunks - 1))),
            ]
            + [ANY] * 7,
            scratch_shapes=scratch + small + gather_scratch(len(FRONT_PIECES)),
        ),
        out_shape=[
            gathered_shape(packed_a),
            gathered_shape(packed_b),
            jax.ShapeDtypeStruct((R_ALL, width), F32),
            jax.ShapeDtypeStruct((tokens, width), F32),
            jax.ShapeDtypeStruct((tokens, 4 * width), BF),
            heads, heads, heads, heads,
            jax.ShapeDtypeStruct(table.shape, BF),
            heads,
            jax.ShapeDtypeStruct(heads_shape, F32),
        ],
        compiler_params=comm_params(cid),
        name="front",
    )(lens, x, table, packed_a, packed_b, slab)


def fill_table(table_ref):
    length, width = table_ref.shape[0] // 2, table_ref.shape[1]
    step = 32
    cols = lax.broadcasted_iota(jnp.int32, (step, width), 1)
    rows = lax.broadcasted_iota(jnp.int32, (step, width), 0)
    rate = jnp.exp((cols // 2 * 2).astype(F32) * (-math.log(10000.0) / width))
    even = cols % 2 == 0
    big = (length - 1 - step * rows).astype(F32) * rate
    small = rows.astype(F32) * rate
    sin_big, cos_big = jnp.sin(big), jnp.cos(big)
    first = jnp.where(even, sin_big, cos_big)
    second = jnp.where(even, cos_big, -sin_big)
    cos_small, sin_small = jnp.cos(small), jnp.sin(small)
    for a in range(2 * length // step):
        block = first[a : a + 1] * cos_small - second[a : a + 1] * sin_small
        table_ref[a * step : (a + 1) * step, :] = block.astype(BF)


def table_call(full, width):
    return pl.pallas_call(
        fill_table,
        out_specs=VM,
        out_shape=jax.ShapeDtypeStruct((2 * full, width), BF),
        name="position_table",
    )()


def conv1_kernel(
    lens, mixed, first, w_out, w_ci, vecs, second_ref, half_ref, conv_ref, stat_ref, pad
):
    u = pl.program_id(0)
    full = first.shape[0]
    count = lens[u]
    part = w_out.shape[2]
    y = row(vecs, 5)
    for t in range(2):
        y = y + nt(mixed[:, t * part : (t + 1) * part], w_out[t])
    second = first[...] + y
    second_ref[...] = second
    scaled, _ = ln_stats(second)
    hn = (scaled * row(vecs, 6) + row(vecs, 7)).astype(BF)
    mask = row_mask(0, full, count)
    pad[0:8, :] = jnp.zeros((8, part), F32)
    pad[full + 8 : full + 16, :] = jnp.zeros((8, part), F32)
    for t in range(2):
        c = slice(t * part, (t + 1) * part)
        proj = nn(hn, w_ci[t])
        za = proj[:, :part] + vecs[R_CV : R_CV + 1, c]
        zg = proj[:, part:] + vecs[R_CV + 1 : R_CV + 2, c]
        half_ref[:, 2 * t * part : (2 * t + 1) * part] = za.astype(BF)
        half_ref[:, (2 * t + 1) * part : (2 * t + 2) * part] = zg.astype(BF)
        pad[8 : full + 8, :] = za * sig(zg) * mask
        total = jnp.zeros((full, part), F32)
        for k in range(9):
            total = total + vecs[R_CV + 4 + k : R_CV + 5 + k, c] * pad[4 + k : 4 + k + full, :]
        conv_ref[:, c] = total
        kept = total * mask
        stat_ref[pl.ds(4 * u, 1), c] = col_sum(kept)
        stat_ref[pl.ds(4 * u + 1, 1), c] = col_sum(kept * total)
    for k in (2, 3):
        stat_ref[pl.ds(4 * u + k, 1), :] = jnp.full((1, 2 * part), 1.0, F32) * count.astype(F32)


def with_sum(kernel, spot, cid):
    def body(*refs):
        sums = refs[-8:]
        refs = list(refs[:-8])
        call, meet = sum_steps(sums)
        out = refs[spot]
        refs[spot] = sums[0]

        @pl.when(pl.program_id(0) == 0)
        def _():
            call()

        kernel(*refs)

        @pl.when(pl.program_id(0) == pl.num_programs(0) - 1)
        def _():
            meet(out)

    return kernel if cid is None else body


def conv1_call(lens, mixed, first, g, vecs, cid=None):
    tokens, width = first.shape
    batch = lens.shape[0]
    full = tokens // batch
    return pl.pallas_call(
        with_sum(conv1_kernel, 9, cid),
        grid_spec=pltpu.PrefetchScalarGridSpec(
            num_scalar_prefetch=1,
            grid=(batch,),
            in_specs=[
                tall(full, width), tall(full, width), seg_spec("out", width),
                seg_spec("ci", width), whole(vecs.shape),
            ],
            out_specs=[
                tall(full, width), tall(full, 2 * width), tall(full, width),
                whole((4 * batch, width)),
            ],
            scratch_shapes=[pltpu.VMEM((full + 16, width // 2), F32)]
            + ([] if cid is None else sum_scratch((4 * batch, width))),
        ),
        out_shape=[
            jax.ShapeDtypeStruct((tokens, width), F32),
            jax.ShapeDtypeStruct((tokens, 2 * width), BF),
            jax.ShapeDtypeStruct((tokens, width), F32),
            jax.ShapeDtypeStruct((4 * batch, width), F32),
        ],
        compiler_params=dense_params() if cid is None else comm_params(cid),
        name="conv_forward",
    )(lens, mixed, first, g, g, vecs)


def bn_of(stats, u):
    n = stats[pl.ds(4 * u + 2, 1), :]
    avg = stats[pl.ds(4 * u, 1), :] / n
    var = stats[pl.ds(4 * u + 1, 1), :] / n - avg * avg
    return avg, lax.rsqrt(var + norm_eps), n


def swish_parts(z):
    s = sig(z)
    a = z * s
    return a, s + a * (1.0 - s)


def middle_kernel(
    lens, second, conv, cot, stats, w_co, w_in, w_out, vecs,
    act_ref, d3_ref, dy_ref, sum_ref, small_ref, gi_ref, go_ref, gc_ref,
    a_s, slope_s, gi, go, gc,
):
    i = pl.program_id(0)
    steps = pl.num_programs(0)
    rows, width = second.shape
    batch = lens.shape[0]
    per = steps // batch
    u = i // per
    mask = row_mask(lax.rem(i, per) * rows, rows, lens[u])

    @pl.when(i == 0)
    def _():
        small_ref[...] = jnp.zeros_like(small_ref)
        sum_ref[...] = jnp.zeros_like(sum_ref)
        gi[...] = jnp.zeros_like(gi)
        go[...] = jnp.zeros_like(go)
        gc[...] = jnp.zeros_like(gc)

    avg, rstd, _ = bn_of(stats, u)
    part = w_co.shape[2]
    half = w_in.shape[2]
    yhat = (conv[...] - avg) * rstd
    bn, bn_slope = swish_parts(yhat * row(vecs, R_CV + 2) + row(vecs, R_CV + 3))
    act = bn.astype(BF)
    y = row(vecs, 8)
    for t in range(2):
        y = y + nt(act[:, t * part : (t + 1) * part], w_co[t])
    third = second[...] + y
    scaled9, inv9 = ln_stats(third)
    hn = (scaled9 * row(vecs, 9) + row(vecs, 10)).astype(BF)
    y = row(vecs, 11)
    for t in range(2):
        c = slice(t * half, (t + 1) * half)
        a, slope = swish_parts(nn(hn, w_in[t]) + bias_half(vecs, R_B2, t))
        a = a.astype(BF)
        a_s[:, c] = a
        slope_s[:, c] = slope
        y = y + nt(a, w_out[t])
    scaled, inv = ln_stats(third + 0.5 * y)
    act_ref[...] = (scaled * row(vecs, 12) + row(vecs, 13)).astype(BF)
    up = cot[...].astype(F32) * mask
    small_ref[12:13, :] += col_sum(up * scaled)
    small_ref[13:14, :] += col_sum(up)
    d4 = ln_back(up, scaled, inv, row(vecs, 12))
    g = (0.5 * d4).astype(BF)
    small_ref[11:12, :] += col_sum(g.astype(F32))
    d_hn = jnp.zeros((rows, width), F32)
    for t in range(2):
        c = slice(t * half, (t + 1) * half)
        go[t] += tn(g, a_s[:, c])
        dz = (nn(g, w_out[t]) * slope_s[:, c]).astype(BF)
        bias = col_sum(dz.astype(F32))
        small_ref[R_B2 + 2 * t : R_B2 + 2 * t + 1, :] += bias[:, :width]
        small_ref[R_B2 + 2 * t + 1 : R_B2 + 2 * t + 2, :] += bias[:, width:]
        gi[t] += tn(hn, dz)
        d_hn = d_hn + nt(dz, w_in[t])
    small_ref[9:10, :] += col_sum(d_hn * scaled9)
    small_ref[10:11, :] += col_sum(d_hn)
    d3 = d4 + ln_back(d_hn, scaled9, inv9, row(vecs, 9))
    d3_ref[...] = d3
    g = d3.astype(BF)
    small_ref[8:9, :] += col_sum(g.astype(F32))
    d_act = []
    for t in range(2):
        gc[t] += tn(g, act[:, t * part : (t + 1) * part])
        d_act.append(nn(g, w_co[t]))
    d_bn = jnp.concatenate(d_act, axis=1) * bn_slope
    small_ref[R_CV + 2 : R_CV + 3, :] += col_sum(d_bn * yhat)
    small_ref[R_CV + 3 : R_CV + 4, :] += col_sum(d_bn)
    d_yhat = d_bn * row(vecs, R_CV + 2)
    dy_ref[...] = d_yhat
    sum_ref[pl.ds(4 * u, 1), :] += col_sum(d_yhat)
    sum_ref[pl.ds(4 * u + 1, 1), :] += col_sum(d_yhat * yhat)

    @pl.when(i == steps - 1)
    def _():
        gi_ref[...] = gi[...].astype(BF)
        go_ref[...] = go[...].astype(BF)
        gc_ref[...] = gc[...].astype(BF)


def grad_shape(name, width):
    return jax.ShapeDtypeStruct((2, width, SEG[name][1]), BF)


def acc(name, width):
    return pltpu.VMEM((2, width, SEG[name][1]), F32)


def once(shape):
    zeros = (0,) * len(shape)
    return pl.BlockSpec(shape, lambda i, *_: zeros, pipeline_mode=pl.Buffered(1))


def middle_call(lens, second, conv, cot, stats, g, vecs, cid=None):
    tokens, width = second.shape
    small = (R_ALL, width)
    names = ("f2i", "f2o", "co")
    return pl.pallas_call(
        with_sum(middle_kernel, 12, cid),
        grid_spec=pltpu.PrefetchScalarGridSpec(
            num_scalar_prefetch=1,
            grid=(tokens // TB,),
            in_specs=[tall(TB, width)] * 3
            + [whole(stats.shape), seg_spec("co", width), seg_spec("f2i", width)]
            + [seg_spec("f2o", width), whole(vecs.shape)],
            out_specs=[tall(TB, width)] * 3
            + [whole(stats.shape), whole(small)]
            + [whole(grad_shape(name, width).shape) for name in names],
            scratch_shapes=[
                pltpu.VMEM((TB, 4 * width), BF),
                pltpu.VMEM((TB, 4 * width), F32),
            ]
            + [acc(name, width) for name in names]
            + ([] if cid is None else sum_scratch(stats.shape)),
        ),
        out_shape=[
            jax.ShapeDtypeStruct((tokens, width), BF),
            jax.ShapeDtypeStruct((tokens, width), F32),
            jax.ShapeDtypeStruct((tokens, width), F32),
            jax.ShapeDtypeStruct(stats.shape, F32),
            jax.ShapeDtypeStruct(small, F32),
        ]
        + [grad_shape(name, width) for name in names],
        compiler_params=dense_params() if cid is None else comm_params(cid),
        name="conv_out_ffn2",
    )(lens, second, conv, cot, stats, g, g, g, vecs)


def conv2_kernel(
    lens, dy, conv, d3, halves, second, mixed, stats, sums, w_ci, w_out, vecs,
    d2_ref, dm_ref, small_ref, gi_ref, go_ref, pad, dh_s, gi, go,
):
    u = pl.program_id(0)
    full, width = d3.shape
    part = w_out.shape[2]

    @pl.when(u == 0)
    def _():
        small_ref[...] = jnp.zeros_like(small_ref)
        gi[...] = jnp.zeros_like(gi)
        go[...] = jnp.zeros_like(go)

    avg, rstd, n = bn_of(stats, u)
    mask = row_mask(0, full, lens[u])
    scaled, inv = ln_stats(second[...])
    hn = (scaled * row(vecs, 6) + row(vecs, 7)).astype(BF)
    pad[0:8, :] = jnp.zeros((8, part), F32)
    pad[full + 8 : full + 16, :] = jnp.zeros((8, part), F32)
    b1 = sums[pl.ds(4 * u, 1), :]
    b2 = sums[pl.ds(4 * u + 1, 1), :]
    dh_s[...] = jnp.zeros_like(dh_s)
    taps = vecs[R_CV : R_CV + 13, :]

    @pl.loop(0, 2)
    def _(t):
        c = pl.ds(pl.multiple_of(t * part, part), part)

        def lanes(v):
            return jnp.where(t == 0, v[:, :part], v[:, part:])

        yhat = (conv[:, c] - lanes(avg)) * lanes(rstd)
        pad[8 : full + 8, :] = lanes(rstd) * (
            dy[:, c] - mask * ((lanes(b1) + yhat * lanes(b2)) / lanes(n))
        )
        za = halves[:, pl.ds(pl.multiple_of(2 * t * part, part), part)].astype(F32)
        zg = halves[:, pl.ds(pl.multiple_of((2 * t + 1) * part, part), part)].astype(F32)
        gate = sig(zg)
        gated = za * gate * mask
        total = jnp.zeros((full, part), F32)
        mine = lanes(taps)
        for k in range(9):
            moved = pad[12 - k : 12 - k + full, :]
            total = total + mine[4 + k : 5 + k, :] * moved
            small_ref[R_CV + 4 + k : R_CV + 5 + k, c] += col_sum(gated * moved)
        d_glu = total * mask
        d_a = (d_glu * gate).astype(BF)
        d_g = (d_glu * gated * (1.0 - gate)).astype(BF)
        small_ref[R_CV : R_CV + 1, c] += col_sum(d_a.astype(F32))
        small_ref[R_CV + 1 : R_CV + 2, c] += col_sum(d_g.astype(F32))
        pair = jnp.concatenate([d_a, d_g], axis=1)
        gi[t] += tn(hn, pair)
        dh_s[...] += nt(pair, w_ci[t])

    d_hn = dh_s[...]
    small_ref[6:7, :] += col_sum(d_hn * scaled)
    small_ref[7:8, :] += col_sum(d_hn)
    d2 = d3[...] + ln_back(d_hn, scaled, inv, row(vecs, 6))
    d2_ref[...] = d2
    g = d2.astype(BF)
    small_ref[5:6, :] += col_sum(g.astype(F32))
    for t in range(2):
        c = slice(t * part, (t + 1) * part)
        go[t] += tn(g, mixed[:, c])
        dm_ref[:, c] = nn(g, w_out[t]).astype(BF)

    @pl.when(u == pl.num_programs(0) - 1)
    def _():
        gi_ref[...] = gi[...].astype(BF)
        go_ref[...] = go[...].astype(BF)


def conv2_call(lens, dy, conv, d3, halves, second, mixed, stats, sums, g, vecs):
    tokens, width = second.shape
    batch = lens.shape[0]
    full = tokens // batch
    small = (R_ALL, width)
    names = ("ci", "out")
    return pl.pallas_call(
        conv2_kernel,
        grid_spec=pltpu.PrefetchScalarGridSpec(
            num_scalar_prefetch=1,
            grid=(batch,),
            in_specs=[tall(full, width)] * 3
            + [tall(full, 2 * width), tall(full, width), tall(full, width)]
            + [whole(stats.shape)] * 2
            + [seg_spec("ci", width), seg_spec("out", width), whole(vecs.shape)],
            out_specs=[tall(full, width)] * 2
            + [whole(small)]
            + [whole(grad_shape(name, width).shape) for name in names],
            scratch_shapes=[
                pltpu.VMEM((full + 16, width // 2), F32), pltpu.VMEM((full, width), F32),
            ]
            + [acc(name, width) for name in names],
        ),
        out_shape=[
            jax.ShapeDtypeStruct((tokens, width), F32),
            jax.ShapeDtypeStruct((tokens, width), BF),
            jax.ShapeDtypeStruct(small, F32),
        ]
        + [grad_shape(name, width) for name in names],
        compiler_params=dense_params(),
        name="conv_backward",
    )(lens, dy, conv, d3, halves, second, mixed, stats, sums, g, g, vecs)


def last_kernel(
    dq, dk, dv, first, x_ref, d2, z_ref, table, dpos, asums, w_qkv, w_in, w_out, vecs,
    d0_ref, small_ref, d1_s, g_s, hn_s, dh_s, gq, gp, z_s, w_in_s, w_out_s, in_sem,
    put, ready, after,
):
    i = pl.program_id(0)
    blocks = x_ref.shape[0] // TB
    rows, width = first.shape
    part = w_qkv.shape[2] // 3
    ahead = [
        pltpu.make_async_copy(w_in.at[:, :, pl.ds(0, w_in_s.shape[2])], w_in_s, in_sem.at[0]),
        pltpu.make_async_copy(
            w_out.at[:, :, pl.ds(w_in_s.shape[2], w_in_s.shape[2])], w_out_s, in_sem.at[1]
        ),
        pltpu.make_async_copy(z_ref, z_s, in_sem.at[2]),
    ]

    @pl.when(i == 0)
    def _():
        small_ref[...] = jnp.zeros_like(small_ref)
        small_ref[R_ATT:R_CV, :] = jnp.sum(asums[...], axis=0)[0:4]
        for copy in ahead:
            copy.start()
        gq[...] = jnp.zeros_like(gq)
        gp[...] = jnp.zeros_like(gp)
        dh_s[...] = jnp.zeros_like(dh_s)

    @pl.when(i < blocks)
    def _():
        here = pl.ds(pl.multiple_of(i * TB, TB), TB)
        scaled, inv = ln_stats(first[...])
        hn = (scaled * row(vecs, 3) + row(vecs, 4)).astype(BF)
        d_hn = jnp.zeros((rows, width), F32)
        for t in range(2):
            c = slice(t * part, (t + 1) * part)
            dp = jnp.concatenate([dq[:, c], dk[:, c], dv[:, c]], axis=1)
            gq[t] += tn(hn, dp)
            for u in range(dpos.shape[0]):
                gp[t] += tn(table[...], dpos[u, :, c])
            d_hn = d_hn + nt(dp, w_qkv[t])
        small_ref[3:4, :] += col_sum(d_hn * scaled)
        small_ref[4:5, :] += col_sum(d_hn)
        d1 = d2[...] + ln_back(d_hn, scaled, inv, row(vecs, 3))
        d1_s[here, :] = d1
        g = (0.5 * d1).astype(BF)
        g_s[here, :] = g
        small_ref[2:3, :] += col_sum(g.astype(F32))
        scaled, inv = ln_stats(x_ref[here, :].astype(F32))
        hn_s[here, :] = (scaled * row(vecs, 0) + row(vecs, 1)).astype(BF)

    @pl.when(i == blocks - 1)
    def _():
        for t in range(2):
            put("pos", t, 0, gp[t])
            put("qkv", t, 0, gq[t])
        for copy in ahead:
            copy.wait()
        ready(-1)

    chunks = w_in_s.shape[2] // HC

    @pl.when(i >= blocks)
    def _():
        j = i - blocks
        at = pl.multiple_of(j * HC, HC)
        c = pl.ds(at, HC)
        odd = lax.rem(j, 2) == 1
        for t in range(2):
            zc = pl.ds(pl.multiple_of((2 * j + t) * HC, HC), HC)
            a, slope = swish_parts(z_s[:, zc].astype(F32))
            put("f1o", t, at, tn(g_s[...], a.astype(BF)))
            dz = (nn(g_s[...], w_out_s[t, :, c]) * slope).astype(BF)
            bias = col_sum(dz.astype(F32))
            none = jnp.zeros_like(bias)
            pair = [jnp.where(odd, none, bias), jnp.where(odd, bias, none)]
            line = pl.ds(R_B1 + 2 * t + j // 2, 1)
            small_ref[line, :] += jnp.concatenate(pair, axis=1)
            put("f1i", t, at, tn(hn_s[...], dz))
            dh_s[...] += nt(dz, w_in_s[t, :, c])
            for k in range(chunks):

                @pl.when(j == k)
                def _(k=k, t=t):
                    after(k, t)
        for k in range(chunks):

            @pl.when(j == k)
            def _(k=k):
                ready(k)

    @pl.when(i == blocks + chunks - 1)
    def _():
        @pl.loop(0, blocks)
        def _(k):
            here = pl.ds(pl.multiple_of(k * TB, TB), TB)
            scaled, inv = ln_stats(x_ref[here, :].astype(F32))
            d_hn = dh_s[here, :]
            small_ref[0:1, :] += col_sum(d_hn * scaled)
            small_ref[1:2, :] += col_sum(d_hn)
            d0 = d1_s[here, :] + ln_back(d_hn, scaled, inv, row(vecs, 0))
            d0_ref[here, :] = d0.astype(BF)


def last_call(dq, dk, dv, first, x, d2, z, table, dpos, asums, g, vecs, others=None, cid=None):
    tokens, width = first.shape
    blocks, chunks = tokens // TB, SEG["f1i"][1] // HC
    small = (R_ALL, width)
    places = table.shape[0] // blocks

    def block(rows, cols):
        return pl.BlockSpec((rows, cols), lambda i: (jnp.minimum(i, blocks - 1), 0))

    in_specs = (
        [block(TB, width)] * 4
        + [whole(x.shape), block(TB, width)]
        + [ANY]
        + [block(places, width)]
        + [
            pl.BlockSpec(
                (dpos.shape[0], places, width), lambda i: (0, jnp.minimum(i, blocks - 1), 0)
            ),
            whole(asums.shape),
        ]
        + [seg_spec("qkv", width), ANY, ANY, whole(vecs.shape)]
    )
    args = [dq, dk, dv, first, x, d2, z, table, dpos, asums, g, g, g, vecs]
    scratch = [
        pltpu.VMEM((tokens, width), F32), pltpu.VMEM((tokens, width), BF),
        pltpu.VMEM((tokens, width), BF), pltpu.VMEM((tokens, width), F32),
        acc("qkv", width), acc("pos", width), pltpu.VMEM(z.shape, BF),
        pltpu.VMEM((2, width, SEG["f1i"][1]), BF), pltpu.VMEM((2, width, SEG["f1o"][1]), BF),
        pltpu.SemaphoreType.DMA((3,)),
    ]
    out_specs = [whole((tokens, width)), whole(small)]
    out_shape = [jax.ShapeDtypeStruct((tokens, width), BF), jax.ShapeDtypeStruct(small, F32)]
    n_own = len(scratch)
    if others is None:
        names = ("qkv", "f1i", "f1o", "pos")
        out_specs += [once(grad_shape(name, width).shape) for name in names]
        out_shape += [grad_shape(name, width) for name in names]

        def body(*refs):
            ins, rest = refs[: len(args)], refs[len(args) :]
            outs = dict(zip(names, rest[2:6]))

            def put(name, t, at, value):
                outs[name][t, :, pl.ds(at, value.shape[1])] = value.astype(BF)

            last_kernel(*ins, *rest[:2], *rest[6:], put, lambda j: None, lambda j, t: None)

        params = dense_params()
    else:
        owned = width // (NZ * NY * NX)
        names = ("pos", "qkv", "f1i", "f1o")
        base = {name: SEG[name][0] for name in names}
        order = [("pos", 0), ("qkv", 0), ("qkv", 256), ("qkv", 512)]
        for j in range(chunks):
            order += [("f1i", j * HC), ("f1o", j * HC)]
        pieces = [(0, base[name] + at, 256, base[name] + at) for name, at in order]
        n_first = 4
        n_in = len(args)
        args += list(others)
        in_specs += [whole(item.shape) for item in others]
        out_specs = out_specs[:1] + [whole((owned, C_A)), whole((R_SUM, width))]
        out_shape = out_shape[:1] + [
            jax.ShapeDtypeStruct((owned, C_A), F32), jax.ShapeDtypeStruct((R_SUM, width), F32)
        ]
        small_scratch = small_sum_scratch(width)
        scratch += [pltpu.VMEM(small, F32), pltpu.VMEM((2, NZ, NY, NX, owned, C_A), BF)]
        scratch += small_scratch + scatter_scratch(pieces, owned)
        params = comm_params(cid)

        def body(*refs):
            i = pl.program_id(0)
            ins, rest = refs[:n_in], refs[n_in:]
            parts, rest = rest[: len(others)], rest[len(others) :]
            (d0_ref, o_ref, ext), rest = rest[:3], rest[3:]
            own, rest = rest[:n_own], rest[n_own:]
            (small_ref, buf), rest = rest[:2], rest[2:]
            sums, sems = rest[: len(small_scratch)], rest[len(small_scratch) :]
            start, advance, finish, rounds = scatter_steps(pieces, [buf], o_ref, sems, 4)
            pp, small_list = small_sum_steps(list(parts) + [small_ref], ext, sums)
            z, y, x, t = place()

            def put(name, t, at, value):
                w = value.shape[1]
                at = base[name] + at
                at = at if isinstance(at, int) else pl.multiple_of(at, HC)
                value = value.astype(BF).reshape(NZ, NY, NX, owned, w)
                buf[t, :, :, :, :, pl.ds(at, w)] = value

            def ready(j):
                for p in range(n_first) if j < 0 else (n_first + 2 * j, n_first + 2 * j + 1):
                    start(p)

            def after(j, t):
                if j == 0:
                    advance(2 * t)
                    advance(2 * t + 1)
                else:
                    advance(n_first + 2 * (j - 1) + t)

            @pl.when(i == 0)
            def _():
                greet(link_peers(z, y, x, t)[: NZ - 1] + pp + [dev(z, y, x, 1 - t)])

            last_kernel(*ins, d0_ref, small_ref, *own, put, ready, after)

            @pl.when(i == blocks + chunks - 1)
            def _():
                todo = [lambda q=q: advance(q) for q in range(n_first + 2 * (chunks - 1), rounds)]
                for k in range(max(len(todo), len(small_list))):
                    if k < len(small_list):
                        small_list[k]()
                    if k < len(todo):
                        todo[k]()
                finish()

    return pl.pallas_call(
        body,
        grid=(blocks + chunks,),
        in_specs=in_specs,
        out_specs=out_specs,
        scratch_shapes=scratch,
        out_shape=out_shape,
        compiler_params=params,
        name="qkv_ffn1_backward",
    )(*args)


def gather_plain(big, kinds, names_a, names_b, small_ins, both, n_dp):
    def pack(names):
        return jnp.concatenate(
            [big[n].T if kinds[n][0] == "flip" else big[n] for n in names], axis=1
        )

    def every(item):
        g = lax.all_gather(item, both, axis=0, tiled=True)
        g = g.reshape(n_dp, 2, item.shape[0], -1).transpose(1, 0, 2, 3)
        return g.reshape(2, n_dp * item.shape[0], -1)

    small = jnp.concatenate([item.reshape(-1) for item in small_ins])
    smalls = lax.all_gather(small, both, axis=0, tiled=False).reshape(n_dp, 2, -1).astype(F32)
    off = 0
    pieces = []
    for item in small_ins:
        pieces.append(smalls[:, :, off : off + item.size].reshape((n_dp, 2) + item.shape))
        off += item.size
    width = small_ins[4].shape[1] * n_dp * 2
    vecs = jnp.concatenate(
        [
            pieces[4].transpose(2, 0, 1, 3).reshape(-1, width),
            pieces[1].transpose(2, 1, 3, 0, 4).reshape(-1, width),
            pieces[2].transpose(2, 1, 3, 0, 4).reshape(-1, width),
            pieces[0].transpose(1, 2, 0, 3).reshape(-1, width),
            pieces[3].transpose(1, 2, 0, 3).reshape(-1, width),
            jnp.zeros((1, width), F32),
        ],
        axis=0,
    )
    return every(pack(names_a)), every(pack(names_b)), vecs


def scatter_plain(grads, kinds, names, small_g, small_ins, both, n_dp):
    vec_g = (
        small_g[R_B1:R_B2].reshape(1, -1), small_g[R_ATT:R_CV], small_g[R_CV:R_B1],
        small_g[R_B2 : R_B2 + 4].reshape(1, -1),
    )

    def small_of(item, like):
        item = item.reshape(item.shape[0], 2, like.shape[-2], n_dp, like.shape[-1])
        return item.transpose(1, 3, 0, 2, 4).reshape(2, n_dp, -1)

    cols = small_ins[4].shape[1]
    norm_g = small_g[:R_ATT].reshape(-1, n_dp, 2, cols).transpose(2, 1, 0, 3).reshape(2, n_dp, -1)
    packed = jnp.concatenate(
        [small_of(item, like) for item, like in zip(vec_g, small_ins)] + [norm_g], axis=2
    )
    packed = packed.swapaxes(0, 1).reshape(n_dp * 2, -1)
    own_small = lax.psum_scatter(packed, both, scatter_dimension=0, tiled=True).reshape(-1)
    wide = jnp.concatenate([grads[name] for name in names], axis=2)
    rows = wide.shape[1] // n_dp
    wide = wide.reshape(2, n_dp, rows, -1).swapaxes(0, 1).reshape(n_dp * 2 * rows, -1)
    own = lax.psum_scatter(wide, both, scatter_dimension=0, tiled=True).astype(F32)
    outs, at = {}, 0
    for name in names:
        w = grads[name].shape[2]
        item = own[:, at : at + w]
        outs[name] = item.T if kinds[name][0] == "flip" else item
        at += w
    small_outs, at = [], 0
    for item in small_ins:
        small_outs.append(own_small[at : at + item.size].reshape(item.shape))
        at += item.size
    return outs, small_outs


def local(
    frames,
    lengths,
    ffn1_in,
    ffn1_out,
    ffn1_bias,
    qkv_weight,
    pos_weight,
    out_weight,
    attn_bias,
    conv_in,
    conv_out,
    conv_channel,
    ffn2_in,
    ffn2_out,
    ffn2_bias,
    norm_params,
    cotangent,
):
    micro, seqs, full, width = frames.shape
    both = ("dp", "tensor")
    n_dp = lax.axis_size("dp")
    rows = ffn1_in.shape[0]
    batch = micro * seqs
    tokens = batch * full
    small_ins = (ffn1_bias, attn_bias, conv_channel, ffn2_bias, norm_params)
    names_a, names_b = ("f1i", "f1o", "pos", "qkv"), ("f2i", "f2o", "ci", "out", "co")
    big = {
        "f1i": ffn1_in, "f1o": ffn1_out, "pos": pos_weight, "qkv": qkv_weight.reshape(rows, -1),
        "f2i": ffn2_in, "f2o": ffn2_out, "ci": conv_in.reshape(rows, -1), "out": out_weight,
        "co": conv_out,
    }
    kinds = {name: ("plain",) for name in big}
    kinds.update({name: ("flip",) for name in ("f1o", "f2o", "out", "co")})
    mine_mesh = own_mesh((n_dp, lax.axis_size("tensor"))) and rows % 16 == 0
    if mine_mesh:
        packed_a, packed_b, slab, table = prep_call(
            [
                ffn1_in, ffn1_out.T, pos_weight, qkv_weight.transpose(1, 0, 2), ffn2_in,
                ffn2_out.T, conv_in, out_weight.T, conv_out.T,
            ],
            [ffn1_bias, attn_bias, conv_channel.transpose(1, 2, 0), ffn2_bias, norm_params],
            full, width,
        )
    else:
        table = table_call(full, width)
        g_a, g_b, vecs = gather_plain(big, kinds, names_a, names_b, small_ins, both, n_dp)

    def reduce_sum(item):
        return item if mine_mesh else lax.psum(item, both)

    cids = (3, 4) if mine_mesh else (None, None)
    mine = lax.axis_index("tensor")
    lens = lax.dynamic_slice_in_dim(lengths, mine * seqs, seqs, 1).reshape(-1)
    x = frames.reshape(tokens, width)
    cot = cotangent.reshape(tokens, width)

    def utt(item):
        return item.reshape(batch, full, -1)

    def flat(item):
        return item.reshape(tokens, -1)

    if mine_mesh:
        g_a, g_b, vecs, first, z1, q_u, q_v, keys, values, pos, mixed, lse = front_call(
            lens, x, table, packed_a, packed_b, slab, batch, 1
        )
        g_a, g_b = g_a.reshape(2, width, -1), g_b.reshape(2, width, -1)
        heads = (lens, q_u, q_v, keys, values, pos)
    else:
        first, z1, q_u, q_v, keys, values, pos = ffn1_call(x, table, g_a, vecs)
        heads = (lens, utt(q_u), utt(q_v), utt(keys), utt(values), pos)
        mixed, lse = attn_fwd_call(*heads)
    second, halves, conv, stats = conv1_call(lens, flat(mixed), first, g_b, vecs, cids[0])
    stats = reduce_sum(stats)
    grads = {}
    result, d3, d_yhat, sums, small_m, grads["f2i"], grads["f2o"], grads["co"] = middle_call(
        lens, second, conv, cot, stats, g_b, vecs, cids[1]
    )
    sums = reduce_sum(sums)
    d2, d_mixed, small_c, grads["ci"], grads["out"] = conv2_call(
        lens, d_yhat, conv, d3, halves, second, flat(mixed), stats, sums, g_b, vecs
    )
    if mine_mesh:
        dq, dk, dv, dpos, asums, own_b = attn_bwd_call(
            *heads, mixed, lse, utt(d_mixed), [grads[name] for name in names_b], 5
        )
        d0, own_a, ext = last_call(
            flat(dq), flat(dk), flat(dv), first, x, d2, z1, table, dpos, asums, g_a, vecs,
            (small_m, small_c), 6,
        )
        outs = finish_call(own_a, own_b, ext, rows)
    else:
        dq, dk, dv, dpos, asums = attn_bwd_call(*heads, mixed, lse, utt(d_mixed))
        d0, small_l, grads["qkv"], grads["f1i"], grads["f1o"], grads["pos"] = last_call(
            flat(dq), flat(dk), flat(dv), first, x, d2, z1, table, dpos, asums, g_a, vecs
        )
        o, small_outs = scatter_plain(
            grads, kinds, names_a + names_b, small_m + small_c + small_l, small_ins, both, n_dp
        )
        outs = (
            o["f1i"], o["f1o"], small_outs[0], o["qkv"].reshape(qkv_weight.shape), o["pos"],
            o["out"], small_outs[1], o["ci"].reshape(conv_in.shape), o["co"], small_outs[2],
            o["f2i"], o["f2o"], small_outs[3], small_outs[4],
        )
    return (result.reshape(frames.shape), d0.reshape(frames.shape)) + tuple(outs)


def solution(mesh):
    in_specs = (
        P(None, ("dp", "tensor"), None, None),
        P(None, "dp"),
        P("dp", "tensor"),
        P("tensor", "dp"),
        P("tensor", "dp"),
        P("dp", None, "tensor"),
        P("dp", "tensor"),
        P("tensor", "dp"),
        P(None, "tensor", "dp"),
        P("dp", None, "tensor"),
        P("tensor", "dp"),
        P(None, "tensor", "dp"),
        P("dp", "tensor"),
        P("tensor", "dp"),
        P("tensor", "dp"),
        P(None, ("dp", "tensor")),
        P(None, ("dp", "tensor"), None, None),
    )
    out_specs = (
        P(None, ("dp", "tensor"), None, None),
        P(None, ("dp", "tensor"), None, None),
        P("dp", "tensor"),
        P("tensor", "dp"),
        P("tensor", "dp"),
        P("dp", None, "tensor"),
        P("dp", "tensor"),
        P("tensor", "dp"),
        P(None, "tensor", "dp"),
        P("dp", None, "tensor"),
        P("tensor", "dp"),
        P(None, "tensor", "dp"),
        P("dp", "tensor"),
        P("tensor", "dp"),
        P("tensor", "dp"),
        P(None, ("dp", "tensor")),
    )
    return jax.shard_map(local, mesh=mesh, in_specs=in_specs, out_specs=out_specs, check_vma=False)
```

```python
import math

import jax
import jax.numpy as jnp
from jax import lax
from jax.experimental import pallas as pl
from jax.experimental.pallas import tpu as pltpu
from jax.sharding import PartitionSpec as P

DK = 64
norm_eps = 1e-05
mask_fill = -1000000000.0
BF = jnp.bfloat16
F32 = jnp.float32
BLK = 128


def nn(a, b):
    return lax.dot_general(a, b, (((1,), (0,)), ((), ())), preferred_element_type=F32)


def nt(a, b):
    return lax.dot_general(a, b, (((1,), (1,)), ((), ())), preferred_element_type=F32)


def tn(a, b):
    return lax.dot_general(a, b, (((0,), (0,)), ((), ())), preferred_element_type=F32)


def attn_fwd_kernel(len_ref, qu, qv, k, v, pos, o_ref, lse_ref, u=None, hook=None):
    count = len_ref[pl.program_id(0) if u is None else u]
    full = k.shape[1]
    lane = lax.broadcasted_iota(jnp.int32, (BLK, 2 * DK), 1)
    col = lax.broadcasted_iota(jnp.int32, (BLK, full), 1)
    keep = col < count
    zero = jnp.zeros((), BF)
    for blk in range(full // BLK):
        i0 = blk * BLK
        base = full - BLK - i0
        if hook is not None:
            hook(blk)
        outs, logs = [], []
        for h in range(2):
            mine = (lane < DK) if h == 0 else (lane >= DK)
            q_u = jnp.where(mine, qu[0, i0 : i0 + BLK, :], zero)
            q_v = jnp.where(mine, qv[0, i0 : i0 + BLK, :], zero)
            rel = nt(q_v, pos[base : base + full + BLK, :])
            rel = pltpu.roll(rel, full + 1, 1, stride=1, stride_axis=0)[:, :full]
            s = (nt(q_u, k[0]) + rel) * (1.0 / math.sqrt(DK))
            s = jnp.where(keep, s, mask_fill)
            top = jnp.max(s, axis=1, keepdims=True)
            e = jnp.exp(s - top)
            total = jnp.sum(e, axis=1, keepdims=True)
            outs.append(nn(e.astype(BF), v[0]) / total)
            logs.append(top + jnp.log(total))
        left = lane < DK
        o_ref[0, i0 : i0 + BLK, :] = jnp.where(left, outs[0], outs[1]).astype(BF)
        lse_ref[0, i0 : i0 + BLK, :] = jnp.where(left, logs[0], logs[1])


def attn_bwd_kernel(
    len_ref, qu, qv, k, v, pos, o, lse, do, dq_ref, dk_ref, dv_ref, dpos_ref, sum_ref, dkt, dvt, dpt,
    hook=None,
):
    count = len_ref[pl.program_id(0)]
    full = k.shape[1]
    scale = 1.0 / math.sqrt(DK)
    lane = lax.broadcasted_iota(jnp.int32, (BLK, 2 * DK), 1)
    left = lane < DK
    keep = lax.broadcasted_iota(jnp.int32, (BLK, full), 1) < count
    zero = jnp.zeros((), BF)
    flip = (lane + lax.broadcasted_iota(jnp.int32, (BLK, 2 * DK), 0) == BLK - 1).astype(F32).astype(BF)
    dkt[...] = jnp.zeros_like(dkt)
    dvt[...] = jnp.zeros_like(dvt)
    dpt[...] = jnp.zeros_like(dpt)
    sum_q = jnp.zeros((1, 2 * DK), F32)
    sum_u = jnp.zeros((1, 2 * DK), F32)
    sum_v = jnp.zeros((1, 2 * DK), F32)
    for blk in range(full // BLK):
        i0 = blk * BLK
        base = full - BLK - i0
        rows = slice(i0, i0 + BLK)
        win = slice(base, base + full + BLK)
        if hook is not None:
            hook(blk)
        qu_t = qu[0, rows, :].astype(F32).T.astype(BF)
        do_t = do[0, rows, :].astype(F32).T.astype(BF)
        qv_t = tn(qv[0, rows, :], flip).astype(BF)
        dot_o = do[0, rows, :].astype(F32) * o[0, rows, :].astype(F32)
        parts_u, parts_v = [], []
        for h in range(2):
            mine = left if h == 0 else lane >= DK
            hs = slice(h * DK, h * DK + DK)
            q_u = jnp.where(mine, qu[0, rows, :], zero)
            q_v = jnp.where(mine, qv[0, rows, :], zero)
            d_o = jnp.where(mine, do[0, rows, :], zero)
            rel = nt(q_v, pos[win, :])
            rel = pltpu.roll(rel, full + 1, 1, stride=1, stride_axis=0)[:, :full]
            s = (nt(q_u, k[0]) + rel) * scale - lse[0, rows, h * DK : h * DK + 1]
            p = jnp.where(keep, jnp.exp(jnp.minimum(s, 0.0)), 0.0)
            delta = jnp.sum(jnp.where(mine, dot_o, 0.0), axis=1, keepdims=True)
            ds = (p * (nt(d_o, v[0]) - delta)).astype(BF)
            dvt[hs, :] += nn(do_t[hs, :], p.astype(BF))
            dkt[hs, :] += nn(qu_t[hs, :], ds)
            parts_u.append(nn(ds, k[0]))
            wide = jnp.concatenate([nn(flip, ds), jnp.zeros((BLK, BLK), F32)], axis=1)
            wide = pltpu.roll(wide, 0, 1, stride=1, stride_axis=0).astype(BF)
            parts_v.append(nn(wide, pos[win, :]))
            dpt[hs, win] += nn(qv_t[hs, :], wide)
        d_u = jnp.where(left, parts_u[0], parts_u[1]) * scale
        d_v = jnp.where(left, parts_v[0], parts_v[1]) * scale
        high = d_v.astype(BF)
        low = (d_v - high.astype(F32)).astype(BF)
        d_q = (d_u + nn(flip, high) + nn(flip, low)).astype(BF)
        dq_ref[0, rows, :] = d_q
        sum_q += jnp.sum(d_q.astype(F32), axis=0, keepdims=True)
        sum_u += jnp.sum(d_u, axis=0, keepdims=True)
        sum_v += jnp.sum(d_v, axis=0, keepdims=True)
    dk_ref[0] = (dkt[...].T * scale).astype(BF)
    d_val = dvt[...].T.astype(BF)
    dv_ref[0] = d_val
    dpos_ref[0] = (dpt[...].T * scale).astype(BF)
    sum_ref[0, 0:1, :] = sum_q
    sum_ref[0, 1:2, :] = jnp.sum(d_val.astype(F32), axis=0, keepdims=True)
    sum_ref[0, 2:3, :] = sum_u
    sum_ref[0, 3:4, :] = sum_v
    sum_ref[0, 4:8, :] = jnp.zeros((4, 2 * DK), F32)


def attn_specs(rows, full, width):
    pairs = width // (2 * DK)
    main = pl.BlockSpec((1, full, 2 * DK), lambda u, p, n: (u, 0, p))
    pos = pl.BlockSpec((2 * full, 2 * DK), lambda u, p, n: (0, p))
    return (rows, pairs), main, pos


def attn_fwd_call(lens, qu, qv, k, v, pos):
    rows, full, width = qu.shape
    grid, main, pspec = attn_specs(rows, full, width)
    return pl.pallas_call(
        attn_fwd_kernel,
        grid_spec=pltpu.PrefetchScalarGridSpec(
            num_scalar_prefetch=1,
            grid=grid,
            in_specs=[main] * 4 + [pspec],
            out_specs=[main, main],
        ),
        out_shape=[
            jax.ShapeDtypeStruct((rows, full, width), BF),
            jax.ShapeDtypeStruct((rows, full, width), F32),
        ],
        compiler_params=dense_params(),
        name="attn_fwd",
    )(lens, qu, qv, k, v, pos)


def attn_bwd_call(lens, qu, qv, k, v, pos, o, lse, do, early=None, cid=None):
    rows, full, width = qu.shape
    grid, main, pspec = attn_specs(rows, full, width)
    args = [lens, qu, qv, k, v, pos, o, lse, do]
    in_specs = [main] * 4 + [pspec] + [main] * 3
    out_specs = [
        main,
        main,
        main,
        pl.BlockSpec((1, 2 * full, 2 * DK), lambda u, p, n: (u, 0, p)),
        pl.BlockSpec((1, 8, 2 * DK), lambda u, p, n: (u, 0, p)),
    ]
    scratch = [
        pltpu.VMEM((2 * DK, full), F32),
        pltpu.VMEM((2 * DK, full), F32),
        pltpu.VMEM((2 * DK, 2 * full), F32),
    ]
    out_shape = [jax.ShapeDtypeStruct((rows, full, width), BF)] * 3 + [
        jax.ShapeDtypeStruct((rows, 2 * full, width), BF),
        jax.ShapeDtypeStruct((rows, 8, width), F32),
    ]
    body, params = attn_bwd_kernel, dense_params()
    if early is not None:
        items = [split_owners(item) for item in early]
        pieces = pieces_of([item.shape[-1] for item in items])
        owned = items[0].shape[-2]
        n_in, n_out, m = len(args) - 1, len(out_shape), len(items)
        args += items
        in_specs += [ANY] * m
        out_specs.append(pl.BlockSpec((owned, C_OWN), lambda u, p, n: (0, 0)))
        out_shape.append(jax.ShapeDtypeStruct((owned, C_OWN), F32))
        scratch += scatter_scratch(pieces, owned)
        params = comm_params(cid)

        def body(*refs):
            at = pl.program_id(0) * grid[1] + pl.program_id(1)
            last = grid[0] * grid[1] - 1
            ins, rest = refs[: 1 + n_in], refs[1 + n_in :]
            g_refs, rest = rest[:m], rest[m:]
            mains, o_ref, rest = rest[:n_out], rest[n_out], rest[n_out + 1 :]
            own, sems = rest[:3], rest[3:]
            start, advance, finish, rounds = scatter_steps(pieces, g_refs, o_ref, sems, 2)
            peers = link_peers(*place())

            @pl.when(at == 0)
            def _():
                hail(peers)

            def begin():
                hear(peers)
                for p in range(len(pieces)):
                    start(p)

            steps = [begin] + [lambda q=q: advance(q) for q in range(rounds)]
            attn_bwd_kernel(*ins, *mains, *own, hook=hooks_of(steps, at, last, full // BLK))

            @pl.when(at == last)
            def _():
                finish()

    return pl.pallas_call(
        body,
        grid_spec=pltpu.PrefetchScalarGridSpec(
            num_scalar_prefetch=1,
            grid=grid,
            in_specs=in_specs,
            out_specs=out_specs,
            scratch_shapes=scratch,
        ),
        out_shape=out_shape,
        compiler_params=params,
        name="attn_bwd",
    )(*args)


def hooks_of(steps, at, last, spots):
    def hook(blk):
        for i, step in enumerate(steps):
            where, spot = divmod(i * (last + 1) * (spots - 1) // len(steps), spots - 1)
            if spot + 1 == blk:

                @pl.when(at == where)
                def _(step=step):
                    step()

    return hook


MESH = pl.DeviceIdType.MESH
NZ, NY, NX = 4, 2, 2
ANY = pl.BlockSpec(memory_space=pl.ANY)
VM = pl.BlockSpec(memory_space=pltpu.VMEM)


def own_mesh(sizes):
    return sizes == (NZ * NY * NX, 2)


def place():
    dp = lax.axis_index("dp")
    return dp // (NY * NX), dp // NX % NY, dp % NX, lax.axis_index("tensor")


def dev(z, y, x, t):
    return (z * (NY * NX) + y * NX + x, t)


def hail(peers):
    barrier = pltpu.get_barrier_semaphore()
    for peer in peers:
        pl.semaphore_signal(barrier, inc=1, device_id=peer, device_id_type=MESH)


def hear(peers):
    pl.semaphore_wait(pltpu.get_barrier_semaphore(), len(peers))


def rcopy(src, dst, send, recv, peer):
    return pltpu.make_async_remote_copy(
        src_ref=src, dst_ref=dst, send_sem=send, recv_sem=recv, device_id=peer, device_id_type=MESH
    )


def link_peers(z, y, x, t):
    peers = [dev(lax.rem(z + d, NZ), y, x, t) for d in range(1, NZ)]
    return peers + [dev(z, 1 - y, x, t), dev(z, y, 1 - x, t), dev(z, y, x, 1 - t)]


def sum_scratch(shape):
    dma = pltpu.SemaphoreType.DMA
    return [
        pltpu.VMEM(shape, F32), pltpu.VMEM(shape, F32), pltpu.VMEM((3,) + shape, F32),
        pltpu.VMEM((7,) + shape, F32), dma((3,)), dma((3,)), dma((7,)), dma((7,)),
    ]


def sum_steps(scratch):
    x_s, mid, b1, b2, s1, r1, s2, r2 = scratch
    z, y, x, t = place()
    spot = (y * NX + x) * 2 + t
    zs = [dev(lax.rem(z + d, NZ), y, x, t) for d in range(1, NZ)]
    flat = [lax.rem(spot + d, 8) for d in range(1, 8)]
    plane = [dev(z, p // 4, p // 2 % 2, p % 2) for p in flat]

    def call(wait=False):
        hear(zs + plane) if wait else hail(zs + plane)

    def meet(o_ref, heard=False):
        first = [rcopy(x_s, b1.at[i], s1.at[i], r1.at[i], peer) for i, peer in enumerate(zs)]
        second = [rcopy(mid, b2.at[i], s2.at[i], r2.at[i], peer) for i, peer in enumerate(plane)]

        def one():
            if not heard:
                hear(zs + plane)
            for copy in first:
                copy.start()

        def two():
            for copy in first:
                copy.wait_recv()
            mid[...] = (x_s[...] + b1[0]) + (b1[1] + b1[2])
            for copy in second:
                copy.start()

        def three():
            for copy in second:
                copy.wait_recv()
            total = mid[...]
            for i in range(7):
                total = total + b2[i]
            o_ref[...] = total
            for copy in first + second:
                copy.wait_send()

        return one, two, three

    return call, meet


def comm_params(cid):
    return pltpu.CompilerParams(
        collective_id=cid, has_side_effects=True, vmem_limit_bytes=60 * 1024 * 1024
    )


def gathered_shape(packed):
    return jax.ShapeDtypeStruct((2, NZ, NY, NX) + packed.shape, packed.dtype)


def gather_scratch(n, groups=3):
    dma = pltpu.SemaphoreType.DMA
    return [dma((n, NZ - 1)), dma((n, NZ - 1))] + [dma((n,))] * 6 + [dma((groups,))]


LEAD = 3


def gather_events(pieces, xs, gs, sems):
    zs, zr, as_, ar, bs, br, cs, cr, own_sem = sems
    z, y, x, t = place()
    along_x, along_y = dev(z, y, 1 - x, t), dev(z, 1 - y, x, t)
    zc, ac, bc, cc = [], [], [], []
    for p, (i, start, w) in enumerate(pieces):
        c = pl.ds(start, w)
        g = gs[i]
        zc.append(
            [
                rcopy(
                    xs[i].at[:, c],
                    g.at[t, z, y, x, :, c],
                    zs.at[p, d - 1],
                    zr.at[p, d - 1],
                    dev(lax.rem(z + d, NZ), y, x, t),
                )
                for d in range(1, NZ)
            ]
        )
        line = g.at[t, :, y, x, :, c]
        ac.append(rcopy(line, line, as_.at[p], ar.at[p], along_x if p % 2 == 0 else along_y))
        half = g.at[t, :, y, :, :, c] if p % 2 == 0 else g.at[t, :, :, x, :, c]
        bc.append(rcopy(half, half, bs.at[p], br.at[p], along_y if p % 2 == 0 else along_x))
        full = g.at[t, :, :, :, :, c]
        cc.append(rcopy(full, full, cs.at[p], cr.at[p], dev(z, y, x, 1 - t)))

    def begin():
        own = [
            pltpu.make_async_copy(item, g.at[t, z, y, x], own_sem.at[i])
            for i, (item, g) in enumerate(zip(xs, gs))
        ]
        for copy in own:
            copy.start()
        for copies in zc[: 2 * LEAD]:
            for copy in copies:
                copy.start()
        for copy in own:
            copy.wait()

    def event(kind, q):
        for p in (2 * q, 2 * q + 1):
            if kind == "z":
                for copy in zc[p]:
                    copy.wait_recv()
                ac[p].start()
                for copy in zc[p + 2 * LEAD] if p + 2 * LEAD < len(pieces) else []:
                    copy.start()
            elif kind == "a":
                ac[p].wait_recv()
                bc[p].start()
            elif kind == "b":
                bc[p].wait_recv()
                cc[p].start()
            else:
                cc[p].wait_recv()

    def finish():
        for copy in sum(zc, []) + ac + bc + cc:
            copy.wait_send()

    return begin, event, finish


def gather_order(pieces):
    unit = [0.42 * (pieces[2 * q][2] + pieces[2 * q + 1][2]) / 512 for q in range(len(pieces) // 2)]
    order, at = [], 3.0
    waiting = []
    for q, step in enumerate(unit):
        at += 8 * step
        waiting.append((at + 2.5, q, "z"))
    free = 0.0
    while waiting:
        waiting.sort()
        now, q, kind = waiting.pop(0)
        order.append((now, kind, q))
        if kind in "za":
            free = max(free, now) + (4 if kind == "z" else 8) * unit[q]
            waiting.append((free + 2.5, q, "a" if kind == "z" else "b"))
        elif kind == "b":
            waiting.append((now + 1.8, q, "c"))
    return order


def small_steps(s_ref, v_ref, mid, b1, b2, s1, r1, s2, r2):
    z, y, x, t = place()
    spot = (y * NX + x) * 2 + t
    zs = [dev(lax.rem(z + d, NZ), y, x, t) for d in range(1, NZ)]
    flat = [lax.rem(spot + d, 8) for d in range(1, 8)]
    plane = [dev(z, p // 4, p // 2 % 2, p % 2) for p in flat]
    first = [rcopy(s_ref, b1.at[i], s1.at[i], r1.at[i], peer) for i, peer in enumerate(zs)]
    second = [rcopy(mid, b2.at[i], s2.at[i], r2.at[i], peer) for i, peer in enumerate(plane)]

    def begin():
        for copy in first:
            copy.start()

    def spread():
        for copy in first:
            copy.wait_recv()
        mid[...] = (s_ref[...] + b1[0]) + (b1[1] + b1[2])
        for copy in second:
            copy.start()

    def finish():
        for copy in second:
            copy.wait_recv()
        same, other = mid[...].astype(F32), b2[0].astype(F32)
        for i in range(1, 7):
            if i % 2 == 1:
                same = same + b2[i].astype(F32)
            else:
                other = other + b2[i].astype(F32)
        low = jnp.where(t == 0, same, other)
        high = jnp.where(t == 0, other, same)
        v_ref[...] = jnp.zeros_like(v_ref)
        for q in range(4):
            r = S_NORM + 14 * q
            v_ref[0:14, 128 * q : 128 * q + 128] = low[r : r + 14] + high[r : r + 14]
        for i, part in enumerate((low, high)):
            for q in range(2):
                c = slice((2 * i + q) * 128, (2 * i + q) * 128 + 128)
                v_ref[R_ATT:R_CV, c] = part[S_ATT + 4 * q : S_ATT + 4 * q + 4]
                v_ref[R_CV:R_B1, c] = part[S_CV + 13 * q : S_CV + 13 * q + 13]
            for q in range(8):
                r, c = 2 * i + q // 4, slice(q % 4 * 128, q % 4 * 128 + 128)
                v_ref[R_B1 + r : R_B1 + r + 1, c] = part[S_B1 + q : S_B1 + q + 1]
                v_ref[R_B2 + r : R_B2 + r + 1, c] = part[S_B2 + q : S_B2 + q + 1]
        for copy in first + second:
            copy.wait_send()

    return plane, begin, spread, finish


S_B1, S_ATT, S_CV, S_B2, S_NORM, S_ALL = 0, 8, 16, 42, 50, 112


def lanes_of(n, offset):
    at = lax.broadcasted_iota(jnp.int32, (n, 128), 0) + offset
    return (lax.broadcasted_iota(jnp.int32, (n, 128), 1) == at).astype(F32)


def prep_kernel(
    f1i, f1o, pos, qkv, f2i, f2o, ci, out, co, b1, att, cv, b2, norm,
    pa_ref, pb_ref, pc_ref, slab_ref, table_ref, slab, first_s, second_s,
):
    def put(ref, name, value, shift=0):
        start = SEG[name][0] + shift
        ref[:, start : start + value.shape[1]] = value

    for ref, name, item in (
        (pa_ref, "f1i", f1i), (pa_ref, "f1o", f1o), (pa_ref, "pos", pos), (pc_ref, "f2i", f2i),
        (pc_ref, "f2o", f2o), (pb_ref, "out", out), (pb_ref, "co", co),
    ):
        put(ref, name, item[...])
    for k in range(3):
        put(pa_ref, "qkv", qkv[k], k * qkv.shape[2])
    for k in range(2):
        put(pb_ref, "ci", ci[:, k, :], k * ci.shape[2])
    z, y, x, t = place()
    dp = z * (NY * NX) + y * NX + x
    sel = lanes_of(8, dp * 8).astype(BF)
    slab[...] = jnp.zeros_like(slab)
    slab[S_B1 : S_B1 + 8] = nn(b1[...], sel)
    for q in range(2):
        slab[S_ATT + 4 * q : S_ATT + 4 * q + 4] = nn(att[:, q, :], sel)
        slab[S_CV + 13 * q : S_CV + 13 * q + 13] = tn(cv[q], sel)
    slab[S_B2 : S_B2 + 8] = nn(b2[...], sel)
    at = dp * 2 + t
    here = nn(norm[...], lanes_of(16, lax.rem(at, 8) * 16).astype(BF))
    for q in range(4):
        slab[S_NORM + 14 * q : S_NORM + 14 * q + 14] = here * (at // 8 == q).astype(F32)
    slab_ref[...] = slab[...].astype(BF)
    fill_table(table_ref, first_s, second_s)


def prep_call(items, smalls, full, width):
    rows = items[0].shape[0]
    return pl.pallas_call(
        prep_kernel,
        in_specs=[VM] * 14,
        out_specs=[VM] * 5,
        out_shape=[
            jax.ShapeDtypeStruct((rows, C_A), BF),
            jax.ShapeDtypeStruct((rows, C_B), BF),
            jax.ShapeDtypeStruct((rows, C_C), BF),
            jax.ShapeDtypeStruct((S_ALL, 128), BF),
            jax.ShapeDtypeStruct((2 * full, width), BF),
        ],
        scratch_shapes=[pltpu.VMEM((S_ALL, 128), F32)] + [pltpu.VMEM((32, width), F32)] * 2,
        name="prepare",
    )(*items, *smalls)


def split_owners(item):
    return item.reshape(2, NZ, NY, NX, item.shape[1] // (NZ * NY * NX), item.shape[2])


def pieces_of(widths, step=256):
    pieces, at = [], 0
    for i, w in enumerate(widths):
        pieces += [(i, k, min(step, w), at + k) for k in range(0, w, step)]
        at += w
    return pieces


def scatter_scratch(pieces, rows):
    n = len(pieces)
    total = sum(piece[2] for piece in pieces)
    dma = pltpu.SemaphoreType.DMA
    shape = (rows, total)
    return [
        pltpu.VMEM((NZ, NY, NX) + shape, BF),
        pltpu.VMEM((NZ, NY, NX) + shape, BF),
        pltpu.VMEM((NZ, 2) + shape, BF),
        pltpu.VMEM((NZ,) + shape, BF),
        pltpu.VMEM((NZ - 1,) + shape, BF),
    ] + [dma((n,))] * 7 + [dma((n, NZ - 1))] * 2


def scatter_steps(pieces, g_refs, o_ref, scratch, lag):
    own, rc, ra, rb, rz, lsem, cs, cr, as_, ar, bs, br, zs, zr = scratch
    z, y, x, t = place()
    along_x, along_y = dev(z, y, 1 - x, t), dev(z, 1 - y, x, t)
    mate = dev(z, y, x, 1 - t)
    count = len(pieces)
    bufs, lc, cc, ac, bc, zc = [], [], [], [], [], []
    for p, (i, start, w, at) in enumerate(pieces):
        c = pl.ds(at, w)
        g = pl.ds(start, w)
        b = dict(
            own=own.at[:, :, :, :, c], rc=rc.at[:, :, :, :, c], ra=ra.at[:, :, :, c],
            rb=rb.at[:, :, c], rz=rz.at[:, :, c],
        )
        bufs.append(b)
        even = p % 2 == 0
        lc.append(
            pltpu.make_async_copy(g_refs[i].at[t, :, :, :, :, g], b["own"], lsem.at[p])
        )
        cc.append(rcopy(g_refs[i].at[1 - t, :, :, :, :, g], b["rc"], cs.at[p], cr.at[p], mate))
        away = b["own"].at[:, 1 - y] if even else b["own"].at[:, :, 1 - x]
        ac.append(rcopy(away, b["ra"], as_.at[p], ar.at[p], along_y if even else along_x))
        line = b["own"].at[:, y, 1 - x] if even else b["own"].at[:, 1 - y, x]
        bc.append(rcopy(line, b["rb"], bs.at[p], br.at[p], along_x if even else along_y))
        zc.append([])
        for d in range(1, NZ):
            far = lax.rem(z + d, NZ)
            zc[p].append(
                rcopy(
                    b["own"].at[far, y, x], b["rz"].at[d - 1], zs.at[p, d - 1], zr.at[p, d - 1],
                    dev(far, y, x, t),
                )
            )

    def start(p):
        lc[p].start()
        cc[p].start()

    def advance(q):
        if q < count:
            lc[q].wait()
            cc[q].wait_recv()
            b = bufs[q]

            @pl.loop(0, NZ)
            def _(i):
                b["own"][i] = b["own"][i] + b["rc"][i]

            ac[q].start()
        p = q - lag
        if 0 <= p < count:
            ac[p].wait_recv()
            b = bufs[p]

            @pl.loop(0, NZ)
            def _(i):
                if p % 2 == 0:
                    b["own"][i, y] = b["own"][i, y] + b["ra"][i]
                else:
                    b["own"][i, :, x] = b["own"][i, :, x] + b["ra"][i]

            bc[p].start()
        p = q - 2 * lag
        if 0 <= p < count:
            bc[p].wait_recv()
            b = bufs[p]

            @pl.loop(0, NZ)
            def _(i):
                b["own"][i, y, x] = b["own"][i, y, x] + b["rb"][i]

            for copy in zc[p]:
                copy.start()
        p = q - 3 * lag
        if 0 <= p < count:
            for copy in zc[p]:
                copy.wait_recv()
            b = bufs[p]
            total = b["own"][z, y, x].astype(F32)
            for d in range(NZ - 1):
                total = total + b["rz"][d].astype(F32)
            o_ref[:, pieces[p][3] : pieces[p][3] + pieces[p][2]] = total

    def finish():
        for copy in cc + ac + bc + sum(zc, []):
            copy.wait_send()

    return start, advance, finish, count + 3 * lag


def small_sum_steps(parts, ext, scratch):
    acc_s, bc_, bz, bp, bm, sc, rc, sz, rz, sp, rp, sm, rm = scratch
    z, y, x, t = place()
    dp = z * (NY * NX) + y * NX + x
    half = acc_s.shape[0] // 2
    mine = pl.ds(pl.multiple_of(t * half, 8), half)
    mate = dev(z, y, x, 1 - t)
    spot = y * NX + x
    zp = [dev(lax.rem(z + d, NZ), y, x, t) for d in range(1, NZ)]
    flat = [lax.rem(spot + d, 4) for d in range(1, 4)]
    pp = [dev(z, p // 2, p % 2, t) for p in flat]
    one = rcopy(acc_s, bc_, sc, rc, mate)
    two = [rcopy(acc_s.at[mine], bz.at[i], sz.at[i], rz.at[i], peer) for i, peer in enumerate(zp)]
    three = [rcopy(bz.at[3], bp.at[i], sp.at[i], rp.at[i], peer) for i, peer in enumerate(pp)]
    four = rcopy(bp.at[3], bm, sm, rm, mate)

    def a():
        acc_s[...] = jnp.zeros_like(acc_s)
        total = parts[0][...]
        for part in parts[1:]:
            total = total + part[...]
        acc_s[0:R_ALL] = total
        one.start()

    def b():
        one.wait()
        acc_s[...] = acc_s[...] + bc_[...]
        for copy in two:
            copy.start()

    def c():
        for copy in two:
            copy.wait()
        bz[3] = (acc_s[mine] + bz[0]) + (bz[1] + bz[2])
        for copy in three:
            copy.start()

    def d():
        for copy in three:
            copy.wait()
        bp[3] = (bz[3] + bp[0]) + (bp[1] + bp[2])
        four.start()
        ext[mine] = bp[3]

    def e():
        four.wait()
        ext[pl.ds(pl.multiple_of((1 - t) * half, 8), half)] = bm[...]

    return pp, [a, b, c, d, e]


def small_sum_scratch(width):
    dma = pltpu.SemaphoreType.DMA
    return [
        pltpu.VMEM((R_SUM, width), F32), pltpu.VMEM((R_SUM, width), F32),
        pltpu.VMEM((4, R_SUM // 2, width), F32), pltpu.VMEM((4, R_SUM // 2, width), F32),
        pltpu.VMEM((R_SUM // 2, width), F32), dma, dma, dma((3,)), dma((3,)), dma((3,)), dma((3,)), dma, dma,
    ]


def finish_kernel(
    oa, ob, ext, f1i, f1o, b1, qkv, pos, out, att, ci, co, cv, f2i, f2o, b2, norm
):
    def take(ref, name):
        start = OWN.get(name, SEG[name][0])
        return ref[:, start : start + SEG[name][1]]

    f1i[...] = take(oa, "f1i")
    f1o[...] = take(oa, "f1o")
    pos[...] = take(oa, "pos")
    f2i[...] = take(ob, "f2i")
    f2o[...] = take(ob, "f2o")
    out[...] = take(ob, "out")
    co[...] = take(ob, "co")
    for ref, src, name in ((qkv, oa, "qkv"), (ci, ob, "ci")):
        start, w = OWN.get(name, SEG[name][0]), SEG[name][1]
        n = 3 if name == "qkv" else 2
        for k in range(n):
            part = src[:, start + k * w // n : start + (k + 1) * w // n]
            if name == "qkv":
                ref[k] = part
            else:
                ref[:, k, :] = part
    z, y, x, t = place()
    dp = z * (NY * NX) + y * NX + x
    sel = lanes_of(8, dp * 8)

    def own(v, pick):
        return lax.dot_general(
            v, pick, (((1,), (1,)), ((), ())), precision=lax.Precision.HIGHEST,
            preferred_element_type=F32,
        )

    for q in range(2):
        c = pl.ds(pl.multiple_of((2 * t + q) * 128, 128), 128)
        att[:, q, :] = own(ext[R_ATT:R_CV, c], sel)
        cv[q] = own(sel, ext[R_CV:R_B1, c])
    for o, at in ((b1, R_B1), (b2, R_B2)):
        for q in range(8):
            r, c = at + q // 4, slice(q % 4 * 128, q % 4 * 128 + 128)
            line = jnp.where(t == 0, ext[r : r + 1, c], ext[r + 2 : r + 3, c])
            o[q : q + 1, :] = own(line, sel)
    at = dp * 2 + t
    lane = pl.ds(pl.multiple_of(at // 8 * 128, 128), 128)
    norm[...] = own(ext[0:14, lane], lanes_of(16, lax.rem(at, 8) * 16))


def finish_call(oa, ob, ext, rows):
    shapes = [
        (rows, 1024), (rows, 1024), (8, 8), (3, rows, 256), (rows, 256), (rows, 256), (4, 2, 8),
        (rows, 2, 256), (rows, 256), (2, 8, 13), (rows, 1024), (rows, 1024), (8, 8), (14, 16),
    ]
    f1i, f1o, b1, qkv, pos, out, att, ci, co, cv, f2i, f2o, b2, norm = pl.pallas_call(
        finish_kernel,
        in_specs=[VM] * 3,
        out_specs=[VM] * 14,
        out_shape=[jax.ShapeDtypeStruct(shape, F32) for shape in shapes],
        name="own_gradients",
    )(oa, ob, ext)
    return (
        f1i, f1o.T, b1, qkv.transpose(1, 0, 2), pos, out.T, att, ci, co.T, cv.transpose(2, 0, 1),
        f2i, f2o.T, b2, norm,
    )

SEG = {
    "f1i": (0, 1024), "f1o": (1024, 1024), "pos": (2048, 256), "qkv": (2304, 768),
    "ci": (0, 512), "out": (512, 256), "co": (768, 256),
    "f2i": (0, 1024), "f2o": (1024, 1024),
}
C_A, C_B, C_C = 3072, 1024, 2048
OWN = {"f2i": 0, "f2o": 1024, "ci": 2048, "out": 2560, "co": 2816}
C_OWN = 3072
R_ATT, R_CV, R_B1, R_B2, R_ALL, R_SUM = 14, 18, 31, 35, 40, 48
TB = 256
HC = 256


def seg_spec(name, depth):
    start, width = SEG[name]
    return pl.BlockSpec(
        (2, depth, width), lambda i, *_: (0, 0, start // width), pipeline_mode=pl.Buffered(1)
    )


def whole(shape):
    zeros = (0,) * len(shape)
    return pl.BlockSpec(shape, lambda i, *_: zeros)


def tall(rows, width):
    return pl.BlockSpec((rows, width), lambda i, *_: (i, 0))


def sig(v):
    return 0.5 * jnp.tanh(0.5 * v) + 0.5


def row(ref, i):
    return ref[i : i + 1, :]


def col_sum(v):
    return jnp.sum(v, axis=0, keepdims=True)


def ln_stats(v):
    centered = v - jnp.mean(v, axis=1, keepdims=True)
    inv = lax.rsqrt(jnp.mean(centered * centered, axis=1, keepdims=True) + norm_eps)
    return centered * inv, inv


def ln_back(up, scaled, inv, gain):
    g = up * gain
    return inv * (
        g
        - jnp.mean(g, axis=1, keepdims=True)
        - scaled * jnp.mean(g * scaled, axis=1, keepdims=True)
    )


def bias_half(vecs, at, t):
    return jnp.concatenate([row(vecs, at + 2 * t), row(vecs, at + 2 * t + 1)], axis=1)


def row_mask(start, rows, count):
    at = start + lax.broadcasted_iota(jnp.int32, (rows, 1), 0)
    return (at < count).astype(F32)


def ffn1_kernel(
    x_ref, table, w_in, w_out, w_qkv, w_pos, vecs,
    first_ref, z_ref, qu_ref, qv_ref, k_ref, v_ref, pos_ref,
):
    x = x_ref[...].astype(F32)
    scaled, _ = ln_stats(x)
    hn = (scaled * row(vecs, 0) + row(vecs, 1)).astype(BF)
    half = w_in.shape[2]
    y = row(vecs, 2)
    for t in range(2):
        z = nn(hn, w_in[t]) + bias_half(vecs, R_B1, t)
        for j in range(half // HC):
            z_ref[:, (2 * j + t) * HC : (2 * j + t + 1) * HC] = z[:, j * HC : (j + 1) * HC].astype(BF)
        y = y + nt((z * sig(z)).astype(BF), w_out[t])
    first = x + 0.5 * y
    first_ref[...] = first
    scaled, _ = ln_stats(first)
    hn = (scaled * row(vecs, 3) + row(vecs, 4)).astype(BF)
    part = w_qkv.shape[2] // 3
    for t in range(2):
        c = slice(t * part, (t + 1) * part)
        proj = nn(hn, w_qkv[t])
        q = proj[:, :part] + vecs[R_ATT : R_ATT + 1, c]
        qu_ref[:, c] = (q + vecs[R_ATT + 2 : R_ATT + 3, c]).astype(BF)
        qv_ref[:, c] = (q + vecs[R_ATT + 3 : R_ATT + 4, c]).astype(BF)
        k_ref[:, c] = proj[:, part : 2 * part].astype(BF)
        v_ref[:, c] = (proj[:, 2 * part :] + vecs[R_ATT + 1 : R_ATT + 2, c]).astype(BF)
        pos_ref[:, c] = nn(table[...], w_pos[t]).astype(BF)


def dense_params(mib=60):
    return pltpu.CompilerParams(vmem_limit_bytes=mib * 1024 * 1024)


def ffn1_call(x, table, g, vecs):
    tokens, width = x.shape
    steps = tokens // TB
    places = tall(table.shape[0] // steps, width)
    return pl.pallas_call(
        ffn1_kernel,
        grid=(steps,),
        in_specs=[
            tall(TB, width), places, seg_spec("f1i", width), seg_spec("f1o", width),
            seg_spec("qkv", width), seg_spec("pos", width), whole(vecs.shape),
        ],
        out_specs=[tall(TB, width), tall(TB, 4 * width)] + [tall(TB, width)] * 4 + [places],
        out_shape=[
            jax.ShapeDtypeStruct((tokens, width), F32),
            jax.ShapeDtypeStruct((tokens, 4 * width), BF),
        ]
        + [jax.ShapeDtypeStruct((tokens, width), BF)] * 4
        + [jax.ShapeDtypeStruct(table.shape, BF)],
        compiler_params=dense_params(),
        name="ffn1_forward",
    )(x, table, g, g, g, g, vecs)


FRONT_PIECES = (
    [(0, at + 256 * j, 256) for j in range(4) for at in (0, 1024)]
    + [(0, 2048 + 256 * k, 256) for k in range(4)]
    + [(1, 256 * k, 256) for k in (2, 0, 1, 3)]
    + [(2, at + 256 * j, 256) for j in range(4) for at in (0, 1024)]
)


def front_call(lens, x, table, packed_a, packed_b, packed_c, slab, batch, cid):
    tokens, width = x.shape
    full = tokens // batch
    pairs = width // (2 * DK)
    chunks = SEG["f1i"][1] // HC
    first_head = chunks + 1
    steps = first_head + batch * pairs
    order = gather_order(FRONT_PIECES)
    dma = pltpu.SemaphoreType.DMA
    small = [
        pltpu.VMEM(slab.shape, BF), pltpu.VMEM((3,) + slab.shape, BF),
        pltpu.VMEM((7,) + slab.shape, BF), dma((3,)), dma((3,)), dma((7,)), dma((7,)),
    ]
    heads_shape = (batch, full, width)
    scratch = [
        pltpu.VMEM((2, NZ, NY, NX) + packed_a.shape, BF),
        pltpu.VMEM((tokens, width), F32),
        pltpu.VMEM((tokens, width), BF),
    ]
    scratch += [pltpu.VMEM(heads_shape, BF)] * 5 + [pltpu.VMEM(heads_shape, F32)]
    scratch += [pltpu.VMEM(table.shape, BF), dma((10,))]
    n_own = len(scratch)

    def body(
        len_ref, x_ref, table_ref, xa_ref, xb_ref, xc_ref, s_ref,
        ga_ref, gb_ref, gc_ref, vecs, first_ref, z_ref, qu_ref, qv_ref, k_ref, v_ref, pos_ref, mix_ref,
        lse_ref, *rest,
    ):
        i = pl.program_id(0)
        ga, y_s, hn_s, qu, qv, k, v, mix, lse, pos, out_sem = rest[:n_own]
        smalls = rest[n_own : n_own + len(small)]
        begin, event, finish = gather_events(
            FRONT_PIECES, (xa_ref, xb_ref, xc_ref), (ga, gb_ref, gc_ref), rest[n_own + len(small) :]
        )
        plane, s_begin, s_spread, s_finish = small_steps(s_ref, vecs, *smalls)
        z, y, xx, t = place()
        sources = (ga, y_s, qu, qv, k, v, pos, mix, lse)
        targets = (ga_ref, first_ref, qu_ref, qv_ref, k_ref, v_ref, pos_ref, mix_ref, lse_ref)
        copies = [
            pltpu.make_async_copy(a, b, out_sem.at[n])
            for n, (a, b) in enumerate(zip(sources, targets))
        ]
        done = [0]

        def until(q):
            while True:
                _, kind, pair = order[done[0]]
                done[0] += 1
                event(kind, pair)
                if (kind, pair) == ("c", q):
                    break

        def weight(t, start, w):
            return ga[t, :, :, :, :, start : start + w].reshape(width, w)

        @pl.when(i == 0)
        def _():
            peers = [dev(lax.rem(z + d, NZ), y, xx, t) for d in range(1, NZ)] + plane
            hail(peers)

            @pl.loop(0, tokens // TB)
            def _(r):
                here = pl.ds(pl.multiple_of(r * TB, TB), TB)
                y_s[here, :] = ln_stats(x_ref[here, :].astype(F32))[0]

            hear(peers)
            begin()
            s_begin()
            for n in range(4):
                event(*order[n][1:])
            s_spread()
            for n in range(4, 7):
                event(*order[n][1:])
            done[0] = 7
            s_finish()

            @pl.loop(0, tokens // TB)
            def _(r):
                here = pl.ds(pl.multiple_of(r * TB, TB), TB)
                hn_s[here, :] = (y_s[here, :] * row(vecs, 0) + row(vecs, 1)).astype(BF)
                y_s[here, :] = jnp.zeros((TB, width), F32) + row(vecs, 2)

        for j in range(chunks):

            @pl.when(i == j)
            def _(j=j):
                until(j)

        @pl.when(i < chunks)
        def _():
            at = pl.multiple_of(i * HC, HC)
            odd = lax.rem(i, 2) == 1
            @pl.loop(0, 2)
            def _(t):
                w_in = ga[t, :, :, :, :, pl.ds(at, HC)].reshape(width, HC)
                w_out = ga[t, :, :, :, :, pl.ds(1024 + at, HC)].reshape(width, HC)
                line = vecs[pl.ds(R_B1 + 2 * t + i // 2, 1), :]
                bias = jnp.where(odd, line[:, HC:], line[:, :HC])
                for k in range(tokens // TB):
                    here = slice(k * TB, (k + 1) * TB)
                    zf = nn(hn_s[here, :], w_in) + bias
                    z_ref[here, pl.ds(pl.multiple_of(t * HC, HC), HC)] = zf.astype(BF)
                    y_s[here, :] += nt((zf * sig(zf)).astype(BF), w_out)

        @pl.when(i == chunks)
        def _():

            @pl.loop(0, tokens // TB)
            def _(r):
                here = pl.ds(pl.multiple_of(r * TB, TB), TB)
                first = x_ref[here, :].astype(F32) + 0.5 * y_s[here, :]
                y_s[here, :] = first
                scaled, _ = ln_stats(first)
                hn_s[here, :] = (scaled * row(vecs, 3) + row(vecs, 4)).astype(BF)
            copies[1].start()
            until(chunks)
            part = width // 2
            for t in range(2):
                c = slice(t * part, (t + 1) * part)
                pos[:, c] = nn(table_ref[...], weight(t, SEG["pos"][0], part)).astype(BF)
            copies[6].start()
            until(chunks + 1)
            copies[0].start()
            at = SEG["qkv"][0]
            @pl.loop(0, 2)
            def _(t):
                c = pl.ds(pl.multiple_of(t * part, part), part)

                lines = vecs[R_ATT:R_CV, :]
                lines = jnp.where(t == 0, lines[:, :part], lines[:, part:])

                @pl.loop(0, batch)
                def _(u):
                    hn = hn_s[pl.ds(pl.multiple_of(u * full, full), full), :]
                    q = nn(hn, weight(t, at, part)) + lines[0:1]
                    qu[u, :, c] = (q + lines[2:3]).astype(BF)
                    qv[u, :, c] = (q + lines[3:4]).astype(BF)
                    k[u, :, c] = nn(hn, weight(t, at + part, part)).astype(BF)
                    val = nn(hn, weight(t, at + 2 * part, part))
                    v[u, :, c] = (val + lines[1:2]).astype(BF)
            for n in (2, 3, 4, 5):
                copies[n].start()

        left = order[done[0] :]
        base = order[done[0] - 1][0] + 6.0
        blocks = full // BLK
        spots = batch * pairs * blocks
        slots = [min(max(int((now + 2.0 - base) / 0.9), 0), spots) for now, _, _ in left]

        def hook(blk):
            for slot, (_, kind, pair) in zip(slots, left):
                if slot % blocks == blk and slot < spots:

                    @pl.when(i == first_head + slot // blocks)
                    def _(kind=kind, pair=pair):
                        event(kind, pair)

        @pl.when(i >= first_head)
        def _():
            n = i - first_head
            u = n // pairs
            c = pl.ds(pl.multiple_of(lax.rem(n, pairs) * (2 * DK), 2 * DK), 2 * DK)

            def view(ref):
                return ref.at[pl.ds(u, 1), :, c]

            attn_fwd_kernel(
                len_ref, view(qu), view(qv), view(k), view(v), pos.at[:, c], view(mix), view(lse),
                u, hook,
            )

        @pl.when(i == steps - 1)
        def _():
            copies[7].start()
            copies[8].start()
            for slot, (_, kind, pair) in zip(slots, left):
                if slot >= spots:
                    event(kind, pair)
            finish()
            for copy in copies:
                copy.wait()

    def const(shape):
        return pl.BlockSpec(shape, lambda i, n: (0,) * len(shape), pipeline_mode=pl.Buffered(1))

    heads = jax.ShapeDtypeStruct(heads_shape, BF)
    return pl.pallas_call(
        body,
        grid_spec=pltpu.PrefetchScalarGridSpec(
            num_scalar_prefetch=1,
            grid=(steps,),
            in_specs=[
                const(x.shape), const(table.shape), const(packed_a.shape), const(packed_b.shape),
                const(packed_c.shape), const(slab.shape),
            ],
            out_specs=[
                ANY, ANY, ANY, pl.BlockSpec((R_ALL, width), lambda i, n: (0, 0)), ANY,
                pl.BlockSpec((tokens, 2 * HC), lambda i, n: (0, jnp.minimum(i, chunks - 1))),
            ]
            + [ANY] * 7,
            scratch_shapes=scratch + small + gather_scratch(len(FRONT_PIECES)),
        ),
        out_shape=[
            gathered_shape(packed_a),
            gathered_shape(packed_b),
            gathered_shape(packed_c),
            jax.ShapeDtypeStruct((R_ALL, width), F32),
            jax.ShapeDtypeStruct((tokens, width), F32),
            jax.ShapeDtypeStruct((tokens, 4 * width), BF),
            heads, heads, heads, heads,
            jax.ShapeDtypeStruct(table.shape, BF),
            heads,
            jax.ShapeDtypeStruct(heads_shape, F32),
        ],
        compiler_params=comm_params(cid),
        name="front",
    )(lens, x, table, packed_a, packed_b, packed_c, slab)


def fill_table(table_ref, first_s, second_s):
    length, width = table_ref.shape[0] // 2, table_ref.shape[1]
    step = 32
    cols = lax.broadcasted_iota(jnp.int32, (step, width), 1)
    rows = lax.broadcasted_iota(jnp.int32, (step, width), 0)
    rate = jnp.exp((cols // 2 * 2).astype(F32) * (-math.log(10000.0) / width))
    even = cols % 2 == 0
    big = (length - 1 - step * rows).astype(F32) * rate
    small = rows.astype(F32) * rate
    sin_big, cos_big = jnp.sin(big), jnp.cos(big)
    first = jnp.where(even, sin_big, cos_big)
    second = jnp.where(even, cos_big, -sin_big)
    cos_small, sin_small = jnp.cos(small), jnp.sin(small)
    first_s[...] = first
    second_s[...] = second

    @pl.loop(0, 2 * length // step)
    def _(a):
        one, two = first_s[pl.ds(a, 1), :], second_s[pl.ds(a, 1), :]
        block = one * cos_small - two * sin_small
        table_ref[pl.ds(pl.multiple_of(a * step, step), step), :] = block.astype(BF)


def table_call(full, width):
    return pl.pallas_call(
        fill_table,
        out_specs=VM,
        out_shape=jax.ShapeDtypeStruct((2 * full, width), BF),
        scratch_shapes=[pltpu.VMEM((32, width), F32)] * 2,
        name="position_table",
    )()


def conv1_kernel(
    lens, mixed, first, w_out, w_ci, vecs, second_ref, half_ref, conv_ref, stat_ref, pad
):
    u = pl.program_id(0)
    full = first.shape[0]
    count = lens[u]
    part = w_out.shape[2]
    y = row(vecs, 5)
    for t in range(2):
        y = y + nt(mixed[:, t * part : (t + 1) * part], w_out[t])
    second = first[...] + y
    second_ref[...] = second
    scaled, _ = ln_stats(second)
    hn = (scaled * row(vecs, 6) + row(vecs, 7)).astype(BF)
    mask = row_mask(0, full, count)
    pad[0:8, :] = jnp.zeros((8, part), F32)
    pad[full + 8 : full + 16, :] = jnp.zeros((8, part), F32)
    for t in range(2):
        c = slice(t * part, (t + 1) * part)
        proj = nn(hn, w_ci[t])
        za = proj[:, :part] + vecs[R_CV : R_CV + 1, c]
        zg = proj[:, part:] + vecs[R_CV + 1 : R_CV + 2, c]
        half_ref[:, 2 * t * part : (2 * t + 1) * part] = za.astype(BF)
        half_ref[:, (2 * t + 1) * part : (2 * t + 2) * part] = zg.astype(BF)
        pad[8 : full + 8, :] = za * sig(zg) * mask
        total = jnp.zeros((full, part), F32)
        for k in range(9):
            total = total + vecs[R_CV + 4 + k : R_CV + 5 + k, c] * pad[4 + k : 4 + k + full, :]
        conv_ref[:, c] = total
        kept = total * mask
        stat_ref[pl.ds(4 * u, 1), c] = col_sum(kept)
        stat_ref[pl.ds(4 * u + 1, 1), c] = col_sum(kept * total)
    for k in (2, 3):
        stat_ref[pl.ds(4 * u + k, 1), :] = jnp.full((1, 2 * part), 1.0, F32) * count.astype(F32)


def with_sum(kernel, spot, cid):
    def body(*refs):
        sums = refs[-8:]
        refs = list(refs[:-8])
        call, meet = sum_steps(sums)
        out = refs[spot]
        refs[spot] = sums[0]

        @pl.when(pl.program_id(0) == 0)
        def _():
            call()

        kernel(*refs)

        @pl.when(pl.program_id(0) == pl.num_programs(0) - 1)
        def _():
            for part in meet(out):
                part()

    return kernel if cid is None else body


def conv1_call(lens, mixed, first, g, vecs, cid=None):
    tokens, width = first.shape
    batch = lens.shape[0]
    full = tokens // batch
    return pl.pallas_call(
        with_sum(conv1_kernel, 9, cid),
        grid_spec=pltpu.PrefetchScalarGridSpec(
            num_scalar_prefetch=1,
            grid=(batch,),
            in_specs=[
                tall(full, width), tall(full, width), seg_spec("out", width),
                seg_spec("ci", width), whole(vecs.shape),
            ],
            out_specs=[
                tall(full, width), tall(full, 2 * width), tall(full, width),
                whole((4 * batch, width)),
            ],
            scratch_shapes=[pltpu.VMEM((full + 16, width // 2), F32)]
            + ([] if cid is None else sum_scratch((4 * batch, width))),
        ),
        out_shape=[
            jax.ShapeDtypeStruct((tokens, width), F32),
            jax.ShapeDtypeStruct((tokens, 2 * width), BF),
            jax.ShapeDtypeStruct((tokens, width), F32),
            jax.ShapeDtypeStruct((4 * batch, width), F32),
        ],
        compiler_params=dense_params() if cid is None else comm_params(cid),
        name="conv_forward",
    )(lens, mixed, first, g, g, vecs)


def bn_of(stats, u):
    n = stats[pl.ds(4 * u + 2, 1), :]
    avg = stats[pl.ds(4 * u, 1), :] / n
    var = stats[pl.ds(4 * u + 1, 1), :] / n - avg * avg
    return avg, lax.rsqrt(var + norm_eps), n


def swish_parts(z):
    s = sig(z)
    a = z * s
    return a, s + a * (1.0 - s)


def middle_kernel(
    lens, second, conv, cot, stats, w_co, w_in, w_out, vecs,
    act_ref, d3_ref, dy_ref, sum_ref, small_ref, gi_ref, go_ref, gc_ref,
    a_s, slope_s, gi, go, gc,
):
    i = pl.program_id(0)
    steps = pl.num_programs(0)
    rows, width = second.shape
    batch = lens.shape[0]
    per = steps // batch
    u = i // per
    mask = row_mask(lax.rem(i, per) * rows, rows, lens[u])

    @pl.when(i == 0)
    def _():
        small_ref[...] = jnp.zeros_like(small_ref)
        sum_ref[...] = jnp.zeros_like(sum_ref)
        gi[...] = jnp.zeros_like(gi)
        go[...] = jnp.zeros_like(go)
        gc[...] = jnp.zeros_like(gc)

    avg, rstd, _ = bn_of(stats, u)
    part = w_co.shape[2]
    half = w_in.shape[2]
    yhat = (conv[...] - avg) * rstd
    bn, bn_slope = swish_parts(yhat * row(vecs, R_CV + 2) + row(vecs, R_CV + 3))
    act = bn.astype(BF)
    y = row(vecs, 8)
    for t in range(2):
        y = y + nt(act[:, t * part : (t + 1) * part], w_co[t])
    third = second[...] + y
    scaled9, inv9 = ln_stats(third)
    hn = (scaled9 * row(vecs, 9) + row(vecs, 10)).astype(BF)
    y = row(vecs, 11)
    for t in range(2):
        c = slice(t * half, (t + 1) * half)
        a, slope = swish_parts(nn(hn, w_in[t]) + bias_half(vecs, R_B2, t))
        a = a.astype(BF)
        a_s[:, c] = a
        slope_s[:, c] = slope
        y = y + nt(a, w_out[t])
    scaled, inv = ln_stats(third + 0.5 * y)
    act_ref[...] = (scaled * row(vecs, 12) + row(vecs, 13)).astype(BF)
    up = cot[...].astype(F32) * mask
    small_ref[12:13, :] += col_sum(up * scaled)
    small_ref[13:14, :] += col_sum(up)
    d4 = ln_back(up, scaled, inv, row(vecs, 12))
    g = (0.5 * d4).astype(BF)
    small_ref[11:12, :] += col_sum(g.astype(F32))
    d_hn = jnp.zeros((rows, width), F32)
    for t in range(2):
        c = slice(t * half, (t + 1) * half)
        go[t] += tn(g, a_s[:, c])
        dz = (nn(g, w_out[t]) * slope_s[:, c]).astype(BF)
        bias = col_sum(dz.astype(F32))
        small_ref[R_B2 + 2 * t : R_B2 + 2 * t + 1, :] += bias[:, :width]
        small_ref[R_B2 + 2 * t + 1 : R_B2 + 2 * t + 2, :] += bias[:, width:]
        gi[t] += tn(hn, dz)
        d_hn = d_hn + nt(dz, w_in[t])
    small_ref[9:10, :] += col_sum(d_hn * scaled9)
    small_ref[10:11, :] += col_sum(d_hn)
    d3 = d4 + ln_back(d_hn, scaled9, inv9, row(vecs, 9))
    d3_ref[...] = d3
    g = d3.astype(BF)
    small_ref[8:9, :] += col_sum(g.astype(F32))
    d_act = []
    for t in range(2):
        gc[t] += tn(g, act[:, t * part : (t + 1) * part])
        d_act.append(nn(g, w_co[t]))
    d_bn = jnp.concatenate(d_act, axis=1) * bn_slope
    small_ref[R_CV + 2 : R_CV + 3, :] += col_sum(d_bn * yhat)
    small_ref[R_CV + 3 : R_CV + 4, :] += col_sum(d_bn)
    d_yhat = d_bn * row(vecs, R_CV + 2)
    dy_ref[...] = d_yhat
    sum_ref[pl.ds(4 * u, 1), :] += col_sum(d_yhat)
    sum_ref[pl.ds(4 * u + 1, 1), :] += col_sum(d_yhat * yhat)

    @pl.when(i == steps - 1)
    def _():
        gi_ref[...] = gi[...].astype(BF)
        go_ref[...] = go[...].astype(BF)
        gc_ref[...] = gc[...].astype(BF)


def grad_shape(name, width):
    return jax.ShapeDtypeStruct((2, width, SEG[name][1]), BF)


def acc(name, width):
    return pltpu.VMEM((2, width, SEG[name][1]), F32)


def once(shape):
    zeros = (0,) * len(shape)
    return pl.BlockSpec(shape, lambda i, *_: zeros, pipeline_mode=pl.Buffered(1))


def middle_call(lens, second, conv, cot, stats, g, g_f2, vecs, cid=None):
    tokens, width = second.shape
    small = (R_ALL, width)
    names = ("f2i", "f2o", "co")
    return pl.pallas_call(
        with_sum(middle_kernel, 12, cid),
        grid_spec=pltpu.PrefetchScalarGridSpec(
            num_scalar_prefetch=1,
            grid=(tokens // TB,),
            in_specs=[tall(TB, width)] * 3
            + [whole(stats.shape), seg_spec("co", width), seg_spec("f2i", width)]
            + [seg_spec("f2o", width), whole(vecs.shape)],
            out_specs=[tall(TB, width)] * 3
            + [whole(stats.shape), whole(small)]
            + [whole(grad_shape(name, width).shape) for name in names],
            scratch_shapes=[
                pltpu.VMEM((TB, 4 * width), BF),
                pltpu.VMEM((TB, 4 * width), F32),
            ]
            + [acc(name, width) for name in names]
            + ([] if cid is None else sum_scratch(stats.shape)),
        ),
        out_shape=[
            jax.ShapeDtypeStruct((tokens, width), BF),
            jax.ShapeDtypeStruct((tokens, width), F32),
            jax.ShapeDtypeStruct((tokens, width), F32),
            jax.ShapeDtypeStruct(stats.shape, F32),
            jax.ShapeDtypeStruct(small, F32),
        ]
        + [grad_shape(name, width) for name in names],
        compiler_params=dense_params() if cid is None else comm_params(cid),
        name="conv_out_ffn2",
    )(lens, second, conv, cot, stats, g, g_f2, g_f2, vecs)


def conv2_kernel(
    lens, dy, conv, d3, halves, second, mixed, stats, sums, w_ci, w_out, vecs,
    d2_ref, dm_ref, small_ref, gi_ref, go_ref, pad, dh_s, gi, go,
):
    u = pl.program_id(0)
    full, width = d3.shape
    part = w_out.shape[2]

    @pl.when(u == 0)
    def _():
        small_ref[...] = jnp.zeros_like(small_ref)
        gi[...] = jnp.zeros_like(gi)
        go[...] = jnp.zeros_like(go)

    avg, rstd, n = bn_of(stats, u)
    mask = row_mask(0, full, lens[u])
    scaled, inv = ln_stats(second[...])
    hn = (scaled * row(vecs, 6) + row(vecs, 7)).astype(BF)
    pad[0:8, :] = jnp.zeros((8, part), F32)
    pad[full + 8 : full + 16, :] = jnp.zeros((8, part), F32)
    b1 = sums[pl.ds(4 * u, 1), :]
    b2 = sums[pl.ds(4 * u + 1, 1), :]
    dh_s[...] = jnp.zeros_like(dh_s)
    taps = vecs[R_CV : R_CV + 13, :]

    @pl.loop(0, 2)
    def _(t):
        c = pl.ds(pl.multiple_of(t * part, part), part)

        def lanes(v):
            return jnp.where(t == 0, v[:, :part], v[:, part:])

        yhat = (conv[:, c] - lanes(avg)) * lanes(rstd)
        pad[8 : full + 8, :] = lanes(rstd) * (
            dy[:, c] - mask * ((lanes(b1) + yhat * lanes(b2)) / lanes(n))
        )
        za = halves[:, pl.ds(pl.multiple_of(2 * t * part, part), part)].astype(F32)
        zg = halves[:, pl.ds(pl.multiple_of((2 * t + 1) * part, part), part)].astype(F32)
        gate = sig(zg)
        gated = za * gate * mask
        total = jnp.zeros((full, part), F32)
        mine = lanes(taps)
        for k in range(9):
            moved = pad[12 - k : 12 - k + full, :]
            total = total + mine[4 + k : 5 + k, :] * moved
            small_ref[R_CV + 4 + k : R_CV + 5 + k, c] += col_sum(gated * moved)
        d_glu = total * mask
        d_a = (d_glu * gate).astype(BF)
        d_g = (d_glu * gated * (1.0 - gate)).astype(BF)
        small_ref[R_CV : R_CV + 1, c] += col_sum(d_a.astype(F32))
        small_ref[R_CV + 1 : R_CV + 2, c] += col_sum(d_g.astype(F32))
        pair = jnp.concatenate([d_a, d_g], axis=1)
        gi[t] += tn(hn, pair)
        dh_s[...] += nt(pair, w_ci[t])

    d_hn = dh_s[...]
    small_ref[6:7, :] += col_sum(d_hn * scaled)
    small_ref[7:8, :] += col_sum(d_hn)
    d2 = d3[...] + ln_back(d_hn, scaled, inv, row(vecs, 6))
    d2_ref[...] = d2
    g = d2.astype(BF)
    small_ref[5:6, :] += col_sum(g.astype(F32))
    @pl.loop(0, 2)
    def _(t):
        c = pl.ds(pl.multiple_of(t * part, part), part)
        go[t] += tn(g, mixed[:, c])
        dm_ref[:, c] = nn(g, w_out[t]).astype(BF)

    @pl.when(u == pl.num_programs(0) - 1)
    def _():
        gi_ref[...] = gi[...].astype(BF)
        go_ref[...] = go[...].astype(BF)


def conv2_call(lens, dy, conv, d3, halves, second, mixed, stats, sums, g, vecs):
    tokens, width = second.shape
    batch = lens.shape[0]
    full = tokens // batch
    small = (R_ALL, width)
    names = ("ci", "out")
    return pl.pallas_call(
        conv2_kernel,
        grid_spec=pltpu.PrefetchScalarGridSpec(
            num_scalar_prefetch=1,
            grid=(batch,),
            in_specs=[tall(full, width)] * 3
            + [tall(full, 2 * width), tall(full, width), tall(full, width)]
            + [whole(stats.shape)] * 2
            + [seg_spec("ci", width), seg_spec("out", width), whole(vecs.shape)],
            out_specs=[tall(full, width)] * 2
            + [whole(small)]
            + [whole(grad_shape(name, width).shape) for name in names],
            scratch_shapes=[
                pltpu.VMEM((full + 16, width // 2), F32), pltpu.VMEM((full, width), F32),
            ]
            + [acc(name, width) for name in names],
        ),
        out_shape=[
            jax.ShapeDtypeStruct((tokens, width), F32),
            jax.ShapeDtypeStruct((tokens, width), BF),
            jax.ShapeDtypeStruct(small, F32),
        ]
        + [grad_shape(name, width) for name in names],
        compiler_params=dense_params(),
        name="conv_backward",
    )(lens, dy, conv, d3, halves, second, mixed, stats, sums, g, g, vecs)


def last_kernel(
    dq, dk, dv, first, x_ref, d2, z_ref, table, dpos, asums, w_qkv, w_in, w_out, vecs,
    d0_ref, small_ref, d1_s, g_s, hn_s, dh_s, gq, gp, z_s, w_in_s, w_out_s, in_sem,
    put, ready, after,
):
    i = pl.program_id(0)
    blocks = x_ref.shape[0] // TB
    rows, width = first.shape
    part = w_qkv.shape[2] // 3
    ahead = [
        pltpu.make_async_copy(w_in.at[:, :, pl.ds(0, w_in_s.shape[2])], w_in_s, in_sem.at[0]),
        pltpu.make_async_copy(
            w_out.at[:, :, pl.ds(w_in_s.shape[2], w_in_s.shape[2])], w_out_s, in_sem.at[1]
        ),
        pltpu.make_async_copy(z_ref, z_s, in_sem.at[2]),
    ]

    @pl.when(i == 0)
    def _():
        small_ref[...] = jnp.zeros_like(small_ref)
        small_ref[R_ATT:R_CV, :] = jnp.sum(asums[...], axis=0)[0:4]
        for copy in ahead:
            copy.start()
        gq[...] = jnp.zeros_like(gq)
        gp[...] = jnp.zeros_like(gp)
        dh_s[...] = jnp.zeros_like(dh_s)

    @pl.when(i < blocks)
    def _():
        here = pl.ds(pl.multiple_of(i * TB, TB), TB)
        scaled, inv = ln_stats(first[...])
        hn = (scaled * row(vecs, 3) + row(vecs, 4)).astype(BF)
        d_hn = jnp.zeros((rows, width), F32)
        for t in range(2):
            c = slice(t * part, (t + 1) * part)
            dp = jnp.concatenate([dq[:, c], dk[:, c], dv[:, c]], axis=1)
            gq[t] += tn(hn, dp)
            for u in range(dpos.shape[0]):
                gp[t] += tn(table[...], dpos[u, :, c])
            d_hn = d_hn + nt(dp, w_qkv[t])
        small_ref[3:4, :] += col_sum(d_hn * scaled)
        small_ref[4:5, :] += col_sum(d_hn)
        d1 = d2[...] + ln_back(d_hn, scaled, inv, row(vecs, 3))
        d1_s[here, :] = d1
        g = (0.5 * d1).astype(BF)
        g_s[here, :] = g
        small_ref[2:3, :] += col_sum(g.astype(F32))
        scaled, inv = ln_stats(x_ref[here, :].astype(F32))
        hn_s[here, :] = (scaled * row(vecs, 0) + row(vecs, 1)).astype(BF)

    @pl.when(i == blocks - 1)
    def _():
        for t in range(2):
            put("pos", t, 0, gp[t])
            put("qkv", t, 0, gq[t])
        for copy in ahead:
            copy.wait()
        ready(-1)

    chunks = w_in_s.shape[2] // HC

    @pl.when(i >= blocks)
    def _():
        j = i - blocks
        at = pl.multiple_of(j * HC, HC)
        c = pl.ds(at, HC)
        odd = lax.rem(j, 2) == 1
        @pl.loop(0, 2)
        def _(t):
            zc = pl.ds(pl.multiple_of((2 * j + t) * HC, HC), HC)
            a, slope = swish_parts(z_s[:, zc].astype(F32))
            put("f1o", t, at, tn(g_s[...], a.astype(BF)))
            dz = (nn(g_s[...], w_out_s[t, :, c]) * slope).astype(BF)
            bias = col_sum(dz.astype(F32))
            none = jnp.zeros_like(bias)
            pair = [jnp.where(odd, none, bias), jnp.where(odd, bias, none)]
            line = pl.ds(R_B1 + 2 * t + j // 2, 1)
            small_ref[line, :] += jnp.concatenate(pair, axis=1)
            put("f1i", t, at, tn(hn_s[...], dz))
            dh_s[...] += nt(dz, w_in_s[t, :, c])
            for k in range(chunks):
                for side in range(2):

                    @pl.when((j == k) & (t == side))
                    def _(k=k, side=side):
                        after(k, side)

        for k in range(chunks):

            @pl.when(j == k)
            def _(k=k):
                ready(k)

    @pl.when(i == blocks + chunks - 1)
    def _():
        @pl.loop(0, blocks)
        def _(k):
            here = pl.ds(pl.multiple_of(k * TB, TB), TB)
            scaled, inv = ln_stats(x_ref[here, :].astype(F32))
            d_hn = dh_s[here, :]
            small_ref[0:1, :] += col_sum(d_hn * scaled)
            small_ref[1:2, :] += col_sum(d_hn)
            d0 = d1_s[here, :] + ln_back(d_hn, scaled, inv, row(vecs, 0))
            d0_ref[here, :] = d0.astype(BF)


def last_call(dq, dk, dv, first, x, d2, z, table, dpos, asums, g, vecs, others=None, cid=None):
    tokens, width = first.shape
    blocks, chunks = tokens // TB, SEG["f1i"][1] // HC
    small = (R_ALL, width)
    places = table.shape[0] // blocks

    def block(rows, cols):
        return pl.BlockSpec((rows, cols), lambda i: (jnp.minimum(i, blocks - 1), 0))

    in_specs = (
        [block(TB, width)] * 4
        + [whole(x.shape), block(TB, width)]
        + [ANY]
        + [block(places, width)]
        + [
            pl.BlockSpec(
                (dpos.shape[0], places, width), lambda i: (0, jnp.minimum(i, blocks - 1), 0)
            ),
            whole(asums.shape),
        ]
        + [seg_spec("qkv", width), ANY, ANY, whole(vecs.shape)]
    )
    args = [dq, dk, dv, first, x, d2, z, table, dpos, asums, g, g, g, vecs]
    scratch = [
        pltpu.VMEM((tokens, width), F32), pltpu.VMEM((tokens, width), BF),
        pltpu.VMEM((tokens, width), BF), pltpu.VMEM((tokens, width), F32),
        acc("qkv", width), acc("pos", width), pltpu.VMEM(z.shape, BF),
        pltpu.VMEM((2, width, SEG["f1i"][1]), BF), pltpu.VMEM((2, width, SEG["f1o"][1]), BF),
        pltpu.SemaphoreType.DMA((3,)),
    ]
    out_specs = [whole((tokens, width)), whole(small)]
    out_shape = [jax.ShapeDtypeStruct((tokens, width), BF), jax.ShapeDtypeStruct(small, F32)]
    n_own = len(scratch)
    if others is None:
        names = ("qkv", "f1i", "f1o", "pos")
        out_specs += [once(grad_shape(name, width).shape) for name in names]
        out_shape += [grad_shape(name, width) for name in names]

        def body(*refs):
            ins, rest = refs[: len(args)], refs[len(args) :]
            outs = dict(zip(names, rest[2:6]))

            def put(name, t, at, value):
                outs[name][t, :, pl.ds(at, value.shape[1])] = value.astype(BF)

            last_kernel(*ins, *rest[:2], *rest[6:], put, lambda j: None, lambda j, t: None)

        params = dense_params()
    else:
        owned = width // (NZ * NY * NX)
        names = ("pos", "qkv", "f1i", "f1o")
        base = {name: SEG[name][0] for name in names}
        order = [("pos", 0), ("qkv", 0), ("qkv", 256), ("qkv", 512)]
        for j in range(chunks):
            order += [("f1i", j * HC), ("f1o", j * HC)]
        pieces = [(0, base[name] + at, 256, base[name] + at) for name, at in order]
        n_first = 4
        n_in = len(args)
        args += list(others)
        in_specs += [whole(item.shape) for item in others]
        out_specs = out_specs[:1] + [whole((owned, C_A)), whole((R_SUM, width))]
        out_shape = out_shape[:1] + [
            jax.ShapeDtypeStruct((owned, C_A), F32), jax.ShapeDtypeStruct((R_SUM, width), F32)
        ]
        small_scratch = small_sum_scratch(width)
        scratch += [pltpu.VMEM(small, F32), pltpu.VMEM((2, NZ, NY, NX, owned, C_A), BF)]
        scratch += small_scratch + scatter_scratch(pieces, owned)
        params = comm_params(cid)

        def body(*refs):
            i = pl.program_id(0)
            ins, rest = refs[:n_in], refs[n_in:]
            parts, rest = rest[: len(others)], rest[len(others) :]
            (d0_ref, o_ref, ext), rest = rest[:3], rest[3:]
            own, rest = rest[:n_own], rest[n_own:]
            (small_ref, buf), rest = rest[:2], rest[2:]
            sums, sems = rest[: len(small_scratch)], rest[len(small_scratch) :]
            start, advance, finish, rounds = scatter_steps(pieces, [buf], o_ref, sems, 4)
            pp, small_list = small_sum_steps(list(parts) + [small_ref], ext, sums)
            z, y, x, t = place()

            def put(name, t, at, value):
                w = value.shape[1]
                at = base[name] + at
                at = at if isinstance(at, int) else pl.multiple_of(at, HC)
                value = value.astype(BF).reshape(NZ, NY, NX, owned, w)
                buf[t, :, :, :, :, pl.ds(at, w)] = value

            def ready(j):
                if j < 0:
                    hear(peers)
                for p in range(n_first) if j < 0 else (n_first + 2 * j, n_first + 2 * j + 1):
                    start(p)

            def after(j, t):
                if j == 0:
                    advance(2 * t)
                    advance(2 * t + 1)
                else:
                    advance(n_first + 2 * (j - 1) + t)

            peers = link_peers(z, y, x, t)[: NZ - 1] + pp + [dev(z, y, x, 1 - t)]

            @pl.when(i == 0)
            def _():
                hail(peers)

            last_kernel(*ins, d0_ref, small_ref, *own, put, ready, after)

            @pl.when(i == blocks + chunks - 1)
            def _():
                todo = [lambda q=q: advance(q) for q in range(n_first + 2 * (chunks - 1), rounds)]
                for k, step in enumerate(todo):
                    if k % 2 == 0 and k // 2 < len(small_list):
                        small_list[k // 2]()
                    step()
                for step in small_list[(len(todo) + 1) // 2 :]:
                    step()
                finish()

    return pl.pallas_call(
        body,
        grid=(blocks + chunks,),
        in_specs=in_specs,
        out_specs=out_specs,
        scratch_shapes=scratch,
        out_shape=out_shape,
        compiler_params=params,
        name="qkv_ffn1_backward",
    )(*args)


def gather_plain(big, kinds, groups, small_ins, both, n_dp):
    def pack(names):
        return jnp.concatenate(
            [big[n].T if kinds[n][0] == "flip" else big[n] for n in names], axis=1
        )

    def every(item):
        g = lax.all_gather(item, both, axis=0, tiled=True)
        g = g.reshape(n_dp, 2, item.shape[0], -1).transpose(1, 0, 2, 3)
        return g.reshape(2, n_dp * item.shape[0], -1)

    small = jnp.concatenate([item.reshape(-1) for item in small_ins])
    smalls = lax.all_gather(small, both, axis=0, tiled=False).reshape(n_dp, 2, -1).astype(F32)
    off = 0
    pieces = []
    for item in small_ins:
        pieces.append(smalls[:, :, off : off + item.size].reshape((n_dp, 2) + item.shape))
        off += item.size
    width = small_ins[4].shape[1] * n_dp * 2
    vecs = jnp.concatenate(
        [
            pieces[4].transpose(2, 0, 1, 3).reshape(-1, width),
            pieces[1].transpose(2, 1, 3, 0, 4).reshape(-1, width),
            pieces[2].transpose(2, 1, 3, 0, 4).reshape(-1, width),
            pieces[0].transpose(1, 2, 0, 3).reshape(-1, width),
            pieces[3].transpose(1, 2, 0, 3).reshape(-1, width),
            jnp.zeros((1, width), F32),
        ],
        axis=0,
    )
    return tuple(every(pack(names)) for names in groups) + (vecs,)


def scatter_plain(grads, kinds, names, small_g, small_ins, both, n_dp):
    vec_g = (
        small_g[R_B1:R_B2].reshape(1, -1), small_g[R_ATT:R_CV], small_g[R_CV:R_B1],
        small_g[R_B2 : R_B2 + 4].reshape(1, -1),
    )

    def small_of(item, like):
        item = item.reshape(item.shape[0], 2, like.shape[-2], n_dp, like.shape[-1])
        return item.transpose(1, 3, 0, 2, 4).reshape(2, n_dp, -1)

    cols = small_ins[4].shape[1]
    norm_g = small_g[:R_ATT].reshape(-1, n_dp, 2, cols).transpose(2, 1, 0, 3).reshape(2, n_dp, -1)
    packed = jnp.concatenate(
        [small_of(item, like) for item, like in zip(vec_g, small_ins)] + [norm_g], axis=2
    )
    packed = packed.swapaxes(0, 1).reshape(n_dp * 2, -1)
    own_small = lax.psum_scatter(packed, both, scatter_dimension=0, tiled=True).reshape(-1)
    wide = jnp.concatenate([grads[name] for name in names], axis=2)
    rows = wide.shape[1] // n_dp
    wide = wide.reshape(2, n_dp, rows, -1).swapaxes(0, 1).reshape(n_dp * 2 * rows, -1)
    own = lax.psum_scatter(wide, both, scatter_dimension=0, tiled=True).astype(F32)
    outs, at = {}, 0
    for name in names:
        w = grads[name].shape[2]
        item = own[:, at : at + w]
        outs[name] = item.T if kinds[name][0] == "flip" else item
        at += w
    small_outs, at = [], 0
    for item in small_ins:
        small_outs.append(own_small[at : at + item.size].reshape(item.shape))
        at += item.size
    return outs, small_outs


def local(
    frames,
    lengths,
    ffn1_in,
    ffn1_out,
    ffn1_bias,
    qkv_weight,
    pos_weight,
    out_weight,
    attn_bias,
    conv_in,
    conv_out,
    conv_channel,
    ffn2_in,
    ffn2_out,
    ffn2_bias,
    norm_params,
    cotangent,
):
    micro, seqs, full, width = frames.shape
    both = ("dp", "tensor")
    n_dp = lax.axis_size("dp")
    rows = ffn1_in.shape[0]
    batch = micro * seqs
    tokens = batch * full
    small_ins = (ffn1_bias, attn_bias, conv_channel, ffn2_bias, norm_params)
    names_a, names_b = ("f1i", "f1o", "pos", "qkv"), tuple(OWN)
    big = {
        "f1i": ffn1_in, "f1o": ffn1_out, "pos": pos_weight, "qkv": qkv_weight.reshape(rows, -1),
        "f2i": ffn2_in, "f2o": ffn2_out, "ci": conv_in.reshape(rows, -1), "out": out_weight,
        "co": conv_out,
    }
    kinds = {name: ("plain",) for name in big}
    kinds.update({name: ("flip",) for name in ("f1o", "f2o", "out", "co")})
    mine_mesh = own_mesh((n_dp, lax.axis_size("tensor"))) and rows % 16 == 0
    if mine_mesh:
        packed_a, packed_b, packed_c, slab, table = prep_call(
            [
                ffn1_in, ffn1_out.T, pos_weight, qkv_weight.transpose(1, 0, 2), ffn2_in,
                ffn2_out.T, conv_in, out_weight.T, conv_out.T,
            ],
            [ffn1_bias, attn_bias, conv_channel.transpose(1, 2, 0), ffn2_bias, norm_params],
            full, width,
        )
    else:
        table = table_call(full, width)
        groups = (names_a, names_b[2:], names_b[:2])
        g_a, g_b, g_c, vecs = gather_plain(big, kinds, groups, small_ins, both, n_dp)

    def reduce_sum(item):
        return item if mine_mesh else lax.psum(item, both)

    mine = lax.axis_index("tensor")
    lens = lax.dynamic_slice_in_dim(lengths, mine * seqs, seqs, 1).reshape(-1)
    x = frames.reshape(tokens, width)
    cot = cotangent.reshape(tokens, width)

    def utt(item):
        return item.reshape(batch, full, -1)

    def flat(item):
        return item.reshape(tokens, -1)

    if mine_mesh:
        g_a, g_b, g_c, vecs, first, z1, q_u, q_v, keys, values, pos, mixed, lse = front_call(
            lens, x, table, packed_a, packed_b, packed_c, slab, batch, 1
        )
        g_a, g_b, g_c = (item.reshape(2, width, -1) for item in (g_a, g_b, g_c))
        heads = (lens, q_u, q_v, keys, values, pos)
    else:
        first, z1, q_u, q_v, keys, values, pos = ffn1_call(x, table, g_a, vecs)
        heads = (lens, utt(q_u), utt(q_v), utt(keys), utt(values), pos)
        mixed, lse = attn_fwd_call(*heads)
    second, halves, conv, stats = conv1_call(
        lens, flat(mixed), first, g_b, vecs, 3 if mine_mesh else None
    )
    stats = reduce_sum(stats)
    grads = {}
    result, d3, d_yhat, sums, small_m, grads["f2i"], grads["f2o"], grads["co"] = middle_call(
        lens, second, conv, cot, stats, g_b, g_c, vecs, 4 if mine_mesh else None
    )
    sums = reduce_sum(sums)
    d2, d_mixed, small_c, grads["ci"], grads["out"] = conv2_call(
        lens, d_yhat, conv, d3, halves, second, flat(mixed), stats, sums, g_b, vecs
    )
    if mine_mesh:
        dq, dk, dv, dpos, asums, own_b = attn_bwd_call(
            *heads, mixed, lse, utt(d_mixed), [grads[name] for name in names_b], 5
        )
        d0, own_a, ext = last_call(
            flat(dq), flat(dk), flat(dv), first, x, d2, z1, table, dpos, asums, g_a, vecs,
            (small_m, small_c), 6,
        )
        outs = finish_call(own_a, own_b, ext, rows)
    else:
        dq, dk, dv, dpos, asums = attn_bwd_call(*heads, mixed, lse, utt(d_mixed))
        d0, small_l, grads["qkv"], grads["f1i"], grads["f1o"], grads["pos"] = last_call(
            flat(dq), flat(dk), flat(dv), first, x, d2, z1, table, dpos, asums, g_a, vecs
        )
        o, small_outs = scatter_plain(
            grads, kinds, names_a + names_b, small_m + small_c + small_l, small_ins, both, n_dp
        )
        outs = (
            o["f1i"], o["f1o"], small_outs[0], o["qkv"].reshape(qkv_weight.shape), o["pos"],
            o["out"], small_outs[1], o["ci"].reshape(conv_in.shape), o["co"], small_outs[2],
            o["f2i"], o["f2o"], small_outs[3], small_outs[4],
        )
    return (result.reshape(frames.shape), d0.reshape(frames.shape)) + tuple(outs)


def solution(mesh):
    in_specs = (
        P(None, ("dp", "tensor"), None, None),
        P(None, "dp"),
        P("dp", "tensor"),
        P("tensor", "dp"),
        P("tensor", "dp"),
        P("dp", None, "tensor"),
        P("dp", "tensor"),
        P("tensor", "dp"),
        P(None, "tensor", "dp"),
        P("dp", None, "tensor"),
        P("tensor", "dp"),
        P(None, "tensor", "dp"),
        P("dp", "tensor"),
        P("tensor", "dp"),
        P("tensor", "dp"),
        P(None, ("dp", "tensor")),
        P(None, ("dp", "tensor"), None, None),
    )
    out_specs = (
        P(None, ("dp", "tensor"), None, None),
        P(None, ("dp", "tensor"), None, None),
        P("dp", "tensor"),
        P("tensor", "dp"),
        P("tensor", "dp"),
        P("dp", None, "tensor"),
        P("dp", "tensor"),
        P("tensor", "dp"),
        P(None, "tensor", "dp"),
        P("dp", None, "tensor"),
        P("tensor", "dp"),
        P(None, "tensor", "dp"),
        P("dp", "tensor"),
        P("tensor", "dp"),
        P("tensor", "dp"),
        P(None, ("dp", "tensor")),
    )
    return jax.shard_map(local, mesh=mesh, in_specs=in_specs, out_specs=out_specs, check_vma=False)
```

```python
import math

import jax
import jax.numpy as jnp
from jax import lax
from jax.experimental import pallas as pl
from jax.experimental.pallas import tpu as pltpu
from jax.sharding import PartitionSpec as P

DK = 64
norm_eps = 1e-05
mask_fill = -1000000000.0
BF = jnp.bfloat16
F32 = jnp.float32
BLK = 128


def nn(a, b):
    return lax.dot_general(a, b, (((1,), (0,)), ((), ())), preferred_element_type=F32)


def nt(a, b):
    return lax.dot_general(a, b, (((1,), (1,)), ((), ())), preferred_element_type=F32)


def tn(a, b):
    return lax.dot_general(a, b, (((0,), (0,)), ((), ())), preferred_element_type=F32)


def attn_fwd_kernel(len_ref, qu, qv, k, v, pos, o_ref, lse_ref, u=None, hook=None):
    count = len_ref[pl.program_id(0) if u is None else u]
    full = k.shape[1]
    lane = lax.broadcasted_iota(jnp.int32, (BLK, 2 * DK), 1)
    col = lax.broadcasted_iota(jnp.int32, (BLK, full), 1)
    keep = col < count
    zero = jnp.zeros((), BF)
    for blk in range(full // BLK):
        i0 = blk * BLK
        base = full - BLK - i0
        if hook is not None:
            hook(blk)
        outs, logs = [], []
        for h in range(2):
            mine = (lane < DK) if h == 0 else (lane >= DK)
            q_u = jnp.where(mine, qu[0, i0 : i0 + BLK, :], zero)
            q_v = jnp.where(mine, qv[0, i0 : i0 + BLK, :], zero)
            rel = nt(q_v, pos[base : base + full + BLK, :])
            rel = pltpu.roll(rel, full + 1, 1, stride=1, stride_axis=0)[:, :full]
            s = (nt(q_u, k[0]) + rel) * (1.0 / math.sqrt(DK))
            s = jnp.where(keep, s, mask_fill)
            top = jnp.max(s, axis=1, keepdims=True)
            e = jnp.exp(s - top)
            total = jnp.sum(e, axis=1, keepdims=True)
            outs.append(nn(e.astype(BF), v[0]) / total)
            logs.append(top + jnp.log(total))
        left = lane < DK
        o_ref[0, i0 : i0 + BLK, :] = jnp.where(left, outs[0], outs[1]).astype(BF)
        lse_ref[0, i0 : i0 + BLK, :] = jnp.where(left, logs[0], logs[1])


def attn_bwd_kernel(
    len_ref, qu, qv, k, v, pos, o, lse, do, dq_ref, dk_ref, dv_ref, dpos_ref, sum_ref, dkt, dvt, dpt,
    hook=None,
):
    count = len_ref[pl.program_id(0)]
    full = k.shape[1]
    scale = 1.0 / math.sqrt(DK)
    lane = lax.broadcasted_iota(jnp.int32, (BLK, 2 * DK), 1)
    left = lane < DK
    keep = lax.broadcasted_iota(jnp.int32, (BLK, full), 1) < count
    zero = jnp.zeros((), BF)
    flip = (lane + lax.broadcasted_iota(jnp.int32, (BLK, 2 * DK), 0) == BLK - 1).astype(F32).astype(BF)
    dkt[...] = jnp.zeros_like(dkt)
    dvt[...] = jnp.zeros_like(dvt)
    dpt[...] = jnp.zeros_like(dpt)
    sum_q = jnp.zeros((1, 2 * DK), F32)
    sum_u = jnp.zeros((1, 2 * DK), F32)
    sum_v = jnp.zeros((1, 2 * DK), F32)
    for blk in range(full // BLK):
        i0 = blk * BLK
        base = full - BLK - i0
        rows = slice(i0, i0 + BLK)
        win = slice(base, base + full + BLK)
        if hook is not None:
            hook(blk)
        qu_t = qu[0, rows, :].astype(F32).T.astype(BF)
        do_t = do[0, rows, :].astype(F32).T.astype(BF)
        qv_t = tn(qv[0, rows, :], flip).astype(BF)
        dot_o = do[0, rows, :].astype(F32) * o[0, rows, :].astype(F32)
        parts_u, parts_v = [], []
        for h in range(2):
            mine = left if h == 0 else lane >= DK
            hs = slice(h * DK, h * DK + DK)
            q_u = jnp.where(mine, qu[0, rows, :], zero)
            q_v = jnp.where(mine, qv[0, rows, :], zero)
            d_o = jnp.where(mine, do[0, rows, :], zero)
            rel = nt(q_v, pos[win, :])
            rel = pltpu.roll(rel, full + 1, 1, stride=1, stride_axis=0)[:, :full]
            s = (nt(q_u, k[0]) + rel) * scale - lse[0, rows, h * DK : h * DK + 1]
            p = jnp.where(keep, jnp.exp(jnp.minimum(s, 0.0)), 0.0)
            delta = jnp.sum(jnp.where(mine, dot_o, 0.0), axis=1, keepdims=True)
            ds = (p * (nt(d_o, v[0]) - delta)).astype(BF)
            dvt[hs, :] += nn(do_t[hs, :], p.astype(BF))
            dkt[hs, :] += nn(qu_t[hs, :], ds)
            parts_u.append(nn(ds, k[0]))
            wide = jnp.concatenate([nn(flip, ds), jnp.zeros((BLK, BLK), F32)], axis=1)
            wide = pltpu.roll(wide, 0, 1, stride=1, stride_axis=0).astype(BF)
            parts_v.append(nn(wide, pos[win, :]))
            dpt[hs, win] += nn(qv_t[hs, :], wide)
        d_u = jnp.where(left, parts_u[0], parts_u[1]) * scale
        d_v = jnp.where(left, parts_v[0], parts_v[1]) * scale
        high = d_v.astype(BF)
        low = (d_v - high.astype(F32)).astype(BF)
        d_q = (d_u + nn(flip, high) + nn(flip, low)).astype(BF)
        dq_ref[0, rows, :] = d_q
        sum_q += jnp.sum(d_q.astype(F32), axis=0, keepdims=True)
        sum_u += jnp.sum(d_u, axis=0, keepdims=True)
        sum_v += jnp.sum(d_v, axis=0, keepdims=True)
    dk_ref[0] = (dkt[...].T * scale).astype(BF)
    d_val = dvt[...].T.astype(BF)
    dv_ref[0] = d_val
    dpos_ref[0] = (dpt[...].T * scale).astype(BF)
    sum_ref[0, 0:1, :] = sum_q
    sum_ref[0, 1:2, :] = jnp.sum(d_val.astype(F32), axis=0, keepdims=True)
    sum_ref[0, 2:3, :] = sum_u
    sum_ref[0, 3:4, :] = sum_v
    sum_ref[0, 4:8, :] = jnp.zeros((4, 2 * DK), F32)


def attn_specs(rows, full, width):
    pairs = width // (2 * DK)
    main = pl.BlockSpec((1, full, 2 * DK), lambda u, p, n: (u, 0, p))
    pos = pl.BlockSpec((2 * full, 2 * DK), lambda u, p, n: (0, p))
    return (rows, pairs), main, pos


def attn_fwd_call(lens, qu, qv, k, v, pos):
    rows, full, width = qu.shape
    grid, main, pspec = attn_specs(rows, full, width)
    return pl.pallas_call(
        attn_fwd_kernel,
        grid_spec=pltpu.PrefetchScalarGridSpec(
            num_scalar_prefetch=1,
            grid=grid,
            in_specs=[main] * 4 + [pspec],
            out_specs=[main, main],
        ),
        out_shape=[
            jax.ShapeDtypeStruct((rows, full, width), BF),
            jax.ShapeDtypeStruct((rows, full, width), F32),
        ],
        compiler_params=dense_params(),
        name="attn_fwd",
    )(lens, qu, qv, k, v, pos)


def attn_bwd_call(lens, qu, qv, k, v, pos, o, lse, do, early=None, cid=None):
    rows, full, width = qu.shape
    grid, main, pspec = attn_specs(rows, full, width)
    args = [lens, qu, qv, k, v, pos, o, lse, do]
    in_specs = [main] * 4 + [pspec] + [main] * 3
    out_specs = [
        main,
        main,
        main,
        pl.BlockSpec((1, 2 * full, 2 * DK), lambda u, p, n: (u, 0, p)),
        pl.BlockSpec((1, 8, 2 * DK), lambda u, p, n: (u, 0, p)),
    ]
    scratch = [
        pltpu.VMEM((2 * DK, full), F32),
        pltpu.VMEM((2 * DK, full), F32),
        pltpu.VMEM((2 * DK, 2 * full), F32),
    ]
    out_shape = [jax.ShapeDtypeStruct((rows, full, width), BF)] * 3 + [
        jax.ShapeDtypeStruct((rows, 2 * full, width), BF),
        jax.ShapeDtypeStruct((rows, 8, width), F32),
    ]
    body, params = attn_bwd_kernel, dense_params()
    if early is not None:
        items = [split_owners(item) for item in early]
        pieces = pieces_of([item.shape[-1] for item in items])
        owned = items[0].shape[-2]
        n_in, n_out, m = len(args) - 1, len(out_shape), len(items)
        args += items
        in_specs += [ANY] * m
        out_specs.append(pl.BlockSpec((owned, C_OWN), lambda u, p, n: (0, 0)))
        out_shape.append(jax.ShapeDtypeStruct((owned, C_OWN), F32))
        scratch += scatter_scratch(pieces, owned)
        params = comm_params(cid)

        def body(*refs):
            at = pl.program_id(0) * grid[1] + pl.program_id(1)
            last = grid[0] * grid[1] - 1
            ins, rest = refs[: 1 + n_in], refs[1 + n_in :]
            g_refs, rest = rest[:m], rest[m:]
            mains, o_ref, rest = rest[:n_out], rest[n_out], rest[n_out + 1 :]
            own, sems = rest[:3], rest[3:]
            start, advance, finish, rounds = scatter_steps(pieces, g_refs, o_ref, sems, 3)
            peers = link_peers(*place())

            @pl.when(at == 0)
            def _():
                hail(peers)

            def begin():
                hear(peers)
                for p in range(len(pieces)):
                    start(p)

            steps = [begin] + [lambda q=q: advance(q) for q in range(rounds)]
            attn_bwd_kernel(*ins, *mains, *own, hook=hooks_of(steps, at, last, full // BLK))

            @pl.when(at == last)
            def _():
                finish()

    return pl.pallas_call(
        body,
        grid_spec=pltpu.PrefetchScalarGridSpec(
            num_scalar_prefetch=1,
            grid=grid,
            in_specs=in_specs,
            out_specs=out_specs,
            scratch_shapes=scratch,
        ),
        out_shape=out_shape,
        compiler_params=params,
        name="attn_bwd",
    )(*args)


def hooks_of(steps, at, last, spots):
    def hook(blk):
        for i, step in enumerate(steps):
            where, spot = divmod(i * (last + 1) * (spots - 1) // len(steps), spots - 1)
            if spot + 1 == blk:

                @pl.when(at == where)
                def _(step=step):
                    step()

    return hook


MESH = pl.DeviceIdType.MESH
NZ, NY, NX = 4, 2, 2
ANY = pl.BlockSpec(memory_space=pl.ANY)
VM = pl.BlockSpec(memory_space=pltpu.VMEM)


def own_mesh(sizes):
    return sizes == (NZ * NY * NX, 2)


def place():
    dp = lax.axis_index("dp")
    return dp // (NY * NX), dp // NX % NY, dp % NX, lax.axis_index("tensor")


def dev(z, y, x, t):
    return (z * (NY * NX) + y * NX + x, t)


def hail(peers):
    barrier = pltpu.get_barrier_semaphore()
    for peer in peers:
        pl.semaphore_signal(barrier, inc=1, device_id=peer, device_id_type=MESH)


def hear(peers):
    pl.semaphore_wait(pltpu.get_barrier_semaphore(), len(peers))


def rcopy(src, dst, send, recv, peer):
    return pltpu.make_async_remote_copy(
        src_ref=src, dst_ref=dst, send_sem=send, recv_sem=recv, device_id=peer, device_id_type=MESH
    )


def link_peers(z, y, x, t):
    peers = [dev(lax.rem(z + d, NZ), y, x, t) for d in range(1, NZ)]
    return peers + [dev(z, 1 - y, x, t), dev(z, y, 1 - x, t), dev(z, y, x, 1 - t)]


def sum_scratch(shape):
    dma = pltpu.SemaphoreType.DMA
    return [
        pltpu.VMEM(shape, F32), pltpu.VMEM(shape, F32), pltpu.VMEM((3,) + shape, F32),
        pltpu.VMEM((7,) + shape, F32), dma((3,)), dma((3,)), dma((7,)), dma((7,)),
    ]


def sum_steps(scratch):
    x_s, mid, b1, b2, s1, r1, s2, r2 = scratch
    z, y, x, t = place()
    spot = (y * NX + x) * 2 + t
    zs = [dev(lax.rem(z + d, NZ), y, x, t) for d in range(1, NZ)]
    flat = [lax.rem(spot + d, 8) for d in range(1, 8)]
    plane = [dev(z, p // 4, p // 2 % 2, p % 2) for p in flat]

    def call(wait=False):
        hear(zs + plane) if wait else hail(zs + plane)

    def meet(o_ref, heard=False):
        first = [rcopy(x_s, b1.at[i], s1.at[i], r1.at[i], peer) for i, peer in enumerate(zs)]
        second = [rcopy(mid, b2.at[i], s2.at[i], r2.at[i], peer) for i, peer in enumerate(plane)]

        def one():
            if not heard:
                hear(zs + plane)
            for copy in first:
                copy.start()

        def two():
            for copy in first:
                copy.wait_recv()
            mid[...] = (x_s[...] + b1[0]) + (b1[1] + b1[2])
            for copy in second:
                copy.start()

        def three():
            for copy in second:
                copy.wait_recv()
            total = mid[...]
            for i in range(7):
                total = total + b2[i]
            o_ref[...] = total
            for copy in first + second:
                copy.wait_send()

        return one, two, three

    return call, meet


def comm_params(cid):
    return pltpu.CompilerParams(
        collective_id=cid, has_side_effects=True, vmem_limit_bytes=60 * 1024 * 1024
    )


def gathered_shape(packed):
    return jax.ShapeDtypeStruct((2, NZ, NY, NX) + packed.shape, packed.dtype)


def gather_scratch(n, groups=3):
    dma = pltpu.SemaphoreType.DMA
    return [dma((n, NZ - 1)), dma((n, NZ - 1))] + [dma((n,))] * 6 + [dma((groups,))]


LEAD = 2


def gather_events(pieces, xs, gs, sems):
    zs, zr, as_, ar, bs, br, cs, cr, own_sem = sems
    z, y, x, t = place()
    along_x, along_y = dev(z, y, 1 - x, t), dev(z, 1 - y, x, t)
    zc, ac, bc, cc = [], [], [], []
    for p, (i, start, w) in enumerate(pieces):
        c = pl.ds(start, w)
        g = gs[i]
        zc.append(
            [
                rcopy(
                    xs[i].at[:, c],
                    g.at[t, z, y, x, :, c],
                    zs.at[p, d - 1],
                    zr.at[p, d - 1],
                    dev(lax.rem(z + d, NZ), y, x, t),
                )
                for d in range(1, NZ)
            ]
        )
        line = g.at[t, :, y, x, :, c]
        ac.append(rcopy(line, line, as_.at[p], ar.at[p], along_x if p % 2 == 0 else along_y))
        half = g.at[t, :, y, :, :, c] if p % 2 == 0 else g.at[t, :, :, x, :, c]
        bc.append(rcopy(half, half, bs.at[p], br.at[p], along_y if p % 2 == 0 else along_x))
        full = g.at[t, :, :, :, :, c]
        cc.append(rcopy(full, full, cs.at[p], cr.at[p], dev(z, y, x, 1 - t)))

    def begin():
        own = [
            pltpu.make_async_copy(item, g.at[t, z, y, x], own_sem.at[i])
            for i, (item, g) in enumerate(zip(xs, gs))
        ]
        for copy in own:
            copy.start()
        for copies in zc[: 2 * LEAD]:
            for copy in copies:
                copy.start()
        for copy in own:
            copy.wait()

    def event(kind, q):
        for p in (2 * q, 2 * q + 1):
            if kind == "z":
                for copy in zc[p]:
                    copy.wait_recv()
                ac[p].start()
                for copy in zc[p + 2 * LEAD] if p + 2 * LEAD < len(pieces) else []:
                    copy.start()
            elif kind == "a":
                ac[p].wait_recv()
                bc[p].start()
            elif kind == "b":
                bc[p].wait_recv()
                cc[p].start()
            else:
                cc[p].wait_recv()

    def finish():
        for copy in sum(zc, []) + ac + bc + cc:
            copy.wait_send()

    return begin, event, finish


def gather_order(pieces):
    unit = [0.42 * (pieces[2 * q][2] + pieces[2 * q + 1][2]) / 512 for q in range(len(pieces) // 2)]
    order, at = [], 3.0
    waiting = []
    for q, step in enumerate(unit):
        at += 8 * step
        waiting.append((at + 2.5, q, "z"))
    free = 0.0
    while waiting:
        waiting.sort()
        now, q, kind = waiting.pop(0)
        order.append((now, kind, q))
        if kind in "za":
            free = max(free, now) + (4 if kind == "z" else 8) * unit[q]
            waiting.append((free + 2.5, q, "a" if kind == "z" else "b"))
        elif kind == "b":
            waiting.append((now + 1.8, q, "c"))
    return order


def small_steps(s_ref, v_ref, mid, b1, b2, s1, r1, s2, r2):
    z, y, x, t = place()
    spot = (y * NX + x) * 2 + t
    zs = [dev(lax.rem(z + d, NZ), y, x, t) for d in range(1, NZ)]
    flat = [lax.rem(spot + d, 8) for d in range(1, 8)]
    plane = [dev(z, p // 4, p // 2 % 2, p % 2) for p in flat]
    first = [rcopy(s_ref, b1.at[i], s1.at[i], r1.at[i], peer) for i, peer in enumerate(zs)]
    second = [rcopy(mid, b2.at[i], s2.at[i], r2.at[i], peer) for i, peer in enumerate(plane)]

    def begin():
        for copy in first:
            copy.start()

    def spread():
        for copy in first:
            copy.wait_recv()
        mid[...] = (s_ref[...] + b1[0]) + (b1[1] + b1[2])
        for copy in second:
            copy.start()

    def finish():
        for copy in second:
            copy.wait_recv()
        same, other = mid[...].astype(F32), b2[0].astype(F32)
        for i in range(1, 7):
            if i % 2 == 1:
                same = same + b2[i].astype(F32)
            else:
                other = other + b2[i].astype(F32)
        low = jnp.where(t == 0, same, other)
        high = jnp.where(t == 0, other, same)
        v_ref[...] = jnp.zeros_like(v_ref)
        for q in range(4):
            r = S_NORM + 14 * q
            v_ref[0:14, 128 * q : 128 * q + 128] = low[r : r + 14] + high[r : r + 14]
        for i, part in enumerate((low, high)):
            for q in range(2):
                c = slice((2 * i + q) * 128, (2 * i + q) * 128 + 128)
                v_ref[R_ATT:R_CV, c] = part[S_ATT + 4 * q : S_ATT + 4 * q + 4]
                v_ref[R_CV:R_B1, c] = part[S_CV + 13 * q : S_CV + 13 * q + 13]
            for q in range(8):
                r, c = 2 * i + q // 4, slice(q % 4 * 128, q % 4 * 128 + 128)
                v_ref[R_B1 + r : R_B1 + r + 1, c] = part[S_B1 + q : S_B1 + q + 1]
                v_ref[R_B2 + r : R_B2 + r + 1, c] = part[S_B2 + q : S_B2 + q + 1]
        for copy in first + second:
            copy.wait_send()

    return plane, begin, spread, finish


S_B1, S_ATT, S_CV, S_B2, S_NORM, S_ALL = 0, 8, 16, 42, 50, 112


def lanes_of(n, offset):
    at = lax.broadcasted_iota(jnp.int32, (n, 128), 0) + offset
    return (lax.broadcasted_iota(jnp.int32, (n, 128), 1) == at).astype(F32)


def prep_kernel(
    f1i, f1o, pos, qkv, f2i, f2o, ci, out, co, b1, att, cv, b2, norm,
    pa_ref, pb_ref, pc_ref, slab_ref, table_ref, slab, first_s, second_s,
):
    def put(ref, name, value, shift=0):
        start = SEG[name][0] + shift
        ref[:, start : start + value.shape[1]] = value

    for ref, name, item in (
        (pa_ref, "f1i", f1i), (pa_ref, "f1o", f1o), (pa_ref, "pos", pos), (pc_ref, "f2i", f2i),
        (pc_ref, "f2o", f2o), (pb_ref, "out", out), (pb_ref, "co", co),
    ):
        put(ref, name, item[...])
    for k in range(3):
        put(pa_ref, "qkv", qkv[k], k * qkv.shape[2])
    for k in range(2):
        put(pb_ref, "ci", ci[:, k, :], k * ci.shape[2])
    z, y, x, t = place()
    dp = z * (NY * NX) + y * NX + x
    sel = lanes_of(8, dp * 8).astype(BF)
    slab[...] = jnp.zeros_like(slab)
    slab[S_B1 : S_B1 + 8] = nn(b1[...], sel)
    for q in range(2):
        slab[S_ATT + 4 * q : S_ATT + 4 * q + 4] = nn(att[:, q, :], sel)
        slab[S_CV + 13 * q : S_CV + 13 * q + 13] = tn(cv[q], sel)
    slab[S_B2 : S_B2 + 8] = nn(b2[...], sel)
    at = dp * 2 + t
    here = nn(norm[...], lanes_of(16, lax.rem(at, 8) * 16).astype(BF))
    for q in range(4):
        slab[S_NORM + 14 * q : S_NORM + 14 * q + 14] = here * (at // 8 == q).astype(F32)
    slab_ref[...] = slab[...].astype(BF)
    fill_table(table_ref, first_s, second_s)


def prep_call(items, smalls, full, width):
    rows = items[0].shape[0]
    return pl.pallas_call(
        prep_kernel,
        in_specs=[VM] * 14,
        out_specs=[VM] * 5,
        out_shape=[
            jax.ShapeDtypeStruct((rows, C_A), BF),
            jax.ShapeDtypeStruct((rows, C_B), BF),
            jax.ShapeDtypeStruct((rows, C_C), BF),
            jax.ShapeDtypeStruct((S_ALL, 128), BF),
            jax.ShapeDtypeStruct((2 * full, width), BF),
        ],
        scratch_shapes=[pltpu.VMEM((S_ALL, 128), F32)] + [pltpu.VMEM((32, width), F32)] * 2,
        name="prepare",
    )(*items, *smalls)


def split_owners(item):
    return item.reshape(2, NZ, NY, NX, item.shape[1] // (NZ * NY * NX), item.shape[2])


def pieces_of(widths, step=256):
    pieces, at = [], 0
    for i, w in enumerate(widths):
        pieces += [(i, k, min(step, w), at + k) for k in range(0, w, step)]
        at += w
    return pieces


def scatter_scratch(pieces, rows):
    n = len(pieces)
    total = sum(piece[2] for piece in pieces)
    dma = pltpu.SemaphoreType.DMA
    shape = (rows, total)
    return [
        pltpu.VMEM((NZ, NY, NX) + shape, BF),
        pltpu.VMEM((NZ, NY, NX) + shape, BF),
        pltpu.VMEM((NZ, 2) + shape, BF),
        pltpu.VMEM((NZ,) + shape, BF),
        pltpu.VMEM((NZ - 1,) + shape, BF),
    ] + [dma((n,))] * 7 + [dma((n, NZ - 1))] * 2


def scatter_steps(pieces, g_refs, o_ref, scratch, lag):
    own, rc, ra, rb, rz, lsem, cs, cr, as_, ar, bs, br, zs, zr = scratch
    z, y, x, t = place()
    along_x, along_y = dev(z, y, 1 - x, t), dev(z, 1 - y, x, t)
    mate = dev(z, y, x, 1 - t)
    count = len(pieces)
    bufs, lc, cc, ac, bc, zc = [], [], [], [], [], []
    for p, (i, start, w, at) in enumerate(pieces):
        c = pl.ds(at, w)
        g = pl.ds(start, w)
        b = dict(
            own=own.at[:, :, :, :, c], rc=rc.at[:, :, :, :, c], ra=ra.at[:, :, :, c],
            rb=rb.at[:, :, c], rz=rz.at[:, :, c],
        )
        bufs.append(b)
        even = p % 2 == 0
        lc.append(
            pltpu.make_async_copy(g_refs[i].at[t, :, :, :, :, g], b["own"], lsem.at[p])
        )
        cc.append(rcopy(g_refs[i].at[1 - t, :, :, :, :, g], b["rc"], cs.at[p], cr.at[p], mate))
        away = b["own"].at[:, 1 - y] if even else b["own"].at[:, :, 1 - x]
        ac.append(rcopy(away, b["ra"], as_.at[p], ar.at[p], along_y if even else along_x))
        line = b["own"].at[:, y, 1 - x] if even else b["own"].at[:, 1 - y, x]
        bc.append(rcopy(line, b["rb"], bs.at[p], br.at[p], along_x if even else along_y))
        zc.append([])
        for d in range(1, NZ):
            far = lax.rem(z + d, NZ)
            zc[p].append(
                rcopy(
                    b["own"].at[far, y, x], b["rz"].at[d - 1], zs.at[p, d - 1], zr.at[p, d - 1],
                    dev(far, y, x, t),
                )
            )

    def start(p):
        lc[p].start()
        cc[p].start()

    def advance(q):
        if q < count:
            lc[q].wait()
            cc[q].wait_recv()
            b = bufs[q]

            @pl.loop(0, NZ)
            def _(i):
                b["own"][i] = b["own"][i] + b["rc"][i]

            ac[q].start()
        p = q - lag
        if 0 <= p < count:
            ac[p].wait_recv()
            b = bufs[p]

            @pl.loop(0, NZ)
            def _(i):
                if p % 2 == 0:
                    b["own"][i, y] = b["own"][i, y] + b["ra"][i]
                else:
                    b["own"][i, :, x] = b["own"][i, :, x] + b["ra"][i]

            bc[p].start()
        p = q - 2 * lag
        if 0 <= p < count:
            bc[p].wait_recv()
            b = bufs[p]

            @pl.loop(0, NZ)
            def _(i):
                b["own"][i, y, x] = b["own"][i, y, x] + b["rb"][i]

            for copy in zc[p]:
                copy.start()
        p = q - 3 * lag
        if 0 <= p < count:
            for copy in zc[p]:
                copy.wait_recv()
            b = bufs[p]
            total = b["own"][z, y, x].astype(F32)
            for d in range(NZ - 1):
                total = total + b["rz"][d].astype(F32)
            o_ref[:, pieces[p][3] : pieces[p][3] + pieces[p][2]] = total

    def finish():
        for copy in cc + ac + bc + sum(zc, []):
            copy.wait_send()

    return start, advance, finish, count + 3 * lag


def small_sum_steps(parts, ext, scratch):
    acc_s, bc_, bz, bp, bm, sc, rc, sz, rz, sp, rp, sm, rm = scratch
    z, y, x, t = place()
    dp = z * (NY * NX) + y * NX + x
    half = acc_s.shape[0] // 2
    mine = pl.ds(pl.multiple_of(t * half, 8), half)
    mate = dev(z, y, x, 1 - t)
    spot = y * NX + x
    zp = [dev(lax.rem(z + d, NZ), y, x, t) for d in range(1, NZ)]
    flat = [lax.rem(spot + d, 4) for d in range(1, 4)]
    pp = [dev(z, p // 2, p % 2, t) for p in flat]
    one = rcopy(acc_s, bc_, sc, rc, mate)
    two = [rcopy(acc_s.at[mine], bz.at[i], sz.at[i], rz.at[i], peer) for i, peer in enumerate(zp)]
    three = [rcopy(bz.at[3], bp.at[i], sp.at[i], rp.at[i], peer) for i, peer in enumerate(pp)]
    four = rcopy(bp.at[3], bm, sm, rm, mate)

    def a():
        acc_s[...] = jnp.zeros_like(acc_s)
        total = parts[0][...]
        for part in parts[1:]:
            total = total + part[...]
        acc_s[0:R_ALL] = total
        one.start()

    def b():
        one.wait()
        acc_s[...] = acc_s[...] + bc_[...]
        for copy in two:
            copy.start()

    def c():
        for copy in two:
            copy.wait()
        bz[3] = (acc_s[mine] + bz[0]) + (bz[1] + bz[2])
        for copy in three:
            copy.start()

    def d():
        for copy in three:
            copy.wait()
        bp[3] = (bz[3] + bp[0]) + (bp[1] + bp[2])
        four.start()
        ext[mine] = bp[3]

    def e():
        four.wait()
        ext[pl.ds(pl.multiple_of((1 - t) * half, 8), half)] = bm[...]

    return pp, [a, b, c, d, e]


def small_sum_scratch(width):
    dma = pltpu.SemaphoreType.DMA
    return [
        pltpu.VMEM((R_SUM, width), F32), pltpu.VMEM((R_SUM, width), F32),
        pltpu.VMEM((4, R_SUM // 2, width), F32), pltpu.VMEM((4, R_SUM // 2, width), F32),
        pltpu.VMEM((R_SUM // 2, width), F32), dma, dma, dma((3,)), dma((3,)), dma((3,)), dma((3,)), dma, dma,
    ]


def finish_kernel(
    oa, ob, ext, f1i, f1o, b1, qkv, pos, out, att, ci, co, cv, f2i, f2o, b2, norm
):
    def take(ref, name):
        start = OWN.get(name, SEG[name][0])
        return ref[:, start : start + SEG[name][1]]

    f1i[...] = take(oa, "f1i")
    f1o[...] = take(oa, "f1o")
    pos[...] = take(oa, "pos")
    f2i[...] = take(ob, "f2i")
    f2o[...] = take(ob, "f2o")
    out[...] = take(ob, "out")
    co[...] = take(ob, "co")
    for ref, src, name in ((qkv, oa, "qkv"), (ci, ob, "ci")):
        start, w = OWN.get(name, SEG[name][0]), SEG[name][1]
        n = 3 if name == "qkv" else 2
        for k in range(n):
            part = src[:, start + k * w // n : start + (k + 1) * w // n]
            if name == "qkv":
                ref[k] = part
            else:
                ref[:, k, :] = part
    z, y, x, t = place()
    dp = z * (NY * NX) + y * NX + x
    sel = lanes_of(8, dp * 8)

    def own(v, pick):
        return lax.dot_general(
            v, pick, (((1,), (1,)), ((), ())), precision=lax.Precision.HIGHEST,
            preferred_element_type=F32,
        )

    for q in range(2):
        c = pl.ds(pl.multiple_of((2 * t + q) * 128, 128), 128)
        att[:, q, :] = own(ext[R_ATT:R_CV, c], sel)
        cv[q] = own(sel, ext[R_CV:R_B1, c])
    for o, at in ((b1, R_B1), (b2, R_B2)):
        for q in range(8):
            r, c = at + q // 4, slice(q % 4 * 128, q % 4 * 128 + 128)
            line = jnp.where(t == 0, ext[r : r + 1, c], ext[r + 2 : r + 3, c])
            o[q : q + 1, :] = own(line, sel)
    at = dp * 2 + t
    lane = pl.ds(pl.multiple_of(at // 8 * 128, 128), 128)
    norm[...] = own(ext[0:14, lane], lanes_of(16, lax.rem(at, 8) * 16))


def finish_call(oa, ob, ext, rows):
    shapes = [
        (rows, 1024), (rows, 1024), (8, 8), (3, rows, 256), (rows, 256), (rows, 256), (4, 2, 8),
        (rows, 2, 256), (rows, 256), (2, 8, 13), (rows, 1024), (rows, 1024), (8, 8), (14, 16),
    ]
    f1i, f1o, b1, qkv, pos, out, att, ci, co, cv, f2i, f2o, b2, norm = pl.pallas_call(
        finish_kernel,
        in_specs=[VM] * 3,
        out_specs=[VM] * 14,
        out_shape=[jax.ShapeDtypeStruct(shape, F32) for shape in shapes],
        name="own_gradients",
    )(oa, ob, ext)
    return (
        f1i, f1o.T, b1, qkv.transpose(1, 0, 2), pos, out.T, att, ci, co.T, cv.transpose(2, 0, 1),
        f2i, f2o.T, b2, norm,
    )

SEG = {
    "f1i": (0, 1024), "f1o": (1024, 1024), "pos": (2048, 256), "qkv": (2304, 768),
    "ci": (0, 512), "out": (512, 256), "co": (768, 256),
    "f2i": (0, 1024), "f2o": (1024, 1024),
}
C_A, C_B, C_C = 3072, 1024, 2048
OWN = {"f2i": 0, "f2o": 1024, "ci": 2048, "out": 2560, "co": 2816}
C_OWN = 3072
R_ATT, R_CV, R_B1, R_B2, R_ALL, R_SUM = 14, 18, 31, 35, 40, 48
TB = 256
HC = 256


def seg_spec(name, depth):
    start, width = SEG[name]
    return pl.BlockSpec(
        (2, depth, width), lambda i, *_: (0, 0, start // width), pipeline_mode=pl.Buffered(1)
    )


def whole(shape):
    zeros = (0,) * len(shape)
    return pl.BlockSpec(shape, lambda i, *_: zeros)


def tall(rows, width):
    return pl.BlockSpec((rows, width), lambda i, *_: (i, 0))


def sig(v):
    return 0.5 * jnp.tanh(0.5 * v) + 0.5


def row(ref, i):
    return ref[i : i + 1, :]


def col_sum(v):
    return jnp.sum(v, axis=0, keepdims=True)


def ln_stats(v):
    centered = v - jnp.mean(v, axis=1, keepdims=True)
    inv = lax.rsqrt(jnp.mean(centered * centered, axis=1, keepdims=True) + norm_eps)
    return centered * inv, inv


def ln_back(up, scaled, inv, gain):
    g = up * gain
    return inv * (
        g
        - jnp.mean(g, axis=1, keepdims=True)
        - scaled * jnp.mean(g * scaled, axis=1, keepdims=True)
    )


def bias_half(vecs, at, t):
    return jnp.concatenate([row(vecs, at + 2 * t), row(vecs, at + 2 * t + 1)], axis=1)


def row_mask(start, rows, count):
    at = start + lax.broadcasted_iota(jnp.int32, (rows, 1), 0)
    return (at < count).astype(F32)


def ffn1_kernel(
    x_ref, table, w_in, w_out, w_qkv, w_pos, vecs,
    first_ref, z_ref, qu_ref, qv_ref, k_ref, v_ref, pos_ref,
):
    x = x_ref[...].astype(F32)
    scaled, _ = ln_stats(x)
    hn = (scaled * row(vecs, 0) + row(vecs, 1)).astype(BF)
    half = w_in.shape[2]
    y = row(vecs, 2)
    for t in range(2):
        z = nn(hn, w_in[t]) + bias_half(vecs, R_B1, t)
        for j in range(half // HC):
            z_ref[:, (2 * j + t) * HC : (2 * j + t + 1) * HC] = z[:, j * HC : (j + 1) * HC].astype(BF)
        y = y + nt((z * sig(z)).astype(BF), w_out[t])
    first = x + 0.5 * y
    first_ref[...] = first
    scaled, _ = ln_stats(first)
    hn = (scaled * row(vecs, 3) + row(vecs, 4)).astype(BF)
    part = w_qkv.shape[2] // 3
    for t in range(2):
        c = slice(t * part, (t + 1) * part)
        proj = nn(hn, w_qkv[t])
        q = proj[:, :part] + vecs[R_ATT : R_ATT + 1, c]
        qu_ref[:, c] = (q + vecs[R_ATT + 2 : R_ATT + 3, c]).astype(BF)
        qv_ref[:, c] = (q + vecs[R_ATT + 3 : R_ATT + 4, c]).astype(BF)
        k_ref[:, c] = proj[:, part : 2 * part].astype(BF)
        v_ref[:, c] = (proj[:, 2 * part :] + vecs[R_ATT + 1 : R_ATT + 2, c]).astype(BF)
        pos_ref[:, c] = nn(table[...], w_pos[t]).astype(BF)


def dense_params(mib=60):
    return pltpu.CompilerParams(vmem_limit_bytes=mib * 1024 * 1024)


def ffn1_call(x, table, g, vecs):
    tokens, width = x.shape
    steps = tokens // TB
    places = tall(table.shape[0] // steps, width)
    return pl.pallas_call(
        ffn1_kernel,
        grid=(steps,),
        in_specs=[
            tall(TB, width), places, seg_spec("f1i", width), seg_spec("f1o", width),
            seg_spec("qkv", width), seg_spec("pos", width), whole(vecs.shape),
        ],
        out_specs=[tall(TB, width), tall(TB, 4 * width)] + [tall(TB, width)] * 4 + [places],
        out_shape=[
            jax.ShapeDtypeStruct((tokens, width), F32),
            jax.ShapeDtypeStruct((tokens, 4 * width), BF),
        ]
        + [jax.ShapeDtypeStruct((tokens, width), BF)] * 4
        + [jax.ShapeDtypeStruct(table.shape, BF)],
        compiler_params=dense_params(),
        name="ffn1_forward",
    )(x, table, g, g, g, g, vecs)


FRONT_PIECES = (
    [(0, at + k, 128) for k in (0, 128) for at in (0, 1024)]
    + [(0, at + 256 * j, 256) for j in range(1, 4) for at in (0, 1024)]
    + [(0, 2048 + 256 * k, 256) for k in range(4)]
    + [(1, 0, 512), (1, 512, 512)]
    + [(2, at + 512 * j, 512) for j in range(2) for at in (0, 1024)]
)


def front_call(lens, x, table, packed_a, packed_b, packed_c, slab, batch, cid):
    tokens, width = x.shape
    full = tokens // batch
    pairs = width // (2 * DK)
    chunks = SEG["f1i"][1] // HC
    first_head = chunks + 1
    steps = first_head + batch * pairs
    order = gather_order(FRONT_PIECES)
    dma = pltpu.SemaphoreType.DMA
    small = [
        pltpu.VMEM(slab.shape, BF), pltpu.VMEM((3,) + slab.shape, BF),
        pltpu.VMEM((7,) + slab.shape, BF), dma((3,)), dma((3,)), dma((7,)), dma((7,)),
    ]
    heads_shape = (batch, full, width)
    scratch = [
        pltpu.VMEM((2, NZ, NY, NX) + packed_a.shape, BF),
        pltpu.VMEM((tokens, width), F32),
        pltpu.VMEM((tokens, width), BF),
    ]
    scratch += [pltpu.VMEM(heads_shape, BF)] * 5 + [pltpu.VMEM(heads_shape, F32)]
    scratch += [pltpu.VMEM(table.shape, BF), dma((10,))]
    n_own = len(scratch)

    def body(
        len_ref, x_ref, table_ref, xa_ref, xb_ref, xc_ref, s_ref,
        ga_ref, gb_ref, gc_ref, vecs, first_ref, z_ref, qu_ref, qv_ref, k_ref, v_ref, pos_ref, mix_ref,
        lse_ref, *rest,
    ):
        i = pl.program_id(0)
        ga, y_s, hn_s, qu, qv, k, v, mix, lse, pos, out_sem = rest[:n_own]
        smalls = rest[n_own : n_own + len(small)]
        begin, event, finish = gather_events(
            FRONT_PIECES, (xa_ref, xb_ref, xc_ref), (ga, gb_ref, gc_ref), rest[n_own + len(small) :]
        )
        plane, s_begin, s_spread, s_finish = small_steps(s_ref, vecs, *smalls)
        z, y, xx, t = place()
        sources = (ga, y_s, qu, qv, k, v, pos, mix, lse)
        targets = (ga_ref, first_ref, qu_ref, qv_ref, k_ref, v_ref, pos_ref, mix_ref, lse_ref)
        copies = [
            pltpu.make_async_copy(a, b, out_sem.at[n])
            for n, (a, b) in enumerate(zip(sources, targets))
        ]
        done = [0]

        def until(q):
            while True:
                _, kind, pair = order[done[0]]
                done[0] += 1
                event(kind, pair)
                if (kind, pair) == ("c", q):
                    break

        def weight(t, start, w):
            return ga[t, :, :, :, :, start : start + w].reshape(width, w)

        @pl.when(i == 0)
        def _():
            peers = [dev(lax.rem(z + d, NZ), y, xx, t) for d in range(1, NZ)] + plane
            hail(peers)

            @pl.loop(0, tokens // TB)
            def _(r):
                here = pl.ds(pl.multiple_of(r * TB, TB), TB)
                y_s[here, :] = ln_stats(x_ref[here, :].astype(F32))[0]

            hear(peers)
            begin()
            s_begin()
            for n in range(4):
                event(*order[n][1:])
            s_spread()
            for n in range(4, 7):
                event(*order[n][1:])
            done[0] = 7
            s_finish()

            @pl.loop(0, tokens // TB)
            def _(r):
                here = pl.ds(pl.multiple_of(r * TB, TB), TB)
                hn_s[here, :] = (y_s[here, :] * row(vecs, 0) + row(vecs, 1)).astype(BF)
                y_s[here, :] = jnp.zeros((TB, width), F32) + row(vecs, 2)

        for j in range(chunks):

            @pl.when(i == j)
            def _(j=j):
                until(j + 1)

        @pl.when(i < chunks)
        def _():
            at = pl.multiple_of(i * HC, HC)
            odd = lax.rem(i, 2) == 1
            @pl.loop(0, 2)
            def _(t):
                w_in = ga[t, :, :, :, :, pl.ds(at, HC)].reshape(width, HC)
                w_out = ga[t, :, :, :, :, pl.ds(1024 + at, HC)].reshape(width, HC)
                line = vecs[pl.ds(R_B1 + 2 * t + i // 2, 1), :]
                bias = jnp.where(odd, line[:, HC:], line[:, :HC])
                for k in range(tokens // TB):
                    here = slice(k * TB, (k + 1) * TB)
                    zf = nn(hn_s[here, :], w_in) + bias
                    z_ref[here, pl.ds(pl.multiple_of(t * HC, HC), HC)] = zf.astype(BF)
                    y_s[here, :] += nt((zf * sig(zf)).astype(BF), w_out)

        @pl.when(i == chunks)
        def _():

            @pl.loop(0, tokens // TB)
            def _(r):
                here = pl.ds(pl.multiple_of(r * TB, TB), TB)
                first = x_ref[here, :].astype(F32) + 0.5 * y_s[here, :]
                y_s[here, :] = first
                scaled, _ = ln_stats(first)
                hn_s[here, :] = (scaled * row(vecs, 3) + row(vecs, 4)).astype(BF)
            copies[1].start()
            until(chunks + 1)
            part = width // 2
            for t in range(2):
                c = slice(t * part, (t + 1) * part)
                pos[:, c] = nn(table_ref[...], weight(t, SEG["pos"][0], part)).astype(BF)
            copies[6].start()
            until(chunks + 2)
            copies[0].start()
            at = SEG["qkv"][0]
            @pl.loop(0, 2)
            def _(t):
                c = pl.ds(pl.multiple_of(t * part, part), part)

                lines = vecs[R_ATT:R_CV, :]
                lines = jnp.where(t == 0, lines[:, :part], lines[:, part:])

                @pl.loop(0, batch)
                def _(u):
                    hn = hn_s[pl.ds(pl.multiple_of(u * full, full), full), :]
                    q = nn(hn, weight(t, at, part)) + lines[0:1]
                    qu[u, :, c] = (q + lines[2:3]).astype(BF)
                    qv[u, :, c] = (q + lines[3:4]).astype(BF)
                    k[u, :, c] = nn(hn, weight(t, at + part, part)).astype(BF)
                    val = nn(hn, weight(t, at + 2 * part, part))
                    v[u, :, c] = (val + lines[1:2]).astype(BF)
            for n in (2, 3, 4, 5):
                copies[n].start()

        left = order[done[0] :]
        base = order[done[0] - 1][0] + 6.0
        blocks = full // BLK
        spots = batch * pairs * blocks
        slots = [min(max(int((now + 5.0 - base) / 0.9), 0), spots) for now, _, _ in left]

        def hook(blk):
            for slot, (_, kind, pair) in zip(slots, left):
                if slot % blocks == blk and slot < spots:

                    @pl.when(i == first_head + slot // blocks)
                    def _(kind=kind, pair=pair):
                        event(kind, pair)

        @pl.when(i >= first_head)
        def _():
            n = i - first_head
            u = n // pairs
            c = pl.ds(pl.multiple_of(lax.rem(n, pairs) * (2 * DK), 2 * DK), 2 * DK)

            def view(ref):
                return ref.at[pl.ds(u, 1), :, c]

            attn_fwd_kernel(
                len_ref, view(qu), view(qv), view(k), view(v), pos.at[:, c], view(mix), view(lse),
                u, hook,
            )

        @pl.when(i == steps - 1)
        def _():
            copies[7].start()
            copies[8].start()
            for slot, (_, kind, pair) in zip(slots, left):
                if slot >= spots:
                    event(kind, pair)
            finish()
            for copy in copies:
                copy.wait()

    def const(shape):
        return pl.BlockSpec(shape, lambda i, n: (0,) * len(shape), pipeline_mode=pl.Buffered(1))

    heads = jax.ShapeDtypeStruct(heads_shape, BF)
    return pl.pallas_call(
        body,
        grid_spec=pltpu.PrefetchScalarGridSpec(
            num_scalar_prefetch=1,
            grid=(steps,),
            in_specs=[
                const(x.shape), const(table.shape), const(packed_a.shape), const(packed_b.shape),
                const(packed_c.shape), const(slab.shape),
            ],
            out_specs=[
                ANY, ANY, ANY, pl.BlockSpec((R_ALL, width), lambda i, n: (0, 0)), ANY,
                pl.BlockSpec((tokens, 2 * HC), lambda i, n: (0, jnp.minimum(i, chunks - 1))),
            ]
            + [ANY] * 7,
            scratch_shapes=scratch + small + gather_scratch(len(FRONT_PIECES)),
        ),
        out_shape=[
            gathered_shape(packed_a),
            gathered_shape(packed_b),
            gathered_shape(packed_c),
            jax.ShapeDtypeStruct((R_ALL, width), F32),
            jax.ShapeDtypeStruct((tokens, width), F32),
            jax.ShapeDtypeStruct((tokens, 4 * width), BF),
            heads, heads, heads, heads,
            jax.ShapeDtypeStruct(table.shape, BF),
            heads,
            jax.ShapeDtypeStruct(heads_shape, F32),
        ],
        compiler_params=comm_params(cid),
        name="front",
    )(lens, x, table, packed_a, packed_b, packed_c, slab)


def fill_table(table_ref, first_s, second_s):
    length, width = table_ref.shape[0] // 2, table_ref.shape[1]
    step = 32
    cols = lax.broadcasted_iota(jnp.int32, (step, width), 1)
    rows = lax.broadcasted_iota(jnp.int32, (step, width), 0)
    rate = jnp.exp((cols // 2 * 2).astype(F32) * (-math.log(10000.0) / width))
    even = cols % 2 == 0
    big = (length - 1 - step * rows).astype(F32) * rate
    small = rows.astype(F32) * rate
    sin_big, cos_big = jnp.sin(big), jnp.cos(big)
    first = jnp.where(even, sin_big, cos_big)
    second = jnp.where(even, cos_big, -sin_big)
    cos_small, sin_small = jnp.cos(small), jnp.sin(small)
    first_s[...] = first
    second_s[...] = second

    @pl.loop(0, 2 * length // step)
    def _(a):
        one, two = first_s[pl.ds(a, 1), :], second_s[pl.ds(a, 1), :]
        block = one * cos_small - two * sin_small
        table_ref[pl.ds(pl.multiple_of(a * step, step), step), :] = block.astype(BF)


def table_call(full, width):
    return pl.pallas_call(
        fill_table,
        out_specs=VM,
        out_shape=jax.ShapeDtypeStruct((2 * full, width), BF),
        scratch_shapes=[pltpu.VMEM((32, width), F32)] * 2,
        name="position_table",
    )()


def conv1_kernel(
    lens, mixed, first, w_out, w_ci, vecs, second_ref, half_ref, conv_ref, stat_ref, pad
):
    u = pl.program_id(0)
    full = first.shape[0]
    count = lens[u]
    part = w_out.shape[2]
    y = row(vecs, 5)
    for t in range(2):
        y = y + nt(mixed[:, t * part : (t + 1) * part], w_out[t])
    second = first[...] + y
    second_ref[...] = second
    scaled, _ = ln_stats(second)
    hn = (scaled * row(vecs, 6) + row(vecs, 7)).astype(BF)
    mask = row_mask(0, full, count)
    pad[0:8, :] = jnp.zeros((8, part), F32)
    pad[full + 8 : full + 16, :] = jnp.zeros((8, part), F32)
    for t in range(2):
        c = slice(t * part, (t + 1) * part)
        proj = nn(hn, w_ci[t])
        za = proj[:, :part] + vecs[R_CV : R_CV + 1, c]
        zg = proj[:, part:] + vecs[R_CV + 1 : R_CV + 2, c]
        half_ref[:, 2 * t * part : (2 * t + 1) * part] = za.astype(BF)
        half_ref[:, (2 * t + 1) * part : (2 * t + 2) * part] = zg.astype(BF)
        pad[8 : full + 8, :] = za * sig(zg) * mask
        total = jnp.zeros((full, part), F32)
        for k in range(9):
            total = total + vecs[R_CV + 4 + k : R_CV + 5 + k, c] * pad[4 + k : 4 + k + full, :]
        conv_ref[:, c] = total
        kept = total * mask
        stat_ref[pl.ds(4 * u, 1), c] = col_sum(kept)
        stat_ref[pl.ds(4 * u + 1, 1), c] = col_sum(kept * total)
    for k in (2, 3):
        stat_ref[pl.ds(4 * u + k, 1), :] = jnp.full((1, 2 * part), 1.0, F32) * count.astype(F32)


def with_sum(kernel, spot, cid):
    def body(*refs):
        sums = refs[-8:]
        refs = list(refs[:-8])
        call, meet = sum_steps(sums)
        out = refs[spot]
        refs[spot] = sums[0]

        @pl.when(pl.program_id(0) == 0)
        def _():
            call()

        kernel(*refs)

        @pl.when(pl.program_id(0) == pl.num_programs(0) - 1)
        def _():
            for part in meet(out):
                part()

    return kernel if cid is None else body


def conv1_call(lens, mixed, first, g, vecs, cid=None):
    tokens, width = first.shape
    batch = lens.shape[0]
    full = tokens // batch
    return pl.pallas_call(
        with_sum(conv1_kernel, 9, cid),
        grid_spec=pltpu.PrefetchScalarGridSpec(
            num_scalar_prefetch=1,
            grid=(batch,),
            in_specs=[
                tall(full, width), tall(full, width), seg_spec("out", width),
                seg_spec("ci", width), whole(vecs.shape),
            ],
            out_specs=[
                tall(full, width), tall(full, 2 * width), tall(full, width),
                whole((4 * batch, width)),
            ],
            scratch_shapes=[pltpu.VMEM((full + 16, width // 2), F32)]
            + ([] if cid is None else sum_scratch((4 * batch, width))),
        ),
        out_shape=[
            jax.ShapeDtypeStruct((tokens, width), F32),
            jax.ShapeDtypeStruct((tokens, 2 * width), BF),
            jax.ShapeDtypeStruct((tokens, width), F32),
            jax.ShapeDtypeStruct((4 * batch, width), F32),
        ],
        compiler_params=dense_params() if cid is None else comm_params(cid),
        name="conv_forward",
    )(lens, mixed, first, g, g, vecs)


def bn_of(stats, u):
    n = stats[pl.ds(4 * u + 2, 1), :]
    avg = stats[pl.ds(4 * u, 1), :] / n
    var = stats[pl.ds(4 * u + 1, 1), :] / n - avg * avg
    return avg, lax.rsqrt(var + norm_eps), n


def swish_parts(z):
    s = sig(z)
    a = z * s
    return a, s + a * (1.0 - s)


def middle_kernel(
    lens, second, conv, cot, stats, w_co, w_in, w_out, vecs,
    act_ref, d3_ref, dy_ref, sum_ref, small_ref, gi_ref, go_ref, gc_ref,
    a_s, slope_s, gi, go, gc,
):
    i = pl.program_id(0)
    steps = pl.num_programs(0)
    rows, width = second.shape
    batch = lens.shape[0]
    per = steps // batch
    u = i // per
    mask = row_mask(lax.rem(i, per) * rows, rows, lens[u])

    @pl.when(i == 0)
    def _():
        small_ref[...] = jnp.zeros_like(small_ref)
        sum_ref[...] = jnp.zeros_like(sum_ref)
        gi[...] = jnp.zeros_like(gi)
        go[...] = jnp.zeros_like(go)
        gc[...] = jnp.zeros_like(gc)

    avg, rstd, _ = bn_of(stats, u)
    part = w_co.shape[2]
    half = w_in.shape[2]
    yhat = (conv[...] - avg) * rstd
    bn, bn_slope = swish_parts(yhat * row(vecs, R_CV + 2) + row(vecs, R_CV + 3))
    act = bn.astype(BF)
    y = row(vecs, 8)
    for t in range(2):
        y = y + nt(act[:, t * part : (t + 1) * part], w_co[t])
    third = second[...] + y
    scaled9, inv9 = ln_stats(third)
    hn = (scaled9 * row(vecs, 9) + row(vecs, 10)).astype(BF)
    y = row(vecs, 11)
    for t in range(2):
        c = slice(t * half, (t + 1) * half)
        a, slope = swish_parts(nn(hn, w_in[t]) + bias_half(vecs, R_B2, t))
        a = a.astype(BF)
        a_s[:, c] = a
        slope_s[:, c] = slope
        y = y + nt(a, w_out[t])
    scaled, inv = ln_stats(third + 0.5 * y)
    act_ref[...] = (scaled * row(vecs, 12) + row(vecs, 13)).astype(BF)
    up = cot[...].astype(F32) * mask
    small_ref[12:13, :] += col_sum(up * scaled)
    small_ref[13:14, :] += col_sum(up)
    d4 = ln_back(up, scaled, inv, row(vecs, 12))
    g = (0.5 * d4).astype(BF)
    small_ref[11:12, :] += col_sum(g.astype(F32))
    d_hn = jnp.zeros((rows, width), F32)
    for t in range(2):
        c = slice(t * half, (t + 1) * half)
        go[t] += tn(g, a_s[:, c])
        dz = (nn(g, w_out[t]) * slope_s[:, c]).astype(BF)
        bias = col_sum(dz.astype(F32))
        small_ref[R_B2 + 2 * t : R_B2 + 2 * t + 1, :] += bias[:, :width]
        small_ref[R_B2 + 2 * t + 1 : R_B2 + 2 * t + 2, :] += bias[:, width:]
        gi[t] += tn(hn, dz)
        d_hn = d_hn + nt(dz, w_in[t])
    small_ref[9:10, :] += col_sum(d_hn * scaled9)
    small_ref[10:11, :] += col_sum(d_hn)
    d3 = d4 + ln_back(d_hn, scaled9, inv9, row(vecs, 9))
    d3_ref[...] = d3
    g = d3.astype(BF)
    small_ref[8:9, :] += col_sum(g.astype(F32))
    d_act = []
    for t in range(2):
        gc[t] += tn(g, act[:, t * part : (t + 1) * part])
        d_act.append(nn(g, w_co[t]))
    d_bn = jnp.concatenate(d_act, axis=1) * bn_slope
    small_ref[R_CV + 2 : R_CV + 3, :] += col_sum(d_bn * yhat)
    small_ref[R_CV + 3 : R_CV + 4, :] += col_sum(d_bn)
    d_yhat = d_bn * row(vecs, R_CV + 2)
    dy_ref[...] = d_yhat
    sum_ref[pl.ds(4 * u, 1), :] += col_sum(d_yhat)
    sum_ref[pl.ds(4 * u + 1, 1), :] += col_sum(d_yhat * yhat)

    @pl.when(i == steps - 1)
    def _():
        gi_ref[...] = gi[...].astype(BF)
        go_ref[...] = go[...].astype(BF)
        gc_ref[...] = gc[...].astype(BF)


def grad_shape(name, width):
    return jax.ShapeDtypeStruct((2, width, SEG[name][1]), BF)


def acc(name, width):
    return pltpu.VMEM((2, width, SEG[name][1]), F32)


def once(shape):
    zeros = (0,) * len(shape)
    return pl.BlockSpec(shape, lambda i, *_: zeros, pipeline_mode=pl.Buffered(1))


def middle_call(lens, second, conv, cot, stats, g, g_f2, vecs, cid=None):
    tokens, width = second.shape
    small = (R_ALL, width)
    names = ("f2i", "f2o", "co")
    return pl.pallas_call(
        with_sum(middle_kernel, 12, cid),
        grid_spec=pltpu.PrefetchScalarGridSpec(
            num_scalar_prefetch=1,
            grid=(tokens // TB,),
            in_specs=[tall(TB, width)] * 3
            + [whole(stats.shape), seg_spec("co", width), seg_spec("f2i", width)]
            + [seg_spec("f2o", width), whole(vecs.shape)],
            out_specs=[tall(TB, width)] * 3
            + [whole(stats.shape), whole(small)]
            + [whole(grad_shape(name, width).shape) for name in names],
            scratch_shapes=[
                pltpu.VMEM((TB, 4 * width), BF),
                pltpu.VMEM((TB, 4 * width), F32),
            ]
            + [acc(name, width) for name in names]
            + ([] if cid is None else sum_scratch(stats.shape)),
        ),
        out_shape=[
            jax.ShapeDtypeStruct((tokens, width), BF),
            jax.ShapeDtypeStruct((tokens, width), F32),
            jax.ShapeDtypeStruct((tokens, width), F32),
            jax.ShapeDtypeStruct(stats.shape, F32),
            jax.ShapeDtypeStruct(small, F32),
        ]
        + [grad_shape(name, width) for name in names],
        compiler_params=dense_params() if cid is None else comm_params(cid),
        name="conv_out_ffn2",
    )(lens, second, conv, cot, stats, g, g_f2, g_f2, vecs)


def conv2_kernel(
    lens, dy, conv, d3, halves, second, mixed, stats, sums, w_ci, w_out, vecs,
    d2_ref, dm_ref, small_ref, gi_ref, go_ref, pad, dh_s, gi, go,
):
    u = pl.program_id(0)
    full, width = d3.shape
    part = w_out.shape[2]

    @pl.when(u == 0)
    def _():
        small_ref[...] = jnp.zeros_like(small_ref)
        gi[...] = jnp.zeros_like(gi)
        go[...] = jnp.zeros_like(go)

    avg, rstd, n = bn_of(stats, u)
    mask = row_mask(0, full, lens[u])
    scaled, inv = ln_stats(second[...])
    hn = (scaled * row(vecs, 6) + row(vecs, 7)).astype(BF)
    pad[0:8, :] = jnp.zeros((8, part), F32)
    pad[full + 8 : full + 16, :] = jnp.zeros((8, part), F32)
    b1 = sums[pl.ds(4 * u, 1), :]
    b2 = sums[pl.ds(4 * u + 1, 1), :]
    dh_s[...] = jnp.zeros_like(dh_s)
    taps = vecs[R_CV : R_CV + 13, :]

    @pl.loop(0, 2)
    def _(t):
        c = pl.ds(pl.multiple_of(t * part, part), part)

        def lanes(v):
            return jnp.where(t == 0, v[:, :part], v[:, part:])

        yhat = (conv[:, c] - lanes(avg)) * lanes(rstd)
        pad[8 : full + 8, :] = lanes(rstd) * (
            dy[:, c] - mask * ((lanes(b1) + yhat * lanes(b2)) / lanes(n))
        )
        za = halves[:, pl.ds(pl.multiple_of(2 * t * part, part), part)].astype(F32)
        zg = halves[:, pl.ds(pl.multiple_of((2 * t + 1) * part, part), part)].astype(F32)
        gate = sig(zg)
        gated = za * gate * mask
        total = jnp.zeros((full, part), F32)
        mine = lanes(taps)
        for k in range(9):
            moved = pad[12 - k : 12 - k + full, :]
            total = total + mine[4 + k : 5 + k, :] * moved
            small_ref[R_CV + 4 + k : R_CV + 5 + k, c] += col_sum(gated * moved)
        d_glu = total * mask
        d_a = (d_glu * gate).astype(BF)
        d_g = (d_glu * gated * (1.0 - gate)).astype(BF)
        small_ref[R_CV : R_CV + 1, c] += col_sum(d_a.astype(F32))
        small_ref[R_CV + 1 : R_CV + 2, c] += col_sum(d_g.astype(F32))
        pair = jnp.concatenate([d_a, d_g], axis=1)
        gi[t] += tn(hn, pair)
        dh_s[...] += nt(pair, w_ci[t])

    d_hn = dh_s[...]
    small_ref[6:7, :] += col_sum(d_hn * scaled)
    small_ref[7:8, :] += col_sum(d_hn)
    d2 = d3[...] + ln_back(d_hn, scaled, inv, row(vecs, 6))
    d2_ref[...] = d2
    g = d2.astype(BF)
    small_ref[5:6, :] += col_sum(g.astype(F32))
    @pl.loop(0, 2)
    def _(t):
        c = pl.ds(pl.multiple_of(t * part, part), part)
        go[t] += tn(g, mixed[:, c])
        dm_ref[:, c] = nn(g, w_out[t]).astype(BF)

    @pl.when(u == pl.num_programs(0) - 1)
    def _():
        gi_ref[...] = gi[...].astype(BF)
        go_ref[...] = go[...].astype(BF)


def conv2_call(lens, dy, conv, d3, halves, second, mixed, stats, sums, g, vecs):
    tokens, width = second.shape
    batch = lens.shape[0]
    full = tokens // batch
    small = (R_ALL, width)
    names = ("ci", "out")
    return pl.pallas_call(
        conv2_kernel,
        grid_spec=pltpu.PrefetchScalarGridSpec(
            num_scalar_prefetch=1,
            grid=(batch,),
            in_specs=[tall(full, width)] * 3
            + [tall(full, 2 * width), tall(full, width), tall(full, width)]
            + [whole(stats.shape)] * 2
            + [seg_spec("ci", width), seg_spec("out", width), whole(vecs.shape)],
            out_specs=[tall(full, width)] * 2
            + [whole(small)]
            + [whole(grad_shape(name, width).shape) for name in names],
            scratch_shapes=[
                pltpu.VMEM((full + 16, width // 2), F32), pltpu.VMEM((full, width), F32),
            ]
            + [acc(name, width) for name in names],
        ),
        out_shape=[
            jax.ShapeDtypeStruct((tokens, width), F32),
            jax.ShapeDtypeStruct((tokens, width), BF),
            jax.ShapeDtypeStruct(small, F32),
        ]
        + [grad_shape(name, width) for name in names],
        compiler_params=dense_params(),
        name="conv_backward",
    )(lens, dy, conv, d3, halves, second, mixed, stats, sums, g, g, vecs)


def last_kernel(
    dq, dk, dv, first, x_ref, d2, z_ref, table, dpos, asums, w_qkv, w_in, w_out, vecs,
    d0_ref, small_ref, d1_s, g_s, hn_s, dh_s, gq, gp, z_s, w_in_s, w_out_s, in_sem,
    put, ready, after,
):
    i = pl.program_id(0)
    blocks = x_ref.shape[0] // TB
    rows, width = first.shape
    part = w_qkv.shape[2] // 3
    ahead = [
        pltpu.make_async_copy(w_in.at[:, :, pl.ds(0, w_in_s.shape[2])], w_in_s, in_sem.at[0]),
        pltpu.make_async_copy(
            w_out.at[:, :, pl.ds(w_in_s.shape[2], w_in_s.shape[2])], w_out_s, in_sem.at[1]
        ),
        pltpu.make_async_copy(z_ref, z_s, in_sem.at[2]),
    ]

    @pl.when(i == 0)
    def _():
        small_ref[...] = jnp.zeros_like(small_ref)
        small_ref[R_ATT:R_CV, :] = jnp.sum(asums[...], axis=0)[0:4]
        for copy in ahead:
            copy.start()
        gq[...] = jnp.zeros_like(gq)
        gp[...] = jnp.zeros_like(gp)
        dh_s[...] = jnp.zeros_like(dh_s)

    @pl.when(i < blocks)
    def _():
        here = pl.ds(pl.multiple_of(i * TB, TB), TB)
        scaled, inv = ln_stats(first[...])
        hn = (scaled * row(vecs, 3) + row(vecs, 4)).astype(BF)
        d_hn = jnp.zeros((rows, width), F32)
        for t in range(2):
            c = slice(t * part, (t + 1) * part)
            dp = jnp.concatenate([dq[:, c], dk[:, c], dv[:, c]], axis=1)
            gq[t] += tn(hn, dp)
            for u in range(dpos.shape[0]):
                gp[t] += tn(table[...], dpos[u, :, c])
            d_hn = d_hn + nt(dp, w_qkv[t])
        small_ref[3:4, :] += col_sum(d_hn * scaled)
        small_ref[4:5, :] += col_sum(d_hn)
        d1 = d2[...] + ln_back(d_hn, scaled, inv, row(vecs, 3))
        d1_s[here, :] = d1
        g = (0.5 * d1).astype(BF)
        g_s[here, :] = g
        small_ref[2:3, :] += col_sum(g.astype(F32))
        scaled, inv = ln_stats(x_ref[here, :].astype(F32))
        hn_s[here, :] = (scaled * row(vecs, 0) + row(vecs, 1)).astype(BF)

    @pl.when(i == blocks - 1)
    def _():
        for t in range(2):
            put("pos", t, 0, gp[t])
            put("qkv", t, 0, gq[t])
        for copy in ahead:
            copy.wait()
        ready(-1)

    chunks = w_in_s.shape[2] // HC

    @pl.when(i >= blocks)
    def _():
        j = i - blocks
        at = pl.multiple_of(j * HC, HC)
        c = pl.ds(at, HC)
        odd = lax.rem(j, 2) == 1
        @pl.loop(0, 2)
        def _(t):
            zc = pl.ds(pl.multiple_of((2 * j + t) * HC, HC), HC)
            a, slope = swish_parts(z_s[:, zc].astype(F32))
            put("f1o", t, at, tn(g_s[...], a.astype(BF)))
            dz = (nn(g_s[...], w_out_s[t, :, c]) * slope).astype(BF)
            bias = col_sum(dz.astype(F32))
            none = jnp.zeros_like(bias)
            pair = [jnp.where(odd, none, bias), jnp.where(odd, bias, none)]
            line = pl.ds(R_B1 + 2 * t + j // 2, 1)
            small_ref[line, :] += jnp.concatenate(pair, axis=1)
            put("f1i", t, at, tn(hn_s[...], dz))
            dh_s[...] += nt(dz, w_in_s[t, :, c])
            for k in range(chunks):
                for side in range(2):

                    @pl.when((j == k) & (t == side))
                    def _(k=k, side=side):
                        after(k, side)

        for k in range(chunks):

            @pl.when(j == k)
            def _(k=k):
                ready(k)

    @pl.when(i == blocks + chunks - 1)
    def _():
        @pl.loop(0, blocks)
        def _(k):
            here = pl.ds(pl.multiple_of(k * TB, TB), TB)
            scaled, inv = ln_stats(x_ref[here, :].astype(F32))
            d_hn = dh_s[here, :]
            small_ref[0:1, :] += col_sum(d_hn * scaled)
            small_ref[1:2, :] += col_sum(d_hn)
            d0 = d1_s[here, :] + ln_back(d_hn, scaled, inv, row(vecs, 0))
            d0_ref[here, :] = d0.astype(BF)


def last_call(dq, dk, dv, first, x, d2, z, table, dpos, asums, g, vecs, others=None, cid=None):
    tokens, width = first.shape
    blocks, chunks = tokens // TB, SEG["f1i"][1] // HC
    small = (R_ALL, width)
    places = table.shape[0] // blocks

    def block(rows, cols):
        return pl.BlockSpec((rows, cols), lambda i: (jnp.minimum(i, blocks - 1), 0))

    in_specs = (
        [block(TB, width)] * 4
        + [whole(x.shape), block(TB, width)]
        + [ANY]
        + [block(places, width)]
        + [
            pl.BlockSpec(
                (dpos.shape[0], places, width), lambda i: (0, jnp.minimum(i, blocks - 1), 0)
            ),
            whole(asums.shape),
        ]
        + [seg_spec("qkv", width), ANY, ANY, whole(vecs.shape)]
    )
    args = [dq, dk, dv, first, x, d2, z, table, dpos, asums, g, g, g, vecs]
    scratch = [
        pltpu.VMEM((tokens, width), F32), pltpu.VMEM((tokens, width), BF),
        pltpu.VMEM((tokens, width), BF), pltpu.VMEM((tokens, width), F32),
        acc("qkv", width), acc("pos", width), pltpu.VMEM(z.shape, BF),
        pltpu.VMEM((2, width, SEG["f1i"][1]), BF), pltpu.VMEM((2, width, SEG["f1o"][1]), BF),
        pltpu.SemaphoreType.DMA((3,)),
    ]
    out_specs = [whole((tokens, width)), whole(small)]
    out_shape = [jax.ShapeDtypeStruct((tokens, width), BF), jax.ShapeDtypeStruct(small, F32)]
    n_own = len(scratch)
    if others is None:
        names = ("qkv", "f1i", "f1o", "pos")
        out_specs += [once(grad_shape(name, width).shape) for name in names]
        out_shape += [grad_shape(name, width) for name in names]

        def body(*refs):
            ins, rest = refs[: len(args)], refs[len(args) :]
            outs = dict(zip(names, rest[2:6]))

            def put(name, t, at, value):
                outs[name][t, :, pl.ds(at, value.shape[1])] = value.astype(BF)

            last_kernel(*ins, *rest[:2], *rest[6:], put, lambda j: None, lambda j, t: None)

        params = dense_params()
    else:
        owned = width // (NZ * NY * NX)
        names = ("pos", "qkv", "f1i", "f1o")
        base = {name: SEG[name][0] for name in names}
        order = [("pos", 0), ("qkv", 0), ("qkv", 256), ("qkv", 512)]
        for j in range(chunks):
            order += [("f1i", j * HC), ("f1o", j * HC)]
        pieces = [(0, base[name] + at, 256, base[name] + at) for name, at in order]
        n_first = 4
        n_in = len(args)
        args += list(others)
        in_specs += [whole(item.shape) for item in others]
        out_specs = out_specs[:1] + [whole((owned, C_A)), whole((R_SUM, width))]
        out_shape = out_shape[:1] + [
            jax.ShapeDtypeStruct((owned, C_A), F32), jax.ShapeDtypeStruct((R_SUM, width), F32)
        ]
        small_scratch = small_sum_scratch(width)
        scratch += [pltpu.VMEM(small, F32), pltpu.VMEM((2, NZ, NY, NX, owned, C_A), BF)]
        scratch += small_scratch + scatter_scratch(pieces, owned)
        params = comm_params(cid)

        def body(*refs):
            i = pl.program_id(0)
            ins, rest = refs[:n_in], refs[n_in:]
            parts, rest = rest[: len(others)], rest[len(others) :]
            (d0_ref, o_ref, ext), rest = rest[:3], rest[3:]
            own, rest = rest[:n_own], rest[n_own:]
            (small_ref, buf), rest = rest[:2], rest[2:]
            sums, sems = rest[: len(small_scratch)], rest[len(small_scratch) :]
            start, advance, finish, rounds = scatter_steps(pieces, [buf], o_ref, sems, 4)
            pp, small_list = small_sum_steps(list(parts) + [small_ref], ext, sums)
            z, y, x, t = place()

            def put(name, t, at, value):
                w = value.shape[1]
                at = base[name] + at
                at = at if isinstance(at, int) else pl.multiple_of(at, HC)
                value = value.astype(BF).reshape(NZ, NY, NX, owned, w)
                buf[t, :, :, :, :, pl.ds(at, w)] = value

            def ready(j):
                if j < 0:
                    hear(peers)
                for p in range(n_first) if j < 0 else (n_first + 2 * j, n_first + 2 * j + 1):
                    start(p)

            def after(j, t):
                if j == 0:
                    advance(2 * t)
                    advance(2 * t + 1)
                else:
                    advance(n_first + 2 * (j - 1) + t)

            peers = link_peers(z, y, x, t)[: NZ - 1] + pp + [dev(z, y, x, 1 - t)]

            @pl.when(i == 0)
            def _():
                hail(peers)

            last_kernel(*ins, d0_ref, small_ref, *own, put, ready, after)

            @pl.when(i == blocks + chunks - 1)
            def _():
                todo = [lambda q=q: advance(q) for q in range(n_first + 2 * (chunks - 1), rounds)]
                for k, step in enumerate(todo):
                    if k % 2 == 0 and k // 2 < len(small_list):
                        small_list[k // 2]()
                    step()
                for step in small_list[(len(todo) + 1) // 2 :]:
                    step()
                finish()

    return pl.pallas_call(
        body,
        grid=(blocks + chunks,),
        in_specs=in_specs,
        out_specs=out_specs,
        scratch_shapes=scratch,
        out_shape=out_shape,
        compiler_params=params,
        name="qkv_ffn1_backward",
    )(*args)


def gather_plain(big, kinds, groups, small_ins, both, n_dp):
    def pack(names):
        return jnp.concatenate(
            [big[n].T if kinds[n][0] == "flip" else big[n] for n in names], axis=1
        )

    def every(item):
        g = lax.all_gather(item, both, axis=0, tiled=True)
        g = g.reshape(n_dp, 2, item.shape[0], -1).transpose(1, 0, 2, 3)
        return g.reshape(2, n_dp * item.shape[0], -1)

    small = jnp.concatenate([item.reshape(-1) for item in small_ins])
    smalls = lax.all_gather(small, both, axis=0, tiled=False).reshape(n_dp, 2, -1).astype(F32)
    off = 0
    pieces = []
    for item in small_ins:
        pieces.append(smalls[:, :, off : off + item.size].reshape((n_dp, 2) + item.shape))
        off += item.size
    width = small_ins[4].shape[1] * n_dp * 2
    vecs = jnp.concatenate(
        [
            pieces[4].transpose(2, 0, 1, 3).reshape(-1, width),
            pieces[1].transpose(2, 1, 3, 0, 4).reshape(-1, width),
            pieces[2].transpose(2, 1, 3, 0, 4).reshape(-1, width),
            pieces[0].transpose(1, 2, 0, 3).reshape(-1, width),
            pieces[3].transpose(1, 2, 0, 3).reshape(-1, width),
            jnp.zeros((1, width), F32),
        ],
        axis=0,
    )
    return tuple(every(pack(names)) for names in groups) + (vecs,)


def scatter_plain(grads, kinds, names, small_g, small_ins, both, n_dp):
    vec_g = (
        small_g[R_B1:R_B2].reshape(1, -1), small_g[R_ATT:R_CV], small_g[R_CV:R_B1],
        small_g[R_B2 : R_B2 + 4].reshape(1, -1),
    )

    def small_of(item, like):
        item = item.reshape(item.shape[0], 2, like.shape[-2], n_dp, like.shape[-1])
        return item.transpose(1, 3, 0, 2, 4).reshape(2, n_dp, -1)

    cols = small_ins[4].shape[1]
    norm_g = small_g[:R_ATT].reshape(-1, n_dp, 2, cols).transpose(2, 1, 0, 3).reshape(2, n_dp, -1)
    packed = jnp.concatenate(
        [small_of(item, like) for item, like in zip(vec_g, small_ins)] + [norm_g], axis=2
    )
    packed = packed.swapaxes(0, 1).reshape(n_dp * 2, -1)
    own_small = lax.psum_scatter(packed, both, scatter_dimension=0, tiled=True).reshape(-1)
    wide = jnp.concatenate([grads[name] for name in names], axis=2)
    rows = wide.shape[1] // n_dp
    wide = wide.reshape(2, n_dp, rows, -1).swapaxes(0, 1).reshape(n_dp * 2 * rows, -1)
    own = lax.psum_scatter(wide, both, scatter_dimension=0, tiled=True).astype(F32)
    outs, at = {}, 0
    for name in names:
        w = grads[name].shape[2]
        item = own[:, at : at + w]
        outs[name] = item.T if kinds[name][0] == "flip" else item
        at += w
    small_outs, at = [], 0
    for item in small_ins:
        small_outs.append(own_small[at : at + item.size].reshape(item.shape))
        at += item.size
    return outs, small_outs


def local(
    frames,
    lengths,
    ffn1_in,
    ffn1_out,
    ffn1_bias,
    qkv_weight,
    pos_weight,
    out_weight,
    attn_bias,
    conv_in,
    conv_out,
    conv_channel,
    ffn2_in,
    ffn2_out,
    ffn2_bias,
    norm_params,
    cotangent,
):
    micro, seqs, full, width = frames.shape
    both = ("dp", "tensor")
    n_dp = lax.axis_size("dp")
    rows = ffn1_in.shape[0]
    batch = micro * seqs
    tokens = batch * full
    small_ins = (ffn1_bias, attn_bias, conv_channel, ffn2_bias, norm_params)
    names_a, names_b = ("f1i", "f1o", "pos", "qkv"), tuple(OWN)
    big = {
        "f1i": ffn1_in, "f1o": ffn1_out, "pos": pos_weight, "qkv": qkv_weight.reshape(rows, -1),
        "f2i": ffn2_in, "f2o": ffn2_out, "ci": conv_in.reshape(rows, -1), "out": out_weight,
        "co": conv_out,
    }
    kinds = {name: ("plain",) for name in big}
    kinds.update({name: ("flip",) for name in ("f1o", "f2o", "out", "co")})
    mine_mesh = own_mesh((n_dp, lax.axis_size("tensor"))) and rows % 16 == 0
    if mine_mesh:
        packed_a, packed_b, packed_c, slab, table = prep_call(
            [
                ffn1_in, ffn1_out.T, pos_weight, qkv_weight.transpose(1, 0, 2), ffn2_in,
                ffn2_out.T, conv_in, out_weight.T, conv_out.T,
            ],
            [ffn1_bias, attn_bias, conv_channel.transpose(1, 2, 0), ffn2_bias, norm_params],
            full, width,
        )
    else:
        table = table_call(full, width)
        groups = (names_a, names_b[2:], names_b[:2])
        g_a, g_b, g_c, vecs = gather_plain(big, kinds, groups, small_ins, both, n_dp)

    def reduce_sum(item):
        return item if mine_mesh else lax.psum(item, both)

    mine = lax.axis_index("tensor")
    lens = lax.dynamic_slice_in_dim(lengths, mine * seqs, seqs, 1).reshape(-1)
    x = frames.reshape(tokens, width)
    cot = cotangent.reshape(tokens, width)

    def utt(item):
        return item.reshape(batch, full, -1)

    def flat(item):
        return item.reshape(tokens, -1)

    if mine_mesh:
        g_a, g_b, g_c, vecs, first, z1, q_u, q_v, keys, values, pos, mixed, lse = front_call(
            lens, x, table, packed_a, packed_b, packed_c, slab, batch, 1
        )
        g_a, g_b, g_c = (item.reshape(2, width, -1) for item in (g_a, g_b, g_c))
        heads = (lens, q_u, q_v, keys, values, pos)
    else:
        first, z1, q_u, q_v, keys, values, pos = ffn1_call(x, table, g_a, vecs)
        heads = (lens, utt(q_u), utt(q_v), utt(keys), utt(values), pos)
        mixed, lse = attn_fwd_call(*heads)
    second, halves, conv, stats = conv1_call(
        lens, flat(mixed), first, g_b, vecs, 3 if mine_mesh else None
    )
    stats = reduce_sum(stats)
    grads = {}
    result, d3, d_yhat, sums, small_m, grads["f2i"], grads["f2o"], grads["co"] = middle_call(
        lens, second, conv, cot, stats, g_b, g_c, vecs, 4 if mine_mesh else None
    )
    sums = reduce_sum(sums)
    d2, d_mixed, small_c, grads["ci"], grads["out"] = conv2_call(
        lens, d_yhat, conv, d3, halves, second, flat(mixed), stats, sums, g_b, vecs
    )
    if mine_mesh:
        dq, dk, dv, dpos, asums, own_b = attn_bwd_call(
            *heads, mixed, lse, utt(d_mixed), [grads[name] for name in names_b], 5
        )
        d0, own_a, ext = last_call(
            flat(dq), flat(dk), flat(dv), first, x, d2, z1, table, dpos, asums, g_a, vecs,
            (small_m, small_c), 6,
        )
        outs = finish_call(own_a, own_b, ext, rows)
    else:
        dq, dk, dv, dpos, asums = attn_bwd_call(*heads, mixed, lse, utt(d_mixed))
        d0, small_l, grads["qkv"], grads["f1i"], grads["f1o"], grads["pos"] = last_call(
            flat(dq), flat(dk), flat(dv), first, x, d2, z1, table, dpos, asums, g_a, vecs
        )
        o, small_outs = scatter_plain(
            grads, kinds, names_a + names_b, small_m + small_c + small_l, small_ins, both, n_dp
        )
        outs = (
            o["f1i"], o["f1o"], small_outs[0], o["qkv"].reshape(qkv_weight.shape), o["pos"],
            o["out"], small_outs[1], o["ci"].reshape(conv_in.shape), o["co"], small_outs[2],
            o["f2i"], o["f2o"], small_outs[3], small_outs[4],
        )
    return (result.reshape(frames.shape), d0.reshape(frames.shape)) + tuple(outs)


def solution(mesh):
    in_specs = (
        P(None, ("dp", "tensor"), None, None),
        P(None, "dp"),
        P("dp", "tensor"),
        P("tensor", "dp"),
        P("tensor", "dp"),
        P("dp", None, "tensor"),
        P("dp", "tensor"),
        P("tensor", "dp"),
        P(None, "tensor", "dp"),
        P("dp", None, "tensor"),
        P("tensor", "dp"),
        P(None, "tensor", "dp"),
        P("dp", "tensor"),
        P("tensor", "dp"),
        P("tensor", "dp"),
        P(None, ("dp", "tensor")),
        P(None, ("dp", "tensor"), None, None),
    )
    out_specs = (
        P(None, ("dp", "tensor"), None, None),
        P(None, ("dp", "tensor"), None, None),
        P("dp", "tensor"),
        P("tensor", "dp"),
        P("tensor", "dp"),
        P("dp", None, "tensor"),
        P("dp", "tensor"),
        P("tensor", "dp"),
        P(None, "tensor", "dp"),
        P("dp", None, "tensor"),
        P("tensor", "dp"),
        P(None, "tensor", "dp"),
        P("dp", "tensor"),
        P("tensor", "dp"),
        P("tensor", "dp"),
        P(None, ("dp", "tensor")),
    )
    return jax.shard_map(local, mesh=mesh, in_specs=in_specs, out_specs=out_specs, check_vma=False)
```

```python
import math

import jax
import jax.numpy as jnp
from jax import lax
from jax.experimental import pallas as pl
from jax.experimental.pallas import tpu as pltpu
from jax.sharding import PartitionSpec as P

DK = 64
norm_eps = 1e-05
mask_fill = -1000000000.0
BF = jnp.bfloat16
F32 = jnp.float32
BLK = 128


def nn(a, b):
    return lax.dot_general(a, b, (((1,), (0,)), ((), ())), preferred_element_type=F32)


def nt(a, b):
    return lax.dot_general(a, b, (((1,), (1,)), ((), ())), preferred_element_type=F32)


def tn(a, b):
    return lax.dot_general(a, b, (((0,), (0,)), ((), ())), preferred_element_type=F32)


def attn_fwd_kernel(len_ref, qu, qv, k, v, pos, o_ref, lse_ref, u=None, hook=None):
    count = len_ref[pl.program_id(0) if u is None else u]
    full = k.shape[1]
    lane = lax.broadcasted_iota(jnp.int32, (BLK, 2 * DK), 1)
    col = lax.broadcasted_iota(jnp.int32, (BLK, full), 1)
    keep = col < count
    zero = jnp.zeros((), BF)
    for blk in range(full // BLK):
        i0 = blk * BLK
        base = full - BLK - i0
        if hook is not None:
            hook(blk)
        outs, logs = [], []
        for h in range(2):
            mine = (lane < DK) if h == 0 else (lane >= DK)
            q_u = jnp.where(mine, qu[0, i0 : i0 + BLK, :], zero)
            q_v = jnp.where(mine, qv[0, i0 : i0 + BLK, :], zero)
            rel = nt(q_v, pos[base : base + full + BLK, :])
            rel = pltpu.roll(rel, full + 1, 1, stride=1, stride_axis=0)[:, :full]
            s = (nt(q_u, k[0]) + rel) * (1.0 / math.sqrt(DK))
            s = jnp.where(keep, s, mask_fill)
            top = jnp.max(s, axis=1, keepdims=True)
            e = jnp.exp(s - top)
            total = jnp.sum(e, axis=1, keepdims=True)
            outs.append(nn(e.astype(BF), v[0]) / total)
            logs.append(top + jnp.log(total))
        left = lane < DK
        o_ref[0, i0 : i0 + BLK, :] = jnp.where(left, outs[0], outs[1]).astype(BF)
        lse_ref[0, i0 : i0 + BLK, :] = jnp.where(left, logs[0], logs[1])


def attn_bwd_kernel(
    len_ref, qu, qv, k, v, pos, o, lse, do, dq_ref, dk_ref, dv_ref, dpos_ref, sum_ref, dkt, dvt, dpt,
    hook=None,
):
    count = len_ref[pl.program_id(0)]
    full = k.shape[1]
    scale = 1.0 / math.sqrt(DK)
    lane = lax.broadcasted_iota(jnp.int32, (BLK, 2 * DK), 1)
    left = lane < DK
    keep = lax.broadcasted_iota(jnp.int32, (BLK, full), 1) < count
    zero = jnp.zeros((), BF)
    flip = (lane + lax.broadcasted_iota(jnp.int32, (BLK, 2 * DK), 0) == BLK - 1).astype(F32).astype(BF)
    dkt[...] = jnp.zeros_like(dkt)
    dvt[...] = jnp.zeros_like(dvt)
    dpt[...] = jnp.zeros_like(dpt)
    sum_q = jnp.zeros((1, 2 * DK), F32)
    sum_u = jnp.zeros((1, 2 * DK), F32)
    sum_v = jnp.zeros((1, 2 * DK), F32)
    for blk in range(full // BLK):
        i0 = blk * BLK
        base = full - BLK - i0
        rows = slice(i0, i0 + BLK)
        win = slice(base, base + full + BLK)
        if hook is not None:
            hook(blk)
        qu_t = qu[0, rows, :].astype(F32).T.astype(BF)
        do_t = do[0, rows, :].astype(F32).T.astype(BF)
        qv_t = tn(qv[0, rows, :], flip).astype(BF)
        dot_o = do[0, rows, :].astype(F32) * o[0, rows, :].astype(F32)
        parts_u, parts_v = [], []
        for h in range(2):
            mine = left if h == 0 else lane >= DK
            hs = slice(h * DK, h * DK + DK)
            q_u = jnp.where(mine, qu[0, rows, :], zero)
            q_v = jnp.where(mine, qv[0, rows, :], zero)
            d_o = jnp.where(mine, do[0, rows, :], zero)
            rel = nt(q_v, pos[win, :])
            rel = pltpu.roll(rel, full + 1, 1, stride=1, stride_axis=0)[:, :full]
            s = (nt(q_u, k[0]) + rel) * scale - lse[0, rows, h * DK : h * DK + 1]
            p = jnp.where(keep, jnp.exp(jnp.minimum(s, 0.0)), 0.0)
            delta = jnp.sum(jnp.where(mine, dot_o, 0.0), axis=1, keepdims=True)
            ds = (p * (nt(d_o, v[0]) - delta)).astype(BF)
            dvt[hs, :] += nn(do_t[hs, :], p.astype(BF))
            dkt[hs, :] += nn(qu_t[hs, :], ds)
            parts_u.append(nn(ds, k[0]))
            wide = jnp.concatenate([nn(flip, ds), jnp.zeros((BLK, BLK), F32)], axis=1)
            wide = pltpu.roll(wide, 0, 1, stride=1, stride_axis=0).astype(BF)
            parts_v.append(nn(wide, pos[win, :]))
            dpt[hs, win] += nn(qv_t[hs, :], wide)
        d_u = jnp.where(left, parts_u[0], parts_u[1]) * scale
        d_v = jnp.where(left, parts_v[0], parts_v[1]) * scale
        high = d_v.astype(BF)
        low = (d_v - high.astype(F32)).astype(BF)
        d_q = (d_u + nn(flip, high) + nn(flip, low)).astype(BF)
        dq_ref[0, rows, :] = d_q
        sum_q += jnp.sum(d_q.astype(F32), axis=0, keepdims=True)
        sum_u += jnp.sum(d_u, axis=0, keepdims=True)
        sum_v += jnp.sum(d_v, axis=0, keepdims=True)
    dk_ref[0] = (dkt[...].T * scale).astype(BF)
    d_val = dvt[...].T.astype(BF)
    dv_ref[0] = d_val
    dpos_ref[0] = (dpt[...].T * scale).astype(BF)
    sum_ref[0, 0:1, :] = sum_q
    sum_ref[0, 1:2, :] = jnp.sum(d_val.astype(F32), axis=0, keepdims=True)
    sum_ref[0, 2:3, :] = sum_u
    sum_ref[0, 3:4, :] = sum_v
    sum_ref[0, 4:8, :] = jnp.zeros((4, 2 * DK), F32)


def attn_specs(rows, full, width):
    pairs = width // (2 * DK)
    main = pl.BlockSpec((1, full, 2 * DK), lambda u, p, n: (u, 0, p))
    pos = pl.BlockSpec((2 * full, 2 * DK), lambda u, p, n: (0, p))
    return (rows, pairs), main, pos


def attn_fwd_call(lens, qu, qv, k, v, pos):
    rows, full, width = qu.shape
    grid, main, pspec = attn_specs(rows, full, width)
    return pl.pallas_call(
        attn_fwd_kernel,
        grid_spec=pltpu.PrefetchScalarGridSpec(
            num_scalar_prefetch=1,
            grid=grid,
            in_specs=[main] * 4 + [pspec],
            out_specs=[main, main],
        ),
        out_shape=[
            jax.ShapeDtypeStruct((rows, full, width), BF),
            jax.ShapeDtypeStruct((rows, full, width), F32),
        ],
        compiler_params=dense_params(),
        name="attn_fwd",
    )(lens, qu, qv, k, v, pos)


def attn_bwd_call(lens, qu, qv, k, v, pos, o, lse, do, early=None, cid=None):
    rows, full, width = qu.shape
    grid, main, pspec = attn_specs(rows, full, width)
    args = [lens, qu, qv, k, v, pos, o, lse, do]
    in_specs = [main] * 4 + [pspec] + [main] * 3
    out_specs = [
        main,
        main,
        main,
        pl.BlockSpec((1, 2 * full, 2 * DK), lambda u, p, n: (u, 0, p)),
        pl.BlockSpec((1, 8, 2 * DK), lambda u, p, n: (u, 0, p)),
    ]
    scratch = [
        pltpu.VMEM((2 * DK, full), F32),
        pltpu.VMEM((2 * DK, full), F32),
        pltpu.VMEM((2 * DK, 2 * full), F32),
    ]
    out_shape = [jax.ShapeDtypeStruct((rows, full, width), BF)] * 3 + [
        jax.ShapeDtypeStruct((rows, 2 * full, width), BF),
        jax.ShapeDtypeStruct((rows, 8, width), F32),
    ]
    body, params = attn_bwd_kernel, dense_params()
    if early is not None:
        items = [split_owners(item) for item in early]
        pieces = pieces_of([item.shape[-1] for item in items], 512)
        owned = items[0].shape[-2]
        n_in, n_out, m = len(args) - 1, len(out_shape), len(items)
        args += items
        in_specs += [ANY] * m
        out_specs.append(pl.BlockSpec((owned, C_OWN), lambda u, p, n: (0, 0)))
        out_shape.append(jax.ShapeDtypeStruct((owned, C_OWN), F32))
        scratch += scatter_scratch(pieces, owned)
        params = comm_params(cid)

        def body(*refs):
            at = pl.program_id(0) * grid[1] + pl.program_id(1)
            last = grid[0] * grid[1] - 1
            ins, rest = refs[: 1 + n_in], refs[1 + n_in :]
            g_refs, rest = rest[:m], rest[m:]
            mains, o_ref, rest = rest[:n_out], rest[n_out], rest[n_out + 1 :]
            own, sems = rest[:3], rest[3:]
            start, advance, finish, rounds = scatter_steps(pieces, g_refs, o_ref, sems, 3)
            peers = link_peers(*place())

            @pl.when(at == 0)
            def _():
                hail(peers)

            def begin():
                hear(peers)
                for p in range(len(pieces)):
                    start(p)

            steps = [begin] + [lambda q=q: advance(q) for q in range(rounds)]
            attn_bwd_kernel(*ins, *mains, *own, hook=hooks_of(steps, at, last, full // BLK))

            @pl.when(at == last)
            def _():
                finish()

    return pl.pallas_call(
        body,
        grid_spec=pltpu.PrefetchScalarGridSpec(
            num_scalar_prefetch=1,
            grid=grid,
            in_specs=in_specs,
            out_specs=out_specs,
            scratch_shapes=scratch,
        ),
        out_shape=out_shape,
        compiler_params=params,
        name="attn_bwd",
    )(*args)


def hooks_of(steps, at, last, spots):
    def hook(blk):
        for i, step in enumerate(steps):
            where, spot = divmod(i * (last + 1) * (spots - 1) // len(steps), spots - 1)
            if spot + 1 == blk:

                @pl.when(at == where)
                def _(step=step):
                    step()

    return hook


MESH = pl.DeviceIdType.MESH
NZ, NY, NX = 4, 2, 2
ANY = pl.BlockSpec(memory_space=pl.ANY)
VM = pl.BlockSpec(memory_space=pltpu.VMEM)


def own_mesh(sizes):
    return sizes == (NZ * NY * NX, 2)


def place():
    dp = lax.axis_index("dp")
    return dp // (NY * NX), dp // NX % NY, dp % NX, lax.axis_index("tensor")


def dev(z, y, x, t):
    return (z * (NY * NX) + y * NX + x, t)


def hail(peers):
    barrier = pltpu.get_barrier_semaphore()
    for peer in peers:
        pl.semaphore_signal(barrier, inc=1, device_id=peer, device_id_type=MESH)


def hear(peers):
    pl.semaphore_wait(pltpu.get_barrier_semaphore(), len(peers))


def rcopy(src, dst, send, recv, peer):
    return pltpu.make_async_remote_copy(
        src_ref=src, dst_ref=dst, send_sem=send, recv_sem=recv, device_id=peer, device_id_type=MESH
    )


def link_peers(z, y, x, t):
    peers = [dev(lax.rem(z + d, NZ), y, x, t) for d in range(1, NZ)]
    return peers + [dev(z, 1 - y, x, t), dev(z, y, 1 - x, t), dev(z, y, x, 1 - t)]


def sum_scratch(shape):
    dma = pltpu.SemaphoreType.DMA
    return [
        pltpu.VMEM(shape, F32), pltpu.VMEM(shape, F32), pltpu.VMEM((3,) + shape, F32),
        pltpu.VMEM((7,) + shape, F32), dma((3,)), dma((3,)), dma((7,)), dma((7,)),
    ]


def sum_steps(scratch):
    x_s, mid, b1, b2, s1, r1, s2, r2 = scratch
    z, y, x, t = place()
    spot = (y * NX + x) * 2 + t
    zs = [dev(lax.rem(z + d, NZ), y, x, t) for d in range(1, NZ)]
    flat = [lax.rem(spot + d, 8) for d in range(1, 8)]
    plane = [dev(z, p // 4, p // 2 % 2, p % 2) for p in flat]

    def call(wait=False):
        hear(zs + plane) if wait else hail(zs + plane)

    def meet(o_ref, heard=False):
        first = [rcopy(x_s, b1.at[i], s1.at[i], r1.at[i], peer) for i, peer in enumerate(zs)]
        second = [rcopy(mid, b2.at[i], s2.at[i], r2.at[i], peer) for i, peer in enumerate(plane)]

        def one():
            if not heard:
                hear(zs + plane)
            for copy in first:
                copy.start()

        def two():
            for copy in first:
                copy.wait_recv()
            mid[...] = (x_s[...] + b1[0]) + (b1[1] + b1[2])
            for copy in second:
                copy.start()

        def three():
            for copy in second:
                copy.wait_recv()
            total = mid[...]
            for i in range(7):
                total = total + b2[i]
            o_ref[...] = total
            for copy in first + second:
                copy.wait_send()

        return one, two, three

    return call, meet


def comm_params(cid):
    return pltpu.CompilerParams(
        collective_id=cid, has_side_effects=True, vmem_limit_bytes=60 * 1024 * 1024
    )


def gathered_shape(packed):
    return jax.ShapeDtypeStruct((2, NZ, NY, NX) + packed.shape, packed.dtype)


def gather_scratch(n, groups=3):
    dma = pltpu.SemaphoreType.DMA
    return [dma((n, NZ - 1)), dma((n, NZ - 1))] + [dma((n,))] * 6 + [dma((groups,))]


LEAD = 2


def gather_events(pieces, xs, gs, sems):
    zs, zr, as_, ar, bs, br, cs, cr, own_sem = sems
    z, y, x, t = place()
    along_x, along_y = dev(z, y, 1 - x, t), dev(z, 1 - y, x, t)
    zc, ac, bc, cc = [], [], [], []
    for p, (i, start, w) in enumerate(pieces):
        c = pl.ds(start, w)
        g = gs[i]
        zc.append(
            [
                rcopy(
                    xs[i].at[:, c],
                    g.at[t, z, y, x, :, c],
                    zs.at[p, d - 1],
                    zr.at[p, d - 1],
                    dev(lax.rem(z + d, NZ), y, x, t),
                )
                for d in range(1, NZ)
            ]
        )
        line = g.at[t, :, y, x, :, c]
        ac.append(rcopy(line, line, as_.at[p], ar.at[p], along_x if p % 2 == 0 else along_y))
        half = g.at[t, :, y, :, :, c] if p % 2 == 0 else g.at[t, :, :, x, :, c]
        bc.append(rcopy(half, half, bs.at[p], br.at[p], along_y if p % 2 == 0 else along_x))
        full = g.at[t, :, :, :, :, c]
        cc.append(rcopy(full, full, cs.at[p], cr.at[p], dev(z, y, x, 1 - t)))

    def begin():
        own = [
            pltpu.make_async_copy(item, g.at[t, z, y, x], own_sem.at[i])
            for i, (item, g) in enumerate(zip(xs, gs))
        ]
        for copy in own:
            copy.start()
        for copies in zc[: 2 * LEAD]:
            for copy in copies:
                copy.start()
        for copy in own:
            copy.wait()

    def event(kind, q):
        for p in (2 * q, 2 * q + 1):
            if kind == "z":
                for copy in zc[p]:
                    copy.wait_recv()
                ac[p].start()
                for copy in zc[p + 2 * LEAD] if p + 2 * LEAD < len(pieces) else []:
                    copy.start()
            elif kind == "a":
                ac[p].wait_recv()
                bc[p].start()
            elif kind == "b":
                bc[p].wait_recv()
                cc[p].start()
            else:
                cc[p].wait_recv()

    def finish():
        for copy in sum(zc, []) + ac + bc + cc:
            copy.wait_send()

    return begin, event, finish


def gather_order(pieces):
    unit = [0.42 * (pieces[2 * q][2] + pieces[2 * q + 1][2]) / 512 for q in range(len(pieces) // 2)]
    order, at = [], 3.0
    waiting = []
    for q, step in enumerate(unit):
        at += 8 * step
        waiting.append((at + 2.5, q, "z"))
    free = 0.0
    while waiting:
        waiting.sort()
        now, q, kind = waiting.pop(0)
        order.append((now, kind, q))
        if kind in "za":
            free = max(free, now) + (4 if kind == "z" else 8) * unit[q]
            waiting.append((free + 2.5, q, "a" if kind == "z" else "b"))
        elif kind == "b":
            waiting.append((now + 1.8, q, "c"))
    return order


def small_steps(s_ref, v_ref, mid, b1, b2, s1, r1, s2, r2):
    z, y, x, t = place()
    spot = (y * NX + x) * 2 + t
    zs = [dev(lax.rem(z + d, NZ), y, x, t) for d in range(1, NZ)]
    flat = [lax.rem(spot + d, 8) for d in range(1, 8)]
    plane = [dev(z, p // 4, p // 2 % 2, p % 2) for p in flat]
    first = [rcopy(s_ref, b1.at[i], s1.at[i], r1.at[i], peer) for i, peer in enumerate(zs)]
    second = [rcopy(mid, b2.at[i], s2.at[i], r2.at[i], peer) for i, peer in enumerate(plane)]

    def begin():
        for copy in first:
            copy.start()

    def spread():
        for copy in first:
            copy.wait_recv()
        mid[...] = (s_ref[...] + b1[0]) + (b1[1] + b1[2])
        for copy in second:
            copy.start()

    def finish():
        for copy in second:
            copy.wait_recv()
        same, other = mid[...].astype(F32), b2[0].astype(F32)
        for i in range(1, 7):
            if i % 2 == 1:
                same = same + b2[i].astype(F32)
            else:
                other = other + b2[i].astype(F32)
        low = jnp.where(t == 0, same, other)
        high = jnp.where(t == 0, other, same)
        v_ref[...] = jnp.zeros_like(v_ref)
        for q in range(4):
            r = S_NORM + 14 * q
            v_ref[0:14, 128 * q : 128 * q + 128] = low[r : r + 14] + high[r : r + 14]
        for i, part in enumerate((low, high)):
            for q in range(2):
                c = slice((2 * i + q) * 128, (2 * i + q) * 128 + 128)
                v_ref[R_ATT:R_CV, c] = part[S_ATT + 4 * q : S_ATT + 4 * q + 4]
                v_ref[R_CV:R_B1, c] = part[S_CV + 13 * q : S_CV + 13 * q + 13]
            for q in range(8):
                r, c = 2 * i + q // 4, slice(q % 4 * 128, q % 4 * 128 + 128)
                v_ref[R_B1 + r : R_B1 + r + 1, c] = part[S_B1 + q : S_B1 + q + 1]
                v_ref[R_B2 + r : R_B2 + r + 1, c] = part[S_B2 + q : S_B2 + q + 1]
        for copy in first + second:
            copy.wait_send()

    return plane, begin, spread, finish


S_B1, S_ATT, S_CV, S_B2, S_NORM, S_ALL = 0, 8, 16, 42, 50, 112


def lanes_of(n, offset):
    at = lax.broadcasted_iota(jnp.int32, (n, 128), 0) + offset
    return (lax.broadcasted_iota(jnp.int32, (n, 128), 1) == at).astype(F32)


def prep_kernel(
    f1i, f1o, pos, qkv, f2i, f2o, ci, out, co, b1, att, cv, b2, norm,
    pa_ref, pb_ref, pc_ref, slab_ref, table_ref, slab, first_s, second_s,
):
    def put(ref, name, value, shift=0):
        start = SEG[name][0] + shift
        ref[:, start : start + value.shape[1]] = value

    for ref, name, item in (
        (pa_ref, "f1i", f1i), (pa_ref, "f1o", f1o), (pa_ref, "pos", pos), (pc_ref, "f2i", f2i),
        (pc_ref, "f2o", f2o), (pb_ref, "out", out), (pb_ref, "co", co),
    ):
        put(ref, name, item[...])
    for k in range(3):
        put(pa_ref, "qkv", qkv[k], k * qkv.shape[2])
    for k in range(2):
        put(pb_ref, "ci", ci[:, k, :], k * ci.shape[2])
    z, y, x, t = place()
    dp = z * (NY * NX) + y * NX + x
    sel = lanes_of(8, dp * 8).astype(BF)
    slab[...] = jnp.zeros_like(slab)
    slab[S_B1 : S_B1 + 8] = nn(b1[...], sel)
    for q in range(2):
        slab[S_ATT + 4 * q : S_ATT + 4 * q + 4] = nn(att[:, q, :], sel)
        slab[S_CV + 13 * q : S_CV + 13 * q + 13] = tn(cv[q], sel)
    slab[S_B2 : S_B2 + 8] = nn(b2[...], sel)
    at = dp * 2 + t
    here = nn(norm[...], lanes_of(16, lax.rem(at, 8) * 16).astype(BF))
    for q in range(4):
        slab[S_NORM + 14 * q : S_NORM + 14 * q + 14] = here * (at // 8 == q).astype(F32)
    slab_ref[...] = slab[...].astype(BF)
    fill_table(table_ref, first_s, second_s)


def prep_call(items, smalls, full, width):
    rows = items[0].shape[0]
    return pl.pallas_call(
        prep_kernel,
        in_specs=[VM] * 14,
        out_specs=[VM] * 5,
        out_shape=[
            jax.ShapeDtypeStruct((rows, C_A), BF),
            jax.ShapeDtypeStruct((rows, C_B), BF),
            jax.ShapeDtypeStruct((rows, C_C), BF),
            jax.ShapeDtypeStruct((S_ALL, 128), BF),
            jax.ShapeDtypeStruct((2 * full, width), BF),
        ],
        scratch_shapes=[pltpu.VMEM((S_ALL, 128), F32)] + [pltpu.VMEM((32, width), F32)] * 2,
        name="prepare",
    )(*items, *smalls)


def split_owners(item):
    return item.reshape(2, NZ, NY, NX, item.shape[1] // (NZ * NY * NX), item.shape[2])


def pieces_of(widths, step=256):
    pieces, at = [], 0
    for i, w in enumerate(widths):
        pieces += [(i, k, min(step, w), at + k) for k in range(0, w, step)]
        at += w
    return pieces


def scatter_scratch(pieces, rows):
    n = len(pieces)
    total = sum(piece[2] for piece in pieces)
    dma = pltpu.SemaphoreType.DMA
    shape = (rows, total)
    return [
        pltpu.VMEM((NZ, NY, NX) + shape, BF),
        pltpu.VMEM((NZ, NY, NX) + shape, BF),
        pltpu.VMEM((NZ, 2) + shape, BF),
        pltpu.VMEM((NZ,) + shape, BF),
        pltpu.VMEM((NZ - 1,) + shape, BF),
    ] + [dma((n,))] * 7 + [dma((n, NZ - 1))] * 2


def scatter_steps(pieces, g_refs, o_ref, scratch, lag):
    own, rc, ra, rb, rz, lsem, cs, cr, as_, ar, bs, br, zs, zr = scratch
    z, y, x, t = place()
    along_x, along_y = dev(z, y, 1 - x, t), dev(z, 1 - y, x, t)
    mate = dev(z, y, x, 1 - t)
    count = len(pieces)
    bufs, lc, cc, ac, bc, zc = [], [], [], [], [], []
    for p, (i, start, w, at) in enumerate(pieces):
        c = pl.ds(at, w)
        g = pl.ds(start, w)
        b = dict(
            own=own.at[:, :, :, :, c], rc=rc.at[:, :, :, :, c], ra=ra.at[:, :, :, c],
            rb=rb.at[:, :, c], rz=rz.at[:, :, c],
        )
        bufs.append(b)
        even = p % 2 == 0
        lc.append(
            pltpu.make_async_copy(g_refs[i].at[t, :, :, :, :, g], b["own"], lsem.at[p])
        )
        cc.append(rcopy(g_refs[i].at[1 - t, :, :, :, :, g], b["rc"], cs.at[p], cr.at[p], mate))
        away = b["own"].at[:, 1 - y] if even else b["own"].at[:, :, 1 - x]
        ac.append(rcopy(away, b["ra"], as_.at[p], ar.at[p], along_y if even else along_x))
        line = b["own"].at[:, y, 1 - x] if even else b["own"].at[:, 1 - y, x]
        bc.append(rcopy(line, b["rb"], bs.at[p], br.at[p], along_x if even else along_y))
        zc.append([])
        for d in range(1, NZ):
            far = lax.rem(z + d, NZ)
            zc[p].append(
                rcopy(
                    b["own"].at[far, y, x], b["rz"].at[d - 1], zs.at[p, d - 1], zr.at[p, d - 1],
                    dev(far, y, x, t),
                )
            )

    def start(p):
        lc[p].start()
        cc[p].start()

    def advance(q):
        if q < count:
            lc[q].wait()
            cc[q].wait_recv()
            b = bufs[q]

            @pl.loop(0, NZ)
            def _(i):
                b["own"][i] = b["own"][i] + b["rc"][i]

            ac[q].start()
        p = q - lag
        if 0 <= p < count:
            ac[p].wait_recv()
            b = bufs[p]

            @pl.loop(0, NZ)
            def _(i):
                if p % 2 == 0:
                    b["own"][i, y] = b["own"][i, y] + b["ra"][i]
                else:
                    b["own"][i, :, x] = b["own"][i, :, x] + b["ra"][i]

            bc[p].start()
        p = q - 2 * lag
        if 0 <= p < count:
            bc[p].wait_recv()
            b = bufs[p]

            @pl.loop(0, NZ)
            def _(i):
                b["own"][i, y, x] = b["own"][i, y, x] + b["rb"][i]

            for copy in zc[p]:
                copy.start()
        p = q - 3 * lag
        if 0 <= p < count:
            for copy in zc[p]:
                copy.wait_recv()
            b = bufs[p]
            total = b["own"][z, y, x].astype(F32)
            for d in range(NZ - 1):
                total = total + b["rz"][d].astype(F32)
            o_ref[:, pieces[p][3] : pieces[p][3] + pieces[p][2]] = total

    def finish():
        for copy in cc + ac + bc + sum(zc, []):
            copy.wait_send()

    return start, advance, finish, count + 3 * lag


def small_sum_steps(parts, ext, scratch):
    acc_s, bc_, bz, bp, bm, sc, rc, sz, rz, sp, rp, sm, rm = scratch
    z, y, x, t = place()
    dp = z * (NY * NX) + y * NX + x
    half = acc_s.shape[0] // 2
    mine = pl.ds(pl.multiple_of(t * half, 8), half)
    mate = dev(z, y, x, 1 - t)
    spot = y * NX + x
    zp = [dev(lax.rem(z + d, NZ), y, x, t) for d in range(1, NZ)]
    flat = [lax.rem(spot + d, 4) for d in range(1, 4)]
    pp = [dev(z, p // 2, p % 2, t) for p in flat]
    one = rcopy(acc_s, bc_, sc, rc, mate)
    two = [rcopy(acc_s.at[mine], bz.at[i], sz.at[i], rz.at[i], peer) for i, peer in enumerate(zp)]
    three = [rcopy(bz.at[3], bp.at[i], sp.at[i], rp.at[i], peer) for i, peer in enumerate(pp)]
    four = rcopy(bp.at[3], bm, sm, rm, mate)

    def a():
        acc_s[...] = jnp.zeros_like(acc_s)
        total = parts[0][...]
        for part in parts[1:]:
            total = total + part[...]
        acc_s[0:R_ALL] = total
        one.start()

    def b():
        one.wait()
        acc_s[...] = acc_s[...] + bc_[...]
        for copy in two:
            copy.start()

    def c():
        for copy in two:
            copy.wait()
        bz[3] = (acc_s[mine] + bz[0]) + (bz[1] + bz[2])
        for copy in three:
            copy.start()

    def d():
        for copy in three:
            copy.wait()
        bp[3] = (bz[3] + bp[0]) + (bp[1] + bp[2])
        four.start()
        ext[mine] = bp[3]

    def e():
        four.wait()
        ext[pl.ds(pl.multiple_of((1 - t) * half, 8), half)] = bm[...]

    return pp, [a, b, c, d, e]


def small_sum_scratch(width):
    dma = pltpu.SemaphoreType.DMA
    return [
        pltpu.VMEM((R_SUM, width), F32), pltpu.VMEM((R_SUM, width), F32),
        pltpu.VMEM((4, R_SUM // 2, width), F32), pltpu.VMEM((4, R_SUM // 2, width), F32),
        pltpu.VMEM((R_SUM // 2, width), F32), dma, dma, dma((3,)), dma((3,)), dma((3,)), dma((3,)), dma, dma,
    ]


def finish_kernel(
    oa, ob, ext, f1i, f1o, b1, qkv, pos, out, att, ci, co, cv, f2i, f2o, b2, norm
):
    def take(ref, name):
        start = OWN.get(name, SEG[name][0])
        return ref[:, start : start + SEG[name][1]]

    f1i[...] = take(oa, "f1i")
    f1o[...] = take(oa, "f1o")
    pos[...] = take(oa, "pos")
    f2i[...] = take(ob, "f2i")
    f2o[...] = take(ob, "f2o")
    out[...] = take(ob, "out")
    co[...] = take(ob, "co")
    for ref, src, name in ((qkv, oa, "qkv"), (ci, ob, "ci")):
        start, w = OWN.get(name, SEG[name][0]), SEG[name][1]
        n = 3 if name == "qkv" else 2
        for k in range(n):
            part = src[:, start + k * w // n : start + (k + 1) * w // n]
            if name == "qkv":
                ref[k] = part
            else:
                ref[:, k, :] = part
    z, y, x, t = place()
    dp = z * (NY * NX) + y * NX + x
    sel = lanes_of(8, dp * 8)

    def own(v, pick):
        return lax.dot_general(
            v, pick, (((1,), (1,)), ((), ())), precision=lax.Precision.HIGHEST,
            preferred_element_type=F32,
        )

    for q in range(2):
        c = pl.ds(pl.multiple_of((2 * t + q) * 128, 128), 128)
        att[:, q, :] = own(ext[R_ATT:R_CV, c], sel)
        cv[q] = own(sel, ext[R_CV:R_B1, c])
    for o, at in ((b1, R_B1), (b2, R_B2)):
        for q in range(8):
            r, c = at + q // 4, slice(q % 4 * 128, q % 4 * 128 + 128)
            line = jnp.where(t == 0, ext[r : r + 1, c], ext[r + 2 : r + 3, c])
            o[q : q + 1, :] = own(line, sel)
    at = dp * 2 + t
    lane = pl.ds(pl.multiple_of(at // 8 * 128, 128), 128)
    norm[...] = own(ext[0:14, lane], lanes_of(16, lax.rem(at, 8) * 16))


def finish_call(oa, ob, ext, rows):
    shapes = [
        (rows, 1024), (rows, 1024), (8, 8), (3, rows, 256), (rows, 256), (rows, 256), (4, 2, 8),
        (rows, 2, 256), (rows, 256), (2, 8, 13), (rows, 1024), (rows, 1024), (8, 8), (14, 16),
    ]
    f1i, f1o, b1, qkv, pos, out, att, ci, co, cv, f2i, f2o, b2, norm = pl.pallas_call(
        finish_kernel,
        in_specs=[VM] * 3,
        out_specs=[VM] * 14,
        out_shape=[jax.ShapeDtypeStruct(shape, F32) for shape in shapes],
        name="own_gradients",
    )(oa, ob, ext)
    return (
        f1i, f1o.T, b1, qkv.transpose(1, 0, 2), pos, out.T, att, ci, co.T, cv.transpose(2, 0, 1),
        f2i, f2o.T, b2, norm,
    )

SEG = {
    "f1i": (0, 1024), "f1o": (1024, 1024), "pos": (2048, 256), "qkv": (2304, 768),
    "ci": (0, 512), "out": (512, 256), "co": (768, 256),
    "f2i": (0, 1024), "f2o": (1024, 1024),
}
C_A, C_B, C_C = 3072, 1024, 2048
OWN = {"f2i": 0, "f2o": 1024, "ci": 2048, "out": 2560, "co": 2816}
C_OWN = 3072
R_ATT, R_CV, R_B1, R_B2, R_ALL, R_SUM = 14, 18, 31, 35, 40, 48
TB = 256
HC = 256


def seg_spec(name, depth):
    start, width = SEG[name]
    return pl.BlockSpec(
        (2, depth, width), lambda i, *_: (0, 0, start // width), pipeline_mode=pl.Buffered(1)
    )


def whole(shape):
    zeros = (0,) * len(shape)
    return pl.BlockSpec(shape, lambda i, *_: zeros)


def tall(rows, width):
    return pl.BlockSpec((rows, width), lambda i, *_: (i, 0))


def sig(v):
    return 0.5 * jnp.tanh(0.5 * v) + 0.5


def row(ref, i):
    return ref[i : i + 1, :]


def col_sum(v):
    return jnp.sum(v, axis=0, keepdims=True)


def ln_stats(v):
    centered = v - jnp.mean(v, axis=1, keepdims=True)
    inv = lax.rsqrt(jnp.mean(centered * centered, axis=1, keepdims=True) + norm_eps)
    return centered * inv, inv


def ln_back(up, scaled, inv, gain):
    g = up * gain
    return inv * (
        g
        - jnp.mean(g, axis=1, keepdims=True)
        - scaled * jnp.mean(g * scaled, axis=1, keepdims=True)
    )


def bias_half(vecs, at, t):
    return jnp.concatenate([row(vecs, at + 2 * t), row(vecs, at + 2 * t + 1)], axis=1)


def row_mask(start, rows, count):
    at = start + lax.broadcasted_iota(jnp.int32, (rows, 1), 0)
    return (at < count).astype(F32)


def ffn1_kernel(
    x_ref, table, w_in, w_out, w_qkv, w_pos, vecs,
    first_ref, z_ref, qu_ref, qv_ref, k_ref, v_ref, pos_ref,
):
    x = x_ref[...].astype(F32)
    scaled, _ = ln_stats(x)
    hn = (scaled * row(vecs, 0) + row(vecs, 1)).astype(BF)
    half = w_in.shape[2]
    y = row(vecs, 2)
    for t in range(2):
        z = nn(hn, w_in[t]) + bias_half(vecs, R_B1, t)
        for j in range(half // HC):
            z_ref[:, (2 * j + t) * HC : (2 * j + t + 1) * HC] = z[:, j * HC : (j + 1) * HC].astype(BF)
        y = y + nt((z * sig(z)).astype(BF), w_out[t])
    first = x + 0.5 * y
    first_ref[...] = first
    scaled, _ = ln_stats(first)
    hn = (scaled * row(vecs, 3) + row(vecs, 4)).astype(BF)
    part = w_qkv.shape[2] // 3
    for t in range(2):
        c = slice(t * part, (t + 1) * part)
        proj = nn(hn, w_qkv[t])
        q = proj[:, :part] + vecs[R_ATT : R_ATT + 1, c]
        qu_ref[:, c] = (q + vecs[R_ATT + 2 : R_ATT + 3, c]).astype(BF)
        qv_ref[:, c] = (q + vecs[R_ATT + 3 : R_ATT + 4, c]).astype(BF)
        k_ref[:, c] = proj[:, part : 2 * part].astype(BF)
        v_ref[:, c] = (proj[:, 2 * part :] + vecs[R_ATT + 1 : R_ATT + 2, c]).astype(BF)
        pos_ref[:, c] = nn(table[...], w_pos[t]).astype(BF)


def dense_params(mib=60):
    return pltpu.CompilerParams(vmem_limit_bytes=mib * 1024 * 1024)


def ffn1_call(x, table, g, vecs):
    tokens, width = x.shape
    steps = tokens // TB
    places = tall(table.shape[0] // steps, width)
    return pl.pallas_call(
        ffn1_kernel,
        grid=(steps,),
        in_specs=[
            tall(TB, width), places, seg_spec("f1i", width), seg_spec("f1o", width),
            seg_spec("qkv", width), seg_spec("pos", width), whole(vecs.shape),
        ],
        out_specs=[tall(TB, width), tall(TB, 4 * width)] + [tall(TB, width)] * 4 + [places],
        out_shape=[
            jax.ShapeDtypeStruct((tokens, width), F32),
            jax.ShapeDtypeStruct((tokens, 4 * width), BF),
        ]
        + [jax.ShapeDtypeStruct((tokens, width), BF)] * 4
        + [jax.ShapeDtypeStruct(table.shape, BF)],
        compiler_params=dense_params(),
        name="ffn1_forward",
    )(x, table, g, g, g, g, vecs)


FRONT_PIECES = (
    [(0, at + k, 128) for k in (0, 128) for at in (0, 1024)]
    + [(0, at + 256 * j, 256) for j in range(1, 4) for at in (0, 1024)]
    + [(0, 2048 + 256 * k, 256) for k in range(4)]
    + [(1, 0, 512), (1, 512, 512)]
    + [(2, at + 512 * j, 512) for j in range(2) for at in (0, 1024)]
)


def front_call(lens, x, table, packed_a, packed_b, packed_c, slab, batch, cid):
    tokens, width = x.shape
    full = tokens // batch
    pairs = width // (2 * DK)
    chunks = SEG["f1i"][1] // HC
    first_head = chunks + 1
    steps = first_head + batch * pairs
    order = gather_order(FRONT_PIECES)
    dma = pltpu.SemaphoreType.DMA
    small = [
        pltpu.VMEM(slab.shape, BF), pltpu.VMEM((3,) + slab.shape, BF),
        pltpu.VMEM((7,) + slab.shape, BF), dma((3,)), dma((3,)), dma((7,)), dma((7,)),
    ]
    heads_shape = (batch, full, width)
    scratch = [
        pltpu.VMEM((2, NZ, NY, NX) + packed_a.shape, BF),
        pltpu.VMEM((tokens, width), F32),
        pltpu.VMEM((tokens, width), BF),
    ]
    scratch += [pltpu.VMEM(heads_shape, BF)] * 5 + [pltpu.VMEM(heads_shape, F32)]
    scratch += [pltpu.VMEM(table.shape, BF), dma((10,))]
    n_own = len(scratch)

    def body(
        len_ref, x_ref, table_ref, xa_ref, xb_ref, xc_ref, s_ref,
        ga_ref, gb_ref, gc_ref, vecs, first_ref, z_ref, qu_ref, qv_ref, k_ref, v_ref, pos_ref, mix_ref,
        lse_ref, *rest,
    ):
        i = pl.program_id(0)
        ga, y_s, hn_s, qu, qv, k, v, mix, lse, pos, out_sem = rest[:n_own]
        smalls = rest[n_own : n_own + len(small)]
        begin, event, finish = gather_events(
            FRONT_PIECES, (xa_ref, xb_ref, xc_ref), (ga, gb_ref, gc_ref), rest[n_own + len(small) :]
        )
        plane, s_begin, s_spread, s_finish = small_steps(s_ref, vecs, *smalls)
        z, y, xx, t = place()
        sources = (ga, y_s, qu, qv, k, v, pos, mix, lse)
        targets = (ga_ref, first_ref, qu_ref, qv_ref, k_ref, v_ref, pos_ref, mix_ref, lse_ref)
        copies = [
            pltpu.make_async_copy(a, b, out_sem.at[n])
            for n, (a, b) in enumerate(zip(sources, targets))
        ]
        done = [0]

        def until(q):
            while True:
                _, kind, pair = order[done[0]]
                done[0] += 1
                event(kind, pair)
                if (kind, pair) == ("c", q):
                    break

        def weight(t, start, w):
            return ga[t, :, :, :, :, start : start + w].reshape(width, w)

        @pl.when(i == 0)
        def _():
            peers = [dev(lax.rem(z + d, NZ), y, xx, t) for d in range(1, NZ)] + plane
            hail(peers)

            @pl.loop(0, tokens // TB)
            def _(r):
                here = pl.ds(pl.multiple_of(r * TB, TB), TB)
                y_s[here, :] = ln_stats(x_ref[here, :].astype(F32))[0]

            hear(peers)
            begin()
            s_begin()
            for n in range(4):
                event(*order[n][1:])
            s_spread()
            for n in range(4, 7):
                event(*order[n][1:])
            done[0] = 7
            s_finish()

            @pl.loop(0, tokens // TB)
            def _(r):
                here = pl.ds(pl.multiple_of(r * TB, TB), TB)
                hn_s[here, :] = (y_s[here, :] * row(vecs, 0) + row(vecs, 1)).astype(BF)
                y_s[here, :] = jnp.zeros((TB, width), F32) + row(vecs, 2)

        for j in range(chunks):

            @pl.when(i == j)
            def _(j=j):
                until(j + 1)

        @pl.when(i < chunks)
        def _():
            at = pl.multiple_of(i * HC, HC)
            odd = lax.rem(i, 2) == 1
            @pl.loop(0, 2)
            def _(t):
                w_in = ga[t, :, :, :, :, pl.ds(at, HC)].reshape(width, HC)
                w_out = ga[t, :, :, :, :, pl.ds(1024 + at, HC)].reshape(width, HC)
                line = vecs[pl.ds(R_B1 + 2 * t + i // 2, 1), :]
                bias = jnp.where(odd, line[:, HC:], line[:, :HC])
                for k in range(tokens // TB):
                    here = slice(k * TB, (k + 1) * TB)
                    zf = nn(hn_s[here, :], w_in) + bias
                    z_ref[here, pl.ds(pl.multiple_of(t * HC, HC), HC)] = zf.astype(BF)
                    y_s[here, :] += nt((zf * sig(zf)).astype(BF), w_out)

        @pl.when(i == chunks)
        def _():

            @pl.loop(0, tokens // TB)
            def _(r):
                here = pl.ds(pl.multiple_of(r * TB, TB), TB)
                first = x_ref[here, :].astype(F32) + 0.5 * y_s[here, :]
                y_s[here, :] = first
                scaled, _ = ln_stats(first)
                hn_s[here, :] = (scaled * row(vecs, 3) + row(vecs, 4)).astype(BF)
            copies[1].start()
            until(chunks + 1)
            part = width // 2
            for t in range(2):
                c = slice(t * part, (t + 1) * part)
                pos[:, c] = nn(table_ref[...], weight(t, SEG["pos"][0], part)).astype(BF)
            copies[6].start()
            until(chunks + 2)
            copies[0].start()
            at = SEG["qkv"][0]
            @pl.loop(0, 2)
            def _(t):
                c = pl.ds(pl.multiple_of(t * part, part), part)

                lines = vecs[R_ATT:R_CV, :]
                lines = jnp.where(t == 0, lines[:, :part], lines[:, part:])

                @pl.loop(0, batch)
                def _(u):
                    hn = hn_s[pl.ds(pl.multiple_of(u * full, full), full), :]
                    q = nn(hn, weight(t, at, part)) + lines[0:1]
                    qu[u, :, c] = (q + lines[2:3]).astype(BF)
                    qv[u, :, c] = (q + lines[3:4]).astype(BF)
                    k[u, :, c] = nn(hn, weight(t, at + part, part)).astype(BF)
                    val = nn(hn, weight(t, at + 2 * part, part))
                    v[u, :, c] = (val + lines[1:2]).astype(BF)
            for n in (2, 3, 4, 5):
                copies[n].start()

        left = order[done[0] :]
        base = order[done[0] - 1][0] + 6.0
        blocks = full // BLK
        spots = batch * pairs * blocks
        slots = [min(max(int((now + 5.0 - base) / 0.9), 0), spots) for now, _, _ in left]

        def hook(blk):
            for slot, (_, kind, pair) in zip(slots, left):
                if slot % blocks == blk and slot < spots:

                    @pl.when(i == first_head + slot // blocks)
                    def _(kind=kind, pair=pair):
                        event(kind, pair)

        @pl.when(i >= first_head)
        def _():
            n = i - first_head
            u = n // pairs
            c = pl.ds(pl.multiple_of(lax.rem(n, pairs) * (2 * DK), 2 * DK), 2 * DK)

            def view(ref):
                return ref.at[pl.ds(u, 1), :, c]

            attn_fwd_kernel(
                len_ref, view(qu), view(qv), view(k), view(v), pos.at[:, c], view(mix), view(lse),
                u, hook,
            )

        @pl.when(i == steps - 1)
        def _():
            copies[7].start()
            copies[8].start()
            for slot, (_, kind, pair) in zip(slots, left):
                if slot >= spots:
                    event(kind, pair)
            finish()
            for copy in copies:
                copy.wait()

    def const(shape):
        return pl.BlockSpec(shape, lambda i, n: (0,) * len(shape), pipeline_mode=pl.Buffered(1))

    heads = jax.ShapeDtypeStruct(heads_shape, BF)
    return pl.pallas_call(
        body,
        grid_spec=pltpu.PrefetchScalarGridSpec(
            num_scalar_prefetch=1,
            grid=(steps,),
            in_specs=[
                const(x.shape), const(table.shape), const(packed_a.shape), const(packed_b.shape),
                const(packed_c.shape), const(slab.shape),
            ],
            out_specs=[
                ANY, ANY, ANY, pl.BlockSpec((R_ALL, width), lambda i, n: (0, 0)), ANY,
                pl.BlockSpec((tokens, 2 * HC), lambda i, n: (0, jnp.minimum(i, chunks - 1))),
            ]
            + [ANY] * 7,
            scratch_shapes=scratch + small + gather_scratch(len(FRONT_PIECES)),
        ),
        out_shape=[
            gathered_shape(packed_a),
            gathered_shape(packed_b),
            gathered_shape(packed_c),
            jax.ShapeDtypeStruct((R_ALL, width), F32),
            jax.ShapeDtypeStruct((tokens, width), F32),
            jax.ShapeDtypeStruct((tokens, 4 * width), BF),
            heads, heads, heads, heads,
            jax.ShapeDtypeStruct(table.shape, BF),
            heads,
            jax.ShapeDtypeStruct(heads_shape, F32),
        ],
        compiler_params=comm_params(cid),
        name="front",
    )(lens, x, table, packed_a, packed_b, packed_c, slab)


def fill_table(table_ref, first_s, second_s):
    length, width = table_ref.shape[0] // 2, table_ref.shape[1]
    step = 32
    cols = lax.broadcasted_iota(jnp.int32, (step, width), 1)
    rows = lax.broadcasted_iota(jnp.int32, (step, width), 0)
    rate = jnp.exp((cols // 2 * 2).astype(F32) * (-math.log(10000.0) / width))
    even = cols % 2 == 0
    big = (length - 1 - step * rows).astype(F32) * rate
    small = rows.astype(F32) * rate
    sin_big, cos_big = jnp.sin(big), jnp.cos(big)
    first = jnp.where(even, sin_big, cos_big)
    second = jnp.where(even, cos_big, -sin_big)
    cos_small, sin_small = jnp.cos(small), jnp.sin(small)
    first_s[...] = first
    second_s[...] = second

    @pl.loop(0, 2 * length // step)
    def _(a):
        one, two = first_s[pl.ds(a, 1), :], second_s[pl.ds(a, 1), :]
        block = one * cos_small - two * sin_small
        table_ref[pl.ds(pl.multiple_of(a * step, step), step), :] = block.astype(BF)


def table_call(full, width):
    return pl.pallas_call(
        fill_table,
        out_specs=VM,
        out_shape=jax.ShapeDtypeStruct((2 * full, width), BF),
        scratch_shapes=[pltpu.VMEM((32, width), F32)] * 2,
        name="position_table",
    )()


def conv1_kernel(
    lens, mixed, first, w_out, w_ci, vecs, second_ref, half_ref, conv_ref, stat_ref, pad
):
    u = pl.program_id(0)
    full = first.shape[0]
    count = lens[u]
    part = w_out.shape[2]
    y = row(vecs, 5)
    for t in range(2):
        y = y + nt(mixed[:, t * part : (t + 1) * part], w_out[t])
    second = first[...] + y
    second_ref[...] = second
    scaled, _ = ln_stats(second)
    hn = (scaled * row(vecs, 6) + row(vecs, 7)).astype(BF)
    mask = row_mask(0, full, count)
    pad[0:8, :] = jnp.zeros((8, part), F32)
    pad[full + 8 : full + 16, :] = jnp.zeros((8, part), F32)
    for t in range(2):
        c = slice(t * part, (t + 1) * part)
        proj = nn(hn, w_ci[t])
        za = proj[:, :part] + vecs[R_CV : R_CV + 1, c]
        zg = proj[:, part:] + vecs[R_CV + 1 : R_CV + 2, c]
        half_ref[:, 2 * t * part : (2 * t + 1) * part] = za.astype(BF)
        half_ref[:, (2 * t + 1) * part : (2 * t + 2) * part] = zg.astype(BF)
        pad[8 : full + 8, :] = za * sig(zg) * mask
        total = jnp.zeros((full, part), F32)
        for k in range(9):
            total = total + vecs[R_CV + 4 + k : R_CV + 5 + k, c] * pad[4 + k : 4 + k + full, :]
        conv_ref[:, c] = total
        kept = total * mask
        stat_ref[pl.ds(4 * u, 1), c] = col_sum(kept)
        stat_ref[pl.ds(4 * u + 1, 1), c] = col_sum(kept * total)
    for k in (2, 3):
        stat_ref[pl.ds(4 * u + k, 1), :] = jnp.full((1, 2 * part), 1.0, F32) * count.astype(F32)


def with_sum(kernel, spot, cid):
    def body(*refs):
        sums = refs[-8:]
        refs = list(refs[:-8])
        call, meet = sum_steps(sums)
        out = refs[spot]
        refs[spot] = sums[0]

        @pl.when(pl.program_id(0) == 0)
        def _():
            call()

        kernel(*refs)

        @pl.when(pl.program_id(0) == pl.num_programs(0) - 1)
        def _():
            for part in meet(out):
                part()

    return kernel if cid is None else body


def conv1_call(lens, mixed, first, g, vecs, cid=None):
    tokens, width = first.shape
    batch = lens.shape[0]
    full = tokens // batch
    return pl.pallas_call(
        with_sum(conv1_kernel, 9, cid),
        grid_spec=pltpu.PrefetchScalarGridSpec(
            num_scalar_prefetch=1,
            grid=(batch,),
            in_specs=[
                tall(full, width), tall(full, width), seg_spec("out", width),
                seg_spec("ci", width), whole(vecs.shape),
            ],
            out_specs=[
                tall(full, width), tall(full, 2 * width), tall(full, width),
                whole((4 * batch, width)),
            ],
            scratch_shapes=[pltpu.VMEM((full + 16, width // 2), F32)]
            + ([] if cid is None else sum_scratch((4 * batch, width))),
        ),
        out_shape=[
            jax.ShapeDtypeStruct((tokens, width), F32),
            jax.ShapeDtypeStruct((tokens, 2 * width), BF),
            jax.ShapeDtypeStruct((tokens, width), F32),
            jax.ShapeDtypeStruct((4 * batch, width), F32),
        ],
        compiler_params=dense_params() if cid is None else comm_params(cid),
        name="conv_forward",
    )(lens, mixed, first, g, g, vecs)


def bn_of(stats, u):
    n = stats[pl.ds(4 * u + 2, 1), :]
    avg = stats[pl.ds(4 * u, 1), :] / n
    var = stats[pl.ds(4 * u + 1, 1), :] / n - avg * avg
    return avg, lax.rsqrt(var + norm_eps), n


def swish_parts(z):
    s = sig(z)
    a = z * s
    return a, s + a * (1.0 - s)


def middle_kernel(
    lens, second, conv, cot, stats, w_co, w_in, w_out, vecs,
    act_ref, d3_ref, dy_ref, sum_ref, small_ref, gi_ref, go_ref, gc_ref,
    a_s, slope_s, gi, go, gc,
):
    i = pl.program_id(0)
    steps = pl.num_programs(0)
    rows, width = second.shape
    batch = lens.shape[0]
    per = steps // batch
    u = i // per
    mask = row_mask(lax.rem(i, per) * rows, rows, lens[u])

    @pl.when(i == 0)
    def _():
        small_ref[...] = jnp.zeros_like(small_ref)
        sum_ref[...] = jnp.zeros_like(sum_ref)
        gi[...] = jnp.zeros_like(gi)
        go[...] = jnp.zeros_like(go)
        gc[...] = jnp.zeros_like(gc)

    avg, rstd, _ = bn_of(stats, u)
    part = w_co.shape[2]
    half = w_in.shape[2]
    yhat = (conv[...] - avg) * rstd
    bn, bn_slope = swish_parts(yhat * row(vecs, R_CV + 2) + row(vecs, R_CV + 3))
    act = bn.astype(BF)
    y = row(vecs, 8)
    for t in range(2):
        y = y + nt(act[:, t * part : (t + 1) * part], w_co[t])
    third = second[...] + y
    scaled9, inv9 = ln_stats(third)
    hn = (scaled9 * row(vecs, 9) + row(vecs, 10)).astype(BF)
    y = row(vecs, 11)
    for t in range(2):
        c = slice(t * half, (t + 1) * half)
        a, slope = swish_parts(nn(hn, w_in[t]) + bias_half(vecs, R_B2, t))
        a = a.astype(BF)
        a_s[:, c] = a
        slope_s[:, c] = slope
        y = y + nt(a, w_out[t])
    scaled, inv = ln_stats(third + 0.5 * y)
    act_ref[...] = (scaled * row(vecs, 12) + row(vecs, 13)).astype(BF)
    up = cot[...].astype(F32) * mask
    small_ref[12:13, :] += col_sum(up * scaled)
    small_ref[13:14, :] += col_sum(up)
    d4 = ln_back(up, scaled, inv, row(vecs, 12))
    g = (0.5 * d4).astype(BF)
    small_ref[11:12, :] += col_sum(g.astype(F32))
    d_hn = jnp.zeros((rows, width), F32)
    for t in range(2):
        c = slice(t * half, (t + 1) * half)
        go[t] += tn(g, a_s[:, c])
        dz = (nn(g, w_out[t]) * slope_s[:, c]).astype(BF)
        bias = col_sum(dz.astype(F32))
        small_ref[R_B2 + 2 * t : R_B2 + 2 * t + 1, :] += bias[:, :width]
        small_ref[R_B2 + 2 * t + 1 : R_B2 + 2 * t + 2, :] += bias[:, width:]
        gi[t] += tn(hn, dz)
        d_hn = d_hn + nt(dz, w_in[t])
    small_ref[9:10, :] += col_sum(d_hn * scaled9)
    small_ref[10:11, :] += col_sum(d_hn)
    d3 = d4 + ln_back(d_hn, scaled9, inv9, row(vecs, 9))
    d3_ref[...] = d3
    g = d3.astype(BF)
    small_ref[8:9, :] += col_sum(g.astype(F32))
    d_act = []
    for t in range(2):
        gc[t] += tn(g, act[:, t * part : (t + 1) * part])
        d_act.append(nn(g, w_co[t]))
    d_bn = jnp.concatenate(d_act, axis=1) * bn_slope
    small_ref[R_CV + 2 : R_CV + 3, :] += col_sum(d_bn * yhat)
    small_ref[R_CV + 3 : R_CV + 4, :] += col_sum(d_bn)
    d_yhat = d_bn * row(vecs, R_CV + 2)
    dy_ref[...] = d_yhat
    sum_ref[pl.ds(4 * u, 1), :] += col_sum(d_yhat)
    sum_ref[pl.ds(4 * u + 1, 1), :] += col_sum(d_yhat * yhat)

    @pl.when(i == steps - 1)
    def _():
        gi_ref[...] = gi[...].astype(BF)
        go_ref[...] = go[...].astype(BF)
        gc_ref[...] = gc[...].astype(BF)


def grad_shape(name, width):
    return jax.ShapeDtypeStruct((2, width, SEG[name][1]), BF)


def acc(name, width):
    return pltpu.VMEM((2, width, SEG[name][1]), F32)


def once(shape):
    zeros = (0,) * len(shape)
    return pl.BlockSpec(shape, lambda i, *_: zeros, pipeline_mode=pl.Buffered(1))


def middle_call(lens, second, conv, cot, stats, g, g_f2, vecs, cid=None):
    tokens, width = second.shape
    small = (R_ALL, width)
    names = ("f2i", "f2o", "co")
    return pl.pallas_call(
        with_sum(middle_kernel, 12, cid),
        grid_spec=pltpu.PrefetchScalarGridSpec(
            num_scalar_prefetch=1,
            grid=(tokens // TB,),
            in_specs=[tall(TB, width)] * 3
            + [whole(stats.shape), seg_spec("co", width), seg_spec("f2i", width)]
            + [seg_spec("f2o", width), whole(vecs.shape)],
            out_specs=[tall(TB, width)] * 3
            + [whole(stats.shape), whole(small)]
            + [whole(grad_shape(name, width).shape) for name in names],
            scratch_shapes=[
                pltpu.VMEM((TB, 4 * width), BF),
                pltpu.VMEM((TB, 4 * width), F32),
            ]
            + [acc(name, width) for name in names]
            + ([] if cid is None else sum_scratch(stats.shape)),
        ),
        out_shape=[
            jax.ShapeDtypeStruct((tokens, width), BF),
            jax.ShapeDtypeStruct((tokens, width), F32),
            jax.ShapeDtypeStruct((tokens, width), F32),
            jax.ShapeDtypeStruct(stats.shape, F32),
            jax.ShapeDtypeStruct(small, F32),
        ]
        + [grad_shape(name, width) for name in names],
        compiler_params=dense_params() if cid is None else comm_params(cid),
        name="conv_out_ffn2",
    )(lens, second, conv, cot, stats, g, g_f2, g_f2, vecs)


def conv2_kernel(
    lens, dy, conv, d3, halves, second, mixed, stats, sums, w_ci, w_out, vecs,
    d2_ref, dm_ref, small_ref, gi_ref, go_ref, pad, dh_s, gi, go,
):
    u = pl.program_id(0)
    full, width = d3.shape
    part = w_out.shape[2]

    @pl.when(u == 0)
    def _():
        small_ref[...] = jnp.zeros_like(small_ref)
        gi[...] = jnp.zeros_like(gi)
        go[...] = jnp.zeros_like(go)

    avg, rstd, n = bn_of(stats, u)
    mask = row_mask(0, full, lens[u])
    scaled, inv = ln_stats(second[...])
    hn = (scaled * row(vecs, 6) + row(vecs, 7)).astype(BF)
    pad[0:8, :] = jnp.zeros((8, part), F32)
    pad[full + 8 : full + 16, :] = jnp.zeros((8, part), F32)
    b1 = sums[pl.ds(4 * u, 1), :]
    b2 = sums[pl.ds(4 * u + 1, 1), :]
    dh_s[...] = jnp.zeros_like(dh_s)
    taps = vecs[R_CV : R_CV + 13, :]

    @pl.loop(0, 2)
    def _(t):
        c = pl.ds(pl.multiple_of(t * part, part), part)

        def lanes(v):
            return jnp.where(t == 0, v[:, :part], v[:, part:])

        yhat = (conv[:, c] - lanes(avg)) * lanes(rstd)
        pad[8 : full + 8, :] = lanes(rstd) * (
            dy[:, c] - mask * ((lanes(b1) + yhat * lanes(b2)) / lanes(n))
        )
        za = halves[:, pl.ds(pl.multiple_of(2 * t * part, part), part)].astype(F32)
        zg = halves[:, pl.ds(pl.multiple_of((2 * t + 1) * part, part), part)].astype(F32)
        gate = sig(zg)
        gated = za * gate * mask
        total = jnp.zeros((full, part), F32)
        mine = lanes(taps)
        for k in range(9):
            moved = pad[12 - k : 12 - k + full, :]
            total = total + mine[4 + k : 5 + k, :] * moved
            small_ref[R_CV + 4 + k : R_CV + 5 + k, c] += col_sum(gated * moved)
        d_glu = total * mask
        d_a = (d_glu * gate).astype(BF)
        d_g = (d_glu * gated * (1.0 - gate)).astype(BF)
        small_ref[R_CV : R_CV + 1, c] += col_sum(d_a.astype(F32))
        small_ref[R_CV + 1 : R_CV + 2, c] += col_sum(d_g.astype(F32))
        pair = jnp.concatenate([d_a, d_g], axis=1)
        gi[t] += tn(hn, pair)
        dh_s[...] += nt(pair, w_ci[t])

    d_hn = dh_s[...]
    small_ref[6:7, :] += col_sum(d_hn * scaled)
    small_ref[7:8, :] += col_sum(d_hn)
    d2 = d3[...] + ln_back(d_hn, scaled, inv, row(vecs, 6))
    d2_ref[...] = d2
    g = d2.astype(BF)
    small_ref[5:6, :] += col_sum(g.astype(F32))
    @pl.loop(0, 2)
    def _(t):
        c = pl.ds(pl.multiple_of(t * part, part), part)
        go[t] += tn(g, mixed[:, c])
        dm_ref[:, c] = nn(g, w_out[t]).astype(BF)

    @pl.when(u == pl.num_programs(0) - 1)
    def _():
        gi_ref[...] = gi[...].astype(BF)
        go_ref[...] = go[...].astype(BF)


def conv2_call(lens, dy, conv, d3, halves, second, mixed, stats, sums, g, vecs):
    tokens, width = second.shape
    batch = lens.shape[0]
    full = tokens // batch
    small = (R_ALL, width)
    names = ("ci", "out")
    return pl.pallas_call(
        conv2_kernel,
        grid_spec=pltpu.PrefetchScalarGridSpec(
            num_scalar_prefetch=1,
            grid=(batch,),
            in_specs=[tall(full, width)] * 3
            + [tall(full, 2 * width), tall(full, width), tall(full, width)]
            + [whole(stats.shape)] * 2
            + [seg_spec("ci", width), seg_spec("out", width), whole(vecs.shape)],
            out_specs=[tall(full, width)] * 2
            + [whole(small)]
            + [whole(grad_shape(name, width).shape) for name in names],
            scratch_shapes=[
                pltpu.VMEM((full + 16, width // 2), F32), pltpu.VMEM((full, width), F32),
            ]
            + [acc(name, width) for name in names],
        ),
        out_shape=[
            jax.ShapeDtypeStruct((tokens, width), F32),
            jax.ShapeDtypeStruct((tokens, width), BF),
            jax.ShapeDtypeStruct(small, F32),
        ]
        + [grad_shape(name, width) for name in names],
        compiler_params=dense_params(),
        name="conv_backward",
    )(lens, dy, conv, d3, halves, second, mixed, stats, sums, g, g, vecs)


def last_kernel(
    dq, dk, dv, first, x_ref, d2, z_ref, table, dpos, asums, w_qkv, w_in, w_out, vecs,
    d0_ref, small_ref, d1_s, g_s, hn_s, dh_s, gq, gp, z_s, w_in_s, w_out_s, in_sem,
    put, ready, after,
):
    i = pl.program_id(0)
    blocks = x_ref.shape[0] // TB
    rows, width = first.shape
    part = w_qkv.shape[2] // 3
    ahead = [
        pltpu.make_async_copy(w_in.at[:, :, pl.ds(0, w_in_s.shape[2])], w_in_s, in_sem.at[0]),
        pltpu.make_async_copy(
            w_out.at[:, :, pl.ds(w_in_s.shape[2], w_in_s.shape[2])], w_out_s, in_sem.at[1]
        ),
        pltpu.make_async_copy(z_ref, z_s, in_sem.at[2]),
    ]

    @pl.when(i == 0)
    def _():
        small_ref[...] = jnp.zeros_like(small_ref)
        small_ref[R_ATT:R_CV, :] = jnp.sum(asums[...], axis=0)[0:4]
        for copy in ahead:
            copy.start()
        gq[...] = jnp.zeros_like(gq)
        gp[...] = jnp.zeros_like(gp)
        dh_s[...] = jnp.zeros_like(dh_s)

    @pl.when(i < blocks)
    def _():
        here = pl.ds(pl.multiple_of(i * TB, TB), TB)
        scaled, inv = ln_stats(first[...])
        hn = (scaled * row(vecs, 3) + row(vecs, 4)).astype(BF)
        d_hn = jnp.zeros((rows, width), F32)
        for t in range(2):
            c = slice(t * part, (t + 1) * part)
            dp = jnp.concatenate([dq[:, c], dk[:, c], dv[:, c]], axis=1)
            gq[t] += tn(hn, dp)
            for u in range(dpos.shape[0]):
                gp[t] += tn(table[...], dpos[u, :, c])
            d_hn = d_hn + nt(dp, w_qkv[t])
        small_ref[3:4, :] += col_sum(d_hn * scaled)
        small_ref[4:5, :] += col_sum(d_hn)
        d1 = d2[...] + ln_back(d_hn, scaled, inv, row(vecs, 3))
        d1_s[here, :] = d1
        g = (0.5 * d1).astype(BF)
        g_s[here, :] = g
        small_ref[2:3, :] += col_sum(g.astype(F32))
        scaled, inv = ln_stats(x_ref[here, :].astype(F32))
        hn_s[here, :] = (scaled * row(vecs, 0) + row(vecs, 1)).astype(BF)

    @pl.when(i == blocks - 1)
    def _():
        for t in range(2):
            put("pos", t, 0, gp[t])
            put("qkv", t, 0, gq[t])
        for copy in ahead:
            copy.wait()
        ready(-1)

    chunks = w_in_s.shape[2] // HC

    @pl.when(i >= blocks)
    def _():
        j = i - blocks
        at = pl.multiple_of(j * HC, HC)
        c = pl.ds(at, HC)
        odd = lax.rem(j, 2) == 1
        @pl.loop(0, 2)
        def _(t):
            zc = pl.ds(pl.multiple_of((2 * j + t) * HC, HC), HC)
            a, slope = swish_parts(z_s[:, zc].astype(F32))
            put("f1o", t, at, tn(g_s[...], a.astype(BF)))
            dz = (nn(g_s[...], w_out_s[t, :, c]) * slope).astype(BF)
            bias = col_sum(dz.astype(F32))
            none = jnp.zeros_like(bias)
            pair = [jnp.where(odd, none, bias), jnp.where(odd, bias, none)]
            line = pl.ds(R_B1 + 2 * t + j // 2, 1)
            small_ref[line, :] += jnp.concatenate(pair, axis=1)
            put("f1i", t, at, tn(hn_s[...], dz))
            dh_s[...] += nt(dz, w_in_s[t, :, c])
            for k in range(chunks):
                for side in range(2):

                    @pl.when((j == k) & (t == side))
                    def _(k=k, side=side):
                        after(k, side)

        for k in range(chunks):

            @pl.when(j == k)
            def _(k=k):
                ready(k)

    @pl.when(i == blocks + chunks - 1)
    def _():
        @pl.loop(0, blocks)
        def _(k):
            here = pl.ds(pl.multiple_of(k * TB, TB), TB)
            scaled, inv = ln_stats(x_ref[here, :].astype(F32))
            d_hn = dh_s[here, :]
            small_ref[0:1, :] += col_sum(d_hn * scaled)
            small_ref[1:2, :] += col_sum(d_hn)
            d0 = d1_s[here, :] + ln_back(d_hn, scaled, inv, row(vecs, 0))
            d0_ref[here, :] = d0.astype(BF)


def last_call(dq, dk, dv, first, x, d2, z, table, dpos, asums, g, vecs, others=None, cid=None):
    tokens, width = first.shape
    blocks, chunks = tokens // TB, SEG["f1i"][1] // HC
    small = (R_ALL, width)
    places = table.shape[0] // blocks

    def block(rows, cols):
        return pl.BlockSpec((rows, cols), lambda i: (jnp.minimum(i, blocks - 1), 0))

    in_specs = (
        [block(TB, width)] * 4
        + [whole(x.shape), block(TB, width)]
        + [ANY]
        + [block(places, width)]
        + [
            pl.BlockSpec(
                (dpos.shape[0], places, width), lambda i: (0, jnp.minimum(i, blocks - 1), 0)
            ),
            whole(asums.shape),
        ]
        + [seg_spec("qkv", width), ANY, ANY, whole(vecs.shape)]
    )
    args = [dq, dk, dv, first, x, d2, z, table, dpos, asums, g, g, g, vecs]
    scratch = [
        pltpu.VMEM((tokens, width), F32), pltpu.VMEM((tokens, width), BF),
        pltpu.VMEM((tokens, width), BF), pltpu.VMEM((tokens, width), F32),
        acc("qkv", width), acc("pos", width), pltpu.VMEM(z.shape, BF),
        pltpu.VMEM((2, width, SEG["f1i"][1]), BF), pltpu.VMEM((2, width, SEG["f1o"][1]), BF),
        pltpu.SemaphoreType.DMA((3,)),
    ]
    out_specs = [whole((tokens, width)), whole(small)]
    out_shape = [jax.ShapeDtypeStruct((tokens, width), BF), jax.ShapeDtypeStruct(small, F32)]
    n_own = len(scratch)
    if others is None:
        names = ("qkv", "f1i", "f1o", "pos")
        out_specs += [once(grad_shape(name, width).shape) for name in names]
        out_shape += [grad_shape(name, width) for name in names]

        def body(*refs):
            ins, rest = refs[: len(args)], refs[len(args) :]
            outs = dict(zip(names, rest[2:6]))

            def put(name, t, at, value):
                outs[name][t, :, pl.ds(at, value.shape[1])] = value.astype(BF)

            last_kernel(*ins, *rest[:2], *rest[6:], put, lambda j: None, lambda j, t: None)

        params = dense_params()
    else:
        owned = width // (NZ * NY * NX)
        names = ("pos", "qkv", "f1i", "f1o")
        base = {name: SEG[name][0] for name in names}
        order = [("pos", 0), ("qkv", 0), ("qkv", 256), ("qkv", 512)]
        for j in range(chunks):
            order += [("f1i", j * HC), ("f1o", j * HC)]
        pieces = [(0, base[name] + at, 256, base[name] + at) for name, at in order]
        n_first = 4
        n_in = len(args)
        args += list(others)
        in_specs += [whole(item.shape) for item in others]
        out_specs = out_specs[:1] + [whole((owned, C_A)), whole((R_SUM, width))]
        out_shape = out_shape[:1] + [
            jax.ShapeDtypeStruct((owned, C_A), F32), jax.ShapeDtypeStruct((R_SUM, width), F32)
        ]
        small_scratch = small_sum_scratch(width)
        scratch += [pltpu.VMEM(small, F32), pltpu.VMEM((2, NZ, NY, NX, owned, C_A), BF)]
        scratch += small_scratch + scatter_scratch(pieces, owned)
        params = comm_params(cid)

        def body(*refs):
            i = pl.program_id(0)
            ins, rest = refs[:n_in], refs[n_in:]
            parts, rest = rest[: len(others)], rest[len(others) :]
            (d0_ref, o_ref, ext), rest = rest[:3], rest[3:]
            own, rest = rest[:n_own], rest[n_own:]
            (small_ref, buf), rest = rest[:2], rest[2:]
            sums, sems = rest[: len(small_scratch)], rest[len(small_scratch) :]
            start, advance, finish, rounds = scatter_steps(pieces, [buf], o_ref, sems, 4)
            pp, small_list = small_sum_steps(list(parts) + [small_ref], ext, sums)
            z, y, x, t = place()

            def put(name, t, at, value):
                w = value.shape[1]
                at = base[name] + at
                at = at if isinstance(at, int) else pl.multiple_of(at, HC)
                value = value.astype(BF).reshape(NZ, NY, NX, owned, w)
                buf[t, :, :, :, :, pl.ds(at, w)] = value

            def ready(j):
                if j < 0:
                    hear(peers)
                for p in range(n_first) if j < 0 else (n_first + 2 * j, n_first + 2 * j + 1):
                    start(p)

            def after(j, t):
                if j == 0:
                    advance(2 * t)
                    advance(2 * t + 1)
                else:
                    advance(n_first + 2 * (j - 1) + t)

            peers = link_peers(z, y, x, t)[: NZ - 1] + pp + [dev(z, y, x, 1 - t)]

            @pl.when(i == 0)
            def _():
                hail(peers)

            last_kernel(*ins, d0_ref, small_ref, *own, put, ready, after)

            @pl.when(i == blocks + chunks - 1)
            def _():
                todo = [lambda q=q: advance(q) for q in range(n_first + 2 * (chunks - 1), rounds)]
                for k, step in enumerate(todo):
                    if k % 2 == 0 and k // 2 < len(small_list):
                        small_list[k // 2]()
                    step()
                for step in small_list[(len(todo) + 1) // 2 :]:
                    step()
                finish()

    return pl.pallas_call(
        body,
        grid=(blocks + chunks,),
        in_specs=in_specs,
        out_specs=out_specs,
        scratch_shapes=scratch,
        out_shape=out_shape,
        compiler_params=params,
        name="qkv_ffn1_backward",
    )(*args)


def gather_plain(big, kinds, groups, small_ins, both, n_dp):
    def pack(names):
        return jnp.concatenate(
            [big[n].T if kinds[n][0] == "flip" else big[n] for n in names], axis=1
        )

    def every(item):
        g = lax.all_gather(item, both, axis=0, tiled=True)
        g = g.reshape(n_dp, 2, item.shape[0], -1).transpose(1, 0, 2, 3)
        return g.reshape(2, n_dp * item.shape[0], -1)

    small = jnp.concatenate([item.reshape(-1) for item in small_ins])
    smalls = lax.all_gather(small, both, axis=0, tiled=False).reshape(n_dp, 2, -1).astype(F32)
    off = 0
    pieces = []
    for item in small_ins:
        pieces.append(smalls[:, :, off : off + item.size].reshape((n_dp, 2) + item.shape))
        off += item.size
    width = small_ins[4].shape[1] * n_dp * 2
    vecs = jnp.concatenate(
        [
            pieces[4].transpose(2, 0, 1, 3).reshape(-1, width),
            pieces[1].transpose(2, 1, 3, 0, 4).reshape(-1, width),
            pieces[2].transpose(2, 1, 3, 0, 4).reshape(-1, width),
            pieces[0].transpose(1, 2, 0, 3).reshape(-1, width),
            pieces[3].transpose(1, 2, 0, 3).reshape(-1, width),
            jnp.zeros((1, width), F32),
        ],
        axis=0,
    )
    return tuple(every(pack(names)) for names in groups) + (vecs,)


def scatter_plain(grads, kinds, names, small_g, small_ins, both, n_dp):
    vec_g = (
        small_g[R_B1:R_B2].reshape(1, -1), small_g[R_ATT:R_CV], small_g[R_CV:R_B1],
        small_g[R_B2 : R_B2 + 4].reshape(1, -1),
    )

    def small_of(item, like):
        item = item.reshape(item.shape[0], 2, like.shape[-2], n_dp, like.shape[-1])
        return item.transpose(1, 3, 0, 2, 4).reshape(2, n_dp, -1)

    cols = small_ins[4].shape[1]
    norm_g = small_g[:R_ATT].reshape(-1, n_dp, 2, cols).transpose(2, 1, 0, 3).reshape(2, n_dp, -1)
    packed = jnp.concatenate(
        [small_of(item, like) for item, like in zip(vec_g, small_ins)] + [norm_g], axis=2
    )
    packed = packed.swapaxes(0, 1).reshape(n_dp * 2, -1)
    own_small = lax.psum_scatter(packed, both, scatter_dimension=0, tiled=True).reshape(-1)
    wide = jnp.concatenate([grads[name] for name in names], axis=2)
    rows = wide.shape[1] // n_dp
    wide = wide.reshape(2, n_dp, rows, -1).swapaxes(0, 1).reshape(n_dp * 2 * rows, -1)
    own = lax.psum_scatter(wide, both, scatter_dimension=0, tiled=True).astype(F32)
    outs, at = {}, 0
    for name in names:
        w = grads[name].shape[2]
        item = own[:, at : at + w]
        outs[name] = item.T if kinds[name][0] == "flip" else item
        at += w
    small_outs, at = [], 0
    for item in small_ins:
        small_outs.append(own_small[at : at + item.size].reshape(item.shape))
        at += item.size
    return outs, small_outs


def local(
    frames,
    lengths,
    ffn1_in,
    ffn1_out,
    ffn1_bias,
    qkv_weight,
    pos_weight,
    out_weight,
    attn_bias,
    conv_in,
    conv_out,
    conv_channel,
    ffn2_in,
    ffn2_out,
    ffn2_bias,
    norm_params,
    cotangent,
):
    micro, seqs, full, width = frames.shape
    both = ("dp", "tensor")
    n_dp = lax.axis_size("dp")
    rows = ffn1_in.shape[0]
    batch = micro * seqs
    tokens = batch * full
    small_ins = (ffn1_bias, attn_bias, conv_channel, ffn2_bias, norm_params)
    names_a, names_b = ("f1i", "f1o", "pos", "qkv"), tuple(OWN)
    big = {
        "f1i": ffn1_in, "f1o": ffn1_out, "pos": pos_weight, "qkv": qkv_weight.reshape(rows, -1),
        "f2i": ffn2_in, "f2o": ffn2_out, "ci": conv_in.reshape(rows, -1), "out": out_weight,
        "co": conv_out,
    }
    kinds = {name: ("plain",) for name in big}
    kinds.update({name: ("flip",) for name in ("f1o", "f2o", "out", "co")})
    mine_mesh = own_mesh((n_dp, lax.axis_size("tensor"))) and rows % 16 == 0
    if mine_mesh:
        packed_a, packed_b, packed_c, slab, table = prep_call(
            [
                ffn1_in, ffn1_out.T, pos_weight, qkv_weight.transpose(1, 0, 2), ffn2_in,
                ffn2_out.T, conv_in, out_weight.T, conv_out.T,
            ],
            [ffn1_bias, attn_bias, conv_channel.transpose(1, 2, 0), ffn2_bias, norm_params],
            full, width,
        )
    else:
        table = table_call(full, width)
        groups = (names_a, names_b[2:], names_b[:2])
        g_a, g_b, g_c, vecs = gather_plain(big, kinds, groups, small_ins, both, n_dp)

    def reduce_sum(item):
        return item if mine_mesh else lax.psum(item, both)

    mine = lax.axis_index("tensor")
    lens = lax.dynamic_slice_in_dim(lengths, mine * seqs, seqs, 1).reshape(-1)
    x = frames.reshape(tokens, width)
    cot = cotangent.reshape(tokens, width)

    def utt(item):
        return item.reshape(batch, full, -1)

    def flat(item):
        return item.reshape(tokens, -1)

    if mine_mesh:
        g_a, g_b, g_c, vecs, first, z1, q_u, q_v, keys, values, pos, mixed, lse = front_call(
            lens, x, table, packed_a, packed_b, packed_c, slab, batch, 1
        )
        g_a, g_b, g_c = (item.reshape(2, width, -1) for item in (g_a, g_b, g_c))
        heads = (lens, q_u, q_v, keys, values, pos)
    else:
        first, z1, q_u, q_v, keys, values, pos = ffn1_call(x, table, g_a, vecs)
        heads = (lens, utt(q_u), utt(q_v), utt(keys), utt(values), pos)
        mixed, lse = attn_fwd_call(*heads)
    second, halves, conv, stats = conv1_call(
        lens, flat(mixed), first, g_b, vecs, 3 if mine_mesh else None
    )
    stats = reduce_sum(stats)
    grads = {}
    result, d3, d_yhat, sums, small_m, grads["f2i"], grads["f2o"], grads["co"] = middle_call(
        lens, second, conv, cot, stats, g_b, g_c, vecs, 4 if mine_mesh else None
    )
    sums = reduce_sum(sums)
    d2, d_mixed, small_c, grads["ci"], grads["out"] = conv2_call(
        lens, d_yhat, conv, d3, halves, second, flat(mixed), stats, sums, g_b, vecs
    )
    if mine_mesh:
        dq, dk, dv, dpos, asums, own_b = attn_bwd_call(
            *heads, mixed, lse, utt(d_mixed), [grads[name] for name in names_b], 5
        )
        d0, own_a, ext = last_call(
            flat(dq), flat(dk), flat(dv), first, x, d2, z1, table, dpos, asums, g_a, vecs,
            (small_m, small_c), 6,
        )
        outs = finish_call(own_a, own_b, ext, rows)
    else:
        dq, dk, dv, dpos, asums = attn_bwd_call(*heads, mixed, lse, utt(d_mixed))
        d0, small_l, grads["qkv"], grads["f1i"], grads["f1o"], grads["pos"] = last_call(
            flat(dq), flat(dk), flat(dv), first, x, d2, z1, table, dpos, asums, g_a, vecs
        )
        o, small_outs = scatter_plain(
            grads, kinds, names_a + names_b, small_m + small_c + small_l, small_ins, both, n_dp
        )
        outs = (
            o["f1i"], o["f1o"], small_outs[0], o["qkv"].reshape(qkv_weight.shape), o["pos"],
            o["out"], small_outs[1], o["ci"].reshape(conv_in.shape), o["co"], small_outs[2],
            o["f2i"], o["f2o"], small_outs[3], small_outs[4],
        )
    return (result.reshape(frames.shape), d0.reshape(frames.shape)) + tuple(outs)


def solution(mesh):
    in_specs = (
        P(None, ("dp", "tensor"), None, None),
        P(None, "dp"),
        P("dp", "tensor"),
        P("tensor", "dp"),
        P("tensor", "dp"),
        P("dp", None, "tensor"),
        P("dp", "tensor"),
        P("tensor", "dp"),
        P(None, "tensor", "dp"),
        P("dp", None, "tensor"),
        P("tensor", "dp"),
        P(None, "tensor", "dp"),
        P("dp", "tensor"),
        P("tensor", "dp"),
        P("tensor", "dp"),
        P(None, ("dp", "tensor")),
        P(None, ("dp", "tensor"), None, None),
    )
    out_specs = (
        P(None, ("dp", "tensor"), None, None),
        P(None, ("dp", "tensor"), None, None),
        P("dp", "tensor"),
        P("tensor", "dp"),
        P("tensor", "dp"),
        P("dp", None, "tensor"),
        P("dp", "tensor"),
        P("tensor", "dp"),
        P(None, "tensor", "dp"),
        P("dp", None, "tensor"),
        P("tensor", "dp"),
        P(None, "tensor", "dp"),
        P("dp", "tensor"),
        P("tensor", "dp"),
        P("tensor", "dp"),
        P(None, ("dp", "tensor")),
    )
    return jax.shard_map(local, mesh=mesh, in_specs=in_specs, out_specs=out_specs, check_vma=False)
```
